32 devices in a mesh: dp: 8 (over y, x, core), fsdp: 4 (over z).
Axes of the slice: x: 2, y: 2, z: 4, core: 2. Of those that a mesh axis runs over, the one named last changes fastest.
Arguments:
- hidden_in: bfloat16 [128, 288, 768], P(('dp', 'fsdp')), may hold values from -6 to 6
- token_mask: int32 [128, 288], P(('dp', 'fsdp')), may hold values from 0 to 1, as said below
- out_grad: bfloat16 [128, 288, 768], P(('dp', 'fsdp')), may hold values from -6 to 6
- query_embed: float32 [16, 128], replicated, may hold values from -1.2 to 1.2
- slot_valid: int32 [16, 8], replicated, may hold values from 0 to 1, as said below
- target_ids: int32 [16, 4], replicated, may hold values from 0 to 30463
- target_pos: int32 [16, 4], replicated, may hold values from 1 to 63
- query_weight: bfloat16 [768, 768], P(('dp', 'fsdp')), may hold values from -0.21875 to 0.21875
- key_weight: bfloat16 [768, 768], P(('dp', 'fsdp')), may hold values from -0.21875 to 0.21875
- value_weight: bfloat16 [768, 768], P(('dp', 'fsdp')), may hold values from -0.21875 to 0.21875
- out_weight: bfloat16 [768, 768], P(('dp', 'fsdp')), may hold values from -2.5 to 2.5
- inner_weight: bfloat16 [768, 3072], P(('dp', 'fsdp')), may hold values from -0.21875 to 0.21875
- outer_weight: bfloat16 [3072, 768], P(('dp', 'fsdp')), may hold values from -0.109375 to 0.109375
- retrieve_weight: bfloat16 [768, 128], P(('dp', 'fsdp')), may hold values from -0.21875 to 0.21875
- query_bias: bfloat16 [768], P(('dp', 'fsdp')), may hold values from -1.796875 to 1.796875
- value_bias: bfloat16 [768], P(('dp', 'fsdp')), may hold values from -1.796875 to 1.796875
- out_bias: bfloat16 [768], P(('dp', 'fsdp')), may hold values from -1.796875 to 1.796875
- norm1_gain: bfloat16 [768], P(('dp', 'fsdp')), may hold values from 0.5 to 1.5
- norm1_bias: bfloat16 [768], P(('dp', 'fsdp')), may hold values from -1.796875 to 1.796875
- inner_bias: bfloat16 [3072], P(('dp', 'fsdp')), may hold values from -1.796875 to 1.796875
- outer_bias: bfloat16 [768], P(('dp', 'fsdp')), may hold values from -1.796875 to 1.796875
- norm2_gain: bfloat16 [768], P(('dp', 'fsdp')), may hold values from 0.5 to 1.5
- norm2_bias: bfloat16 [768], P(('dp', 'fsdp')), may hold values from -1.796875 to 1.796875
- embedding: bfloat16 [30464, 768], P(('dp', 'fsdp')), may hold values from -0.6484375 to 0.6484375
- vocab_bias: bfloat16 [30464], P(('dp', 'fsdp')), may hold values from -3 to 3
Outputs:
- layer_out: bfloat16 [128, 288, 768], P(('dp', 'fsdp'))
- pair_loglik: float32 [64], P(('dp', 'fsdp'))
- input_grad: float32 [128, 288, 768], P(('dp', 'fsdp'))
- grad_query_weight: float32 [768, 768], P(('dp', 'fsdp'))
- grad_key_weight: float32 [768, 768], P(('dp', 'fsdp'))
- grad_value_weight: float32 [768, 768], P(('dp', 'fsdp'))
- grad_out_weight: float32 [768, 768], P(('dp', 'fsdp'))
- grad_inner_weight: float32 [768, 3072], P(('dp', 'fsdp'))
- grad_outer_weight: float32 [3072, 768], P(('dp', 'fsdp'))
- grad_retrieve_weight: float32 [768, 128], P(('dp', 'fsdp'))
- grad_query_bias: float32 [768], P(('dp', 'fsdp'))
- grad_value_bias: float32 [768], P(('dp', 'fsdp'))
- grad_out_bias: float32 [768], P(('dp', 'fsdp'))
- grad_norm1_gain: float32 [768], P(('dp', 'fsdp'))
- grad_norm1_bias: float32 [768], P(('dp', 'fsdp'))
- grad_inner_bias: float32 [3072], P(('dp', 'fsdp'))
- grad_outer_bias: float32 [768], P(('dp', 'fsdp'))
- grad_norm2_gain: float32 [768], P(('dp', 'fsdp'))
- grad_norm2_bias: float32 [768], P(('dp', 'fsdp'))
- grad_embedding: float32 [30464, 768], P(('dp', 'fsdp'))
- grad_vocab_bias: float32 [30464], P(('dp', 'fsdp'))
The draws below stay inside these ranges and needn't reach their ends.
Inputs may be any that keep to these rules, and one draw needn't show every extreme that they name: `token_mask`: each row is ones followed by zeros, with 144 to 288 ones; some row has 288 ones and some row 144. `slot_valid`: each row has 4 to 8 ones; some row has 4 and some row 8.
All inputs are finite; a program needn't handle non-finite values.
Results may differ from the reference program's by a relative error of at most 0.03.
Values may be sent and summed in bfloat16 or wider, within the bound.
A program may use at most 256 MiB of HBM per device.

```python
import math
import jax
import jax.numpy as jnp
import numpy as np
from jax import lax

D = 768
H = 12
HD = 64
FF = 3072
P_SIZE = 128
V = 30464
LEN = 288
QUERY_TOK = 64
MASKS = 4
SLOTS = 8
SLOT_DEV = 2
QDEV = 2
GROUP = 4
SEQS = 128
QUERIES = 16


def draw_token_mask(key, part):
    lengths = jax.random.randint(key, (SEQS,), LEN // 2, LEN + 1)
    lengths = lengths.at[0].set(LEN).at[1].set(LEN // 2)
    places = jnp.arange(LEN, dtype=jnp.int32)[None, :]
    return (places < lengths[:, None]).astype(jnp.int32)


def draw_slot_valid(key, part):
    count_key, order_key = jax.random.split(key)
    counts = jax.random.randint(count_key, (QUERIES,), 4, SLOTS + 1)
    counts = counts.at[0].set(4).at[1].set(SLOTS)
    order_keys = jax.random.split(order_key, QUERIES)
    ranks = jax.vmap(lambda sub_key: jax.random.permutation(sub_key, SLOTS))(order_keys)
    return (ranks < counts[:, None]).astype(jnp.int32)


def set_ends(result, rng, low, high):
    longest = result.shape.index(max(result.shape))
    spots = []
    for shift in (0, 1):
        where = [jax.random.randint(jax.random.fold_in(rng, axis), (), 0, length) for axis, length in enumerate(result.shape)]
        where[longest] = (where[longest] + shift) % result.shape[longest]
        spots.append(tuple(where))
    return result.at[spots[0]].set(low).at[spots[1]].set(high)


def level_of(rng, shape, shards, low, high):
    gain, own = 1.0, jax.random.fold_in(rng, 6)
    for position, shards_of in shards:
        heights = jnp.exp(jax.random.uniform(jax.random.fold_in(own, position), (shards_of,), jnp.float32, low / len(shards), high / len(shards)))
        gain = gain * jnp.repeat(heights, shape[position] // shards_of).reshape([-1 if axis == position else 1 for axis in range(len(shape))])
    return gain


def rank_bounds(number_of, slope):
    loads = [(1 << 20) // math.isqrt(grade ** slope) + 1 for grade in range(1, number_of + 1)]
    scale = 1 + sum(loads) // (1 << 30)
    return np.cumsum(np.array([max(1, weight // scale) for weight in loads]))


def skewed_ids(rng, extent, number_of, skew):
    listing = rank_bounds(number_of, skew)
    pick = jax.random.randint(jax.random.fold_in(rng, 1), extent, 0, int(listing[number_of - 1]))
    standing = jnp.searchsorted(jnp.asarray(listing, jnp.int32), pick, side="right")
    return jax.random.permutation(jax.random.fold_in(rng, 2), number_of)[standing].astype(jnp.int32)


def gaussian(key, dims, width, most, shards=(), kind=jnp.bfloat16):
    gain = level_of(key, dims, shards, -0.22, 0.18) if shards else 1.0
    drawn = jax.random.normal(key, dims, jnp.float32) * width * gain
    return jnp.minimum(jnp.maximum(drawn, -most), most).astype(kind)


def setup_inputs(seed: int = 0) -> dict:
    streams_of = jax.random.split(jax.random.key(seed), 26)
    hidden_in = gaussian(streams_of[0], (SEQS, LEN, D), 1.0, 6.0, ((0, 32),))
    token_mask = draw_token_mask(jax.random.fold_in(streams_of[25], 71), 0)
    out_grad = gaussian(streams_of[2], (SEQS, LEN, D), 1.0, 6.0, ((0, 32),))
    query_embed = gaussian(streams_of[3], (QUERIES, P_SIZE), 0.18, 1.2, (), jnp.float32)
    slot_valid = draw_slot_valid(jax.random.fold_in(streams_of[25], 71), 0)
    target_ids = set_ends(skewed_ids(streams_of[5], (QUERIES, MASKS), V, 2), jax.random.fold_in(streams_of[5], 3), 0, V - 1).astype(jnp.int32)
    target_pos = set_ends(jax.random.randint(streams_of[6], (QUERIES, MASKS), 1, QUERY_TOK), jax.random.fold_in(streams_of[6], 1), 1, QUERY_TOK - 1).astype(jnp.int32)
    query_weight = gaussian(streams_of[7], (D, D), D ** -0.5, 0.21875, ((0, 32),))
    key_weight = gaussian(streams_of[8], (D, D), D ** -0.5, 0.21875, ((0, 32),))
    value_weight = gaussian(streams_of[9], (D, D), D ** -0.5, 0.21875, ((0, 32),))
    out_weight = gaussian(streams_of[10], (D, D), (D * 2 // LEN) ** -0.5, 2.5, ((0, 32),))
    inner_weight = gaussian(streams_of[11], (D, FF), D ** -0.5, 0.21875, ((0, 32),))
    outer_weight = gaussian(streams_of[12], (FF, D), FF ** -0.5, 0.109375, ((0, 32),))
    retrieve_weight = gaussian(streams_of[13], (D, P_SIZE), D ** -0.5, 0.21875, ((0, 32),))
    query_bias = gaussian(streams_of[14], (D,), 0.3, 1.796875, ((0, 32),))
    value_bias = gaussian(streams_of[15], (D,), 0.3, 1.796875, ((0, 32),))
    out_bias = gaussian(streams_of[16], (D,), 0.3, 1.796875, ((0, 32),))
    norm1_gain = jnp.clip(1.0 + 0.1 * jax.random.normal(streams_of[17], (D,), jnp.float32), 0.5, 1.5).astype(jnp.bfloat16)
    norm1_bias = gaussian(streams_of[18], (D,), 0.3, 1.796875, ((0, 32),))
    inner_bias = gaussian(streams_of[19], (FF,), 0.3, 1.796875, ((0, 32),))
    outer_bias = gaussian(streams_of[20], (D,), 0.3, 1.796875, ((0, 32),))
    norm2_gain = jnp.clip(1.0 + 0.1 * jax.random.normal(streams_of[21], (D,), jnp.float32), 0.5, 1.5).astype(jnp.bfloat16)
    norm2_bias = gaussian(streams_of[22], (D,), 0.3, 1.796875, ((0, 32),))
    embedding = gaussian(streams_of[23], (V, D), (3.0 * D ** -0.5), 0.6484375, ((0, 32),))
    vocab_bias = gaussian(streams_of[24], (V,), 0.5, 3.0, ((0, 32),))
    return {"hidden_in": hidden_in, "token_mask": token_mask, "out_grad": out_grad, "query_embed": query_embed, "slot_valid": slot_valid, "target_ids": target_ids, "target_pos": target_pos, "query_weight": query_weight, "key_weight": key_weight, "value_weight": value_weight, "out_weight": out_weight, "inner_weight": inner_weight, "outer_weight": outer_weight, "retrieve_weight": retrieve_weight, "query_bias": query_bias, "value_bias": value_bias, "out_bias": out_bias, "norm1_gain": norm1_gain, "norm1_bias": norm1_bias, "inner_bias": inner_bias, "outer_bias": outer_bias, "norm2_gain": norm2_gain, "norm2_bias": norm2_bias, "embedding": embedding, "vocab_bias": vocab_bias}


@jax.custom_vjp
def low(v):
    return lax.optimization_barrier(v.astype(jnp.bfloat16)).astype(jnp.float32)

@jax.custom_vjp
def low_back(v):
    return v

def low_keep(v):
    return (low(v), None)

def low_pass(kept, grad):
    return (grad,)

def back_keep(v):
    return (v, None)

def back_low(kept, grad):
    return (low(grad),)
low.defvjp(low_keep, low_pass)
low_back.defvjp(back_keep, back_low)
EPS = 1e-12
NEG = -1000000000.0
HIGH = lax.Precision.HIGHEST
LOSS_WEIGHT = 32.0
block_seqs = 8

def as_float(array_in):
    return array_in.astype(jnp.float32)

def matmul(left, right):
    return jnp.dot(left, right, precision=HIGH)

def layer_norm(residual, gain_vec, shift_vec):
    row_mean = lax.optimization_barrier(jnp.mean(residual, -1, keepdims=True))
    centred = residual - row_mean
    row_var = lax.optimization_barrier(jnp.mean(centred * centred, -1, keepdims=True))
    return centred * lax.rsqrt(row_var + EPS) * gain_vec + shift_vec

def exact_gelu(pre_act):
    return jax.nn.gelu(pre_act, approximate=False)

def layer_block(layer_params, hidden, keys_ok):
    query_weight, key_weight, value_weight, out_weight, inner_weight, outer_weight, query_bias, value_bias, out_bias, norm1_gain, norm1_bias, inner_bias, outer_bias, norm2_gain, norm2_bias = layer_params
    seq_count = hidden.shape[0]
    head_shape = (seq_count, LEN, H, HD)
    flat_rows = hidden.reshape(seq_count * LEN, D)
    queries = low_back(low(matmul(flat_rows, query_weight) + query_bias)).reshape(head_shape)
    key_rows = low_back(low(matmul(flat_rows, key_weight))).reshape(head_shape)
    values = low_back(low(matmul(flat_rows, value_weight) + value_bias)).reshape(head_shape)
    scores = low_back(jnp.einsum('sqhe,skhe->shqk', queries, key_rows, precision=HIGH) * HD ** (-0.5))
    scores = jnp.where(keys_ok[:, None, None, :] > 0, scores, NEG)
    attn_probs = low(jax.nn.softmax(scores, axis=-1))
    attended = jnp.einsum('shqk,skhe->sqhe', attn_probs, values, precision=HIGH).reshape(seq_count * LEN, D)
    attended = low_back(low(attended))
    first_in = flat_rows + low_back(matmul(attended, out_weight)) + out_bias
    normed_one = low(layer_norm(first_in, norm1_gain, norm1_bias))
    pre_act = low_back(matmul(normed_one, inner_weight) + inner_bias)
    active = low(exact_gelu(pre_act))
    second_in = normed_one + low_back(matmul(active, outer_weight)) + outer_bias
    return low(layer_norm(second_in, norm2_gain, norm2_bias)).reshape(seq_count, LEN, D)

def sequence_maps():
    seq_index = jnp.arange(SEQS, dtype=jnp.int32)
    block_index = seq_index // (QDEV * SLOT_DEV)
    within = seq_index % (QDEV * SLOT_DEV)
    seq_query = block_index // GROUP * QDEV + within // SLOT_DEV
    seq_slot = block_index % GROUP * SLOT_DEV + within % SLOT_DEV
    return (seq_query, seq_slot)

def per_query(seq_values, slot_ok):
    arranged = jnp.where(slot_ok, seq_values, NEG)
    arranged = arranged.reshape(QUERIES // QDEV, GROUP, QDEV, SLOT_DEV).transpose(0, 2, 1, 3).reshape(QUERIES, SLOTS)
    return jax.nn.logsumexp(arranged, axis=-1)

def reference(hidden_in, token_mask, out_grad, query_embed, slot_valid, target_ids, target_pos, query_weight, key_weight, value_weight, out_weight, inner_weight, outer_weight, retrieve_weight, query_bias, value_bias, out_bias, norm1_gain, norm1_bias, inner_bias, outer_bias, norm2_gain, norm2_bias, embedding, vocab_bias):
    seq_query, seq_slot = sequence_maps()
    slot_ok = slot_valid[seq_query, seq_slot] > 0
    embeds = query_embed[seq_query]
    positions = target_pos[seq_query]
    targets = target_ids[seq_query].reshape(SEQS * MASKS, 1)
    layer_params = tuple(map(as_float, (query_weight, key_weight, value_weight, out_weight, inner_weight, outer_weight, query_bias, value_bias, out_bias, norm1_gain, norm1_bias, inner_bias, outer_bias, norm2_gain, norm2_bias)))
    vocab_params = (as_float(embedding), as_float(vocab_bias))
    checked = jax.checkpoint(layer_block)
    mask_blocks = token_mask.reshape(SEQS // block_seqs, block_seqs, LEN)

    def forward(layer_weights, retrieve_full, vocab_weights, hidden):
        hidden_blocks = hidden.reshape(SEQS // block_seqs, block_seqs, LEN, D)

        def one_block(pieces):
            return checked(layer_weights, pieces[0], pieces[1])
        layer_out = lax.map(one_block, (hidden_blocks, mask_blocks)).reshape(SEQS, LEN, D)
        projected = matmul(layer_out[:, 0, :], retrieve_full)
        retrieval = lax.optimization_barrier(jnp.sum(projected * embeds, -1))
        seq_ids = jnp.arange(SEQS, dtype=jnp.int32)
        picked = layer_out[seq_ids[:, None], positions].reshape(SEQS * MASKS, D)
        embed_full, bias_full = vocab_weights
        logits = low_back(matmul(picked, embed_full.T)) + bias_full
        lse_rows = jax.nn.logsumexp(logits, axis=-1)
        target_logit = jnp.take_along_axis(logits, targets, axis=1)[:, 0]
        seq_ll = lax.optimization_barrier(jnp.mean((target_logit - lse_rows).reshape(SEQS, MASKS), -1))
        log_marginal = per_query(retrieval + seq_ll, slot_ok) - per_query(retrieval, slot_ok)
        return (layer_out, log_marginal)
    (layer_out, log_marginal), pullback = jax.vjp(forward, layer_params, as_float(retrieve_weight), vocab_params, as_float(hidden_in))
    grad_layer, grad_retrieve, grad_vocab, grad_hidden = pullback((as_float(out_grad), -LOSS_WEIGHT * jnp.ones_like(log_marginal)))
    pair_query = seq_query[::SLOT_DEV]
    return (layer_out.astype(jnp.bfloat16), log_marginal[pair_query], grad_hidden, grad_layer[0], grad_layer[1], grad_layer[2], grad_layer[3], grad_layer[4], grad_layer[5], grad_retrieve, grad_layer[6], grad_layer[7], grad_layer[8], grad_layer[9], grad_layer[10], grad_layer[11], grad_layer[12], grad_layer[13], grad_layer[14], grad_vocab[0], grad_vocab[1])
```

```python
import functools

import jax
import jax.numpy as jnp
from jax import lax
from jax.experimental import pallas as pl
from jax.experimental.pallas import tpu as pltpu
from jax.sharding import PartitionSpec as P

MESH = pl.DeviceIdType.MESH
F32 = jnp.float32
BF = jnp.bfloat16


D = 768
H = 12
HD = 64
LEN = 288
MASKS = 4
SLOT_DEV = 2
GROUP = 4


EPS = 1e-12
NEG = -1000000000.0
HIGH = lax.Precision.HIGHEST
LOSS_WEIGHT = 32.0


def combined_all(value, axis, join):
    pieces = jax.tree.map(lambda part: lax.all_gather(part, axis), value)
    head = jax.tree.map(lambda part: part[0], pieces)
    tail = jax.tree.map(lambda part: part[1:], pieces)
    subtotal, _ = lax.scan(lambda subtotal, share: (join(subtotal, share), None), head, tail)
    return subtotal


def partner(value, axis, stride):
    mask = 2**stride
    pairs = [(source, source ^ mask) for source in range(lax.axis_size(axis))]
    return lax.ppermute(value, axis, pairs)


def layer_norm(residual, gain_vec, shift_vec):
    row_mean = jnp.mean(residual, -1, keepdims=True)
    centred = residual - row_mean
    row_var = jnp.mean(centred * centred, -1, keepdims=True)
    return centred * lax.rsqrt(row_var + EPS) * gain_vec + shift_vec


def exact_gelu(pre_act):
    return jax.nn.gelu(pre_act, approximate=False)


def collect_plain(params):
    (
        query_weight,
        key_weight,
        value_weight,
        out_weight,
        inner_weight,
        outer_weight,
        retrieve_weight,
        query_bias,
        value_bias,
        out_bias,
        norm1_gain,
        norm1_bias,
        inner_bias,
        outer_bias,
        norm2_gain,
        norm2_bias,
    ) = params
    return (
        lax.all_gather(query_weight, ("dp", "fsdp"), axis=0, tiled=True),
        lax.all_gather(key_weight, ("dp", "fsdp"), axis=0, tiled=True),
        lax.all_gather(value_weight, ("dp", "fsdp"), axis=0, tiled=True),
        lax.all_gather(out_weight, ("dp", "fsdp"), axis=0, tiled=True),
        lax.all_gather(inner_weight, ("dp", "fsdp"), axis=0, tiled=True),
        lax.all_gather(outer_weight, ("dp", "fsdp"), axis=0, tiled=True),
        lax.all_gather(retrieve_weight, ("dp", "fsdp"), axis=0, tiled=True),
        lax.all_gather(query_bias, ("dp", "fsdp"), axis=0, tiled=True),
        lax.all_gather(value_bias, ("dp", "fsdp"), axis=0, tiled=True),
        lax.all_gather(out_bias, ("dp", "fsdp"), axis=0, tiled=True),
        lax.all_gather(norm1_gain, ("dp", "fsdp"), axis=0, tiled=True),
        lax.all_gather(norm1_bias, ("dp", "fsdp"), axis=0, tiled=True),
        lax.all_gather(inner_bias, ("dp", "fsdp"), axis=0, tiled=True),
        lax.all_gather(outer_bias, ("dp", "fsdp"), axis=0, tiled=True),
        lax.all_gather(norm2_gain, ("dp", "fsdp"), axis=0, tiled=True),
        lax.all_gather(norm2_bias, ("dp", "fsdp"), axis=0, tiled=True),
    )


def spread_plain(grads):
    (
        grad_qw,
        grad_kw,
        grad_vw,
        grad_ow,
        grad_iw,
        grad_uw,
        grad_rw,
        grad_qb,
        grad_vb,
        grad_ob,
        grad_ga,
        grad_sa,
        grad_ib,
        grad_ub,
        grad_gb,
        grad_sb,
    ) = grads
    return (
        lax.psum_scatter(grad_qw, ("dp", "fsdp"), scatter_dimension=0, tiled=True),
        lax.psum_scatter(grad_kw, ("dp", "fsdp"), scatter_dimension=0, tiled=True),
        lax.psum_scatter(grad_vw, ("dp", "fsdp"), scatter_dimension=0, tiled=True),
        lax.psum_scatter(grad_ow, ("dp", "fsdp"), scatter_dimension=0, tiled=True),
        lax.psum_scatter(grad_iw, ("dp", "fsdp"), scatter_dimension=0, tiled=True),
        lax.psum_scatter(grad_uw, ("dp", "fsdp"), scatter_dimension=0, tiled=True),
        lax.psum_scatter(grad_rw, ("dp", "fsdp"), scatter_dimension=0, tiled=True),
        lax.psum_scatter(grad_qb, ("dp", "fsdp"), scatter_dimension=0, tiled=True),
        lax.psum_scatter(grad_vb, ("dp", "fsdp"), scatter_dimension=0, tiled=True),
        lax.psum_scatter(grad_ob, ("dp", "fsdp"), scatter_dimension=0, tiled=True),
        lax.psum_scatter(grad_ga, ("dp", "fsdp"), scatter_dimension=0, tiled=True),
        lax.psum_scatter(grad_sa, ("dp", "fsdp"), scatter_dimension=0, tiled=True),
        lax.psum_scatter(grad_ib, ("dp", "fsdp"), scatter_dimension=0, tiled=True),
        lax.psum_scatter(grad_ub, ("dp", "fsdp"), scatter_dimension=0, tiled=True),
        lax.psum_scatter(grad_gb, ("dp", "fsdp"), scatter_dimension=0, tiled=True),
        lax.psum_scatter(grad_sb, ("dp", "fsdp"), scatter_dimension=0, tiled=True),
    )


def coords():
    d = lax.axis_index("dp"); f = lax.axis_index("fsdp")
    return d // 4, (d // 2) % 2, d % 2, f

def dev(y, x, c, z):
    return ((y * 2 + x) * 2 + c, z)

def rdma(src, dst, ss, rs, to):
    return pltpu.make_async_remote_copy(src, dst, ss, rs, device_id=to, device_id_type=MESH)

def greet():
    y, x, c, z = coords()
    bar = pltpu.get_barrier_semaphore()
    tos = [dev(y, x, c, lax.rem(z + k, 4)) for k in (1, 2, 3)] + [dev(y, 1 - x, c, z), dev(1 - y, x, c, z), dev(y, x, 1 - c, z)]
    for t in tos:
        pl.semaphore_signal(bar, inc=1, device_id=t, device_id_type=MESH)
    pl.semaphore_wait(bar, len(tos))

class Gather:
    def __init__(self, src, dst, ss, rs, ls, a):
        self.src, self.dst, self.ss, self.rs, self.ls, self.a = src, dst, ss, rs, ls, a
        N = src.shape[-1]
        self.split = (N // 2) % 128 == 0
        self.h = N // 2
        self.y, self.x, self.c, self.z = coords()
        self.me = self.y * 2 + self.x
        self.xn = self.y * 2 + (1 - self.x)
        self.yn = (1 - self.y) * 2 + self.x
        self.dg = (1 - self.y) * 2 + (1 - self.x)
        self.sent = []
    def send(self, src, dst, slot, to):
        cp = rdma(src, dst, self.ss.at[self.a, slot], self.rs.at[self.a, slot], to)
        cp.start()
        self.sent.append(cp)
    def wait(self, ref, slot):
        rdma(ref, ref, self.ss.at[self.a, slot], self.rs.at[self.a, slot], dev(self.y, 1 - self.x, self.c, self.z)).wait_recv()
    def own(self):
        y, x, c, z = self.y, self.x, self.c, self.z
        d = self.dst.at[self.me, c, z]
        self.lc = pltpu.make_async_copy(self.src, d, self.ls.at[self.a])
        self.lc.start()
        self.send(self.src, d, 4, dev(y, 1 - x, c, z))
        self.send(self.src, d, 8, dev(1 - y, x, c, z))
        for k in (1, 3, 2):
            self.send(self.src, d, k, dev(y, x, c, lax.rem(z + k, 4)))
    def zrecv(self, k):
        y, x, c = self.y, self.x, self.c
        zz = lax.rem(self.z + 4 - k, 4)
        d = self.dst.at[self.me, c, zz]
        self.wait(d, k)
        self.send(d, d, 4 + k, dev(y, 1 - x, c, self.z))
        self.send(d, d, 8 + k, dev(1 - y, x, c, self.z))
    def column_core(self, col, slot):
        d = self.dst.at[col, self.c]
        self.send(d, d, 20 + slot, dev(self.y, self.x, 1 - self.c, self.z))
    def xyrecv(self, k):
        y, x, c = self.y, self.x, self.c
        zz = lax.rem(self.z + 4 - k, 4)
        dx = self.dst.at[self.xn, c, zz]
        self.wait(dx, 4 + k)
        if self.split:
            dxa = dx.at[:, pl.ds(0, self.h)]
            self.send(dxa, dxa, 12 + k, dev(1 - y, x, c, self.z))
        else:
            self.send(dx, dx, 12 + k, dev(1 - y, x, c, self.z))
        dy = self.dst.at[self.yn, c, zz]
        self.wait(dy, 8 + k)
        if self.split:
            dyb = dy.at[:, pl.ds(self.h, self.h)]
            self.send(dyb, dyb, 16 + k, dev(y, 1 - x, c, self.z))
    def dgrecv(self, k):
        zz = lax.rem(self.z + 4 - k, 4)
        d = self.dst.at[self.dg, self.c, zz]
        if self.split:
            self.wait(d.at[:, pl.ds(0, self.h)], 12 + k)
            self.wait(d.at[:, pl.ds(self.h, self.h)], 16 + k)
        else:
            self.wait(d, 12 + k)
    def finish(self):
        for slot, col in enumerate((self.me, self.xn, self.yn, self.dg)):
            self.wait(self.dst.at[col, 1 - self.c], 20 + slot)
        for cp in self.sent:
            cp.wait_send()

def ag_body(n, *refs):
    srcs, dsts = refs[:n], refs[n:2 * n]
    ss, rs, ls = refs[2 * n:]
    greet()
    gs = [Gather(srcs[a], dsts[a], ss, rs, ls, a) for a in range(n)]
    gs[0].own()
    for a in range(n + 1):
        if a + 1 < n:
            gs[a + 1].own()
        if a < n:
            for k in (1, 3, 2):
                gs[a].zrecv(k)
        if a >= 1:
            for k in (0, 1, 3, 2):
                gs[a - 1].dgrecv(k)
            gs[a - 1].column_core(gs[a - 1].dg, 3)
        if a < n:
            gs[a].lc.wait()
            gs[a].column_core(gs[a].me, 0)
            for k in (0, 1, 3, 2):
                gs[a].xyrecv(k)
            gs[a].column_core(gs[a].xn, 1)
            gs[a].column_core(gs[a].yn, 2)
    for g in gs:
        g.finish()

def all_gather_pallas(shards, cid=0, name="gather_weights"):
    n = len(shards)
    any_ = pl.BlockSpec(memory_space=pltpu.HBM)
    outs = pl.pallas_call(
        functools.partial(ag_body, n), name=name,
        out_shape=[jax.ShapeDtypeStruct((4, 2, 4) + s.shape, s.dtype) for s in shards],
        in_specs=[any_] * n, out_specs=[any_] * n,
        scratch_shapes=[pltpu.SemaphoreType.DMA((n, 24)), pltpu.SemaphoreType.DMA((n, 24)), pltpu.SemaphoreType.DMA((n,))],
        compiler_params=pltpu.CompilerParams(collective_id=cid, has_side_effects=True),
    )(*shards)
    return [o.reshape((32 * s.shape[0],) + s.shape[1:]) for o, s in zip(outs, shards)]


class Scatter:
    def __init__(self, g, out, bufs, ss, rs, ls, a):
        self.g, self.out, self.ss, self.rs, self.ls, self.a = g, out, ss, rs, ls, a
        self.own, self.rc, self.ray, self.rax, self.rbx, self.rby, self.rz = bufs
        self.N = g.shape[-1]
        self.split = (self.N // 2) % 128 == 0
        self.h = self.N // 2 if self.split else self.N
        self.y, self.x, self.c, self.z = coords()
        self.me = self.y * 2 + self.x
        self.sent = []
    def send(self, src, dst, slot, to):
        cp = rdma(src, dst, self.ss.at[self.a, slot], self.rs.at[self.a, slot], to)
        cp.start(); self.sent.append(cp)
    def wait(self, ref, slot):
        rdma(ref, ref, self.ss.at[self.a, slot], self.rs.at[self.a, slot], dev(self.y, 1 - self.x, self.c, self.z)).wait_recv()
    def core(self):
        y, x, c, z = self.y, self.x, self.c, self.z
        self.lc = []
        for j in range(4):
            cp = pltpu.make_async_copy(self.g.at[j, c], self.own.at[j], self.ls.at[self.a, j]); cp.start(); self.lc.append(cp)
            self.send(self.g.at[j, 1 - c], self.rc.at[j], j, dev(y, x, 1 - c, z))
    def add(self, dst, src):
        @pl.loop(0, 4)
        def _(i):
            dst[i] = (dst[i].astype(F32) + src[i].astype(F32)).astype(BF)
    def first(self):
        y, x, c, z, h = self.y, self.x, self.c, self.z, self.h
        for j in range(4):
            self.lc[j].wait()
            self.wait(self.rc.at[j], j)
        for j in range(4):
            self.add(self.own.at[j], self.rc.at[j])
        for xi in range(2):
            self.send(self.own.at[(1 - y) * 2 + xi, :, :, pl.ds(0, h)], self.ray.at[xi], 4 + xi, dev(1 - y, x, c, z))
        if self.split:
            for yi in range(2):
                self.send(self.own.at[yi * 2 + 1 - x, :, :, pl.ds(h, h)], self.rbx.at[yi], 8 + yi, dev(y, 1 - x, c, z))
    def second(self):
        y, x, c, z, h = self.y, self.x, self.c, self.z, self.h
        for xi in range(2):
            self.wait(self.ray.at[xi], 4 + xi)
            self.add(self.own.at[y * 2 + xi, :, :, pl.ds(0, h)], self.ray.at[xi])
        self.send(self.own.at[y * 2 + 1 - x, :, :, pl.ds(0, h)], self.rax, 6, dev(y, 1 - x, c, z))
        if self.split:
            for yi in range(2):
                self.wait(self.rbx.at[yi], 8 + yi)
                self.add(self.own.at[yi * 2 + x, :, :, pl.ds(h, h)], self.rbx.at[yi])
            self.send(self.own.at[(1 - y) * 2 + x, :, :, pl.ds(h, h)], self.rby, 10, dev(1 - y, x, c, z))
    def third(self):
        y, x, c, z, h = self.y, self.x, self.c, self.z, self.h
        self.wait(self.rax, 6)
        self.add(self.own.at[self.me, :, :, pl.ds(0, h)], self.rax)
        if self.split:
            self.wait(self.rby, 10)
            self.add(self.own.at[self.me, :, :, pl.ds(h, h)], self.rby)
        for k in (2, 1, 3):
            zz = lax.rem(z + k, 4)
            self.send(self.own.at[self.me, zz], self.rz.at[k - 1], 12 + k - 1, dev(y, x, c, zz))
    def last(self):
        for k in (1, 2, 3):
            self.wait(self.rz.at[k - 1], 12 + k - 1)
        t = self.own[self.me, self.z].astype(F32)
        for k in range(3):
            t = t + self.rz[k].astype(F32)
        self.out[...] = t
    def finish(self):
        for cp in self.sent:
            cp.wait_send()

def bufs_for(r, N):
    split = (N // 2) % 128 == 0
    h = N // 2 if split else N
    return [pltpu.VMEM((4, 4, r, N), BF), pltpu.VMEM((4, 4, r, N), BF), pltpu.VMEM((2, 4, r, h), BF), pltpu.VMEM((4, r, h), BF),
            pltpu.VMEM((2, 4, r, h), BF), pltpu.VMEM((4, r, h), BF), pltpu.VMEM((3, r, N), BF)]

def rs_body(n, *refs):
    gs, outs = refs[:n], refs[n:2 * n]
    ss, rs, ls = refs[2 * n:2 * n + 3]
    bufs = refs[2 * n + 3:]
    greet()
    sc = [Scatter(gs[a], outs[a], bufs[7 * a:7 * a + 7], ss, rs, ls, a) for a in range(n)]
    sc[0].core()
    for t in range(n + 3):
        if t + 1 < n: sc[t + 1].core()
        if 0 <= t < n: sc[t].first()
        if 0 <= t - 1 < n: sc[t - 1].second()
        if 0 <= t - 2 < n: sc[t - 2].third()
        if 0 <= t - 3 < n: sc[t - 3].last()
    for s in sc: s.finish()

def reduce_scatter_pallas(gs, cid=1, name="reduce_grads"):
    n = len(gs)
    shapes = [(g.shape[0] // 32, g.shape[1]) for g in gs]
    ins = [g.reshape((4, 2, 4) + s) for g, s in zip(gs, shapes)]
    return pl.pallas_call(
        functools.partial(rs_body, n), name=name,
        out_shape=[jax.ShapeDtypeStruct(s, F32) for s in shapes],
        in_specs=[pl.BlockSpec(memory_space=pltpu.HBM)] * n,
        out_specs=[pl.BlockSpec(memory_space=pltpu.VMEM)] * n,
        scratch_shapes=[pltpu.SemaphoreType.DMA((n, 16)), pltpu.SemaphoreType.DMA((n, 16)), pltpu.SemaphoreType.DMA((n, 4))] + sum([bufs_for(*s) for s in shapes], []),
        compiler_params=pltpu.CompilerParams(collective_id=cid, has_side_effects=True, vmem_limit_bytes=56 << 20),
    )(*ins)


def own_links():
    return lax.axis_size("dp") == 8 and lax.axis_size("fsdp") == 4


def pack_vectors(vectors, inner):
    block = jnp.pad(jnp.stack(vectors), ((0, 0), (0, 104)))
    return block.at[0, 32:].set(inner)


def collect(params):
    if not own_links():
        return collect_plain(params)
    qw, kw, vw, ow, iw, uw, rw, qb, vb, ob, ga, sa, ib, ub, gb, sb = params
    small = jnp.concatenate([rw, pack_vectors((qb, vb, ob, ga, sa, ub, gb, sb), ib)], 0)
    small, qkv, ow, iw, uw = all_gather_pallas((small, jnp.concatenate([qw, kw, vw], 1), ow, iw, uw))
    small = small.reshape(32, 32, 128)
    rw = small[:, :24].reshape(D, 128)
    vec = [small[:, 24 + k, :24].reshape(D) for k in range(8)]
    ib = small[:, 24, 32:].reshape(4 * D)
    qb, vb, ob, ga, sa, ub, gb, sb = vec
    return (qkv[:, :D], qkv[:, D : 2 * D], qkv[:, 2 * D :], ow, iw, uw, rw, qb, vb, ob, ga, sa, ib, ub, gb, sb)


def spread(grads):
    if not own_links():
        return spread_plain(grads)
    qw, kw, vw, ow, iw, uw, rw, qb, vb, ob, ga, sa, ib, ub, gb, sb = grads
    vec = jnp.stack([v.reshape(32, 24) for v in (qb, vb, ob, ga, sa, ub, gb, sb)], 1)
    vec = jnp.pad(vec, ((0, 0), (0, 0), (0, 104))).at[:, 0, 32:].set(ib.reshape(32, 96))
    small = jnp.concatenate([rw.reshape(32, 24, 128), vec], 1).reshape(1024, 128)
    parts = [uw, iw, ow, jnp.concatenate([qw, kw, vw], 1), small]
    uw, iw, ow, qkv, small = reduce_scatter_pallas([p.astype(BF) for p in parts])
    vec = small[24:]
    qb, vb, ob, ga, sa, ub, gb, sb = [vec[k, :24] for k in range(8)]
    return (qkv[:, :D], qkv[:, D : 2 * D], qkv[:, 2 * D :], ow, iw, uw, small[:24], qb, vb, ob, ga, sa, vec[0, 32:], ub, gb, sb)


def attention(query_heads, key_heads, value_heads, keys_ok):
    head_scale = HD ** (-0.5)
    scores = (
        jnp.einsum("sqhe,skhe->shqk", query_heads, key_heads, preferred_element_type=jnp.float32)
        * head_scale
    )
    scores = jnp.where(keys_ok[:, None, None, :] > 0, scores, NEG)
    row_peak = jnp.max(scores, -1, keepdims=True)
    exp_scores = jnp.exp(scores - row_peak)
    totals = jnp.sum(exp_scores, -1, keepdims=True)
    attn_probs = (exp_scores / totals).astype(jnp.bfloat16)
    attended = jnp.einsum(
        "shqk,skhe->sqhe", attn_probs, value_heads, preferred_element_type=jnp.float32
    )
    return (attended, row_peak + jnp.log(totals))


def forward_layer(hidden, keys_ok, gathered):
    (
        query_weight,
        key_weight,
        value_weight,
        out_weight,
        inner_weight,
        outer_weight,
        retrieve_weight,
        query_bias,
        value_bias,
        out_bias,
        norm1_gain,
        norm1_bias,
        inner_bias,
        outer_bias,
        norm2_gain,
        norm2_bias,
    ) = gathered
    seq_count = hidden.shape[0]
    head_shape = (seq_count, LEN, H, HD)
    flat_rows = hidden.reshape(seq_count * LEN, D)
    queries = (
        jnp.dot(flat_rows, query_weight, preferred_element_type=jnp.float32)
        + query_bias.astype(jnp.float32)
    ).astype(jnp.bfloat16)
    key_rows = jnp.dot(flat_rows, key_weight, preferred_element_type=jnp.float32).astype(
        jnp.bfloat16
    )
    values = (
        jnp.dot(flat_rows, value_weight, preferred_element_type=jnp.float32)
        + value_bias.astype(jnp.float32)
    ).astype(jnp.bfloat16)
    attended, log_totals = attention(
        queries.reshape(head_shape),
        key_rows.reshape(head_shape),
        values.reshape(head_shape),
        keys_ok,
    )
    attended = attended.reshape(seq_count * LEN, D).astype(jnp.bfloat16)
    first_in = (
        flat_rows.astype(jnp.float32)
        + jnp.dot(attended, out_weight, preferred_element_type=jnp.float32)
        + out_bias.astype(jnp.float32)
    )
    normed_one = layer_norm(
        first_in, norm1_gain.astype(jnp.float32), norm1_bias.astype(jnp.float32)
    ).astype(jnp.bfloat16)
    pre_act = jnp.dot(
        normed_one, inner_weight, preferred_element_type=jnp.float32
    ) + inner_bias.astype(jnp.float32)
    active = exact_gelu(pre_act).astype(jnp.bfloat16)
    second_in = (
        normed_one.astype(jnp.float32)
        + jnp.dot(active, outer_weight, preferred_element_type=jnp.float32)
        + outer_bias.astype(jnp.float32)
    )
    layer_out = layer_norm(
        second_in, norm2_gain.astype(jnp.float32), norm2_bias.astype(jnp.float32)
    ).astype(jnp.bfloat16)
    return (
        queries,
        key_rows,
        values,
        log_totals,
        attended,
        first_in,
        normed_one,
        pre_act,
        active,
        second_in,
        layer_out,
    )


def backward_layer(hidden, keys_ok, gathered, kept_acts, grad_out):
    (
        query_weight,
        key_weight,
        value_weight,
        out_weight,
        inner_weight,
        outer_weight,
        retrieve_weight,
        query_bias,
        value_bias,
        out_bias,
        norm1_gain,
        norm1_bias,
        inner_bias,
        outer_bias,
        norm2_gain,
        norm2_bias,
    ) = gathered
    (
        queries,
        key_rows,
        values,
        log_totals,
        attended,
        first_in,
        normed_one,
        pre_act,
        active,
        second_in,
        layer_out,
    ) = kept_acts
    seq_count = hidden.shape[0]
    head_shape = (seq_count, LEN, H, HD)
    flat_rows = hidden.reshape(seq_count * LEN, D)
    unused_two, norm_two_back = jax.vjp(
        layer_norm, second_in, norm2_gain.astype(jnp.float32), norm2_bias.astype(jnp.float32)
    )
    grad_second, grad_norm2_gain, grad_norm2_bias = norm_two_back(grad_out)
    second_low = grad_second.astype(jnp.bfloat16)
    grad_outer_weight = jnp.dot(active.T, second_low, preferred_element_type=jnp.float32)
    grad_outer_bias = jnp.sum(grad_second, 0)
    grad_active = jnp.dot(second_low, outer_weight.T, preferred_element_type=jnp.float32)
    unused_act, gelu_back = jax.vjp(exact_gelu, pre_act)
    grad_pre = gelu_back(grad_active)[0].astype(jnp.bfloat16)
    grad_inner_weight = jnp.dot(normed_one.T, grad_pre, preferred_element_type=jnp.float32)
    grad_inner_bias = jnp.sum(grad_pre.astype(jnp.float32), 0)
    grad_normed = grad_second + jnp.dot(
        grad_pre, inner_weight.T, preferred_element_type=jnp.float32
    )
    unused_one, norm_one_back = jax.vjp(
        layer_norm, first_in, norm1_gain.astype(jnp.float32), norm1_bias.astype(jnp.float32)
    )
    grad_first, grad_norm1_gain, grad_norm1_bias = norm_one_back(grad_normed)
    first_low = grad_first.astype(jnp.bfloat16)
    grad_out_weight = jnp.dot(attended.T, first_low, preferred_element_type=jnp.float32)
    grad_out_bias = jnp.sum(grad_first, 0)
    grad_attended = (
        jnp.dot(first_low, out_weight.T, preferred_element_type=jnp.float32)
        .astype(jnp.bfloat16)
        .reshape(head_shape)
    )
    query_heads = queries.reshape(head_shape)
    key_heads = key_rows.reshape(head_shape)
    value_heads = values.reshape(head_shape)
    head_scale = HD ** (-0.5)
    scores = (
        jnp.einsum("sqhe,skhe->shqk", query_heads, key_heads, preferred_element_type=jnp.float32)
        * head_scale
    )
    scores = jnp.where(keys_ok[:, None, None, :] > 0, scores, NEG)
    attn_probs = jnp.exp(scores - log_totals)
    grad_probs = jnp.einsum(
        "sqhe,skhe->shqk", grad_attended, value_heads, preferred_element_type=jnp.float32
    )
    grad_value_heads = jnp.einsum(
        "shqk,sqhe->skhe",
        attn_probs.astype(jnp.bfloat16),
        grad_attended,
        preferred_element_type=jnp.float32,
    )
    grad_scores = (
        attn_probs * (grad_probs - jnp.sum(attn_probs * grad_probs, -1, keepdims=True))
    ).astype(jnp.bfloat16)
    grad_query_heads = (
        jnp.einsum("shqk,skhe->sqhe", grad_scores, key_heads, preferred_element_type=jnp.float32)
        * head_scale
    )
    grad_key_heads = (
        jnp.einsum("shqk,sqhe->skhe", grad_scores, query_heads, preferred_element_type=jnp.float32)
        * head_scale
    )
    grad_queries = grad_query_heads.reshape(seq_count * LEN, D).astype(jnp.bfloat16)
    grad_keys = grad_key_heads.reshape(seq_count * LEN, D).astype(jnp.bfloat16)
    grad_values = grad_value_heads.reshape(seq_count * LEN, D).astype(jnp.bfloat16)
    grad_query_weight = jnp.dot(flat_rows.T, grad_queries, preferred_element_type=jnp.float32)
    grad_key_weight = jnp.dot(flat_rows.T, grad_keys, preferred_element_type=jnp.float32)
    grad_value_weight = jnp.dot(flat_rows.T, grad_values, preferred_element_type=jnp.float32)
    grad_query_bias = jnp.sum(grad_queries.astype(jnp.float32), 0)
    grad_value_bias = jnp.sum(grad_values.astype(jnp.float32), 0)
    grad_hidden = (
        grad_first
        + jnp.dot(grad_queries, query_weight.T, preferred_element_type=jnp.float32)
        + jnp.dot(grad_keys, key_weight.T, preferred_element_type=jnp.float32)
        + jnp.dot(grad_values, value_weight.T, preferred_element_type=jnp.float32)
    )
    return (
        grad_hidden,
        (
            grad_query_weight,
            grad_key_weight,
            grad_value_weight,
            grad_out_weight,
            grad_inner_weight,
            grad_outer_weight,
            grad_query_bias,
            grad_value_bias,
            grad_out_bias,
            grad_norm1_gain,
            grad_norm1_bias,
            grad_inner_bias,
            grad_outer_bias,
            grad_norm2_gain,
            grad_norm2_bias,
        ),
    )


def merge_pair(peak_one, total_one, peak_two, total_two):
    peak_new = jnp.maximum(peak_one, peak_two)
    return (
        peak_new,
        total_one * jnp.exp(peak_one - peak_new) + total_two * jnp.exp(peak_two - peak_new),
    )


def merge_rows(one_side, other_side):
    peak_new, total_new = merge_pair(one_side[0], one_side[1], other_side[0], other_side[1])
    return (peak_new, total_new, one_side[2] + other_side[2])


def slot_partial(score_vec, slot_ok):
    grouped = jnp.where(slot_ok, score_vec, NEG).reshape(-1, SLOT_DEV)
    ok_grouped = slot_ok.reshape(-1, SLOT_DEV)
    group_peak = jnp.max(grouped, -1)
    group_total = jnp.sum(jnp.where(ok_grouped, jnp.exp(grouped - group_peak[:, None]), 0.0), -1)
    return (group_peak, group_total)


def body(
    hidden_in,
    token_mask,
    out_grad,
    query_embed,
    slot_valid,
    target_ids,
    target_pos,
    query_weight,
    key_weight,
    value_weight,
    out_weight,
    inner_weight,
    outer_weight,
    retrieve_weight,
    query_bias,
    value_bias,
    out_bias,
    norm1_gain,
    norm1_bias,
    inner_bias,
    outer_bias,
    norm2_gain,
    norm2_bias,
    embedding,
    vocab_bias,
):
    params = (
        query_weight,
        key_weight,
        value_weight,
        out_weight,
        inner_weight,
        outer_weight,
        retrieve_weight,
        query_bias,
        value_bias,
        out_bias,
        norm1_gain,
        norm1_bias,
        inner_bias,
        outer_bias,
        norm2_gain,
        norm2_bias,
    )
    gathered = collect(params)
    kept_acts = forward_layer(hidden_in, token_mask, gathered)
    seq_count = hidden_in.shape[0]
    query_count = seq_count // SLOT_DEV
    out_seq = kept_acts[10].reshape(seq_count, LEN, D)
    devices = lax.axis_size("dp") * lax.axis_size("fsdp")
    device = lax.axis_index("dp") * lax.axis_size("fsdp") + lax.axis_index("fsdp")
    member = lax.axis_index("fsdp") % GROUP
    local_seq = jnp.arange(seq_count, dtype=jnp.int32)
    local_query = device // GROUP * query_count + local_seq // SLOT_DEV
    local_slot = member * SLOT_DEV + local_seq % SLOT_DEV
    slot_ok = slot_valid[local_query, local_slot] > 0
    embeds = query_embed[local_query]
    positions = target_pos[local_query]
    cls_rows = out_seq[:, 0, :].astype(jnp.float32)
    retrieve_full = gathered[6].astype(jnp.float32)
    projected = jnp.dot(cls_rows, retrieve_full, precision=HIGH)
    retrieval = jnp.sum(projected * embeds, -1)
    own_rows = seq_count * MASKS
    sent_rows = out_seq[local_seq[:, None], positions].reshape(own_rows, D)
    all_rows = lax.all_gather(sent_rows, ("dp", "fsdp"), axis=0, tiled=True)
    group_count = devices // GROUP
    all_targets = jnp.broadcast_to(
        target_ids.reshape(group_count, 1, query_count, 1, MASKS),
        (group_count, GROUP, query_count, SLOT_DEV, MASKS),
    ).reshape(-1)
    vocab_rows = embedding.shape[0]
    local_ids = all_targets - device * vocab_rows
    target_hit = jnp.arange(vocab_rows, dtype=jnp.int32)[None, :] == local_ids[:, None]
    logits = jnp.einsum(
        "rd,vd->rv", all_rows, embedding, preferred_element_type=jnp.float32
    ) + vocab_bias.astype(jnp.float32)
    row_peak = jnp.max(logits, -1)
    sum_exp = jnp.sum(jnp.exp(logits - row_peak[:, None]), -1)
    target_logit = jnp.sum(jnp.where(target_hit, logits, 0.0), -1)
    peak_all, total_all, target_all = combined_all(
        (row_peak, sum_exp, target_logit), ("dp", "fsdp"), merge_rows
    )
    lse_rows = peak_all + jnp.log(total_all)
    log_prob = lax.dynamic_slice_in_dim(target_all - lse_rows, device * own_rows, own_rows)
    seq_ll = jnp.mean(log_prob.reshape(seq_count, MASKS), -1)
    joint_score = retrieval + seq_ll
    joint_peak, joint_total = slot_partial(joint_score, slot_ok)
    prior_peak, prior_total = slot_partial(retrieval, slot_ok)
    for bit_number in range(GROUP.bit_length() - 1):
        far_joint_peak, far_joint_total, far_prior_peak, far_prior_total = partner(
            (joint_peak, joint_total, prior_peak, prior_total), "fsdp", bit_number
        )
        joint_peak, joint_total = merge_pair(
            joint_peak, joint_total, far_joint_peak, far_joint_total
        )
        prior_peak, prior_total = merge_pair(
            prior_peak, prior_total, far_prior_peak, far_prior_total
        )
    joint_lse = joint_peak + jnp.log(joint_total)
    prior_lse = prior_peak + jnp.log(prior_total)
    pair_loglik = joint_lse - prior_lse
    post_weight = jnp.where(slot_ok, jnp.exp(joint_score - jnp.repeat(joint_lse, SLOT_DEV)), 0.0)
    prior_weight = jnp.where(slot_ok, jnp.exp(retrieval - jnp.repeat(prior_lse, SLOT_DEV)), 0.0)
    grad_retrieval = LOSS_WEIGHT * (prior_weight - post_weight)
    row_scale = jnp.repeat(-LOSS_WEIGHT * post_weight / MASKS, MASKS)
    all_scales = lax.all_gather(row_scale, ("dp", "fsdp"), axis=0, tiled=True)
    vocab_probs = jnp.exp(logits - lse_rows[:, None])
    grad_logits = all_scales[:, None] * (target_hit.astype(jnp.float32) - vocab_probs)
    grad_vocab_bias = jnp.sum(grad_logits, 0)
    logits_low = grad_logits.astype(jnp.bfloat16)
    grad_embedding = jnp.einsum(
        "rv,rd->vd", logits_low, all_rows, preferred_element_type=jnp.float32
    )
    grad_picked = lax.psum_scatter(
        jnp.dot(logits_low, embedding, preferred_element_type=jnp.float32),
        ("dp", "fsdp"),
        scatter_dimension=0,
        tiled=True,
    )
    grad_project = grad_retrieval[:, None] * embeds
    grad_retrieve_weight = jnp.dot(cls_rows.T, grad_project, precision=HIGH)
    grad_cls = jnp.dot(grad_project, retrieve_full.T, precision=HIGH)
    grad_total = out_grad.astype(jnp.float32)
    grad_total = grad_total.at[local_seq[:, None], positions].add(
        grad_picked.reshape(seq_count, MASKS, D)
    )
    grad_total = grad_total.at[:, 0, :].add(grad_cls)
    grad_total = grad_total.reshape(seq_count * LEN, D)
    grad_hidden, layer_grads = backward_layer(
        hidden_in, token_mask, gathered, kept_acts, grad_total
    )
    (
        grad_query_weight,
        grad_key_weight,
        grad_value_weight,
        grad_out_weight,
        grad_inner_weight,
        grad_outer_weight,
        grad_query_bias,
        grad_value_bias,
        grad_out_bias,
        grad_norm1_gain,
        grad_norm1_bias,
        grad_inner_bias,
        grad_outer_bias,
        grad_norm2_gain,
        grad_norm2_bias,
    ) = layer_grads
    (
        shard_query_weight,
        shard_key_weight,
        shard_value_weight,
        shard_out_weight,
        shard_inner_weight,
        shard_outer_weight,
        shard_retrieve_weight,
        shard_query_bias,
        shard_value_bias,
        shard_out_bias,
        shard_norm1_gain,
        shard_norm1_bias,
        shard_inner_bias,
        shard_outer_bias,
        shard_norm2_gain,
        shard_norm2_bias,
    ) = spread(
        (
            grad_query_weight,
            grad_key_weight,
            grad_value_weight,
            grad_out_weight,
            grad_inner_weight,
            grad_outer_weight,
            grad_retrieve_weight,
            grad_query_bias,
            grad_value_bias,
            grad_out_bias,
            grad_norm1_gain,
            grad_norm1_bias,
            grad_inner_bias,
            grad_outer_bias,
            grad_norm2_gain,
            grad_norm2_bias,
        )
    )
    return (
        out_seq,
        pair_loglik,
        grad_hidden.reshape(seq_count, LEN, D),
        shard_query_weight,
        shard_key_weight,
        shard_value_weight,
        shard_out_weight,
        shard_inner_weight,
        shard_outer_weight,
        shard_retrieve_weight,
        shard_query_bias,
        shard_value_bias,
        shard_out_bias,
        shard_norm1_gain,
        shard_norm1_bias,
        shard_inner_bias,
        shard_outer_bias,
        shard_norm2_gain,
        shard_norm2_bias,
        grad_embedding,
        grad_vocab_bias,
    )


def solution(mesh):
    placed = (
        P(("dp", "fsdp"), None, None),
        P(("dp", "fsdp"), None),
        P(("dp", "fsdp"), None, None),
        P(),
        P(),
        P(),
        P(),
        P(("dp", "fsdp"), None),
        P(("dp", "fsdp"), None),
        P(("dp", "fsdp"), None),
        P(("dp", "fsdp"), None),
        P(("dp", "fsdp"), None),
        P(("dp", "fsdp"), None),
        P(("dp", "fsdp"), None),
        P(("dp", "fsdp")),
        P(("dp", "fsdp")),
        P(("dp", "fsdp")),
        P(("dp", "fsdp")),
        P(("dp", "fsdp")),
        P(("dp", "fsdp")),
        P(("dp", "fsdp")),
        P(("dp", "fsdp")),
        P(("dp", "fsdp")),
        P(("dp", "fsdp"), None),
        P(("dp", "fsdp")),
    )
    return jax.shard_map(
        body,
        mesh=mesh,
        in_specs=placed,
        out_specs=(
            P(("dp", "fsdp"), None, None),
            P(("dp", "fsdp")),
            P(("dp", "fsdp"), None, None),
            P(("dp", "fsdp"), None),
            P(("dp", "fsdp"), None),
            P(("dp", "fsdp"), None),
            P(("dp", "fsdp"), None),
            P(("dp", "fsdp"), None),
            P(("dp", "fsdp"), None),
            P(("dp", "fsdp"), None),
            P(("dp", "fsdp")),
            P(("dp", "fsdp")),
            P(("dp", "fsdp")),
            P(("dp", "fsdp")),
            P(("dp", "fsdp")),
            P(("dp", "fsdp")),
            P(("dp", "fsdp")),
            P(("dp", "fsdp")),
            P(("dp", "fsdp")),
            P(("dp", "fsdp"), None),
            P(("dp", "fsdp")),
        ),
        check_vma=False,
    )
```

```python
import functools

import jax
import jax.numpy as jnp
from jax import lax
from jax.experimental import pallas as pl
from jax.experimental.pallas import tpu as pltpu
from jax.sharding import PartitionSpec as P


D = 768
H = 12
HD = 64
LEN = 288
MASKS = 4
SLOT_DEV = 2
GROUP = 4


EPS = 1e-12
NEG = -1000000000.0
HIGH = lax.Precision.HIGHEST
LOSS_WEIGHT = 32.0


def combined_all(value, axis, join):
    pieces = jax.tree.map(lambda part: lax.all_gather(part, axis), value)
    head = jax.tree.map(lambda part: part[0], pieces)
    tail = jax.tree.map(lambda part: part[1:], pieces)
    subtotal, _ = lax.scan(lambda subtotal, share: (join(subtotal, share), None), head, tail)
    return subtotal


def partner(value, axis, stride):
    mask = 2**stride
    pairs = [(source, source ^ mask) for source in range(lax.axis_size(axis))]
    return lax.ppermute(value, axis, pairs)


def layer_norm(residual, gain_vec, shift_vec):
    row_mean = jnp.mean(residual, -1, keepdims=True)
    centred = residual - row_mean
    row_var = jnp.mean(centred * centred, -1, keepdims=True)
    return centred * lax.rsqrt(row_var + EPS) * gain_vec + shift_vec


def exact_gelu(pre_act):
    return jax.nn.gelu(pre_act, approximate=False)


def collect(params):
    (
        query_weight,
        key_weight,
        value_weight,
        out_weight,
        inner_weight,
        outer_weight,
        retrieve_weight,
        query_bias,
        value_bias,
        out_bias,
        norm1_gain,
        norm1_bias,
        inner_bias,
        outer_bias,
        norm2_gain,
        norm2_bias,
    ) = params
    return (
        lax.all_gather(query_weight, ("dp", "fsdp"), axis=0, tiled=True),
        lax.all_gather(key_weight, ("dp", "fsdp"), axis=0, tiled=True),
        lax.all_gather(value_weight, ("dp", "fsdp"), axis=0, tiled=True),
        lax.all_gather(out_weight, ("dp", "fsdp"), axis=0, tiled=True),
        lax.all_gather(inner_weight, ("dp", "fsdp"), axis=0, tiled=True),
        lax.all_gather(outer_weight, ("dp", "fsdp"), axis=0, tiled=True),
        lax.all_gather(retrieve_weight, ("dp", "fsdp"), axis=0, tiled=True),
        lax.all_gather(query_bias, ("dp", "fsdp"), axis=0, tiled=True),
        lax.all_gather(value_bias, ("dp", "fsdp"), axis=0, tiled=True),
        lax.all_gather(out_bias, ("dp", "fsdp"), axis=0, tiled=True),
        lax.all_gather(norm1_gain, ("dp", "fsdp"), axis=0, tiled=True),
        lax.all_gather(norm1_bias, ("dp", "fsdp"), axis=0, tiled=True),
        lax.all_gather(inner_bias, ("dp", "fsdp"), axis=0, tiled=True),
        lax.all_gather(outer_bias, ("dp", "fsdp"), axis=0, tiled=True),
        lax.all_gather(norm2_gain, ("dp", "fsdp"), axis=0, tiled=True),
        lax.all_gather(norm2_bias, ("dp", "fsdp"), axis=0, tiled=True),
    )


def spread(grads):
    (
        grad_qw,
        grad_kw,
        grad_vw,
        grad_ow,
        grad_iw,
        grad_uw,
        grad_rw,
        grad_qb,
        grad_vb,
        grad_ob,
        grad_ga,
        grad_sa,
        grad_ib,
        grad_ub,
        grad_gb,
        grad_sb,
    ) = grads
    return (
        lax.psum_scatter(grad_qw, ("dp", "fsdp"), scatter_dimension=0, tiled=True),
        lax.psum_scatter(grad_kw, ("dp", "fsdp"), scatter_dimension=0, tiled=True),
        lax.psum_scatter(grad_vw, ("dp", "fsdp"), scatter_dimension=0, tiled=True),
        lax.psum_scatter(grad_ow, ("dp", "fsdp"), scatter_dimension=0, tiled=True),
        lax.psum_scatter(grad_iw, ("dp", "fsdp"), scatter_dimension=0, tiled=True),
        lax.psum_scatter(grad_uw, ("dp", "fsdp"), scatter_dimension=0, tiled=True),
        lax.psum_scatter(grad_rw, ("dp", "fsdp"), scatter_dimension=0, tiled=True),
        lax.psum_scatter(grad_qb, ("dp", "fsdp"), scatter_dimension=0, tiled=True),
        lax.psum_scatter(grad_vb, ("dp", "fsdp"), scatter_dimension=0, tiled=True),
        lax.psum_scatter(grad_ob, ("dp", "fsdp"), scatter_dimension=0, tiled=True),
        lax.psum_scatter(grad_ga, ("dp", "fsdp"), scatter_dimension=0, tiled=True),
        lax.psum_scatter(grad_sa, ("dp", "fsdp"), scatter_dimension=0, tiled=True),
        lax.psum_scatter(grad_ib, ("dp", "fsdp"), scatter_dimension=0, tiled=True),
        lax.psum_scatter(grad_ub, ("dp", "fsdp"), scatter_dimension=0, tiled=True),
        lax.psum_scatter(grad_gb, ("dp", "fsdp"), scatter_dimension=0, tiled=True),
        lax.psum_scatter(grad_sb, ("dp", "fsdp"), scatter_dimension=0, tiled=True),
    )


def attention(query_heads, key_heads, value_heads, keys_ok):
    head_scale = HD ** (-0.5)
    scores = (
        jnp.einsum("sqhe,skhe->shqk", query_heads, key_heads, preferred_element_type=jnp.float32)
        * head_scale
    )
    scores = jnp.where(keys_ok[:, None, None, :] > 0, scores, NEG)
    row_peak = jnp.max(scores, -1, keepdims=True)
    exp_scores = jnp.exp(scores - row_peak)
    totals = jnp.sum(exp_scores, -1, keepdims=True)
    attn_probs = (exp_scores / totals).astype(jnp.bfloat16)
    attended = jnp.einsum(
        "shqk,skhe->sqhe", attn_probs, value_heads, preferred_element_type=jnp.float32
    )
    return (attended, row_peak + jnp.log(totals))


def forward_layer(hidden, keys_ok, gathered):
    (
        query_weight,
        key_weight,
        value_weight,
        out_weight,
        inner_weight,
        outer_weight,
        retrieve_weight,
        query_bias,
        value_bias,
        out_bias,
        norm1_gain,
        norm1_bias,
        inner_bias,
        outer_bias,
        norm2_gain,
        norm2_bias,
    ) = gathered
    seq_count = hidden.shape[0]
    head_shape = (seq_count, LEN, H, HD)
    flat_rows = hidden.reshape(seq_count * LEN, D)
    queries = (
        jnp.dot(flat_rows, query_weight, preferred_element_type=jnp.float32)
        + query_bias.astype(jnp.float32)
    ).astype(jnp.bfloat16)
    key_rows = jnp.dot(flat_rows, key_weight, preferred_element_type=jnp.float32).astype(
        jnp.bfloat16
    )
    values = (
        jnp.dot(flat_rows, value_weight, preferred_element_type=jnp.float32)
        + value_bias.astype(jnp.float32)
    ).astype(jnp.bfloat16)
    attended, log_totals = attention(
        queries.reshape(head_shape),
        key_rows.reshape(head_shape),
        values.reshape(head_shape),
        keys_ok,
    )
    attended = attended.reshape(seq_count * LEN, D).astype(jnp.bfloat16)
    first_in = (
        flat_rows.astype(jnp.float32)
        + jnp.dot(attended, out_weight, preferred_element_type=jnp.float32)
        + out_bias.astype(jnp.float32)
    )
    normed_one = layer_norm(
        first_in, norm1_gain.astype(jnp.float32), norm1_bias.astype(jnp.float32)
    ).astype(jnp.bfloat16)
    pre_act = jnp.dot(
        normed_one, inner_weight, preferred_element_type=jnp.float32
    ) + inner_bias.astype(jnp.float32)
    active = exact_gelu(pre_act).astype(jnp.bfloat16)
    second_in = (
        normed_one.astype(jnp.float32)
        + jnp.dot(active, outer_weight, preferred_element_type=jnp.float32)
        + outer_bias.astype(jnp.float32)
    )
    layer_out = layer_norm(
        second_in, norm2_gain.astype(jnp.float32), norm2_bias.astype(jnp.float32)
    ).astype(jnp.bfloat16)
    return (
        queries,
        key_rows,
        values,
        log_totals,
        attended,
        first_in,
        normed_one,
        pre_act,
        active,
        second_in,
        layer_out,
    )


def backward_layer(hidden, keys_ok, gathered, kept_acts, grad_out):
    (
        query_weight,
        key_weight,
        value_weight,
        out_weight,
        inner_weight,
        outer_weight,
        retrieve_weight,
        query_bias,
        value_bias,
        out_bias,
        norm1_gain,
        norm1_bias,
        inner_bias,
        outer_bias,
        norm2_gain,
        norm2_bias,
    ) = gathered
    (
        queries,
        key_rows,
        values,
        log_totals,
        attended,
        first_in,
        normed_one,
        pre_act,
        active,
        second_in,
        layer_out,
    ) = kept_acts
    seq_count = hidden.shape[0]
    head_shape = (seq_count, LEN, H, HD)
    flat_rows = hidden.reshape(seq_count * LEN, D)
    unused_two, norm_two_back = jax.vjp(
        layer_norm, second_in, norm2_gain.astype(jnp.float32), norm2_bias.astype(jnp.float32)
    )
    grad_second, grad_norm2_gain, grad_norm2_bias = norm_two_back(grad_out)
    second_low = grad_second.astype(jnp.bfloat16)
    grad_outer_weight = jnp.dot(active.T, second_low, preferred_element_type=jnp.float32)
    grad_outer_bias = jnp.sum(grad_second, 0)
    grad_active = jnp.dot(second_low, outer_weight.T, preferred_element_type=jnp.float32)
    unused_act, gelu_back = jax.vjp(exact_gelu, pre_act)
    grad_pre = gelu_back(grad_active)[0].astype(jnp.bfloat16)
    grad_inner_weight = jnp.dot(normed_one.T, grad_pre, preferred_element_type=jnp.float32)
    grad_inner_bias = jnp.sum(grad_pre.astype(jnp.float32), 0)
    grad_normed = grad_second + jnp.dot(
        grad_pre, inner_weight.T, preferred_element_type=jnp.float32
    )
    unused_one, norm_one_back = jax.vjp(
        layer_norm, first_in, norm1_gain.astype(jnp.float32), norm1_bias.astype(jnp.float32)
    )
    grad_first, grad_norm1_gain, grad_norm1_bias = norm_one_back(grad_normed)
    first_low = grad_first.astype(jnp.bfloat16)
    grad_out_weight = jnp.dot(attended.T, first_low, preferred_element_type=jnp.float32)
    grad_out_bias = jnp.sum(grad_first, 0)
    grad_attended = (
        jnp.dot(first_low, out_weight.T, preferred_element_type=jnp.float32)
        .astype(jnp.bfloat16)
        .reshape(head_shape)
    )
    query_heads = queries.reshape(head_shape)
    key_heads = key_rows.reshape(head_shape)
    value_heads = values.reshape(head_shape)
    head_scale = HD ** (-0.5)
    scores = (
        jnp.einsum("sqhe,skhe->shqk", query_heads, key_heads, preferred_element_type=jnp.float32)
        * head_scale
    )
    scores = jnp.where(keys_ok[:, None, None, :] > 0, scores, NEG)
    attn_probs = jnp.exp(scores - log_totals)
    grad_probs = jnp.einsum(
        "sqhe,skhe->shqk", grad_attended, value_heads, preferred_element_type=jnp.float32
    )
    grad_value_heads = jnp.einsum(
        "shqk,sqhe->skhe",
        attn_probs.astype(jnp.bfloat16),
        grad_attended,
        preferred_element_type=jnp.float32,
    )
    grad_scores = (
        attn_probs * (grad_probs - jnp.sum(attn_probs * grad_probs, -1, keepdims=True))
    ).astype(jnp.bfloat16)
    grad_query_heads = (
        jnp.einsum("shqk,skhe->sqhe", grad_scores, key_heads, preferred_element_type=jnp.float32)
        * head_scale
    )
    grad_key_heads = (
        jnp.einsum("shqk,sqhe->skhe", grad_scores, query_heads, preferred_element_type=jnp.float32)
        * head_scale
    )
    grad_queries = grad_query_heads.reshape(seq_count * LEN, D).astype(jnp.bfloat16)
    grad_keys = grad_key_heads.reshape(seq_count * LEN, D).astype(jnp.bfloat16)
    grad_values = grad_value_heads.reshape(seq_count * LEN, D).astype(jnp.bfloat16)
    grad_query_weight = jnp.dot(flat_rows.T, grad_queries, preferred_element_type=jnp.float32)
    grad_key_weight = jnp.dot(flat_rows.T, grad_keys, preferred_element_type=jnp.float32)
    grad_value_weight = jnp.dot(flat_rows.T, grad_values, preferred_element_type=jnp.float32)
    grad_query_bias = jnp.sum(grad_queries.astype(jnp.float32), 0)
    grad_value_bias = jnp.sum(grad_values.astype(jnp.float32), 0)
    grad_hidden = (
        grad_first
        + jnp.dot(grad_queries, query_weight.T, preferred_element_type=jnp.float32)
        + jnp.dot(grad_keys, key_weight.T, preferred_element_type=jnp.float32)
        + jnp.dot(grad_values, value_weight.T, preferred_element_type=jnp.float32)
    )
    return (
        grad_hidden,
        (
            grad_query_weight,
            grad_key_weight,
            grad_value_weight,
            grad_out_weight,
            grad_inner_weight,
            grad_outer_weight,
            grad_query_bias,
            grad_value_bias,
            grad_out_bias,
            grad_norm1_gain,
            grad_norm1_bias,
            grad_inner_bias,
            grad_outer_bias,
            grad_norm2_gain,
            grad_norm2_bias,
        ),
    )


def merge_pair(peak_one, total_one, peak_two, total_two):
    peak_new = jnp.maximum(peak_one, peak_two)
    return (
        peak_new,
        total_one * jnp.exp(peak_one - peak_new) + total_two * jnp.exp(peak_two - peak_new),
    )


def merge_rows(one_side, other_side):
    peak_new, total_new = merge_pair(one_side[0], one_side[1], other_side[0], other_side[1])
    return (peak_new, total_new, one_side[2] + other_side[2])


def slot_partial(score_vec, slot_ok):
    grouped = jnp.where(slot_ok, score_vec, NEG).reshape(-1, SLOT_DEV)
    ok_grouped = slot_ok.reshape(-1, SLOT_DEV)
    group_peak = jnp.max(grouped, -1)
    group_total = jnp.sum(jnp.where(ok_grouped, jnp.exp(grouped - group_peak[:, None]), 0.0), -1)
    return (group_peak, group_total)


def plain_body(
    hidden_in,
    token_mask,
    out_grad,
    query_embed,
    slot_valid,
    target_ids,
    target_pos,
    query_weight,
    key_weight,
    value_weight,
    out_weight,
    inner_weight,
    outer_weight,
    retrieve_weight,
    query_bias,
    value_bias,
    out_bias,
    norm1_gain,
    norm1_bias,
    inner_bias,
    outer_bias,
    norm2_gain,
    norm2_bias,
    embedding,
    vocab_bias,
):
    params = (
        query_weight,
        key_weight,
        value_weight,
        out_weight,
        inner_weight,
        outer_weight,
        retrieve_weight,
        query_bias,
        value_bias,
        out_bias,
        norm1_gain,
        norm1_bias,
        inner_bias,
        outer_bias,
        norm2_gain,
        norm2_bias,
    )
    gathered = collect(params)
    kept_acts = forward_layer(hidden_in, token_mask, gathered)
    seq_count = hidden_in.shape[0]
    query_count = seq_count // SLOT_DEV
    out_seq = kept_acts[10].reshape(seq_count, LEN, D)
    devices = lax.axis_size("dp") * lax.axis_size("fsdp")
    device = lax.axis_index("dp") * lax.axis_size("fsdp") + lax.axis_index("fsdp")
    member = lax.axis_index("fsdp") % GROUP
    local_seq = jnp.arange(seq_count, dtype=jnp.int32)
    local_query = device // GROUP * query_count + local_seq // SLOT_DEV
    local_slot = member * SLOT_DEV + local_seq % SLOT_DEV
    slot_ok = slot_valid[local_query, local_slot] > 0
    embeds = query_embed[local_query]
    positions = target_pos[local_query]
    cls_rows = out_seq[:, 0, :].astype(jnp.float32)
    retrieve_full = gathered[6].astype(jnp.float32)
    projected = jnp.dot(cls_rows, retrieve_full, precision=HIGH)
    retrieval = jnp.sum(projected * embeds, -1)
    own_rows = seq_count * MASKS
    sent_rows = out_seq[local_seq[:, None], positions].reshape(own_rows, D)
    all_rows = lax.all_gather(sent_rows, ("dp", "fsdp"), axis=0, tiled=True)
    group_count = devices // GROUP
    all_targets = jnp.broadcast_to(
        target_ids.reshape(group_count, 1, query_count, 1, MASKS),
        (group_count, GROUP, query_count, SLOT_DEV, MASKS),
    ).reshape(-1)
    vocab_rows = embedding.shape[0]
    local_ids = all_targets - device * vocab_rows
    target_hit = jnp.arange(vocab_rows, dtype=jnp.int32)[None, :] == local_ids[:, None]
    logits = jnp.einsum(
        "rd,vd->rv", all_rows, embedding, preferred_element_type=jnp.float32
    ) + vocab_bias.astype(jnp.float32)
    row_peak = jnp.max(logits, -1)
    sum_exp = jnp.sum(jnp.exp(logits - row_peak[:, None]), -1)
    target_logit = jnp.sum(jnp.where(target_hit, logits, 0.0), -1)
    peak_all, total_all, target_all = combined_all(
        (row_peak, sum_exp, target_logit), ("dp", "fsdp"), merge_rows
    )
    lse_rows = peak_all + jnp.log(total_all)
    log_prob = lax.dynamic_slice_in_dim(target_all - lse_rows, device * own_rows, own_rows)
    seq_ll = jnp.mean(log_prob.reshape(seq_count, MASKS), -1)
    joint_score = retrieval + seq_ll
    joint_peak, joint_total = slot_partial(joint_score, slot_ok)
    prior_peak, prior_total = slot_partial(retrieval, slot_ok)
    for bit_number in range(GROUP.bit_length() - 1):
        far_joint_peak, far_joint_total, far_prior_peak, far_prior_total = partner(
            (joint_peak, joint_total, prior_peak, prior_total), "fsdp", bit_number
        )
        joint_peak, joint_total = merge_pair(
            joint_peak, joint_total, far_joint_peak, far_joint_total
        )
        prior_peak, prior_total = merge_pair(
            prior_peak, prior_total, far_prior_peak, far_prior_total
        )
    joint_lse = joint_peak + jnp.log(joint_total)
    prior_lse = prior_peak + jnp.log(prior_total)
    pair_loglik = joint_lse - prior_lse
    post_weight = jnp.where(slot_ok, jnp.exp(joint_score - jnp.repeat(joint_lse, SLOT_DEV)), 0.0)
    prior_weight = jnp.where(slot_ok, jnp.exp(retrieval - jnp.repeat(prior_lse, SLOT_DEV)), 0.0)
    grad_retrieval = LOSS_WEIGHT * (prior_weight - post_weight)
    row_scale = jnp.repeat(-LOSS_WEIGHT * post_weight / MASKS, MASKS)
    all_scales = lax.all_gather(row_scale, ("dp", "fsdp"), axis=0, tiled=True)
    vocab_probs = jnp.exp(logits - lse_rows[:, None])
    grad_logits = all_scales[:, None] * (target_hit.astype(jnp.float32) - vocab_probs)
    grad_vocab_bias = jnp.sum(grad_logits, 0)
    logits_low = grad_logits.astype(jnp.bfloat16)
    grad_embedding = jnp.einsum(
        "rv,rd->vd", logits_low, all_rows, preferred_element_type=jnp.float32
    )
    grad_picked = lax.psum_scatter(
        jnp.dot(logits_low, embedding, preferred_element_type=jnp.float32),
        ("dp", "fsdp"),
        scatter_dimension=0,
        tiled=True,
    )
    grad_project = grad_retrieval[:, None] * embeds
    grad_retrieve_weight = jnp.dot(cls_rows.T, grad_project, precision=HIGH)
    grad_cls = jnp.dot(grad_project, retrieve_full.T, precision=HIGH)
    grad_total = out_grad.astype(jnp.float32)
    grad_total = grad_total.at[local_seq[:, None], positions].add(
        grad_picked.reshape(seq_count, MASKS, D)
    )
    grad_total = grad_total.at[:, 0, :].add(grad_cls)
    grad_total = grad_total.reshape(seq_count * LEN, D)
    grad_hidden, layer_grads = backward_layer(
        hidden_in, token_mask, gathered, kept_acts, grad_total
    )
    (
        grad_query_weight,
        grad_key_weight,
        grad_value_weight,
        grad_out_weight,
        grad_inner_weight,
        grad_outer_weight,
        grad_query_bias,
        grad_value_bias,
        grad_out_bias,
        grad_norm1_gain,
        grad_norm1_bias,
        grad_inner_bias,
        grad_outer_bias,
        grad_norm2_gain,
        grad_norm2_bias,
    ) = layer_grads
    (
        shard_query_weight,
        shard_key_weight,
        shard_value_weight,
        shard_out_weight,
        shard_inner_weight,
        shard_outer_weight,
        shard_retrieve_weight,
        shard_query_bias,
        shard_value_bias,
        shard_out_bias,
        shard_norm1_gain,
        shard_norm1_bias,
        shard_inner_bias,
        shard_outer_bias,
        shard_norm2_gain,
        shard_norm2_bias,
    ) = spread(
        (
            grad_query_weight,
            grad_key_weight,
            grad_value_weight,
            grad_out_weight,
            grad_inner_weight,
            grad_outer_weight,
            grad_retrieve_weight,
            grad_query_bias,
            grad_value_bias,
            grad_out_bias,
            grad_norm1_gain,
            grad_norm1_bias,
            grad_inner_bias,
            grad_outer_bias,
            grad_norm2_gain,
            grad_norm2_bias,
        )
    )
    return (
        out_seq,
        pair_loglik,
        grad_hidden.reshape(seq_count, LEN, D),
        shard_query_weight,
        shard_key_weight,
        shard_value_weight,
        shard_out_weight,
        shard_inner_weight,
        shard_outer_weight,
        shard_retrieve_weight,
        shard_query_bias,
        shard_value_bias,
        shard_out_bias,
        shard_norm1_gain,
        shard_norm1_bias,
        shard_inner_bias,
        shard_outer_bias,
        shard_norm2_gain,
        shard_norm2_bias,
        grad_embedding,
        grad_vocab_bias,
    )

MESH = pl.DeviceIdType.MESH

def coords():
    d = lax.axis_index("dp"); f = lax.axis_index("fsdp")
    return d // 4, (d // 2) % 2, d % 2, f

def dev(y, x, c, z):
    return ((y * 2 + x) * 2 + c, z)

def rdma(src, dst, ss, rs, to):
    return pltpu.make_async_remote_copy(src, dst, ss, rs, device_id=to, device_id_type=MESH)

def greet():
    y, x, c, z = coords()
    bar = pltpu.get_barrier_semaphore()
    tos = [dev(y, x, c, lax.rem(z + k, 4)) for k in (1, 2, 3)] + [dev(y, 1 - x, c, z), dev(1 - y, x, c, z), dev(y, x, 1 - c, z)]
    for t in tos:
        pl.semaphore_signal(bar, inc=1, device_id=t, device_id_type=MESH)
    pl.semaphore_wait(bar, len(tos))

class Gather:
    def __init__(self, src, dst, ss, rs, ls, a):
        self.src, self.dst, self.ss, self.rs, self.ls, self.a = src, dst, ss, rs, ls, a
        N = src.shape[-1]
        self.split = (N // 2) % 128 == 0
        self.h = N // 2
        self.y, self.x, self.c, self.z = coords()
        self.me = self.y * 2 + self.x
        self.xn = self.y * 2 + (1 - self.x)
        self.yn = (1 - self.y) * 2 + self.x
        self.dg = (1 - self.y) * 2 + (1 - self.x)
        self.sent = []
    def send(self, src, dst, slot, to):
        cp = rdma(src, dst, self.ss.at[self.a, slot], self.rs.at[self.a, slot], to)
        cp.start()
        self.sent.append(cp)
    def wait(self, ref, slot):
        rdma(ref, ref, self.ss.at[self.a, slot], self.rs.at[self.a, slot], dev(self.y, 1 - self.x, self.c, self.z)).wait_recv()
    def own(self):
        y, x, c, z = self.y, self.x, self.c, self.z
        d = self.dst.at[self.me, c, z]
        self.lc = pltpu.make_async_copy(self.src, d, self.ls.at[self.a])
        self.lc.start()
        self.send(self.src, d, 4, dev(y, 1 - x, c, z))
        self.send(self.src, d, 8, dev(1 - y, x, c, z))
        for k in (1, 3, 2):
            self.send(self.src, d, k, dev(y, x, c, lax.rem(z + k, 4)))
    def zrecv(self, k):
        y, x, c = self.y, self.x, self.c
        zz = lax.rem(self.z + 4 - k, 4)
        d = self.dst.at[self.me, c, zz]
        self.wait(d, k)
        self.send(d, d, 4 + k, dev(y, 1 - x, c, self.z))
        self.send(d, d, 8 + k, dev(1 - y, x, c, self.z))
    def column_core(self, col, slot):
        d = self.dst.at[col, self.c]
        self.send(d, d, 20 + slot, dev(self.y, self.x, 1 - self.c, self.z))
    def xyrecv(self, k):
        y, x, c = self.y, self.x, self.c
        zz = lax.rem(self.z + 4 - k, 4)
        dx = self.dst.at[self.xn, c, zz]
        self.wait(dx, 4 + k)
        if self.split:
            dxa = dx.at[:, pl.ds(0, self.h)]
            self.send(dxa, dxa, 12 + k, dev(1 - y, x, c, self.z))
        else:
            self.send(dx, dx, 12 + k, dev(1 - y, x, c, self.z))
        dy = self.dst.at[self.yn, c, zz]
        self.wait(dy, 8 + k)
        if self.split:
            dyb = dy.at[:, pl.ds(self.h, self.h)]
            self.send(dyb, dyb, 16 + k, dev(y, 1 - x, c, self.z))
    def dgrecv(self, k):
        zz = lax.rem(self.z + 4 - k, 4)
        d = self.dst.at[self.dg, self.c, zz]
        if self.split:
            self.wait(d.at[:, pl.ds(0, self.h)], 12 + k)
            self.wait(d.at[:, pl.ds(self.h, self.h)], 16 + k)
        else:
            self.wait(d, 12 + k)
    def finish(self):
        for slot, col in enumerate((self.me, self.xn, self.yn, self.dg)):
            self.wait(self.dst.at[col, 1 - self.c], 20 + slot)
        for cp in self.sent:
            cp.wait_send()

def ag_body(n, *refs):
    srcs, dsts = refs[:n], refs[n:2 * n]
    ss, rs, ls = refs[2 * n:]
    greet()
    gs = [Gather(srcs[a], dsts[a], ss, rs, ls, a) for a in range(n)]
    gs[0].own()
    for a in range(n + 1):
        if a + 1 < n:
            gs[a + 1].own()
        if a < n:
            for k in (1, 3, 2):
                gs[a].zrecv(k)
        if a >= 1:
            for k in (0, 1, 3, 2):
                gs[a - 1].dgrecv(k)
            gs[a - 1].column_core(gs[a - 1].dg, 3)
        if a < n:
            gs[a].lc.wait()
            gs[a].column_core(gs[a].me, 0)
            for k in (0, 1, 3, 2):
                gs[a].xyrecv(k)
            gs[a].column_core(gs[a].xn, 1)
            gs[a].column_core(gs[a].yn, 2)
    for g in gs:
        g.finish()

def all_gather_pallas(shards, cid=0, name="gather_weights"):
    n = len(shards)
    any_ = pl.BlockSpec(memory_space=pltpu.HBM)
    outs = pl.pallas_call(
        functools.partial(ag_body, n), name=name,
        out_shape=[jax.ShapeDtypeStruct((4, 2, 4) + s.shape, s.dtype) for s in shards],
        in_specs=[any_] * n, out_specs=[any_] * n,
        scratch_shapes=[pltpu.SemaphoreType.DMA((n, 24)), pltpu.SemaphoreType.DMA((n, 24)), pltpu.SemaphoreType.DMA((n,))],
        compiler_params=pltpu.CompilerParams(collective_id=cid, has_side_effects=True),
    )(*shards)
    return [o.reshape((32 * s.shape[0],) + s.shape[1:]) for o, s in zip(outs, shards)]


F32 = jnp.float32; BF = jnp.bfloat16

class Scatter:
    def __init__(self, g, out, bufs, ss, rs, ls, a):
        self.g, self.out, self.ss, self.rs, self.ls, self.a = g, out, ss, rs, ls, a
        self.own, self.rc, self.ray, self.rax, self.rbx, self.rby, self.rz = bufs
        self.N = g.shape[-1]
        self.split = (self.N // 2) % 128 == 0
        self.h = self.N // 2 if self.split else self.N
        self.y, self.x, self.c, self.z = coords()
        self.me = self.y * 2 + self.x
        self.sent = []
    def send(self, src, dst, slot, to):
        cp = rdma(src, dst, self.ss.at[self.a, slot], self.rs.at[self.a, slot], to)
        cp.start(); self.sent.append(cp)
    def wait(self, ref, slot):
        rdma(ref, ref, self.ss.at[self.a, slot], self.rs.at[self.a, slot], dev(self.y, 1 - self.x, self.c, self.z)).wait_recv()
    def core(self):
        y, x, c, z = self.y, self.x, self.c, self.z
        self.lc = []
        for j in range(4):
            cp = pltpu.make_async_copy(self.g.at[j, c], self.own.at[j], self.ls.at[self.a, j]); cp.start(); self.lc.append(cp)
            self.send(self.g.at[j, 1 - c], self.rc.at[j], j, dev(y, x, 1 - c, z))
    def add(self, dst, src):
        @pl.loop(0, 4)
        def _(i):
            dst[i] = (dst[i].astype(F32) + src[i].astype(F32)).astype(BF)
    def first(self):
        y, x, c, z, h = self.y, self.x, self.c, self.z, self.h
        for j in range(4):
            self.lc[j].wait()
            self.wait(self.rc.at[j], j)
        for j in range(4):
            self.add(self.own.at[j], self.rc.at[j])
        for xi in range(2):
            self.send(self.own.at[(1 - y) * 2 + xi, :, :, pl.ds(0, h)], self.ray.at[xi], 4 + xi, dev(1 - y, x, c, z))
        if self.split:
            for yi in range(2):
                self.send(self.own.at[yi * 2 + 1 - x, :, :, pl.ds(h, h)], self.rbx.at[yi], 8 + yi, dev(y, 1 - x, c, z))
    def second(self):
        y, x, c, z, h = self.y, self.x, self.c, self.z, self.h
        for xi in range(2):
            self.wait(self.ray.at[xi], 4 + xi)
            self.add(self.own.at[y * 2 + xi, :, :, pl.ds(0, h)], self.ray.at[xi])
        self.send(self.own.at[y * 2 + 1 - x, :, :, pl.ds(0, h)], self.rax, 6, dev(y, 1 - x, c, z))
        if self.split:
            for yi in range(2):
                self.wait(self.rbx.at[yi], 8 + yi)
                self.add(self.own.at[yi * 2 + x, :, :, pl.ds(h, h)], self.rbx.at[yi])
            self.send(self.own.at[(1 - y) * 2 + x, :, :, pl.ds(h, h)], self.rby, 10, dev(1 - y, x, c, z))
    def third(self):
        y, x, c, z, h = self.y, self.x, self.c, self.z, self.h
        self.wait(self.rax, 6)
        self.add(self.own.at[self.me, :, :, pl.ds(0, h)], self.rax)
        if self.split:
            self.wait(self.rby, 10)
            self.add(self.own.at[self.me, :, :, pl.ds(h, h)], self.rby)
        for k in (2, 1, 3):
            zz = lax.rem(z + k, 4)
            self.send(self.own.at[self.me, zz], self.rz.at[k - 1], 12 + k - 1, dev(y, x, c, zz))
    def last(self):
        for k in (1, 2, 3):
            self.wait(self.rz.at[k - 1], 12 + k - 1)
        t = self.own[self.me, self.z].astype(F32)
        for k in range(3):
            t = t + self.rz[k].astype(F32)
        self.out[...] = t
    def finish(self):
        for cp in self.sent:
            cp.wait_send()

def bufs_for(r, N):
    split = (N // 2) % 128 == 0
    h = N // 2 if split else N
    return [pltpu.VMEM((4, 4, r, N), BF), pltpu.VMEM((4, 4, r, N), BF), pltpu.VMEM((2, 4, r, h), BF), pltpu.VMEM((4, r, h), BF),
            pltpu.VMEM((2, 4, r, h), BF), pltpu.VMEM((4, r, h), BF), pltpu.VMEM((3, r, N), BF)]

def rs_body(n, *refs):
    gs, outs = refs[:n], refs[n:2 * n]
    ss, rs, ls = refs[2 * n:2 * n + 3]
    bufs = refs[2 * n + 3:]
    greet()
    sc = [Scatter(gs[a], outs[a], bufs[7 * a:7 * a + 7], ss, rs, ls, a) for a in range(n)]
    sc[0].core()
    for t in range(n + 3):
        if t + 1 < n: sc[t + 1].core()
        if 0 <= t < n: sc[t].first()
        if 0 <= t - 1 < n: sc[t - 1].second()
        if 0 <= t - 2 < n: sc[t - 2].third()
        if 0 <= t - 3 < n: sc[t - 3].last()
    for s in sc: s.finish()

def reduce_scatter_pallas(gs, cid=1, name="reduce_grads"):
    n = len(gs)
    shapes = [(g.shape[0] // 32, g.shape[1]) for g in gs]
    ins = [g.reshape((4, 2, 4) + s) for g, s in zip(gs, shapes)]
    return pl.pallas_call(
        functools.partial(rs_body, n), name=name,
        out_shape=[jax.ShapeDtypeStruct(s, F32) for s in shapes],
        in_specs=[pl.BlockSpec(memory_space=pltpu.HBM)] * n,
        out_specs=[pl.BlockSpec(memory_space=pltpu.VMEM)] * n,
        scratch_shapes=[pltpu.SemaphoreType.DMA((n, 16)), pltpu.SemaphoreType.DMA((n, 16)), pltpu.SemaphoreType.DMA((n, 4))] + sum([bufs_for(*s) for s in shapes], []),
        compiler_params=pltpu.CompilerParams(collective_id=cid, has_side_effects=True, vmem_limit_bytes=56 << 20),
    )(*ins)


F32 = jnp.float32; BF = jnp.bfloat16
D = 768; H = 12; HD = 64; LEN = 288; FF = 3072
NEG = -1000000000.0
EPS = 1e-12

def dot(a, b):
    return lax.dot_general(a, b, (((1,), (0,)), ((), ())), preferred_element_type=F32)

def dot_nt(a, b):
    return lax.dot_general(a, b, (((1,), (1,)), ((), ())), preferred_element_type=F32)

def dot_tn(a, b):
    return lax.dot_general(a, b, (((0,), (0,)), ((), ())), preferred_element_type=F32)

def iota(shape, dim):
    return lax.broadcasted_iota(jnp.int32, shape, dim)

def over(index, n):
    return jnp.floor((index.astype(F32) + 0.5) * (1.0 / n)).astype(jnp.int32)

def expand_vectors(blocks):
    lane, col = iota((128, D), 0), iota((128, D), 1)
    pick = (lane == col - over(col, 24) * 24).astype(F32).astype(BF)
    spread = dot(blocks.reshape(256, 128), pick)
    row, col = iota((256, D), 0), iota((256, D), 1)
    spread = jnp.where(over(row, 8) == over(col, 24), spread, 0.0)
    vec = jnp.sum(spread.reshape(32, 8, D), 0)
    lane, col = iota((128, FF), 0), iota((128, FF), 1)
    pick = (lane - 32 == col - over(col, 96) * 96).astype(F32).astype(BF)
    spread = dot(blocks.reshape(256, 128), pick)
    row, col = iota((256, FF), 0), iota((256, FF), 1)
    inner = jnp.sum(jnp.where(row == over(col, 96) * 8, spread, 0.0), 0, keepdims=True)
    return vec, inner

def norm_stats(r):
    mean = jnp.mean(r, -1, keepdims=True)
    cen = r - mean
    var = jnp.mean(cen * cen, -1, keepdims=True)
    inv = lax.rsqrt(var + EPS)
    return cen * inv, inv

def attn_fwd_pair(s, hp, q_ref, k_ref, v_ref, p_ref, o_ref, keys_ok):
    cols = pl.ds(pl.multiple_of(hp * 128, 128), 128)
    q2 = q_ref[s, :, cols]; k2 = k_ref[s, :, cols]; v2 = v_ref[s, :, cols]
    low = iota((LEN, 128), 1) < HD
    os_ = []
    for h in range(2):
        mine = low if h == 0 else jnp.logical_not(low)
        qm = jnp.where(mine, q2 * 0.125, 0.0).astype(BF)
        st = dot_nt(k2, qm)
        st = jnp.where(keys_ok, st, NEG)
        e = jnp.exp(st - jnp.max(st, 0, keepdims=True))
        p = (e * (1.0 / jnp.sum(e, 0, keepdims=True))).astype(BF)
        p_ref[s, hp * 2 + h] = p
        os_.append(dot_tn(p, v2))
    o_ref[s, :, cols] = jnp.where(low, os_[0], os_[1]).astype(BF)

def fwd1_seq(s, x_ref, m_ref, wqkv_ref, wo_ref, vec_ref, q_ref, k_ref, v_ref, p_ref, o_ref, n1_ref, xh1_ref, inv1_ref):
    x = x_ref[s]
    for j, ref in enumerate((q_ref, k_ref, v_ref)):
        t = dot(x, wqkv_ref[:, pl.ds(j * D, D)])
        if j != 1:
            t = t + vec_ref[0 if j == 0 else 1][None]
        ref[s] = t.astype(BF)
    count = jnp.sum(m_ref[pl.ds(s, 1), :], -1, keepdims=True)
    keys_ok = iota((LEN, 1), 0) < count
    @pl.loop(0, H // 2)
    def _(hp):
        attn_fwd_pair(s, hp, q_ref, k_ref, v_ref, p_ref, o_ref, keys_ok)
    r1 = x.astype(F32) + dot(o_ref[s], wo_ref[...]) + vec_ref[2][None]
    xh, inv = norm_stats(r1)
    xh1_ref[s] = xh.astype(BF)
    inv1_ref[s] = jnp.broadcast_to(inv, (LEN, 128))
    n1_ref[s] = (xh * vec_ref[3][None] + vec_ref[4][None]).astype(BF)

def fwd1_body(x_ref, m_ref, wqkv_ref, wo_ref, small_ref, vec_ref, ib_ref, q_ref, k_ref, v_ref, p_ref, o_ref, n1_ref, xh1_ref, inv1_ref):
    vec, inner = expand_vectors(small_ref[:, pl.ds(24, 8), :])
    vec_ref[...] = vec
    ib_ref[...] = inner
    @pl.loop(0, 4)
    def _(s):
        fwd1_seq(s, x_ref, m_ref, wqkv_ref, wo_ref, vec_ref, q_ref, k_ref, v_ref, p_ref, o_ref, n1_ref, xh1_ref, inv1_ref)

VM = pl.BlockSpec(memory_space=pltpu.VMEM)
def vcall(body, outs, *args, name, limit=58):
    return pl.pallas_call(body, name=name, out_shape=[jax.ShapeDtypeStruct(s, t) for s, t in outs],
        in_specs=[VM] * len(args), out_specs=[VM] * len(outs),
        compiler_params=pltpu.CompilerParams(vmem_limit_bytes=limit << 20))(*args)

ACT = ((4, LEN, D), BF)
def fwd1(x, mask, wqkv, wo, small):
    return vcall(fwd1_body, [((8, D), F32), ((1, FF), F32), ACT, ACT, ACT, ((4, H, LEN, LEN), BF), ACT, ACT, ACT, ((4, LEN, 128), F32)],
        x, mask, wqkv, wo, small, name="attention_forward")

def gelu_pair(z):
    e = jnp.exp(-0.5 * z * z)
    t = 1.0 / (1.0 + (0.3275911 * 0.7071067811865476) * jnp.abs(z))
    poly = t * (0.254829592 + t * (-0.284496736 + t * (1.421413741 + t * (-1.453152027 + t * 1.061405429))))
    tail = 0.5 * poly * e
    cdf = jnp.where(z >= 0, 1.0 - tail, tail)
    return z * cdf, cdf + z * e * 0.3989422804014327

def fwd2_seq(s, n1_ref, wi_ref, wu_ref, vec_ref, ib_ref, pos_ref, g_ref, dg_ref, lo_ref, xh2_ref, inv2_ref, picked_ref):
    n1 = n1_ref[s]
    acc = n1.astype(F32) + vec_ref[5][None]
    for j in range(4):
        cols = pl.ds(j * D, D)
        g, dg = gelu_pair(dot(n1, wi_ref[:, cols]) + ib_ref[:, cols])
        g = g.astype(BF)
        g_ref[s, :, cols] = g
        dg_ref[s, :, cols] = dg.astype(BF)
        acc = acc + dot(g, wu_ref[cols, :])
    xh, inv = norm_stats(acc)
    xh2_ref[s] = xh.astype(BF)
    inv2_ref[s] = jnp.broadcast_to(inv, (LEN, 128))
    lo = (xh * vec_ref[6][None] + vec_ref[7][None]).astype(BF)
    lo_ref[s] = lo
    picked_ref[s] = dot((iota((8, LEN), 1) == pos_ref[s]).astype(F32).astype(BF), lo).astype(BF)

def fwd2_body(*refs):
    @pl.loop(0, 4)
    def _(s):
        fwd2_seq(s, *refs)

def fwd2(n1, wi, wu, vec, ib, pos):
    big = ((4, LEN, FF), BF)
    return vcall(fwd2_body, [big, big, ACT, ACT, ((4, LEN, 128), F32), ((4, 8, D), BF)], n1, wi, wu, vec, ib, pos, name="feed_forward")

def norm_back(dy, xh, inv, gain):
    c = dy * gain
    return (c - jnp.mean(c, -1, keepdims=True) - xh * jnp.mean(c * xh, -1, keepdims=True)) * inv

def bwd1_body(og_ref, add_ref, pos_ref, xh2_ref, inv2_ref, vec_ref, g_ref, dg_ref, n1_ref, wi_ref, wu_ref,
              gu_ref, gi_ref, dn1_ref, sums_ref, sumi_ref, d2_ref, dz_ref):
    sums_ref[...] = jnp.zeros_like(sums_ref)
    sumi_ref[...] = jnp.zeros_like(sumi_ref)
    @pl.loop(0, 4)
    def _(s):
        hit = (iota((LEN, 8), 0) == pos_ref[s]).astype(F32)
        extra = lax.dot_general(hit, add_ref[s], (((1,), (0,)), ((), ())), preferred_element_type=F32, precision=lax.Precision.HIGHEST)
        dy = og_ref[s].astype(F32) + extra
        xh = xh2_ref[s].astype(F32)
        dr2 = norm_back(dy, xh, inv2_ref[s][:, 0:1], vec_ref[6][None])
        sums_ref[0] += jnp.sum(dy * xh, 0)
        sums_ref[1] += jnp.sum(dy, 0)
        sums_ref[2] += jnp.sum(dr2, 0)
        d2 = dr2.astype(BF)
        d2_ref[pl.ds(s * LEN, LEN)] = d2
        acc = dr2
        for j in range(4):
            cols = pl.ds(j * D, D)
            dz = dot_nt(d2, wu_ref[cols, :]) * dg_ref[s, :, cols].astype(F32)
            dz = dz.astype(BF)
            sumi_ref[0:1, cols] += jnp.sum(dz.astype(F32), 0, keepdims=True)
            dz_ref[pl.ds(s * LEN, LEN), cols] = dz
            acc = acc + dot_nt(dz, wi_ref[:, cols])
        dn1_ref[s] = acc
    d2 = d2_ref[...]
    n1 = n1_ref[...].reshape(4 * LEN, D)
    for j in range(4):
        cols = pl.ds(j * D, D)
        gu_ref[cols, :] = dot_tn(g_ref[:, :, cols].reshape(4 * LEN, D), d2).astype(BF)
        gi_ref[:, cols] = dot_tn(n1, dz_ref[:, cols]).astype(BF)

def bwd1(og, add, pos, xh2, inv2, vec, g, dg, n1, wi, wu):
    outs = [((FF, D), BF), ((D, FF), BF), ((4, LEN, D), F32), ((8, D), F32), ((8, FF), F32)]
    args = (og, add, pos, xh2, inv2, vec, g, dg, n1, wi, wu)
    return pl.pallas_call(bwd1_body, name="feed_forward_backward", out_shape=[jax.ShapeDtypeStruct(s, t) for s, t in outs],
        in_specs=[VM] * len(args), out_specs=[VM] * len(outs),
        scratch_shapes=[pltpu.VMEM((4 * LEN, D), BF), pltpu.VMEM((4 * LEN, FF), BF)],
        compiler_params=pltpu.CompilerParams(vmem_limit_bytes=62 << 20))(*args)

def attn_bwd_pair(s, hp, q_ref, k_ref, v_ref, p_ref, do_ref, dqkv_ref):
    cols = pl.ds(pl.multiple_of(hp * 128, 128), 128)
    q2 = q_ref[s, :, cols]; k2 = k_ref[s, :, cols]; v2 = v_ref[s, :, cols]; do2 = do_ref[:, cols]
    low = iota((LEN, 128), 1) < HD
    dq, dk, dv = [], [], []
    for h in range(2):
        mine = low if h == 0 else jnp.logical_not(low)
        pt = p_ref[s, hp * 2 + h]
        dom = jnp.where(mine, do2, jnp.zeros_like(do2))
        dpt = dot_nt(v2, dom)
        pf = pt.astype(F32)
        ds = (pf * (dpt - jnp.sum(pf * dpt, 0, keepdims=True))).astype(BF)
        dv.append(dot(pt, do2))
        dk.append(dot(ds, q2))
        dq.append(dot_tn(ds, k2))
    rows = pl.ds(s * LEN, LEN)
    for i, (pair, scale) in enumerate(((dq, 0.125), (dk, 0.125), (dv, 1.0))):
        c = pl.ds(pl.multiple_of(i * D + hp * 128, 128), 128)
        dqkv_ref[rows, c] = (jnp.where(low, pair[0], pair[1]) * scale).astype(BF)

def bwd2_body(dn1_ref, xh1_ref, inv1_ref, vec_ref, x_ref, q_ref, k_ref, v_ref, p_ref, o_ref, wqkv_ref, wo_ref, grw_ref, s2_ref, si_ref,
              go_ref, gqkv_ref, dx_ref, small_ref, sums_ref, sumq_ref, d1_ref, dqkv_ref, do_ref):
    sums_ref[...] = jnp.zeros_like(sums_ref)
    sumq_ref[...] = jnp.zeros_like(sumq_ref)
    @pl.loop(0, 4)
    def _(s):
        dy = dn1_ref[s]
        xh = xh1_ref[s].astype(F32)
        dr1 = norm_back(dy, xh, inv1_ref[s][:, 0:1], vec_ref[3][None])
        sums_ref[0] += jnp.sum(dy * xh, 0)
        sums_ref[1] += jnp.sum(dy, 0)
        sums_ref[2] += jnp.sum(dr1, 0)
        d1 = dr1.astype(BF)
        rows = pl.ds(s * LEN, LEN)
        d1_ref[rows] = d1
        do_ref[...] = dot_nt(d1, wo_ref[...]).astype(BF)
        @pl.loop(0, H // 2)
        def _(hp):
            attn_bwd_pair(s, hp, q_ref, k_ref, v_ref, p_ref, do_ref, dqkv_ref)
        acc = dr1
        for j in range(3):
            dq = dqkv_ref[rows, pl.ds(j * D, D)]
            sumq_ref[0:1, pl.ds(j * D, D)] += jnp.sum(dq.astype(F32), 0, keepdims=True)
            acc = acc + dot_nt(dq, wqkv_ref[:, pl.ds(j * D, D)])
        dx_ref[s] = acc
    go_ref[...] = dot_tn(o_ref[...].reshape(4 * LEN, D), d1_ref[...]).astype(BF)
    x = x_ref[...].reshape(4 * LEN, D)
    for j in range(3):
        gqkv_ref[:, pl.ds(j * D, D)] = dot_tn(x, dqkv_ref[:, pl.ds(j * D, D)]).astype(BF)
    small_ref[...] = small_grads(grw_ref[...], sums_ref[...], s2_ref[...], sumq_ref[...], si_ref[...])

def bwd2(dn1, xh1, inv1, vec, x, q, k, v, p, o, wqkv, wo, grw, s2, si):
    outs = [((D, D), BF), ((D, 3 * D), BF), ((4, LEN, D), F32), ((32, 32, 128), BF)]
    args = (dn1, xh1, inv1, vec, x, q, k, v, p, o, wqkv, wo, grw, s2, si)
    return pl.pallas_call(bwd2_body, name="attention_backward", out_shape=[jax.ShapeDtypeStruct(s, t) for s, t in outs],
        in_specs=[VM] * len(args), out_specs=[VM] * len(outs),
        scratch_shapes=[pltpu.VMEM((8, D), F32), pltpu.VMEM((8, 3 * D), F32), pltpu.VMEM((4 * LEN, D), BF), pltpu.VMEM((4 * LEN, 3 * D), BF), pltpu.VMEM((LEN, D), BF)],
        compiler_params=pltpu.CompilerParams(vmem_limit_bytes=62 << 20))(*args)


HI = lax.Precision.HIGHEST
WEIGHT = 32.0

def exact(a, b, dims=((1,), (0,))):
    return lax.dot_general(a, b, (dims, ((), ())), preferred_element_type=F32, precision=HI)

def as_f(cond):
    return cond.astype(F32)

def greet_all():
    me = lax.axis_index("dp") * 4 + lax.axis_index("fsdp")
    bar = pltpu.get_barrier_semaphore()
    @pl.loop(1, 32)
    def _(k):
        t = lax.rem(me + k, 32)
        pl.semaphore_signal(bar, inc=1, device_id=(t // 4, lax.rem(t, 4)), device_id_type=MESH)
    pl.semaphore_wait(bar, 31)

def loss_body(picked_ref, emb_ref, vb_ref, ids_ref, valid_ref, qe_ref, small_ref,
              add_ref, grw_ref, pair_ref, ge_ref, gvb_ref,
              own_ref, rows_ref, lt_ref, st_ref, all_ref, dh_ref, dhout_ref, gss, grs, gls, sss, srs, sls, xs, xr, *bufs):
    me = lax.axis_index("dp") * 4 + lax.axis_index("fsdp")
    VS = emb_ref.shape[0]
    greet_all()
    own_ref[...] = picked_ref[:, 0:4, :].astype(F32).reshape(16, D).astype(BF)
    g = Gather(own_ref, rows_ref, gss, grs, gls, 0)
    g.own()
    cls = picked_ref[:, 4:5, :].astype(F32).reshape(4, D)
    cls8 = jnp.concatenate([cls, jnp.zeros((4, D), F32)], 0)
    rw = small_ref[:, 0:24, :].reshape(D, 128)
    row8, lane8 = iota((8, 128), 0), iota((8, 128), 1)
    qpick = as_f(jnp.logical_and(iota((8, 16), 1) == (me // 4) * 2 + iota((8, 16), 0) // 2, iota((8, 16), 0) < 4))
    qe_own = exact(qpick, qe_ref[...])
    score = jnp.sum(dot(cls8.astype(BF), rw) * qe_own, -1, keepdims=True)
    st_ref[12:13] = jnp.sum(jnp.where(row8 == lane8, score, 0.0), 0, keepdims=True)
    r512 = iota((16, 512), 1)
    s_of = r512 >> 2
    q_of = (s_of >> 4) * 2 + ((s_of & 3) >> 1)
    spread = exact(ids_ref[...].astype(F32), as_f(iota((4, 512), 0) == (iota((4, 512), 1) & 3)))
    ids = jnp.sum(jnp.where(iota((16, 512), 0) == q_of, spread, 0.0), 0, keepdims=True)
    local = ids.astype(jnp.int32) - me * VS
    for k in (1, 3, 2):
        g.zrecv(k)
    g.lc.wait()
    g.column_core(g.me, 0)
    for k in (0, 1, 3, 2):
        g.xyrecv(k)
    g.column_core(g.xn, 1)
    g.column_core(g.yn, 2)
    for k in (0, 1, 3, 2):
        g.dgrecv(k)
    g.column_core(g.dg, 3)
    g.finish()
    rows = rows_ref[...].reshape(512, D)
    lt = dot_nt(emb_ref[...], rows) + vb_ref[...]
    lt_ref[...] = lt
    hit = iota((VS, 512), 0) == local
    peak = jnp.max(lt, 0, keepdims=True)
    total = jnp.sum(jnp.exp(lt - peak), 0, keepdims=True)
    target = jnp.sum(jnp.where(hit, lt, 0.0), 0, keepdims=True)
    for a in range(4):
        cols = slice(a * 128, a * 128 + 128)
        st_ref[a:a + 1] = peak[:, cols]
        st_ref[4 + a:5 + a] = total[:, cols]
        st_ref[8 + a:9 + a] = target[:, cols]
    sends = []
    for k in range(1, 32):
        t = lax.rem(me + k, 32)
        cp = rdma(st_ref, all_ref.at[me], xs.at[k], xr.at[k], (t // 4, lax.rem(t, 4)))
        cp.start()
        sends.append(cp)
    all_ref[me] = st_ref[...]
    for k in range(1, 32):
        f = lax.rem(me + 32 - k, 32)
        rdma(st_ref, all_ref.at[f], xs.at[k], xr.at[k], (f // 4, lax.rem(f, 4))).wait_recv()
    peaks = all_ref[:, 0:4, :]
    top = jnp.max(peaks, 0)
    tot = jnp.sum(all_ref[:, 4:8, :] * jnp.exp(peaks - top[None]), 0)
    lse = top + jnp.log(tot)
    logp = jnp.sum(all_ref[:, 8:12, :], 0) - lse
    i0, i1 = iota((128, 128), 0), iota((128, 128), 1)
    logp8 = jnp.concatenate([logp, jnp.zeros((4, 128), F32)], 0)
    spread = exact(logp8, 0.25 * as_f((i0 >> 2) == (i1 & 31)))
    seq_ll = jnp.sum(jnp.where((lane8 >> 5) == row8, spread, 0.0), 0, keepdims=True)
    spread = exact(all_ref[:, 12, :], as_f(i0 == (i1 & 3)))
    retrieval = jnp.sum(jnp.where((iota((32, 128), 1) >> 2) == iota((32, 128), 0), spread, 0.0), 0, keepdims=True)
    q16, s16 = iota((16, 128), 0), iota((16, 128), 1)
    mine = q16 == (s16 >> 4) * 2 + ((s16 & 3) >> 1)
    s8 = iota((8, 128), 1)
    slot_pick = as_f(iota((8, 128), 0) == ((s8 >> 2) & 3) * 2 + (s8 & 1))
    ok16 = jnp.logical_and(mine, exact(valid_ref[...].astype(F32), slot_pick) > 0.5)
    joint = retrieval + seq_ll
    def slot_lse(v):
        m = jnp.max(jnp.where(ok16, v, NEG), -1, keepdims=True)
        return m + jnp.log(jnp.sum(jnp.where(ok16, jnp.exp(v - m), 0.0), -1, keepdims=True))
    def to_seq(v):
        return jnp.sum(jnp.where(mine, v, 0.0), 0, keepdims=True)
    joint_lse, prior_lse = slot_lse(joint), slot_lse(retrieval)
    ok = to_seq(as_f(ok16)) > 0.5
    post = jnp.where(ok, jnp.exp(joint - to_seq(joint_lse)), 0.0)
    prior = jnp.where(ok, jnp.exp(retrieval - to_seq(prior_lse)), 0.0)
    pair = jnp.sum(jnp.where(q16 == (me // 4) * 2 + s16, joint_lse - prior_lse, 0.0), 0, keepdims=True)
    pair_ref[...] = jnp.broadcast_to(pair, (8, 128))
    d_score = WEIGHT * (prior - post)
    scale = exact(jnp.broadcast_to(-WEIGHT * post / 4.0, (8, 128)), as_f(iota((128, 512), 0) == (iota((128, 512), 1) >> 2)))[0:1]
    lse_row = jnp.concatenate([lse[a:a + 1] for a in range(4)], 1)
    dl = scale * (as_f(hit) - jnp.exp(lt_ref[...] - lse_row))
    gvb_ref[...] = jnp.sum(dl, -1, keepdims=True)
    db = dl.astype(BF)
    dh_ref[...] = dot_tn(db, emb_ref[...]).astype(BF).reshape(4, 2, 4, 16, D)
    sc = Scatter(dh_ref, dhout_ref, bufs, sss, srs, sls, 0)
    sc.core()
    du = jnp.sum(jnp.where(jnp.logical_and(lane8 == me * 4 + row8, row8 < 4), d_score, 0.0), -1, keepdims=True) * qe_own
    grw_ref[...] = exact(cls8, du, ((0,), (0,)))
    dcls = exact(du, rw.astype(F32), ((1,), (1,)))
    add_ref[...] = jnp.zeros_like(add_ref)
    for l in range(4):
        add_ref[l, 4:5] = dcls[l:l + 1]
    sc.first()
    ge_ref[...] = dot(db, rows)
    sc.second()
    sc.third()
    sc.last()
    sc.finish()
    for l in range(4):
        add_ref[l, 0:4] = dhout_ref[4 * l:4 * l + 4]
    for cp in sends:
        cp.wait_send()

def loss_call(picked, emb, vb, ids, valid, qe, small, cid=2):
    VS = emb.shape[0]
    outs = [((4, 8, D), F32), ((D, 128), F32), ((8, 128), F32), ((VS, D), F32), ((VS, 1), F32)]
    args = (picked, emb, vb, ids, valid, qe, small)
    dma = pltpu.SemaphoreType.DMA
    return pl.pallas_call(loss_body, name="slot_loss", out_shape=[jax.ShapeDtypeStruct(s, t) for s, t in outs],
        in_specs=[VM] * len(args), out_specs=[VM] * len(outs),
        scratch_shapes=[pltpu.VMEM((16, D), BF), pltpu.VMEM((4, 2, 4, 16, D), BF), pltpu.VMEM((VS, 512), F32), pltpu.VMEM((16, 128), F32),
            pltpu.VMEM((32, 16, 128), F32), pltpu.VMEM((4, 2, 4, 16, D), BF), pltpu.VMEM((16, D), F32),
            dma((1, 24)), dma((1, 24)), dma((1,)), dma((1, 16)), dma((1, 16)), dma((1, 4)), dma((32,)), dma((32,))] + bufs_for(16, D),
        compiler_params=pltpu.CompilerParams(collective_id=cid, has_side_effects=True, vmem_limit_bytes=58 << 20))(*args)

def small_grads(grw, s1, s2, sq, si):
    vec = jnp.concatenate([sq[0:1, 0:D], sq[0:1, 2 * D:], s1[2:3], s1[0:1], s1[1:2], s2[2:3], s2[0:1], s2[1:2]], 0)
    row, col = iota((256, D), 0), iota((256, D), 1)
    tiled = jnp.broadcast_to(vec[None], (32, 8, D)).reshape(256, D)
    part = jnp.where(over(row, 8) == over(col, 24), tiled, 0.0).astype(BF)
    lane, col = iota((128, D), 0), iota((128, D), 1)
    pick = as_f(lane == col - over(col, 24) * 24).astype(BF)
    out = dot_nt(part, pick).reshape(32, 8, 128)
    row, col = iota((32, FF), 0), iota((32, FF), 1)
    part = jnp.where(row == over(col, 96), si[0:1], 0.0).astype(BF)
    lane, col = iota((128, FF), 0), iota((128, FF), 1)
    pick = as_f(lane - 32 == col - over(col, 96) * 96).astype(BF)
    inner = dot_nt(part, pick)
    out = out + jnp.where(iota((32, 8, 128), 1) == 0, inner[:, None, :], 0.0)
    return jnp.concatenate([grw.reshape(32, 24, 128), out], 1).astype(BF)


def linked_body(hidden_in, token_mask, out_grad, query_embed, slot_valid, target_ids, target_pos,
                qw, kw, vw, ow, iw, uw, rw, qb, vb, ob, ga, sa, ib, ub, gb, sb, embedding, vocab_bias):
    block = jnp.pad(jnp.stack([qb, vb, ob, ga, sa, ub, gb, sb]), ((0, 0), (0, 104)))
    block = jnp.concatenate([rw, block + jnp.pad(ib[None], ((0, 7), (32, 0)))], 0)
    small, wqkv, wo, wi, wu = all_gather_pallas((block, jnp.concatenate([qw, kw, vw], 1), ow, iw, uw))
    small = small.reshape(32, 32, 128)
    group = (lax.axis_index("dp") * lax.axis_size("fsdp") + lax.axis_index("fsdp")) // GROUP
    pos = lax.dynamic_slice_in_dim(target_pos, group * 2, 2)
    pos = jnp.concatenate([pos, jnp.zeros((2, 1), jnp.int32), jnp.full((2, 3), -1, jnp.int32)], 1)
    pos = jnp.repeat(pos, 2, 0)
    pos_row, pos_col = pos[:, None, :], pos[:, :, None]
    vec, inner, q, k, v, p, o, n1, xh1, inv1 = fwd1(hidden_in, token_mask, wqkv, wo, small)
    g, dg, out_seq, xh2, inv2, picked = fwd2(n1, wi, wu, vec, inner, pos_col)
    add, grw, pair, ge, gvb = loss_call(picked, embedding, vocab_bias.astype(F32)[:, None], target_ids, slot_valid, query_embed, small)
    gu, gi, dn1, s2, si = bwd1(out_grad, add, pos_row, xh2, inv2, vec, g, dg, n1, wi, wu)
    go, gqkv, dx, small_out = bwd2(dn1, xh1, inv1, vec, hidden_in, q, k, v, p, o, wqkv, wo, grw, s2, si)
    gu, gi, go, gqkv, gsm = reduce_scatter_pallas([gu, gi, go, gqkv, small_out.reshape(1024, 128)])
    vecs = [gsm[24 + i, :24] for i in range(8)]
    return (out_seq, pair[0, :2], dx, gqkv[:, :D], gqkv[:, D:2 * D], gqkv[:, 2 * D:], go, gi, gu, gsm[:24],
            vecs[0], vecs[1], vecs[2], vecs[3], vecs[4], gsm[24, 32:], vecs[5], vecs[6], vecs[7], ge, gvb[:, 0])


def solution(mesh):
    placed = (
        P(("dp", "fsdp"), None, None),
        P(("dp", "fsdp"), None),
        P(("dp", "fsdp"), None, None),
        P(),
        P(),
        P(),
        P(),
        P(("dp", "fsdp"), None),
        P(("dp", "fsdp"), None),
        P(("dp", "fsdp"), None),
        P(("dp", "fsdp"), None),
        P(("dp", "fsdp"), None),
        P(("dp", "fsdp"), None),
        P(("dp", "fsdp"), None),
        P(("dp", "fsdp")),
        P(("dp", "fsdp")),
        P(("dp", "fsdp")),
        P(("dp", "fsdp")),
        P(("dp", "fsdp")),
        P(("dp", "fsdp")),
        P(("dp", "fsdp")),
        P(("dp", "fsdp")),
        P(("dp", "fsdp")),
        P(("dp", "fsdp"), None),
        P(("dp", "fsdp")),
    )
    own = mesh.shape["dp"] == 8 and mesh.shape["fsdp"] == 4
    return jax.shard_map(
        linked_body if own else plain_body,
        mesh=mesh,
        in_specs=placed,
        out_specs=(
            P(("dp", "fsdp"), None, None),
            P(("dp", "fsdp")),
            P(("dp", "fsdp"), None, None),
            P(("dp", "fsdp"), None),
            P(("dp", "fsdp"), None),
            P(("dp", "fsdp"), None),
            P(("dp", "fsdp"), None),
            P(("dp", "fsdp"), None),
            P(("dp", "fsdp"), None),
            P(("dp", "fsdp"), None),
            P(("dp", "fsdp")),
            P(("dp", "fsdp")),
            P(("dp", "fsdp")),
            P(("dp", "fsdp")),
            P(("dp", "fsdp")),
            P(("dp", "fsdp")),
            P(("dp", "fsdp")),
            P(("dp", "fsdp")),
            P(("dp", "fsdp")),
            P(("dp", "fsdp"), None),
            P(("dp", "fsdp")),
        ),
        check_vma=False,
    )
```

```python
import functools

import jax
import jax.numpy as jnp
from jax import lax
from jax.experimental import pallas as pl
from jax.experimental.pallas import tpu as pltpu
from jax.sharding import PartitionSpec as P


D = 768
H = 12
HD = 64
LEN = 288
MASKS = 4
SLOT_DEV = 2
GROUP = 4


EPS = 1e-12
NEG = -1000000000.0
HIGH = lax.Precision.HIGHEST
LOSS_WEIGHT = 32.0


def combined_all(value, axis, join):
    pieces = jax.tree.map(lambda part: lax.all_gather(part, axis), value)
    head = jax.tree.map(lambda part: part[0], pieces)
    tail = jax.tree.map(lambda part: part[1:], pieces)
    subtotal, _ = lax.scan(lambda subtotal, share: (join(subtotal, share), None), head, tail)
    return subtotal


def partner(value, axis, stride):
    mask = 2**stride
    pairs = [(source, source ^ mask) for source in range(lax.axis_size(axis))]
    return lax.ppermute(value, axis, pairs)


def layer_norm(residual, gain_vec, shift_vec):
    row_mean = jnp.mean(residual, -1, keepdims=True)
    centred = residual - row_mean
    row_var = jnp.mean(centred * centred, -1, keepdims=True)
    return centred * lax.rsqrt(row_var + EPS) * gain_vec + shift_vec


def exact_gelu(pre_act):
    return jax.nn.gelu(pre_act, approximate=False)


def collect(params):
    (
        query_weight,
        key_weight,
        value_weight,
        out_weight,
        inner_weight,
        outer_weight,
        retrieve_weight,
        query_bias,
        value_bias,
        out_bias,
        norm1_gain,
        norm1_bias,
        inner_bias,
        outer_bias,
        norm2_gain,
        norm2_bias,
    ) = params
    return (
        lax.all_gather(query_weight, ("dp", "fsdp"), axis=0, tiled=True),
        lax.all_gather(key_weight, ("dp", "fsdp"), axis=0, tiled=True),
        lax.all_gather(value_weight, ("dp", "fsdp"), axis=0, tiled=True),
        lax.all_gather(out_weight, ("dp", "fsdp"), axis=0, tiled=True),
        lax.all_gather(inner_weight, ("dp", "fsdp"), axis=0, tiled=True),
        lax.all_gather(outer_weight, ("dp", "fsdp"), axis=0, tiled=True),
        lax.all_gather(retrieve_weight, ("dp", "fsdp"), axis=0, tiled=True),
        lax.all_gather(query_bias, ("dp", "fsdp"), axis=0, tiled=True),
        lax.all_gather(value_bias, ("dp", "fsdp"), axis=0, tiled=True),
        lax.all_gather(out_bias, ("dp", "fsdp"), axis=0, tiled=True),
        lax.all_gather(norm1_gain, ("dp", "fsdp"), axis=0, tiled=True),
        lax.all_gather(norm1_bias, ("dp", "fsdp"), axis=0, tiled=True),
        lax.all_gather(inner_bias, ("dp", "fsdp"), axis=0, tiled=True),
        lax.all_gather(outer_bias, ("dp", "fsdp"), axis=0, tiled=True),
        lax.all_gather(norm2_gain, ("dp", "fsdp"), axis=0, tiled=True),
        lax.all_gather(norm2_bias, ("dp", "fsdp"), axis=0, tiled=True),
    )


def spread(grads):
    (
        grad_qw,
        grad_kw,
        grad_vw,
        grad_ow,
        grad_iw,
        grad_uw,
        grad_rw,
        grad_qb,
        grad_vb,
        grad_ob,
        grad_ga,
        grad_sa,
        grad_ib,
        grad_ub,
        grad_gb,
        grad_sb,
    ) = grads
    return (
        lax.psum_scatter(grad_qw, ("dp", "fsdp"), scatter_dimension=0, tiled=True),
        lax.psum_scatter(grad_kw, ("dp", "fsdp"), scatter_dimension=0, tiled=True),
        lax.psum_scatter(grad_vw, ("dp", "fsdp"), scatter_dimension=0, tiled=True),
        lax.psum_scatter(grad_ow, ("dp", "fsdp"), scatter_dimension=0, tiled=True),
        lax.psum_scatter(grad_iw, ("dp", "fsdp"), scatter_dimension=0, tiled=True),
        lax.psum_scatter(grad_uw, ("dp", "fsdp"), scatter_dimension=0, tiled=True),
        lax.psum_scatter(grad_rw, ("dp", "fsdp"), scatter_dimension=0, tiled=True),
        lax.psum_scatter(grad_qb, ("dp", "fsdp"), scatter_dimension=0, tiled=True),
        lax.psum_scatter(grad_vb, ("dp", "fsdp"), scatter_dimension=0, tiled=True),
        lax.psum_scatter(grad_ob, ("dp", "fsdp"), scatter_dimension=0, tiled=True),
        lax.psum_scatter(grad_ga, ("dp", "fsdp"), scatter_dimension=0, tiled=True),
        lax.psum_scatter(grad_sa, ("dp", "fsdp"), scatter_dimension=0, tiled=True),
        lax.psum_scatter(grad_ib, ("dp", "fsdp"), scatter_dimension=0, tiled=True),
        lax.psum_scatter(grad_ub, ("dp", "fsdp"), scatter_dimension=0, tiled=True),
        lax.psum_scatter(grad_gb, ("dp", "fsdp"), scatter_dimension=0, tiled=True),
        lax.psum_scatter(grad_sb, ("dp", "fsdp"), scatter_dimension=0, tiled=True),
    )


def attention(query_heads, key_heads, value_heads, keys_ok):
    head_scale = HD ** (-0.5)
    scores = (
        jnp.einsum("sqhe,skhe->shqk", query_heads, key_heads, preferred_element_type=jnp.float32)
        * head_scale
    )
    scores = jnp.where(keys_ok[:, None, None, :] > 0, scores, NEG)
    row_peak = jnp.max(scores, -1, keepdims=True)
    exp_scores = jnp.exp(scores - row_peak)
    totals = jnp.sum(exp_scores, -1, keepdims=True)
    attn_probs = (exp_scores / totals).astype(jnp.bfloat16)
    attended = jnp.einsum(
        "shqk,skhe->sqhe", attn_probs, value_heads, preferred_element_type=jnp.float32
    )
    return (attended, row_peak + jnp.log(totals))


def forward_layer(hidden, keys_ok, gathered):
    (
        query_weight,
        key_weight,
        value_weight,
        out_weight,
        inner_weight,
        outer_weight,
        retrieve_weight,
        query_bias,
        value_bias,
        out_bias,
        norm1_gain,
        norm1_bias,
        inner_bias,
        outer_bias,
        norm2_gain,
        norm2_bias,
    ) = gathered
    seq_count = hidden.shape[0]
    head_shape = (seq_count, LEN, H, HD)
    flat_rows = hidden.reshape(seq_count * LEN, D)
    queries = (
        jnp.dot(flat_rows, query_weight, preferred_element_type=jnp.float32)
        + query_bias.astype(jnp.float32)
    ).astype(jnp.bfloat16)
    key_rows = jnp.dot(flat_rows, key_weight, preferred_element_type=jnp.float32).astype(
        jnp.bfloat16
    )
    values = (
        jnp.dot(flat_rows, value_weight, preferred_element_type=jnp.float32)
        + value_bias.astype(jnp.float32)
    ).astype(jnp.bfloat16)
    attended, log_totals = attention(
        queries.reshape(head_shape),
        key_rows.reshape(head_shape),
        values.reshape(head_shape),
        keys_ok,
    )
    attended = attended.reshape(seq_count * LEN, D).astype(jnp.bfloat16)
    first_in = (
        flat_rows.astype(jnp.float32)
        + jnp.dot(attended, out_weight, preferred_element_type=jnp.float32)
        + out_bias.astype(jnp.float32)
    )
    normed_one = layer_norm(
        first_in, norm1_gain.astype(jnp.float32), norm1_bias.astype(jnp.float32)
    ).astype(jnp.bfloat16)
    pre_act = jnp.dot(
        normed_one, inner_weight, preferred_element_type=jnp.float32
    ) + inner_bias.astype(jnp.float32)
    active = exact_gelu(pre_act).astype(jnp.bfloat16)
    second_in = (
        normed_one.astype(jnp.float32)
        + jnp.dot(active, outer_weight, preferred_element_type=jnp.float32)
        + outer_bias.astype(jnp.float32)
    )
    layer_out = layer_norm(
        second_in, norm2_gain.astype(jnp.float32), norm2_bias.astype(jnp.float32)
    ).astype(jnp.bfloat16)
    return (
        queries,
        key_rows,
        values,
        log_totals,
        attended,
        first_in,
        normed_one,
        pre_act,
        active,
        second_in,
        layer_out,
    )


def backward_layer(hidden, keys_ok, gathered, kept_acts, grad_out):
    (
        query_weight,
        key_weight,
        value_weight,
        out_weight,
        inner_weight,
        outer_weight,
        retrieve_weight,
        query_bias,
        value_bias,
        out_bias,
        norm1_gain,
        norm1_bias,
        inner_bias,
        outer_bias,
        norm2_gain,
        norm2_bias,
    ) = gathered
    (
        queries,
        key_rows,
        values,
        log_totals,
        attended,
        first_in,
        normed_one,
        pre_act,
        active,
        second_in,
        layer_out,
    ) = kept_acts
    seq_count = hidden.shape[0]
    head_shape = (seq_count, LEN, H, HD)
    flat_rows = hidden.reshape(seq_count * LEN, D)
    unused_two, norm_two_back = jax.vjp(
        layer_norm, second_in, norm2_gain.astype(jnp.float32), norm2_bias.astype(jnp.float32)
    )
    grad_second, grad_norm2_gain, grad_norm2_bias = norm_two_back(grad_out)
    second_low = grad_second.astype(jnp.bfloat16)
    grad_outer_weight = jnp.dot(active.T, second_low, preferred_element_type=jnp.float32)
    grad_outer_bias = jnp.sum(grad_second, 0)
    grad_active = jnp.dot(second_low, outer_weight.T, preferred_element_type=jnp.float32)
    unused_act, gelu_back = jax.vjp(exact_gelu, pre_act)
    grad_pre = gelu_back(grad_active)[0].astype(jnp.bfloat16)
    grad_inner_weight = jnp.dot(normed_one.T, grad_pre, preferred_element_type=jnp.float32)
    grad_inner_bias = jnp.sum(grad_pre.astype(jnp.float32), 0)
    grad_normed = grad_second + jnp.dot(
        grad_pre, inner_weight.T, preferred_element_type=jnp.float32
    )
    unused_one, norm_one_back = jax.vjp(
        layer_norm, first_in, norm1_gain.astype(jnp.float32), norm1_bias.astype(jnp.float32)
    )
    grad_first, grad_norm1_gain, grad_norm1_bias = norm_one_back(grad_normed)
    first_low = grad_first.astype(jnp.bfloat16)
    grad_out_weight = jnp.dot(attended.T, first_low, preferred_element_type=jnp.float32)
    grad_out_bias = jnp.sum(grad_first, 0)
    grad_attended = (
        jnp.dot(first_low, out_weight.T, preferred_element_type=jnp.float32)
        .astype(jnp.bfloat16)
        .reshape(head_shape)
    )
    query_heads = queries.reshape(head_shape)
    key_heads = key_rows.reshape(head_shape)
    value_heads = values.reshape(head_shape)
    head_scale = HD ** (-0.5)
    scores = (
        jnp.einsum("sqhe,skhe->shqk", query_heads, key_heads, preferred_element_type=jnp.float32)
        * head_scale
    )
    scores = jnp.where(keys_ok[:, None, None, :] > 0, scores, NEG)
    attn_probs = jnp.exp(scores - log_totals)
    grad_probs = jnp.einsum(
        "sqhe,skhe->shqk", grad_attended, value_heads, preferred_element_type=jnp.float32
    )
    grad_value_heads = jnp.einsum(
        "shqk,sqhe->skhe",
        attn_probs.astype(jnp.bfloat16),
        grad_attended,
        preferred_element_type=jnp.float32,
    )
    grad_scores = (
        attn_probs * (grad_probs - jnp.sum(attn_probs * grad_probs, -1, keepdims=True))
    ).astype(jnp.bfloat16)
    grad_query_heads = (
        jnp.einsum("shqk,skhe->sqhe", grad_scores, key_heads, preferred_element_type=jnp.float32)
        * head_scale
    )
    grad_key_heads = (
        jnp.einsum("shqk,sqhe->skhe", grad_scores, query_heads, preferred_element_type=jnp.float32)
        * head_scale
    )
    grad_queries = grad_query_heads.reshape(seq_count * LEN, D).astype(jnp.bfloat16)
    grad_keys = grad_key_heads.reshape(seq_count * LEN, D).astype(jnp.bfloat16)
    grad_values = grad_value_heads.reshape(seq_count * LEN, D).astype(jnp.bfloat16)
    grad_query_weight = jnp.dot(flat_rows.T, grad_queries, preferred_element_type=jnp.float32)
    grad_key_weight = jnp.dot(flat_rows.T, grad_keys, preferred_element_type=jnp.float32)
    grad_value_weight = jnp.dot(flat_rows.T, grad_values, preferred_element_type=jnp.float32)
    grad_query_bias = jnp.sum(grad_queries.astype(jnp.float32), 0)
    grad_value_bias = jnp.sum(grad_values.astype(jnp.float32), 0)
    grad_hidden = (
        grad_first
        + jnp.dot(grad_queries, query_weight.T, preferred_element_type=jnp.float32)
        + jnp.dot(grad_keys, key_weight.T, preferred_element_type=jnp.float32)
        + jnp.dot(grad_values, value_weight.T, preferred_element_type=jnp.float32)
    )
    return (
        grad_hidden,
        (
            grad_query_weight,
            grad_key_weight,
            grad_value_weight,
            grad_out_weight,
            grad_inner_weight,
            grad_outer_weight,
            grad_query_bias,
            grad_value_bias,
            grad_out_bias,
            grad_norm1_gain,
            grad_norm1_bias,
            grad_inner_bias,
            grad_outer_bias,
            grad_norm2_gain,
            grad_norm2_bias,
        ),
    )


def merge_pair(peak_one, total_one, peak_two, total_two):
    peak_new = jnp.maximum(peak_one, peak_two)
    return (
        peak_new,
        total_one * jnp.exp(peak_one - peak_new) + total_two * jnp.exp(peak_two - peak_new),
    )


def merge_rows(one_side, other_side):
    peak_new, total_new = merge_pair(one_side[0], one_side[1], other_side[0], other_side[1])
    return (peak_new, total_new, one_side[2] + other_side[2])


def slot_partial(score_vec, slot_ok):
    grouped = jnp.where(slot_ok, score_vec, NEG).reshape(-1, SLOT_DEV)
    ok_grouped = slot_ok.reshape(-1, SLOT_DEV)
    group_peak = jnp.max(grouped, -1)
    group_total = jnp.sum(jnp.where(ok_grouped, jnp.exp(grouped - group_peak[:, None]), 0.0), -1)
    return (group_peak, group_total)


def plain_body(
    hidden_in,
    token_mask,
    out_grad,
    query_embed,
    slot_valid,
    target_ids,
    target_pos,
    query_weight,
    key_weight,
    value_weight,
    out_weight,
    inner_weight,
    outer_weight,
    retrieve_weight,
    query_bias,
    value_bias,
    out_bias,
    norm1_gain,
    norm1_bias,
    inner_bias,
    outer_bias,
    norm2_gain,
    norm2_bias,
    embedding,
    vocab_bias,
):
    params = (
        query_weight,
        key_weight,
        value_weight,
        out_weight,
        inner_weight,
        outer_weight,
        retrieve_weight,
        query_bias,
        value_bias,
        out_bias,
        norm1_gain,
        norm1_bias,
        inner_bias,
        outer_bias,
        norm2_gain,
        norm2_bias,
    )
    gathered = collect(params)
    kept_acts = forward_layer(hidden_in, token_mask, gathered)
    seq_count = hidden_in.shape[0]
    query_count = seq_count // SLOT_DEV
    out_seq = kept_acts[10].reshape(seq_count, LEN, D)
    devices = lax.axis_size("dp") * lax.axis_size("fsdp")
    device = lax.axis_index("dp") * lax.axis_size("fsdp") + lax.axis_index("fsdp")
    member = lax.axis_index("fsdp") % GROUP
    local_seq = jnp.arange(seq_count, dtype=jnp.int32)
    local_query = device // GROUP * query_count + local_seq // SLOT_DEV
    local_slot = member * SLOT_DEV + local_seq % SLOT_DEV
    slot_ok = slot_valid[local_query, local_slot] > 0
    embeds = query_embed[local_query]
    positions = target_pos[local_query]
    cls_rows = out_seq[:, 0, :].astype(jnp.float32)
    retrieve_full = gathered[6].astype(jnp.float32)
    projected = jnp.dot(cls_rows, retrieve_full, precision=HIGH)
    retrieval = jnp.sum(projected * embeds, -1)
    own_rows = seq_count * MASKS
    sent_rows = out_seq[local_seq[:, None], positions].reshape(own_rows, D)
    all_rows = lax.all_gather(sent_rows, ("dp", "fsdp"), axis=0, tiled=True)
    group_count = devices // GROUP
    all_targets = jnp.broadcast_to(
        target_ids.reshape(group_count, 1, query_count, 1, MASKS),
        (group_count, GROUP, query_count, SLOT_DEV, MASKS),
    ).reshape(-1)
    vocab_rows = embedding.shape[0]
    local_ids = all_targets - device * vocab_rows
    target_hit = jnp.arange(vocab_rows, dtype=jnp.int32)[None, :] == local_ids[:, None]
    logits = jnp.einsum(
        "rd,vd->rv", all_rows, embedding, preferred_element_type=jnp.float32
    ) + vocab_bias.astype(jnp.float32)
    row_peak = jnp.max(logits, -1)
    sum_exp = jnp.sum(jnp.exp(logits - row_peak[:, None]), -1)
    target_logit = jnp.sum(jnp.where(target_hit, logits, 0.0), -1)
    peak_all, total_all, target_all = combined_all(
        (row_peak, sum_exp, target_logit), ("dp", "fsdp"), merge_rows
    )
    lse_rows = peak_all + jnp.log(total_all)
    log_prob = lax.dynamic_slice_in_dim(target_all - lse_rows, device * own_rows, own_rows)
    seq_ll = jnp.mean(log_prob.reshape(seq_count, MASKS), -1)
    joint_score = retrieval + seq_ll
    joint_peak, joint_total = slot_partial(joint_score, slot_ok)
    prior_peak, prior_total = slot_partial(retrieval, slot_ok)
    for bit_number in range(GROUP.bit_length() - 1):
        far_joint_peak, far_joint_total, far_prior_peak, far_prior_total = partner(
            (joint_peak, joint_total, prior_peak, prior_total), "fsdp", bit_number
        )
        joint_peak, joint_total = merge_pair(
            joint_peak, joint_total, far_joint_peak, far_joint_total
        )
        prior_peak, prior_total = merge_pair(
            prior_peak, prior_total, far_prior_peak, far_prior_total
        )
    joint_lse = joint_peak + jnp.log(joint_total)
    prior_lse = prior_peak + jnp.log(prior_total)
    pair_loglik = joint_lse - prior_lse
    post_weight = jnp.where(slot_ok, jnp.exp(joint_score - jnp.repeat(joint_lse, SLOT_DEV)), 0.0)
    prior_weight = jnp.where(slot_ok, jnp.exp(retrieval - jnp.repeat(prior_lse, SLOT_DEV)), 0.0)
    grad_retrieval = LOSS_WEIGHT * (prior_weight - post_weight)
    row_scale = jnp.repeat(-LOSS_WEIGHT * post_weight / MASKS, MASKS)
    all_scales = lax.all_gather(row_scale, ("dp", "fsdp"), axis=0, tiled=True)
    vocab_probs = jnp.exp(logits - lse_rows[:, None])
    grad_logits = all_scales[:, None] * (target_hit.astype(jnp.float32) - vocab_probs)
    grad_vocab_bias = jnp.sum(grad_logits, 0)
    logits_low = grad_logits.astype(jnp.bfloat16)
    grad_embedding = jnp.einsum(
        "rv,rd->vd", logits_low, all_rows, preferred_element_type=jnp.float32
    )
    grad_picked = lax.psum_scatter(
        jnp.dot(logits_low, embedding, preferred_element_type=jnp.float32),
        ("dp", "fsdp"),
        scatter_dimension=0,
        tiled=True,
    )
    grad_project = grad_retrieval[:, None] * embeds
    grad_retrieve_weight = jnp.dot(cls_rows.T, grad_project, precision=HIGH)
    grad_cls = jnp.dot(grad_project, retrieve_full.T, precision=HIGH)
    grad_total = out_grad.astype(jnp.float32)
    grad_total = grad_total.at[local_seq[:, None], positions].add(
        grad_picked.reshape(seq_count, MASKS, D)
    )
    grad_total = grad_total.at[:, 0, :].add(grad_cls)
    grad_total = grad_total.reshape(seq_count * LEN, D)
    grad_hidden, layer_grads = backward_layer(
        hidden_in, token_mask, gathered, kept_acts, grad_total
    )
    (
        grad_query_weight,
        grad_key_weight,
        grad_value_weight,
        grad_out_weight,
        grad_inner_weight,
        grad_outer_weight,
        grad_query_bias,
        grad_value_bias,
        grad_out_bias,
        grad_norm1_gain,
        grad_norm1_bias,
        grad_inner_bias,
        grad_outer_bias,
        grad_norm2_gain,
        grad_norm2_bias,
    ) = layer_grads
    (
        shard_query_weight,
        shard_key_weight,
        shard_value_weight,
        shard_out_weight,
        shard_inner_weight,
        shard_outer_weight,
        shard_retrieve_weight,
        shard_query_bias,
        shard_value_bias,
        shard_out_bias,
        shard_norm1_gain,
        shard_norm1_bias,
        shard_inner_bias,
        shard_outer_bias,
        shard_norm2_gain,
        shard_norm2_bias,
    ) = spread(
        (
            grad_query_weight,
            grad_key_weight,
            grad_value_weight,
            grad_out_weight,
            grad_inner_weight,
            grad_outer_weight,
            grad_retrieve_weight,
            grad_query_bias,
            grad_value_bias,
            grad_out_bias,
            grad_norm1_gain,
            grad_norm1_bias,
            grad_inner_bias,
            grad_outer_bias,
            grad_norm2_gain,
            grad_norm2_bias,
        )
    )
    return (
        out_seq,
        pair_loglik,
        grad_hidden.reshape(seq_count, LEN, D),
        shard_query_weight,
        shard_key_weight,
        shard_value_weight,
        shard_out_weight,
        shard_inner_weight,
        shard_outer_weight,
        shard_retrieve_weight,
        shard_query_bias,
        shard_value_bias,
        shard_out_bias,
        shard_norm1_gain,
        shard_norm1_bias,
        shard_inner_bias,
        shard_outer_bias,
        shard_norm2_gain,
        shard_norm2_bias,
        grad_embedding,
        grad_vocab_bias,
    )

MESH = pl.DeviceIdType.MESH
F32 = jnp.float32
BF = jnp.bfloat16
DMA = pltpu.SemaphoreType.DMA


def coords():
    d = lax.axis_index("dp")
    return d // 4, (d // 2) % 2, d % 2, lax.axis_index("fsdp")


def dev(y, x, c, z):
    return ((y * 2 + x) * 2 + c, z)


def rdma(src, dst, ss, rs, to):
    return pltpu.make_async_remote_copy(src, dst, ss, rs, device_id=to, device_id_type=MESH)


def greet():
    y, x, c, z = coords()
    bar = pltpu.get_barrier_semaphore()
    tos = [dev(y, x, c, lax.rem(z + k, 4)) for k in (1, 2, 3)]
    tos += [dev(y, 1 - x, c, z), dev(1 - y, x, c, z), dev(y, x, 1 - c, z)]
    for t in tos:
        pl.semaphore_signal(bar, inc=1, device_id=t, device_id_type=MESH)
    pl.semaphore_wait(bar, len(tos))


def rows_at(start, size):
    return pl.ds(pl.multiple_of(start, 8), size)


class Gather:
    def __init__(self, src, dst, sems, a):
        self.src, self.dst, self.a = src, dst, a
        self.ss, self.rs, self.ls = sems
        self.r, n = src.shape
        self.split = (n // 2) % 128 == 0
        self.h = n // 2

    def chips(self):
        y, x, c, z = coords()
        return y * 2 + x, y * 2 + 1 - x, (1 - y) * 2 + x, (1 - y) * 2 + 1 - x

    def block(self, chip, k):
        y, x, c, z = coords()
        zz = lax.rem(z + 4 - k, 4)
        return self.dst.at[rows_at(((chip * 2 + c) * 4 + zz) * self.r, self.r)]

    def column(self, chip, c):
        return self.dst.at[rows_at((chip * 2 + c) * 4 * self.r, 4 * self.r)]

    def half(self, ref, right):
        if not self.split:
            return ref
        return ref.at[:, pl.ds(self.h if right else 0, self.h)]

    def copy(self, src, dst, slot, to):
        return rdma(src, dst, self.ss.at[self.a, slot], self.rs.at[self.a, slot], to)

    def send(self, ref, slot, to, src=None):
        self.copy(ref if src is None else src, ref, slot, to).start()

    def wait(self, ref, slot):
        y, x, c, z = coords()
        self.copy(ref, ref, slot, dev(y, 1 - x, c, z)).wait_recv()

    def kept(self):
        return pltpu.make_async_copy(self.src, self.block(self.chips()[0], 0), self.ls.at[self.a])

    def own(self):
        y, x, c, z = coords()
        d = self.block(self.chips()[0], 0)
        self.kept().start()
        self.send(d, 4, dev(y, 1 - x, c, z), self.src)
        self.send(d, 8, dev(1 - y, x, c, z), self.src)
        for k in (1, 3, 2):
            self.send(d, k, dev(y, x, c, lax.rem(z + k, 4)), self.src)

    def z(self, k):
        y, x, c, z = coords()
        d = self.block(self.chips()[0], k)
        self.wait(d, k)
        self.send(d, 4 + k, dev(y, 1 - x, c, z))
        self.send(d, 8 + k, dev(1 - y, x, c, z))

    def core(self, i):
        y, x, c, z = coords()
        if i == 0:
            self.kept().wait()
        self.send(self.column(self.chips()[i], c), 20 + i, dev(y, x, 1 - c, z))

    def xy(self, k):
        y, x, c, z = coords()
        dx = self.block(self.chips()[1], k)
        self.wait(dx, 4 + k)
        self.send(self.half(dx, False), 12 + k, dev(1 - y, x, c, z))
        dy = self.block(self.chips()[2], k)
        self.wait(dy, 8 + k)
        if self.split:
            self.send(self.half(dy, True), 16 + k, dev(y, 1 - x, c, z))

    def dg(self, k):
        d = self.block(self.chips()[3], k)
        self.wait(self.half(d, False), 12 + k)
        if self.split:
            self.wait(self.half(d, True), 16 + k)

    def arrived(self):
        y, x, c, z = coords()
        for i, chip in enumerate(self.chips()):
            self.wait(self.column(chip, 1 - c), 20 + i)

    def sent(self):
        y, x, c, z = coords()
        to = dev(y, 1 - x, c, z)
        d = self.block(self.chips()[0], 0)
        for k in range(4):
            if k:
                self.copy(d, d, k, to).wait_send()
            self.copy(d, d, 4 + k, to).wait_send()
            self.copy(d, d, 8 + k, to).wait_send()
            half = self.half(d, False)
            self.copy(half, half, 12 + k, to).wait_send()
            if self.split:
                self.copy(half, half, 16 + k, to).wait_send()
            col = self.column(self.chips()[0], 0)
            self.copy(col, col, 20 + k, to).wait_send()

    def steps(self):
        out = [functools.partial(self.z, k) for k in (1, 3, 2)]
        out[2] = lambda: (self.z(2), self.core(0))
        out += [functools.partial(self.xy, k) for k in (0, 1, 3)]
        out += [lambda: (self.xy(2), self.core(1), self.core(2))]
        out += [lambda: (self.dg(0), self.dg(1)), lambda: (self.dg(3), self.dg(2), self.core(3))]
        return out


def gather_sems(n):
    return [DMA((n, 24)), DMA((n, 24)), DMA((n,))]


class Scatter:
    def __init__(self, source, bufs, sems, a, done, in_hbm=False):
        self.source, self.a, self.done, self.in_hbm = source, a, done, in_hbm
        self.ss, self.rs, self.ls = sems
        self.held, self.rc, self.ray, self.rax, self.rbx, self.rby, self.rz = bufs
        self.split = self.rbx is not None
        self.h = self.rax.shape[-1]

    def copy(self, src, dst, slot, to):
        return rdma(src, dst, self.ss.at[self.a, slot], self.rs.at[self.a, slot], to)

    def wait(self, ref, slot):
        y, x, c, z = coords()
        self.copy(ref, ref, slot, dev(y, 1 - x, c, z)).wait_recv()

    def local(self, j):
        y, x, c, z = coords()
        return pltpu.make_async_copy(self.source(j, c), self.held.at[j], self.ls.at[self.a, j])

    def core(self, j):
        y, x, c, z = coords()
        if self.in_hbm:
            self.local(j).start()
        self.copy(self.source(j, 1 - c), self.rc.at[j], j, dev(y, x, 1 - c, z)).start()

    def add(self, dst, one, two):
        for i in range(4):
            dst[i] = (one[i].astype(F32) + two[i].astype(F32)).astype(BF)

    def left(self, chip):
        return self.held.at[chip, :, :, pl.ds(0, self.h)]

    def right(self, chip):
        return self.held.at[chip, :, :, pl.ds(self.h, self.h)]

    def first(self):
        y, x, c, z = coords()
        @pl.loop(0, 4)
        def _(j):
            if self.in_hbm:
                self.local(j).wait()
            self.wait(self.rc.at[j], j)
            self.add(self.held.at[j], self.held.at[j] if self.in_hbm else self.source(j, c), self.rc.at[j])
        for xi in range(2):
            self.copy(self.left((1 - y) * 2 + xi), self.ray.at[xi], 4 + xi, dev(1 - y, x, c, z)).start()
        if self.split:
            for yi in range(2):
                self.copy(self.right(yi * 2 + 1 - x), self.rbx.at[yi], 6 + yi, dev(y, 1 - x, c, z)).start()

    def second(self):
        y, x, c, z = coords()
        for xi in range(2):
            self.wait(self.ray.at[xi], 4 + xi)
            d = self.left(y * 2 + xi)
            self.add(d, d, self.ray.at[xi])
        self.copy(self.left(y * 2 + 1 - x), self.rax, 8, dev(y, 1 - x, c, z)).start()
        if self.split:
            for yi in range(2):
                self.wait(self.rbx.at[yi], 6 + yi)
                d = self.right(yi * 2 + x)
                self.add(d, d, self.rbx.at[yi])
            self.copy(self.right((1 - y) * 2 + x), self.rby, 9, dev(1 - y, x, c, z)).start()

    def third(self):
        y, x, c, z = coords()
        me = y * 2 + x
        self.wait(self.rax, 8)
        self.add(self.left(me), self.left(me), self.rax)
        if self.split:
            self.wait(self.rby, 9)
            self.add(self.right(me), self.right(me), self.rby)
        for k in (2, 1, 3):
            zz = lax.rem(z + k, 4)
            self.copy(self.held.at[me, zz], self.rz.at[k - 1], 9 + k, dev(y, x, c, zz)).start()

    def last(self):
        y, x, c, z = coords()
        total = self.held[y * 2 + x, z].astype(F32)
        for k in (1, 2, 3):
            self.wait(self.rz.at[k - 1], 9 + k)
            total = total + self.rz[k - 1].astype(F32)
        self.done(total)

    def sent(self):
        y, x, c, z = coords()
        to = dev(y, 1 - x, c, z)
        refs = [self.rc.at[j] for j in range(4)] + [self.ray.at[0], self.ray.at[1]]
        refs += [self.rbx.at[0], self.rbx.at[1]] if self.split else [None, None]
        refs += [self.rax, self.rby] + [self.rz.at[k] for k in range(3)]
        for slot, ref in enumerate(refs):
            if ref is not None:
                self.copy(ref, ref, slot, to).wait_send()


def scatter_sems(n):
    return [DMA((n, 13)), DMA((n, 13)), DMA((n, 4))]


def scatter_bufs(r, n):
    split = (n // 2) % 128 == 0
    h = n // 2 if split else n
    full, pair, one = pltpu.VMEM((4, 4, r, n), BF), pltpu.VMEM((2, 4, r, h), BF), pltpu.VMEM((4, r, h), BF)
    return [full, full, pair, one] + ([pair, one] if split else []) + [pltpu.VMEM((3, r, n), BF)]


def scatter_refs(refs):
    if len(refs) >= 7 and refs[4].shape == refs[2].shape:
        return refs[:7], refs[7:]
    return (*refs[:4], None, None, refs[4]), refs[5:]


def pipelined(jobs):
    out = []
    for t in range(len(jobs) + 3):
        for lag, name in enumerate(("first", "second", "third", "last")):
            if 0 <= t - lag < len(jobs):
                out.append(getattr(jobs[t - lag], name))
    return out


def at_step(t, steps, start=0, every=1):
    for i, step in enumerate(steps):
        @pl.when(t == start + i * every)
        def _(step=step):
            step()


FF = 4 * D
HI = lax.Precision.HIGHEST

def dot(a, b):
    return lax.dot_general(a, b, (((1,), (0,)), ((), ())), preferred_element_type=F32)

def dot_nt(a, b):
    return lax.dot_general(a, b, (((1,), (1,)), ((), ())), preferred_element_type=F32)

def dot_tn(a, b):
    return lax.dot_general(a, b, (((0,), (0,)), ((), ())), preferred_element_type=F32)

def iota(shape, dim):
    return lax.broadcasted_iota(jnp.int32, shape, dim)

def over(index, n):
    return jnp.floor((index.astype(F32) + 0.5) * (1.0 / n)).astype(jnp.int32)

def expand_vectors(blocks):
    lane, col = iota((128, D), 0), iota((128, D), 1)
    pick = (lane == col - over(col, 24) * 24).astype(F32).astype(BF)
    spread = dot(blocks.reshape(256, 128), pick)
    row, col = iota((256, D), 0), iota((256, D), 1)
    spread = jnp.where(over(row, 8) == over(col, 24), spread, 0.0)
    vec = jnp.sum(spread.reshape(32, 8, D), 0)
    lane, col = iota((128, FF), 0), iota((128, FF), 1)
    pick = (lane - 32 == col - over(col, 96) * 96).astype(F32).astype(BF)
    spread = dot(blocks.reshape(256, 128), pick)
    row, col = iota((256, FF), 0), iota((256, FF), 1)
    inner = jnp.sum(jnp.where(row == over(col, 96) * 8, spread, 0.0), 0, keepdims=True)
    return vec, inner

def norm_stats(r):
    mean = jnp.mean(r, -1, keepdims=True)
    cen = r - mean
    var = jnp.mean(cen * cen, -1, keepdims=True)
    inv = lax.rsqrt(var + EPS)
    return cen * inv, inv


HBM = pl.BlockSpec(memory_space=pltpu.HBM)
VM = pl.BlockSpec(memory_space=pltpu.VMEM)
ACT = ((4, LEN, D), BF)


def sds(shape, dtype):
    return jax.ShapeDtypeStruct(shape, dtype)


def attn_fwd_pair(s, hp, q_ref, k_ref, v_ref, p_ref, o_ref, keys_ok):
    cols = pl.ds(pl.multiple_of(hp * 128, 128), 128)
    q2 = q_ref[s, :, cols]
    k2 = k_ref[s, :, cols]
    v2 = v_ref[s, :, cols]
    low = iota((LEN, 128), 1) < HD
    parts = []
    for h in range(2):
        mine = low if h == 0 else jnp.logical_not(low)
        st = dot_nt(k2, jnp.where(mine, q2 * 0.125, 0.0).astype(BF))
        st = jnp.where(keys_ok, st, NEG)
        e = jnp.exp(st - jnp.max(st, 0, keepdims=True))
        p = (e * (1.0 / jnp.sum(e, 0, keepdims=True))).astype(BF)
        p_ref[s, hp * 2 + h] = p
        parts.append(dot_tn(p, v2))
    o_ref[s, :, cols] = jnp.where(low, parts[0], parts[1]).astype(BF)


def fwd1_body(x_ref, m_ref, sh_small, sh_qkv, sh_wo, sh_wi,
              small, wqkv, wo, wi, q, k, v, p, o, n1, xh1, inv1, vec_ref, ib_ref,
              small_v, wqkv_v, wo_v, q_v, k_v, v_v, p_v, o_v, n1_v, xh1_v, inv1_v, gss, grs, gls, wsem, osem):
    sems = (gss, grs, gls)
    greet()
    gs = [Gather(s, d, sems, a) for a, (s, d) in enumerate(((sh_small, small), (sh_qkv, wqkv), (sh_wo, wo), (sh_wi, wi)))]
    g_small, g_qkv, g_wo, g_wi = gs
    g_small.own()
    g_qkv.own()
    st_small, st_qkv = g_small.steps(), g_qkv.steps()
    for a, b in zip(st_small[:3], st_qkv[:3]):
        a()
        b()
    g_wo.own()
    g_wi.own()
    for a, b in zip(st_small[3:], st_qkv[3:]):
        a()
        b()
    g_small.arrived()
    g_qkv.arrived()
    loads = [pltpu.make_async_copy(small, small_v, wsem.at[0]), pltpu.make_async_copy(wqkv, wqkv_v, wsem.at[1])]
    for cp in loads:
        cp.start()
    loads[0].wait()
    vec, inner = expand_vectors(small_v[...].reshape(32, 32, 128)[:, 24:, :])
    vec_ref[...] = vec
    ib_ref[...] = inner
    loads[1].wait()
    wo_steps, wi_steps = g_wo.steps(), g_wi.steps()
    steps = wo_steps[:3] + wi_steps[:1] + wo_steps[3:7] + wi_steps[1:2] + wo_steps[7:] + wi_steps[2:]
    outs = [(q_v, q), (k_v, k), (v_v, v), (p_v, p), (o_v, o)]
    def put(a, s):
        return pltpu.make_async_copy(outs[a][0].at[s], outs[a][1].at[s], osem.at[a, s])
    @pl.loop(0, 4)
    def _(s):
        x = x_ref[s]
        for j, ref in enumerate((q_v, k_v, v_v)):
            t = dot(x, wqkv_v[:, pl.ds(j * D, D)])
            if j != 1:
                t = t + vec_ref[0 if j == 0 else 1][None]
            ref[s] = t.astype(BF)
            put(j, s).start()
        count = jnp.sum(m_ref[pl.ds(s, 1), :], -1, keepdims=True)
        keys_ok = iota((LEN, 1), 0) < count
        @pl.loop(0, H // 2)
        def _(hp):
            at_step(s * 6 + hp, steps, 2)
            attn_fwd_pair(s, hp, q_v, k_v, v_v, p_v, o_v, keys_ok)
        put(3, s).start()
        put(4, s).start()
    g_wo.arrived()
    load = pltpu.make_async_copy(wo, wo_v, wsem.at[2])
    load.start()
    load.wait()
    more = [(n1_v, n1), (xh1_v, xh1), (inv1_v, inv1)]
    def put2(a, s):
        return pltpu.make_async_copy(more[a][0].at[s], more[a][1].at[s], osem.at[5 + a, s])
    @pl.loop(0, 4)
    def _(s):
        r1 = x_ref[s].astype(F32) + dot(o_v[s], wo_v[...]) + vec_ref[2][None]
        xh, inv = norm_stats(r1)
        xh1_v[s] = xh.astype(BF)
        inv1_v[s] = jnp.broadcast_to(inv, (LEN, 128))
        n1_v[s] = (xh * vec_ref[3][None] + vec_ref[4][None]).astype(BF)
        for a in range(3):
            put2(a, s).start()
    g_wi.arrived()
    for s in range(4):
        for a in range(5):
            put(a, s).wait()
        for a in range(3):
            put2(a, s).wait()
    for g in gs:
        g.sent()


def fwd1(x, mask, small, qkv, wo, wi, cid):
    shards = (small, qkv, wo, wi)
    full = [((32 * s.shape[0], s.shape[1]), BF) for s in shards]
    probs, stat = ((4, H, LEN, LEN), BF), ((4, LEN, 128), F32)
    outs = full + [ACT, ACT, ACT, probs, ACT, ACT, ACT, stat] + [((8, D), F32), ((1, FF), F32)]
    return pl.pallas_call(
        fwd1_body, name="attention_forward", out_shape=[sds(*o) for o in outs],
        in_specs=[VM, VM] + [HBM] * 4, out_specs=[HBM] * 12 + [VM] * 2,
        scratch_shapes=[pltpu.VMEM(*o) for o in full[:3] + [ACT, ACT, ACT, probs, ACT, ACT, ACT, stat]]
        + gather_sems(4) + [DMA((3,)), DMA((8, 4))],
        compiler_params=pltpu.CompilerParams(collective_id=cid, has_side_effects=True, vmem_limit_bytes=58 << 20),
    )(x, mask, *shards)


def gelu_pair(z):
    e = jnp.exp(-0.5 * z * z)
    t = 1.0 / (1.0 + (0.3275911 * 0.7071067811865476) * jnp.abs(z))
    poly = t * (0.254829592 + t * (-0.284496736 + t * (1.421413741 + t * (-1.453152027 + t * 1.061405429))))
    tail = 0.5 * poly * e
    cdf = jnp.where(z >= 0, 1.0 - tail, tail)
    return z * cdf, cdf + z * e * 0.3989422804014327


def fwd2_body(n1_ref, wi, vec_ref, ib_ref, pos_ref, sh_wu,
              wu, g, dg, lo, xh2, inv2, picked_ref,
              wi_v, wu_v, g_v, dg_v, lo_v, xh2_v, inv2_v, gss, grs, gls, wsem, osem):
    loads = [pltpu.make_async_copy(wi.at[:, pl.ds(j * D, D)], wi_v.at[:, pl.ds(j * D, D)], wsem.at[j]) for j in range(4)]
    for cp in loads:
        cp.start()
    greet()
    g_wu = Gather(sh_wu, wu, (gss, grs, gls), 0)
    g_wu.own()
    steps = g_wu.steps()
    for cp in loads:
        cp.wait()
    outs = [(g_v, g), (dg_v, dg), (lo_v, lo), (xh2_v, xh2), (inv2_v, inv2)]
    def put(a, s):
        return pltpu.make_async_copy(outs[a][0].at[s], outs[a][1].at[s], osem.at[a, s])
    @pl.loop(0, 4)
    def _(s):
        n1 = n1_ref[s]
        @pl.loop(0, 4)
        def _(j):
            at_step(s * 4 + j, steps, 3)
            cols = pl.ds(pl.multiple_of(j * D, D), D)
            act, slope = gelu_pair(dot(n1, wi_v[:, cols]) + ib_ref[:, cols])
            g_v[s, :, cols] = act.astype(BF)
            dg_v[s, :, cols] = slope.astype(BF)
        put(0, s).start()
        put(1, s).start()
    g_wu.arrived()
    load = pltpu.make_async_copy(wu, wu_v, wsem.at[4])
    load.start()
    load.wait()
    @pl.loop(0, 4)
    def _(s):
        r2 = n1_ref[s].astype(F32) + dot(g_v[s], wu_v[...]) + vec_ref[5][None]
        xh, inv = norm_stats(r2)
        xh2_v[s] = xh.astype(BF)
        inv2_v[s] = jnp.broadcast_to(inv, (LEN, 128))
        out = (xh * vec_ref[6][None] + vec_ref[7][None]).astype(BF)
        lo_v[s] = out
        picked_ref[s] = dot((iota((8, LEN), 1) == pos_ref[s]).astype(F32).astype(BF), out).astype(BF)
        for a in (2, 3, 4):
            put(a, s).start()
    for s in range(4):
        for a in range(5):
            put(a, s).wait()
    g_wu.sent()


def fwd2(n1, wi, vec, ib, pos, wu, cid):
    big, stat = ((4, LEN, FF), BF), ((4, LEN, 128), F32)
    outs = [((FF, D), BF), big, big, ACT, ACT, stat, ((4, 8, D), BF)]
    return pl.pallas_call(
        fwd2_body, name="feed_forward", out_shape=[sds(*o) for o in outs],
        in_specs=[VM, HBM, VM, VM, VM, HBM], out_specs=[HBM] * 6 + [VM],
        scratch_shapes=[pltpu.VMEM(*o) for o in [((D, FF), BF), ((FF, D), BF), big, big, ACT, ACT, stat]]
        + gather_sems(1) + [DMA((5,)), DMA((5, 4))],
        compiler_params=pltpu.CompilerParams(collective_id=cid, has_side_effects=True, vmem_limit_bytes=58 << 20),
    )(n1, wi, vec, ib, pos, wu)


def norm_back(dy, xh, inv, gain):
    c = dy * gain
    return (c - jnp.mean(c, -1, keepdims=True) - xh * jnp.mean(c * xh, -1, keepdims=True)) * inv


def bwd1_body(og_ref, add_ref, pos_ref, xh2_ref, inv2_ref, vec_ref, g, dg, n1, wi, wu,
              gu_ref, gi, dn1, sums_ref, sumi_ref,
              g_v, dg_v, n1_v, wi_v, wu_v, d2_v, dn1_v, gu_v, gi_v, sss, srs, sls, isem, osem, *bufs):
    ins = [(g, g_v), (wu, wu_v), (dg, dg_v), (wi, wi_v), (n1, n1_v)]
    loads = [pltpu.make_async_copy(a, b, isem.at[i]) for i, (a, b) in enumerate(ins)]
    for cp in loads:
        cp.start()
    sems = (sss, srs, sls)
    greet()
    jobs = []
    for t in range(3):
        own, bufs = scatter_refs(bufs)
        def source(j, c, t=t):
            return gu_v.at[j, c, :, :, pl.ds(256 * t, 256)]
        def done(total, t=t):
            gu_ref[:, pl.ds(256 * t, 256)] = total
        jobs.append(Scatter(source, own, sems, t, done))
    sums_ref[...] = jnp.zeros_like(sums_ref)
    sumi_ref[...] = jnp.zeros_like(sumi_ref)
    @pl.loop(0, 4)
    def _(s):
        hit = (iota((LEN, 8), 0) == pos_ref[s]).astype(F32)
        extra = lax.dot_general(hit, add_ref[s], (((1,), (0,)), ((), ())), preferred_element_type=F32, precision=HI)
        dy = og_ref[s].astype(F32) + extra
        xh = xh2_ref[s].astype(F32)
        dr2 = norm_back(dy, xh, inv2_ref[s][:, 0:1], vec_ref[6][None])
        sums_ref[0] += jnp.sum(dy * xh, 0)
        sums_ref[1] += jnp.sum(dy, 0)
        sums_ref[2] += jnp.sum(dr2, 0)
        d2_v[pl.ds(s * LEN, LEN)] = dr2.astype(BF)
        dn1_v[s] = dr2
    loads[0].wait()
    @pl.loop(0, 4)
    def _(j):
        cols = pl.ds(pl.multiple_of(j * D, D), D)
        t = dot_tn(g_v[:, :, cols].reshape(4 * LEN, D), d2_v[...])
        gu_v[j] = t.astype(BF).reshape(2, 4, 96, D)
        for job in jobs:
            job.core(j)
    for cp in loads[1:]:
        cp.wait()
    steps = pipelined(jobs)
    def put(s):
        return pltpu.make_async_copy(dn1_v.at[s], dn1.at[s], osem.at[s])
    @pl.loop(0, 4)
    def _(s):
        @pl.loop(0, 4)
        def _(j):
            at_step(s * 4 + j, steps, 2)
            cols = pl.ds(pl.multiple_of(j * D, D), D)
            dz = dot_nt(d2_v[pl.ds(s * LEN, LEN)], wu_v[pl.ds(pl.multiple_of(j * D, D), D), :]) * dg_v[s, :, cols].astype(F32)
            dz = dz.astype(BF)
            sumi_ref[0:1, cols] += jnp.sum(dz.astype(F32), 0, keepdims=True)
            dg_v[s, :, cols] = dz
            dn1_v[s] += dot_nt(dz, wi_v[:, cols])
        put(s).start()
    def puti(j):
        return pltpu.make_async_copy(gi_v.at[:, pl.ds(pl.multiple_of(j * D, D), D)], gi.at[:, pl.ds(pl.multiple_of(j * D, D), D)], osem.at[4 + j])
    @pl.loop(0, 4)
    def _(j):
        cols = pl.ds(pl.multiple_of(j * D, D), D)
        gi_v[:, cols] = dot_tn(n1_v[...].reshape(4 * LEN, D), dg_v[:, :, cols].reshape(4 * LEN, D)).astype(BF)
        puti(j).start()
    for i in range(4):
        put(i).wait()
        puti(i).wait()
    for job in jobs:
        job.sent()


def bwd1(og, add, pos, xh2, inv2, vec, g, dg, n1, wi, wu, cid):
    outs = [((96, D), F32), ((D, FF), BF), ((4, LEN, D), F32), ((8, D), F32), ((8, FF), F32)]
    big = ((4, LEN, FF), BF)
    scratch = [big, big, ACT, ((D, FF), BF), ((FF, D), BF), ((4 * LEN, D), BF), ((4, LEN, D), F32), ((4, 2, 4, 96, D), BF), ((D, FF), BF)]
    return pl.pallas_call(
        bwd1_body, name="feed_forward_backward", out_shape=[sds(*o) for o in outs],
        in_specs=[VM] * 6 + [HBM] * 5, out_specs=[VM, HBM, HBM, VM, VM],
        scratch_shapes=[pltpu.VMEM(*s) for s in scratch] + scatter_sems(3) + [DMA((5,)), DMA((8,))] + scatter_bufs(96, 256) * 3,
        compiler_params=pltpu.CompilerParams(collective_id=cid, has_side_effects=True, vmem_limit_bytes=61 << 20),
    )(og, add, pos, xh2, inv2, vec, g, dg, n1, wi, wu)


def attn_bwd_pair(s, hp, q_ref, k_ref, v_ref, p_ref, slot, do_ref, dqkv_ref):
    cols = pl.ds(pl.multiple_of(hp * 128, 128), 128)
    rows = pl.ds(pl.multiple_of(s * LEN, LEN), LEN)
    q2 = q_ref[s, :, cols]
    k2 = k_ref[s, :, cols]
    v2 = v_ref[s, :, cols]
    do2 = do_ref[rows, cols]
    low = iota((LEN, 128), 1) < HD
    dq, dk, dv = [], [], []
    for h in range(2):
        mine = low if h == 0 else jnp.logical_not(low)
        pt = p_ref[slot, h]
        dpt = dot_nt(v2, jnp.where(mine, do2, jnp.zeros_like(do2)))
        pf = pt.astype(F32)
        ds = (pf * (dpt - jnp.sum(pf * dpt, 0, keepdims=True))).astype(BF)
        dv.append(dot(pt, do2))
        dk.append(dot(ds, q2))
        dq.append(dot_tn(ds, k2))
    for i, (pair, scale) in enumerate(((dq, 0.125), (dk, 0.125), (dv, 1.0))):
        dqkv_ref[i, rows, cols] = (jnp.where(low, pair[0], pair[1]) * scale).astype(BF)


def bwd2_body(dn1, xh1, inv1, vec_ref, x, q, k, v, p, o, wqkv, wo, gi, grw_ref, s2_ref, si_ref,
              ggq, ggk, ggv, ggo, ggi, ggs, dx,
              dn1_v, xh1_v, inv1_v, x_v, q_v, k_v, v_v, o_v, p_v, wqkv_v, wo_v, sums_v, sumq_v, d1_v, do_v, dqkv_v, go_v, gg_v, gsm_v,
              sss, srs, sls, isem, psem, osem, *bufs):
    ins = [(dn1, dn1_v), (xh1, xh1_v), (inv1, inv1_v), (o, o_v), (wo, wo_v), (q, q_v), (k, k_v), (v, v_v), (x, x_v), (wqkv, wqkv_v)]
    loads = [pltpu.make_async_copy(a, b, isem.at[i]) for i, (a, b) in enumerate(ins)]
    for cp in loads:
        cp.start()
    sems = (sss, srs, sls)
    greet()
    jobs = []
    def add_job(source, done, in_hbm=False):
        nonlocal bufs
        own, bufs = scatter_refs(bufs)
        jobs.append(Scatter(source, own, sems, len(jobs), done, in_hbm))
    for t in range(4):
        def done(total, t=t):
            ggi[:, pl.ds(t * D, D)] = total
        add_job(lambda j, c, t=t: gi.at[j, c, :, :, pl.ds(t * D, D)], done, True)
    def done_o(total):
        ggo[...] = total
    add_job(lambda j, c: go_v.at[j, c], done_o)
    for t in range(3):
        def done(total, t=t):
            for i, ref in enumerate((ggq, ggk, ggv)):
                ref[:, pl.ds(256 * t, 256)] = total[:, 256 * i : 256 * i + 256]
        add_job(lambda j, c, t=t: gg_v.at[t, j, c], done)
    def done_s(total):
        ggs[...] = total
    add_job(lambda j, c: gsm_v.at[j, c], done_s)
    for t in range(4):
        for j in range(4):
            jobs[t].core(j)
    sums_v[...] = jnp.zeros_like(sums_v)
    sumq_v[...] = jnp.zeros_like(sumq_v)
    for cp in loads[:3]:
        cp.wait()
    @pl.loop(0, 4)
    def _(s):
        dy = dn1_v[s]
        xh = xh1_v[s].astype(F32)
        dr1 = norm_back(dy, xh, inv1_v[s][:, 0:1], vec_ref[3][None])
        sums_v[0] += jnp.sum(dy * xh, 0)
        sums_v[1] += jnp.sum(dy, 0)
        sums_v[2] += jnp.sum(dr1, 0)
        dn1_v[s] = dr1
        d1_v[pl.ds(s * LEN, LEN)] = dr1.astype(BF)
    for cp in loads[3:5]:
        cp.wait()
    go_v[...] = dot_tn(o_v[...].reshape(4 * LEN, D), d1_v[...]).astype(BF).reshape(4, 2, 4, 24, D)
    for j in range(4):
        jobs[4].core(j)
    @pl.loop(0, 4)
    def _(s):
        rows = pl.ds(pl.multiple_of(s * LEN, LEN), LEN)
        do_v[rows] = dot_nt(d1_v[rows], wo_v[...]).astype(BF)
    for cp in loads[5:9]:
        cp.wait()
    steps = pipelined(jobs[:5])
    def probs(t):
        hp, s = t // 4, lax.rem(t, 4)
        return pltpu.make_async_copy(p.at[s, pl.ds(hp * 2, 2)], p_v.at[lax.rem(t, 2)], psem.at[lax.rem(t, 2)])
    probs(0).start()
    for grp in range(3):
        @pl.loop(0, 8)
        def _(i, grp=grp):
            t = grp * 8 + i
            @pl.when(t + 1 < 24)
            def _():
                probs(t + 1).start()
            at_step(i, steps[8 * grp : 8 * grp + 8])
            probs(t).wait()
            attn_bwd_pair(lax.rem(t, 4), t // 4, q_v, k_v, v_v, p_v, lax.rem(t, 2), do_v, dqkv_v)
        cols = pl.ds(256 * grp, 256)
        for i in range(3):
            d = dqkv_v[i, :, cols]
            sumq_v[i : i + 1, cols] = jnp.sum(d.astype(F32), 0, keepdims=True)
            gg_v[grp, :, :, :, :, pl.ds(256 * i, 256)] = dot_tn(x_v[...].reshape(4 * LEN, D), d).astype(BF).reshape(4, 2, 4, 24, 256)
        for j in range(4):
            jobs[5 + grp].core(j)
    gsm_v[...] = small_grads(grw_ref[...], sums_v[...], s2_ref[...], sumq_v[...], si_ref[...]).reshape(4, 2, 4, 32, 128)
    for j in range(4):
        jobs[8].core(j)
    loads[9].wait()
    late = pipelined(jobs[5:])
    def put(s):
        return pltpu.make_async_copy(dn1_v.at[s], dx.at[s], osem.at[s])
    @pl.loop(0, 4)
    def _(s):
        rows = pl.ds(pl.multiple_of(s * LEN, LEN), LEN)
        for i in range(3):
            at_step(s * 3 + i, late)
            dn1_v[s] += dot_nt(dqkv_v[i, rows], wqkv_v[:, pl.ds(i * D, D)])
        put(s).start()
    for step in late[12:]:
        step()
    for s in range(4):
        put(s).wait()
    for job in jobs:
        job.sent()


def small_grads(grw, s1, s2, sq, si):
    vec = jnp.concatenate([sq[0:1], sq[2:3], s1[2:3], s1[0:1], s1[1:2], s2[2:3], s2[0:1], s2[1:2]], 0)
    row, col = iota((256, D), 0), iota((256, D), 1)
    tiled = jnp.broadcast_to(vec[None], (32, 8, D)).reshape(256, D)
    part = jnp.where(over(row, 8) == over(col, 24), tiled, 0.0).astype(BF)
    lane, col = iota((128, D), 0), iota((128, D), 1)
    pick = (lane == col - over(col, 24) * 24).astype(F32).astype(BF)
    out = dot_nt(part, pick).reshape(32, 8, 128)
    row, col = iota((32, FF), 0), iota((32, FF), 1)
    part = jnp.where(row == over(col, 96), si[0:1], 0.0).astype(BF)
    lane, col = iota((128, FF), 0), iota((128, FF), 1)
    pick = (lane - 32 == col - over(col, 96) * 96).astype(F32).astype(BF)
    inner = dot_nt(part, pick)
    out = out + jnp.where(iota((32, 8, 128), 1) == 0, inner[:, None, :], 0.0)
    return jnp.concatenate([grw.reshape(32, 24, 128), out], 1).astype(BF)


def bwd2(dn1, xh1, inv1, vec, x, q, k, v, p, o, wqkv, wo, gi, grw, s2, si, cid):
    own = ((24, D), F32)
    outs = [own, own, own, own, ((24, FF), F32), ((32, 128), F32), ((4, LEN, D), F32)]
    six = ((4, 2, 4, 24, D), BF)
    scratch = [((4, LEN, D), F32), ACT, ((4, LEN, 128), F32), ACT, ACT, ACT, ACT, ACT, ((2, 2, LEN, LEN), BF), ((D, 3 * D), BF), ((D, D), BF),
               ((8, D), F32), ((8, D), F32), ((4 * LEN, D), BF), ((4 * LEN, D), BF), ((3, 4 * LEN, D), BF), six, ((3,) + six[0], BF), ((4, 2, 4, 32, 128), BF)]
    return pl.pallas_call(
        bwd2_body, name="attention_backward", out_shape=[sds(*s) for s in outs],
        in_specs=[HBM] * 3 + [VM] + [HBM] * 9 + [VM] * 3, out_specs=[VM] * 6 + [HBM],
        scratch_shapes=[pltpu.VMEM(*s) for s in scratch] + scatter_sems(9) + [DMA((10,)), DMA((2,)), DMA((4,))]
        + scatter_bufs(24, D) * 8 + scatter_bufs(32, 128),
        compiler_params=pltpu.CompilerParams(collective_id=cid, has_side_effects=True, vmem_limit_bytes=61 << 20),
    )(dn1, xh1, inv1, vec, x, q, k, v, p, o, wqkv, wo, gi.reshape(4, 2, 4, 24, FF), grw, s2, si)


def exact(a, b, dims=((1,), (0,))):
    return lax.dot_general(a, b, (dims, ((), ())), preferred_element_type=F32, precision=HI)

def as_f(cond):
    return cond.astype(F32)

def greet_all():
    me = lax.axis_index("dp") * 4 + lax.axis_index("fsdp")
    bar = pltpu.get_barrier_semaphore()
    @pl.loop(1, 32)
    def _(k):
        t = lax.rem(me + k, 32)
        pl.semaphore_signal(bar, inc=1, device_id=(t // 4, lax.rem(t, 4)), device_id_type=MESH)
    pl.semaphore_wait(bar, 31)

def loss_body(picked_ref, emb_ref, vb_ref, ids_ref, valid_ref, qe_ref, small_ref,
              add_ref, grw_ref, pair_ref, ge_ref, gvb_ref,
              own_ref, rows_ref, lt_ref, st_ref, all_ref, dh_ref, dhout_ref, gss, grs, gls, sss, srs, sls, xs, xr, *bufs):
    me = lax.axis_index("dp") * 4 + lax.axis_index("fsdp")
    VS = emb_ref.shape[0]
    greet_all()
    own_ref[...] = picked_ref[:, 0:4, :].astype(F32).reshape(16, D).astype(BF)
    g = Gather(own_ref, rows_ref, (gss, grs, gls), 0)
    g.own()
    cls = picked_ref[:, 4:5, :].astype(F32).reshape(4, D)
    cls8 = jnp.concatenate([cls, jnp.zeros((4, D), F32)], 0)
    rw = small_ref[:, 0:24, :].reshape(D, 128)
    row8, lane8 = iota((8, 128), 0), iota((8, 128), 1)
    qpick = as_f(jnp.logical_and(iota((8, 16), 1) == (me // 4) * 2 + iota((8, 16), 0) // 2, iota((8, 16), 0) < 4))
    qe_own = exact(qpick, qe_ref[...])
    score = jnp.sum(dot(cls8.astype(BF), rw) * qe_own, -1, keepdims=True)
    st_ref[12:13] = jnp.sum(jnp.where(row8 == lane8, score, 0.0), 0, keepdims=True)
    r512 = iota((16, 512), 1)
    s_of = r512 >> 2
    q_of = (s_of >> 4) * 2 + ((s_of & 3) >> 1)
    spread = exact(ids_ref[...].astype(F32), as_f(iota((4, 512), 0) == (iota((4, 512), 1) & 3)))
    ids = jnp.sum(jnp.where(iota((16, 512), 0) == q_of, spread, 0.0), 0, keepdims=True)
    local = ids.astype(jnp.int32) - me * VS
    for step in g.steps():
        step()
    g.arrived()
    g.sent()
    rows = rows_ref[...]
    lt = dot_nt(emb_ref[...], rows) + vb_ref[...]
    lt_ref[...] = lt
    hit = iota((VS, 512), 0) == local
    peak = jnp.max(lt, 0, keepdims=True)
    total = jnp.sum(jnp.exp(lt - peak), 0, keepdims=True)
    target = jnp.sum(jnp.where(hit, lt, 0.0), 0, keepdims=True)
    for a in range(4):
        cols = slice(a * 128, a * 128 + 128)
        st_ref[a:a + 1] = peak[:, cols]
        st_ref[4 + a:5 + a] = total[:, cols]
        st_ref[8 + a:9 + a] = target[:, cols]
    sends = []
    for k in range(1, 32):
        t = lax.rem(me + k, 32)
        cp = rdma(st_ref, all_ref.at[me], xs.at[k], xr.at[k], (t // 4, lax.rem(t, 4)))
        cp.start()
        sends.append(cp)
    all_ref[me] = st_ref[...]
    for k in range(1, 32):
        f = lax.rem(me + 32 - k, 32)
        rdma(st_ref, all_ref.at[f], xs.at[k], xr.at[k], (f // 4, lax.rem(f, 4))).wait_recv()
    peaks = all_ref[:, 0:4, :]
    top = jnp.max(peaks, 0)
    tot = jnp.sum(all_ref[:, 4:8, :] * jnp.exp(peaks - top[None]), 0)
    lse = top + jnp.log(tot)
    logp = jnp.sum(all_ref[:, 8:12, :], 0) - lse
    i0, i1 = iota((128, 128), 0), iota((128, 128), 1)
    logp8 = jnp.concatenate([logp, jnp.zeros((4, 128), F32)], 0)
    spread = exact(logp8, 0.25 * as_f((i0 >> 2) == (i1 & 31)))
    seq_ll = jnp.sum(jnp.where((lane8 >> 5) == row8, spread, 0.0), 0, keepdims=True)
    spread = exact(all_ref[:, 12, :], as_f(i0 == (i1 & 3)))
    retrieval = jnp.sum(jnp.where((iota((32, 128), 1) >> 2) == iota((32, 128), 0), spread, 0.0), 0, keepdims=True)
    q16, s16 = iota((16, 128), 0), iota((16, 128), 1)
    mine = q16 == (s16 >> 4) * 2 + ((s16 & 3) >> 1)
    s8 = iota((8, 128), 1)
    slot_pick = as_f(iota((8, 128), 0) == ((s8 >> 2) & 3) * 2 + (s8 & 1))
    ok16 = jnp.logical_and(mine, exact(valid_ref[...].astype(F32), slot_pick) > 0.5)
    joint = retrieval + seq_ll
    def slot_lse(v):
        m = jnp.max(jnp.where(ok16, v, NEG), -1, keepdims=True)
        return m + jnp.log(jnp.sum(jnp.where(ok16, jnp.exp(v - m), 0.0), -1, keepdims=True))
    def to_seq(v):
        return jnp.sum(jnp.where(mine, v, 0.0), 0, keepdims=True)
    joint_lse, prior_lse = slot_lse(joint), slot_lse(retrieval)
    ok = to_seq(as_f(ok16)) > 0.5
    post = jnp.where(ok, jnp.exp(joint - to_seq(joint_lse)), 0.0)
    prior = jnp.where(ok, jnp.exp(retrieval - to_seq(prior_lse)), 0.0)
    pair = jnp.sum(jnp.where(q16 == (me // 4) * 2 + s16, joint_lse - prior_lse, 0.0), 0, keepdims=True)
    pair_ref[...] = jnp.broadcast_to(pair, (8, 128))
    d_score = LOSS_WEIGHT * (prior - post)
    scale = exact(jnp.broadcast_to(-LOSS_WEIGHT * post / 4.0, (8, 128)), as_f(iota((128, 512), 0) == (iota((128, 512), 1) >> 2)))[0:1]
    lse_row = jnp.concatenate([lse[a:a + 1] for a in range(4)], 1)
    dl = scale * (as_f(hit) - jnp.exp(lt_ref[...] - lse_row))
    gvb_ref[...] = jnp.sum(dl, -1, keepdims=True)
    db = dl.astype(BF)
    dh_ref[...] = dot_tn(db, emb_ref[...]).astype(BF).reshape(4, 2, 4, 16, D)
    def done(total):
        dhout_ref[...] = total
    sc = Scatter(lambda j, c: dh_ref.at[j, c], scatter_refs(bufs)[0], (sss, srs, sls), 0, done)
    for j in range(4):
        sc.core(j)
    du = jnp.sum(jnp.where(jnp.logical_and(lane8 == me * 4 + row8, row8 < 4), d_score, 0.0), -1, keepdims=True) * qe_own
    grw_ref[...] = exact(cls8, du, ((0,), (0,)))
    dcls = exact(du, rw.astype(F32), ((1,), (1,)))
    add_ref[...] = jnp.zeros_like(add_ref)
    for l in range(4):
        add_ref[l, 4:5] = dcls[l:l + 1]
    sc.first()
    ge_ref[...] = dot(db, rows)
    sc.second()
    sc.third()
    sc.last()
    sc.sent()
    for l in range(4):
        add_ref[l, 0:4] = dhout_ref[4 * l:4 * l + 4]
    for cp in sends:
        cp.wait_send()

def loss_call(picked, emb, vb, ids, valid, qe, small, cid):
    VS = emb.shape[0]
    outs = [((4, 8, D), F32), ((D, 128), F32), ((8, 128), F32), ((VS, D), F32), ((VS, 1), F32)]
    args = (picked, emb, vb, ids, valid, qe, small)
    return pl.pallas_call(loss_body, name="slot_loss", out_shape=[jax.ShapeDtypeStruct(s, t) for s, t in outs],
        in_specs=[VM] * len(args), out_specs=[VM] * len(outs),
        scratch_shapes=[pltpu.VMEM((16, D), BF), pltpu.VMEM((512, D), BF), pltpu.VMEM((VS, 512), F32), pltpu.VMEM((16, 128), F32),
            pltpu.VMEM((32, 16, 128), F32), pltpu.VMEM((4, 2, 4, 16, D), BF), pltpu.VMEM((16, D), F32),
            *gather_sems(1), *scatter_sems(1), DMA((32,)), DMA((32,))] + scatter_bufs(16, D),
        compiler_params=pltpu.CompilerParams(collective_id=cid, has_side_effects=True, vmem_limit_bytes=58 << 20))(*args)


def linked_body(hidden_in, token_mask, out_grad, query_embed, slot_valid, target_ids, target_pos,
                qw, kw, vw, ow, iw, uw, rw, qb, vb, ob, ga, sa, ib, ub, gb, sb, embedding, vocab_bias):
    block = jnp.pad(jnp.stack([qb, vb, ob, ga, sa, ub, gb, sb]), ((0, 0), (0, 104)))
    block = jnp.concatenate([rw, block + jnp.pad(ib[None], ((0, 7), (32, 0)))], 0)
    group = (lax.axis_index("dp") * lax.axis_size("fsdp") + lax.axis_index("fsdp")) // GROUP
    pos = lax.dynamic_slice_in_dim(target_pos, group * 2, 2)
    pos = jnp.concatenate([pos, jnp.zeros((2, 1), jnp.int32), jnp.full((2, 3), -1, jnp.int32)], 1)
    pos = jnp.repeat(pos, 2, 0)
    pos_row, pos_col = pos[:, None, :], pos[:, :, None]
    small, wqkv, wo, wi, q, k, v, p, o, n1, xh1, inv1, vec, inner = fwd1(
        hidden_in, token_mask, block, jnp.concatenate([qw, kw, vw], 1), ow, iw, 0)
    wu, g, dg, out_seq, xh2, inv2, picked = fwd2(n1, wi, vec, inner, pos_col, uw, 1)
    add, grw, pair, ge, gvb = loss_call(
        picked, embedding, vocab_bias.astype(F32)[:, None], target_ids, slot_valid, query_embed, small.reshape(32, 32, 128), 2)
    gu, gi, dn1, s2, si = bwd1(out_grad, add, pos_row, xh2, inv2, vec, g, dg, n1, wi, wu, 3)
    gq, gk, gv, go, gi, gsm, dx = bwd2(dn1, xh1, inv1, vec, hidden_in, q, k, v, p, o, wqkv, wo, gi, grw, s2, si, 4)
    vecs = [gsm[24 + i, :24] for i in range(8)]
    return (out_seq, pair[0, :2], dx, gq, gk, gv, go, gi, gu, gsm[:24],
            vecs[0], vecs[1], vecs[2], vecs[3], vecs[4], gsm[24, 32:], vecs[5], vecs[6], vecs[7], ge, gvb[:, 0])


def solution(mesh):
    placed = (
        P(("dp", "fsdp"), None, None),
        P(("dp", "fsdp"), None),
        P(("dp", "fsdp"), None, None),
        P(),
        P(),
        P(),
        P(),
        P(("dp", "fsdp"), None),
        P(("dp", "fsdp"), None),
        P(("dp", "fsdp"), None),
        P(("dp", "fsdp"), None),
        P(("dp", "fsdp"), None),
        P(("dp", "fsdp"), None),
        P(("dp", "fsdp"), None),
        P(("dp", "fsdp")),
        P(("dp", "fsdp")),
        P(("dp", "fsdp")),
        P(("dp", "fsdp")),
        P(("dp", "fsdp")),
        P(("dp", "fsdp")),
        P(("dp", "fsdp")),
        P(("dp", "fsdp")),
        P(("dp", "fsdp")),
        P(("dp", "fsdp"), None),
        P(("dp", "fsdp")),
    )
    own = mesh.shape["dp"] == 8 and mesh.shape["fsdp"] == 4
    return jax.shard_map(
        linked_body if own else plain_body,
        mesh=mesh,
        in_specs=placed,
        out_specs=(
            P(("dp", "fsdp"), None, None),
            P(("dp", "fsdp")),
            P(("dp", "fsdp"), None, None),
            P(("dp", "fsdp"), None),
            P(("dp", "fsdp"), None),
            P(("dp", "fsdp"), None),
            P(("dp", "fsdp"), None),
            P(("dp", "fsdp"), None),
            P(("dp", "fsdp"), None),
            P(("dp", "fsdp"), None),
            P(("dp", "fsdp")),
            P(("dp", "fsdp")),
            P(("dp", "fsdp")),
            P(("dp", "fsdp")),
            P(("dp", "fsdp")),
            P(("dp", "fsdp")),
            P(("dp", "fsdp")),
            P(("dp", "fsdp")),
            P(("dp", "fsdp")),
            P(("dp", "fsdp"), None),
            P(("dp", "fsdp")),
        ),
        check_vma=False,
    )
```

```python
import functools

import jax
import jax.numpy as jnp
from jax import lax
from jax.experimental import pallas as pl
from jax.experimental.pallas import tpu as pltpu
from jax.sharding import PartitionSpec as P


D = 768
H = 12
HD = 64
LEN = 288
MASKS = 4
SLOT_DEV = 2
GROUP = 4


EPS = 1e-12
NEG = -1000000000.0
HIGH = lax.Precision.HIGHEST
LOSS_WEIGHT = 32.0


def combined_all(value, axis, join):
    pieces = jax.tree.map(lambda part: lax.all_gather(part, axis), value)
    head = jax.tree.map(lambda part: part[0], pieces)
    tail = jax.tree.map(lambda part: part[1:], pieces)
    subtotal, _ = lax.scan(lambda subtotal, share: (join(subtotal, share), None), head, tail)
    return subtotal


def partner(value, axis, stride):
    mask = 2**stride
    pairs = [(source, source ^ mask) for source in range(lax.axis_size(axis))]
    return lax.ppermute(value, axis, pairs)


def layer_norm(residual, gain_vec, shift_vec):
    row_mean = jnp.mean(residual, -1, keepdims=True)
    centred = residual - row_mean
    row_var = jnp.mean(centred * centred, -1, keepdims=True)
    return centred * lax.rsqrt(row_var + EPS) * gain_vec + shift_vec


def exact_gelu(pre_act):
    return jax.nn.gelu(pre_act, approximate=False)


def collect(params):
    (
        query_weight,
        key_weight,
        value_weight,
        out_weight,
        inner_weight,
        outer_weight,
        retrieve_weight,
        query_bias,
        value_bias,
        out_bias,
        norm1_gain,
        norm1_bias,
        inner_bias,
        outer_bias,
        norm2_gain,
        norm2_bias,
    ) = params
    return (
        lax.all_gather(query_weight, ("dp", "fsdp"), axis=0, tiled=True),
        lax.all_gather(key_weight, ("dp", "fsdp"), axis=0, tiled=True),
        lax.all_gather(value_weight, ("dp", "fsdp"), axis=0, tiled=True),
        lax.all_gather(out_weight, ("dp", "fsdp"), axis=0, tiled=True),
        lax.all_gather(inner_weight, ("dp", "fsdp"), axis=0, tiled=True),
        lax.all_gather(outer_weight, ("dp", "fsdp"), axis=0, tiled=True),
        lax.all_gather(retrieve_weight, ("dp", "fsdp"), axis=0, tiled=True),
        lax.all_gather(query_bias, ("dp", "fsdp"), axis=0, tiled=True),
        lax.all_gather(value_bias, ("dp", "fsdp"), axis=0, tiled=True),
        lax.all_gather(out_bias, ("dp", "fsdp"), axis=0, tiled=True),
        lax.all_gather(norm1_gain, ("dp", "fsdp"), axis=0, tiled=True),
        lax.all_gather(norm1_bias, ("dp", "fsdp"), axis=0, tiled=True),
        lax.all_gather(inner_bias, ("dp", "fsdp"), axis=0, tiled=True),
        lax.all_gather(outer_bias, ("dp", "fsdp"), axis=0, tiled=True),
        lax.all_gather(norm2_gain, ("dp", "fsdp"), axis=0, tiled=True),
        lax.all_gather(norm2_bias, ("dp", "fsdp"), axis=0, tiled=True),
    )


def spread(grads):
    (
        grad_qw,
        grad_kw,
        grad_vw,
        grad_ow,
        grad_iw,
        grad_uw,
        grad_rw,
        grad_qb,
        grad_vb,
        grad_ob,
        grad_ga,
        grad_sa,
        grad_ib,
        grad_ub,
        grad_gb,
        grad_sb,
    ) = grads
    return (
        lax.psum_scatter(grad_qw, ("dp", "fsdp"), scatter_dimension=0, tiled=True),
        lax.psum_scatter(grad_kw, ("dp", "fsdp"), scatter_dimension=0, tiled=True),
        lax.psum_scatter(grad_vw, ("dp", "fsdp"), scatter_dimension=0, tiled=True),
        lax.psum_scatter(grad_ow, ("dp", "fsdp"), scatter_dimension=0, tiled=True),
        lax.psum_scatter(grad_iw, ("dp", "fsdp"), scatter_dimension=0, tiled=True),
        lax.psum_scatter(grad_uw, ("dp", "fsdp"), scatter_dimension=0, tiled=True),
        lax.psum_scatter(grad_rw, ("dp", "fsdp"), scatter_dimension=0, tiled=True),
        lax.psum_scatter(grad_qb, ("dp", "fsdp"), scatter_dimension=0, tiled=True),
        lax.psum_scatter(grad_vb, ("dp", "fsdp"), scatter_dimension=0, tiled=True),
        lax.psum_scatter(grad_ob, ("dp", "fsdp"), scatter_dimension=0, tiled=True),
        lax.psum_scatter(grad_ga, ("dp", "fsdp"), scatter_dimension=0, tiled=True),
        lax.psum_scatter(grad_sa, ("dp", "fsdp"), scatter_dimension=0, tiled=True),
        lax.psum_scatter(grad_ib, ("dp", "fsdp"), scatter_dimension=0, tiled=True),
        lax.psum_scatter(grad_ub, ("dp", "fsdp"), scatter_dimension=0, tiled=True),
        lax.psum_scatter(grad_gb, ("dp", "fsdp"), scatter_dimension=0, tiled=True),
        lax.psum_scatter(grad_sb, ("dp", "fsdp"), scatter_dimension=0, tiled=True),
    )


def attention(query_heads, key_heads, value_heads, keys_ok):
    head_scale = HD ** (-0.5)
    scores = (
        jnp.einsum("sqhe,skhe->shqk", query_heads, key_heads, preferred_element_type=jnp.float32)
        * head_scale
    )
    scores = jnp.where(keys_ok[:, None, None, :] > 0, scores, NEG)
    row_peak = jnp.max(scores, -1, keepdims=True)
    exp_scores = jnp.exp(scores - row_peak)
    totals = jnp.sum(exp_scores, -1, keepdims=True)
    attn_probs = (exp_scores / totals).astype(jnp.bfloat16)
    attended = jnp.einsum(
        "shqk,skhe->sqhe", attn_probs, value_heads, preferred_element_type=jnp.float32
    )
    return (attended, row_peak + jnp.log(totals))


def forward_layer(hidden, keys_ok, gathered):
    (
        query_weight,
        key_weight,
        value_weight,
        out_weight,
        inner_weight,
        outer_weight,
        retrieve_weight,
        query_bias,
        value_bias,
        out_bias,
        norm1_gain,
        norm1_bias,
        inner_bias,
        outer_bias,
        norm2_gain,
        norm2_bias,
    ) = gathered
    seq_count = hidden.shape[0]
    head_shape = (seq_count, LEN, H, HD)
    flat_rows = hidden.reshape(seq_count * LEN, D)
    queries = (
        jnp.dot(flat_rows, query_weight, preferred_element_type=jnp.float32)
        + query_bias.astype(jnp.float32)
    ).astype(jnp.bfloat16)
    key_rows = jnp.dot(flat_rows, key_weight, preferred_element_type=jnp.float32).astype(
        jnp.bfloat16
    )
    values = (
        jnp.dot(flat_rows, value_weight, preferred_element_type=jnp.float32)
        + value_bias.astype(jnp.float32)
    ).astype(jnp.bfloat16)
    attended, log_totals = attention(
        queries.reshape(head_shape),
        key_rows.reshape(head_shape),
        values.reshape(head_shape),
        keys_ok,
    )
    attended = attended.reshape(seq_count * LEN, D).astype(jnp.bfloat16)
    first_in = (
        flat_rows.astype(jnp.float32)
        + jnp.dot(attended, out_weight, preferred_element_type=jnp.float32)
        + out_bias.astype(jnp.float32)
    )
    normed_one = layer_norm(
        first_in, norm1_gain.astype(jnp.float32), norm1_bias.astype(jnp.float32)
    ).astype(jnp.bfloat16)
    pre_act = jnp.dot(
        normed_one, inner_weight, preferred_element_type=jnp.float32
    ) + inner_bias.astype(jnp.float32)
    active = exact_gelu(pre_act).astype(jnp.bfloat16)
    second_in = (
        normed_one.astype(jnp.float32)
        + jnp.dot(active, outer_weight, preferred_element_type=jnp.float32)
        + outer_bias.astype(jnp.float32)
    )
    layer_out = layer_norm(
        second_in, norm2_gain.astype(jnp.float32), norm2_bias.astype(jnp.float32)
    ).astype(jnp.bfloat16)
    return (
        queries,
        key_rows,
        values,
        log_totals,
        attended,
        first_in,
        normed_one,
        pre_act,
        active,
        second_in,
        layer_out,
    )


def backward_layer(hidden, keys_ok, gathered, kept_acts, grad_out):
    (
        query_weight,
        key_weight,
        value_weight,
        out_weight,
        inner_weight,
        outer_weight,
        retrieve_weight,
        query_bias,
        value_bias,
        out_bias,
        norm1_gain,
        norm1_bias,
        inner_bias,
        outer_bias,
        norm2_gain,
        norm2_bias,
    ) = gathered
    (
        queries,
        key_rows,
        values,
        log_totals,
        attended,
        first_in,
        normed_one,
        pre_act,
        active,
        second_in,
        layer_out,
    ) = kept_acts
    seq_count = hidden.shape[0]
    head_shape = (seq_count, LEN, H, HD)
    flat_rows = hidden.reshape(seq_count * LEN, D)
    unused_two, norm_two_back = jax.vjp(
        layer_norm, second_in, norm2_gain.astype(jnp.float32), norm2_bias.astype(jnp.float32)
    )
    grad_second, grad_norm2_gain, grad_norm2_bias = norm_two_back(grad_out)
    second_low = grad_second.astype(jnp.bfloat16)
    grad_outer_weight = jnp.dot(active.T, second_low, preferred_element_type=jnp.float32)
    grad_outer_bias = jnp.sum(grad_second, 0)
    grad_active = jnp.dot(second_low, outer_weight.T, preferred_element_type=jnp.float32)
    unused_act, gelu_back = jax.vjp(exact_gelu, pre_act)
    grad_pre = gelu_back(grad_active)[0].astype(jnp.bfloat16)
    grad_inner_weight = jnp.dot(normed_one.T, grad_pre, preferred_element_type=jnp.float32)
    grad_inner_bias = jnp.sum(grad_pre.astype(jnp.float32), 0)
    grad_normed = grad_second + jnp.dot(
        grad_pre, inner_weight.T, preferred_element_type=jnp.float32
    )
    unused_one, norm_one_back = jax.vjp(
        layer_norm, first_in, norm1_gain.astype(jnp.float32), norm1_bias.astype(jnp.float32)
    )
    grad_first, grad_norm1_gain, grad_norm1_bias = norm_one_back(grad_normed)
    first_low = grad_first.astype(jnp.bfloat16)
    grad_out_weight = jnp.dot(attended.T, first_low, preferred_element_type=jnp.float32)
    grad_out_bias = jnp.sum(grad_first, 0)
    grad_attended = (
        jnp.dot(first_low, out_weight.T, preferred_element_type=jnp.float32)
        .astype(jnp.bfloat16)
        .reshape(head_shape)
    )
    query_heads = queries.reshape(head_shape)
    key_heads = key_rows.reshape(head_shape)
    value_heads = values.reshape(head_shape)
    head_scale = HD ** (-0.5)
    scores = (
        jnp.einsum("sqhe,skhe->shqk", query_heads, key_heads, preferred_element_type=jnp.float32)
        * head_scale
    )
    scores = jnp.where(keys_ok[:, None, None, :] > 0, scores, NEG)
    attn_probs = jnp.exp(scores - log_totals)
    grad_probs = jnp.einsum(
        "sqhe,skhe->shqk", grad_attended, value_heads, preferred_element_type=jnp.float32
    )
    grad_value_heads = jnp.einsum(
        "shqk,sqhe->skhe",
        attn_probs.astype(jnp.bfloat16),
        grad_attended,
        preferred_element_type=jnp.float32,
    )
    grad_scores = (
        attn_probs * (grad_probs - jnp.sum(attn_probs * grad_probs, -1, keepdims=True))
    ).astype(jnp.bfloat16)
    grad_query_heads = (
        jnp.einsum("shqk,skhe->sqhe", grad_scores, key_heads, preferred_element_type=jnp.float32)
        * head_scale
    )
    grad_key_heads = (
        jnp.einsum("shqk,sqhe->skhe", grad_scores, query_heads, preferred_element_type=jnp.float32)
        * head_scale
    )
    grad_queries = grad_query_heads.reshape(seq_count * LEN, D).astype(jnp.bfloat16)
    grad_keys = grad_key_heads.reshape(seq_count * LEN, D).astype(jnp.bfloat16)
    grad_values = grad_value_heads.reshape(seq_count * LEN, D).astype(jnp.bfloat16)
    grad_query_weight = jnp.dot(flat_rows.T, grad_queries, preferred_element_type=jnp.float32)
    grad_key_weight = jnp.dot(flat_rows.T, grad_keys, preferred_element_type=jnp.float32)
    grad_value_weight = jnp.dot(flat_rows.T, grad_values, preferred_element_type=jnp.float32)
    grad_query_bias = jnp.sum(grad_queries.astype(jnp.float32), 0)
    grad_value_bias = jnp.sum(grad_values.astype(jnp.float32), 0)
    grad_hidden = (
        grad_first
        + jnp.dot(grad_queries, query_weight.T, preferred_element_type=jnp.float32)
        + jnp.dot(grad_keys, key_weight.T, preferred_element_type=jnp.float32)
        + jnp.dot(grad_values, value_weight.T, preferred_element_type=jnp.float32)
    )
    return (
        grad_hidden,
        (
            grad_query_weight,
            grad_key_weight,
            grad_value_weight,
            grad_out_weight,
            grad_inner_weight,
            grad_outer_weight,
            grad_query_bias,
            grad_value_bias,
            grad_out_bias,
            grad_norm1_gain,
            grad_norm1_bias,
            grad_inner_bias,
            grad_outer_bias,
            grad_norm2_gain,
            grad_norm2_bias,
        ),
    )


def merge_pair(peak_one, total_one, peak_two, total_two):
    peak_new = jnp.maximum(peak_one, peak_two)
    return (
        peak_new,
        total_one * jnp.exp(peak_one - peak_new) + total_two * jnp.exp(peak_two - peak_new),
    )


def merge_rows(one_side, other_side):
    peak_new, total_new = merge_pair(one_side[0], one_side[1], other_side[0], other_side[1])
    return (peak_new, total_new, one_side[2] + other_side[2])


def slot_partial(score_vec, slot_ok):
    grouped = jnp.where(slot_ok, score_vec, NEG).reshape(-1, SLOT_DEV)
    ok_grouped = slot_ok.reshape(-1, SLOT_DEV)
    group_peak = jnp.max(grouped, -1)
    group_total = jnp.sum(jnp.where(ok_grouped, jnp.exp(grouped - group_peak[:, None]), 0.0), -1)
    return (group_peak, group_total)


def plain_body(
    hidden_in,
    token_mask,
    out_grad,
    query_embed,
    slot_valid,
    target_ids,
    target_pos,
    query_weight,
    key_weight,
    value_weight,
    out_weight,
    inner_weight,
    outer_weight,
    retrieve_weight,
    query_bias,
    value_bias,
    out_bias,
    norm1_gain,
    norm1_bias,
    inner_bias,
    outer_bias,
    norm2_gain,
    norm2_bias,
    embedding,
    vocab_bias,
):
    params = (
        query_weight,
        key_weight,
        value_weight,
        out_weight,
        inner_weight,
        outer_weight,
        retrieve_weight,
        query_bias,
        value_bias,
        out_bias,
        norm1_gain,
        norm1_bias,
        inner_bias,
        outer_bias,
        norm2_gain,
        norm2_bias,
    )
    gathered = collect(params)
    kept_acts = forward_layer(hidden_in, token_mask, gathered)
    seq_count = hidden_in.shape[0]
    query_count = seq_count // SLOT_DEV
    out_seq = kept_acts[10].reshape(seq_count, LEN, D)
    devices = lax.axis_size("dp") * lax.axis_size("fsdp")
    device = lax.axis_index("dp") * lax.axis_size("fsdp") + lax.axis_index("fsdp")
    member = lax.axis_index("fsdp") % GROUP
    local_seq = jnp.arange(seq_count, dtype=jnp.int32)
    local_query = device // GROUP * query_count + local_seq // SLOT_DEV
    local_slot = member * SLOT_DEV + local_seq % SLOT_DEV
    slot_ok = slot_valid[local_query, local_slot] > 0
    embeds = query_embed[local_query]
    positions = target_pos[local_query]
    cls_rows = out_seq[:, 0, :].astype(jnp.float32)
    retrieve_full = gathered[6].astype(jnp.float32)
    projected = jnp.dot(cls_rows, retrieve_full, precision=HIGH)
    retrieval = jnp.sum(projected * embeds, -1)
    own_rows = seq_count * MASKS
    sent_rows = out_seq[local_seq[:, None], positions].reshape(own_rows, D)
    all_rows = lax.all_gather(sent_rows, ("dp", "fsdp"), axis=0, tiled=True)
    group_count = devices // GROUP
    all_targets = jnp.broadcast_to(
        target_ids.reshape(group_count, 1, query_count, 1, MASKS),
        (group_count, GROUP, query_count, SLOT_DEV, MASKS),
    ).reshape(-1)
    vocab_rows = embedding.shape[0]
    local_ids = all_targets - device * vocab_rows
    target_hit = jnp.arange(vocab_rows, dtype=jnp.int32)[None, :] == local_ids[:, None]
    logits = jnp.einsum(
        "rd,vd->rv", all_rows, embedding, preferred_element_type=jnp.float32
    ) + vocab_bias.astype(jnp.float32)
    row_peak = jnp.max(logits, -1)
    sum_exp = jnp.sum(jnp.exp(logits - row_peak[:, None]), -1)
    target_logit = jnp.sum(jnp.where(target_hit, logits, 0.0), -1)
    peak_all, total_all, target_all = combined_all(
        (row_peak, sum_exp, target_logit), ("dp", "fsdp"), merge_rows
    )
    lse_rows = peak_all + jnp.log(total_all)
    log_prob = lax.dynamic_slice_in_dim(target_all - lse_rows, device * own_rows, own_rows)
    seq_ll = jnp.mean(log_prob.reshape(seq_count, MASKS), -1)
    joint_score = retrieval + seq_ll
    joint_peak, joint_total = slot_partial(joint_score, slot_ok)
    prior_peak, prior_total = slot_partial(retrieval, slot_ok)
    for bit_number in range(GROUP.bit_length() - 1):
        far_joint_peak, far_joint_total, far_prior_peak, far_prior_total = partner(
            (joint_peak, joint_total, prior_peak, prior_total), "fsdp", bit_number
        )
        joint_peak, joint_total = merge_pair(
            joint_peak, joint_total, far_joint_peak, far_joint_total
        )
        prior_peak, prior_total = merge_pair(
            prior_peak, prior_total, far_prior_peak, far_prior_total
        )
    joint_lse = joint_peak + jnp.log(joint_total)
    prior_lse = prior_peak + jnp.log(prior_total)
    pair_loglik = joint_lse - prior_lse
    post_weight = jnp.where(slot_ok, jnp.exp(joint_score - jnp.repeat(joint_lse, SLOT_DEV)), 0.0)
    prior_weight = jnp.where(slot_ok, jnp.exp(retrieval - jnp.repeat(prior_lse, SLOT_DEV)), 0.0)
    grad_retrieval = LOSS_WEIGHT * (prior_weight - post_weight)
    row_scale = jnp.repeat(-LOSS_WEIGHT * post_weight / MASKS, MASKS)
    all_scales = lax.all_gather(row_scale, ("dp", "fsdp"), axis=0, tiled=True)
    vocab_probs = jnp.exp(logits - lse_rows[:, None])
    grad_logits = all_scales[:, None] * (target_hit.astype(jnp.float32) - vocab_probs)
    grad_vocab_bias = jnp.sum(grad_logits, 0)
    logits_low = grad_logits.astype(jnp.bfloat16)
    grad_embedding = jnp.einsum(
        "rv,rd->vd", logits_low, all_rows, preferred_element_type=jnp.float32
    )
    grad_picked = lax.psum_scatter(
        jnp.dot(logits_low, embedding, preferred_element_type=jnp.float32),
        ("dp", "fsdp"),
        scatter_dimension=0,
        tiled=True,
    )
    grad_project = grad_retrieval[:, None] * embeds
    grad_retrieve_weight = jnp.dot(cls_rows.T, grad_project, precision=HIGH)
    grad_cls = jnp.dot(grad_project, retrieve_full.T, precision=HIGH)
    grad_total = out_grad.astype(jnp.float32)
    grad_total = grad_total.at[local_seq[:, None], positions].add(
        grad_picked.reshape(seq_count, MASKS, D)
    )
    grad_total = grad_total.at[:, 0, :].add(grad_cls)
    grad_total = grad_total.reshape(seq_count * LEN, D)
    grad_hidden, layer_grads = backward_layer(
        hidden_in, token_mask, gathered, kept_acts, grad_total
    )
    (
        grad_query_weight,
        grad_key_weight,
        grad_value_weight,
        grad_out_weight,
        grad_inner_weight,
        grad_outer_weight,
        grad_query_bias,
        grad_value_bias,
        grad_out_bias,
        grad_norm1_gain,
        grad_norm1_bias,
        grad_inner_bias,
        grad_outer_bias,
        grad_norm2_gain,
        grad_norm2_bias,
    ) = layer_grads
    (
        shard_query_weight,
        shard_key_weight,
        shard_value_weight,
        shard_out_weight,
        shard_inner_weight,
        shard_outer_weight,
        shard_retrieve_weight,
        shard_query_bias,
        shard_value_bias,
        shard_out_bias,
        shard_norm1_gain,
        shard_norm1_bias,
        shard_inner_bias,
        shard_outer_bias,
        shard_norm2_gain,
        shard_norm2_bias,
    ) = spread(
        (
            grad_query_weight,
            grad_key_weight,
            grad_value_weight,
            grad_out_weight,
            grad_inner_weight,
            grad_outer_weight,
            grad_retrieve_weight,
            grad_query_bias,
            grad_value_bias,
            grad_out_bias,
            grad_norm1_gain,
            grad_norm1_bias,
            grad_inner_bias,
            grad_outer_bias,
            grad_norm2_gain,
            grad_norm2_bias,
        )
    )
    return (
        out_seq,
        pair_loglik,
        grad_hidden.reshape(seq_count, LEN, D),
        shard_query_weight,
        shard_key_weight,
        shard_value_weight,
        shard_out_weight,
        shard_inner_weight,
        shard_outer_weight,
        shard_retrieve_weight,
        shard_query_bias,
        shard_value_bias,
        shard_out_bias,
        shard_norm1_gain,
        shard_norm1_bias,
        shard_inner_bias,
        shard_outer_bias,
        shard_norm2_gain,
        shard_norm2_bias,
        grad_embedding,
        grad_vocab_bias,
    )

MESH = pl.DeviceIdType.MESH
F32 = jnp.float32
BF = jnp.bfloat16
DMA = pltpu.SemaphoreType.DMA


def coords():
    d = lax.axis_index("dp")
    return d // 4, (d // 2) % 2, d % 2, lax.axis_index("fsdp")


def dev(y, x, c, z):
    return ((y * 2 + x) * 2 + c, z)


def rdma(src, dst, ss, rs, to):
    return pltpu.make_async_remote_copy(src, dst, ss, rs, device_id=to, device_id_type=MESH)


def greet():
    y, x, c, z = coords()
    bar = pltpu.get_barrier_semaphore()
    tos = [dev(y, x, c, lax.rem(z + k, 4)) for k in (1, 2, 3)]
    tos += [dev(y, 1 - x, c, z), dev(1 - y, x, c, z), dev(y, x, 1 - c, z)]
    for t in tos:
        pl.semaphore_signal(bar, inc=1, device_id=t, device_id_type=MESH)
    pl.semaphore_wait(bar, len(tos))


def rows_at(start, size):
    return pl.ds(pl.multiple_of(start, 8), size)


class Gather:
    def __init__(self, src, dst, sems, a):
        self.src, self.dst, self.a = src, dst, a
        self.ss, self.rs, self.ls = sems
        self.r, n = src.shape
        self.split = (n // 2) % 128 == 0
        self.h = n // 2

    def chips(self):
        y, x, c, z = coords()
        return y * 2 + x, y * 2 + 1 - x, (1 - y) * 2 + x, (1 - y) * 2 + 1 - x

    def block(self, chip, k):
        y, x, c, z = coords()
        zz = lax.rem(z + 4 - k, 4)
        return self.dst.at[rows_at(((chip * 2 + c) * 4 + zz) * self.r, self.r)]

    def column(self, chip, c):
        return self.dst.at[rows_at((chip * 2 + c) * 4 * self.r, 4 * self.r)]

    def half(self, ref, right):
        if not self.split:
            return ref
        return ref.at[:, pl.ds(self.h if right else 0, self.h)]

    def copy(self, src, dst, slot, to):
        return rdma(src, dst, self.ss.at[self.a, slot], self.rs.at[self.a, slot], to)

    def send(self, ref, slot, to, src=None):
        self.copy(ref if src is None else src, ref, slot, to).start()

    def wait(self, ref, slot):
        y, x, c, z = coords()
        self.copy(ref, ref, slot, dev(y, 1 - x, c, z)).wait_recv()

    def kept(self):
        return pltpu.make_async_copy(self.src, self.block(self.chips()[0], 0), self.ls.at[self.a])

    def own(self):
        y, x, c, z = coords()
        d = self.block(self.chips()[0], 0)
        self.kept().start()
        self.send(d, 4, dev(y, 1 - x, c, z), self.src)
        self.send(d, 8, dev(1 - y, x, c, z), self.src)
        for k in (1, 3, 2):
            self.send(d, k, dev(y, x, c, lax.rem(z + k, 4)), self.src)

    def z(self, k):
        y, x, c, z = coords()
        d = self.block(self.chips()[0], k)
        self.wait(d, k)
        self.send(d, 4 + k, dev(y, 1 - x, c, z))
        self.send(d, 8 + k, dev(1 - y, x, c, z))

    def core(self, i):
        y, x, c, z = coords()
        if i == 0:
            self.kept().wait()
        self.send(self.column(self.chips()[i], c), 20 + i, dev(y, x, 1 - c, z))

    def xy(self, k):
        y, x, c, z = coords()
        dx = self.block(self.chips()[1], k)
        self.wait(dx, 4 + k)
        self.send(self.half(dx, False), 12 + k, dev(1 - y, x, c, z))
        dy = self.block(self.chips()[2], k)
        self.wait(dy, 8 + k)
        if self.split:
            self.send(self.half(dy, True), 16 + k, dev(y, 1 - x, c, z))

    def dg(self, k):
        d = self.block(self.chips()[3], k)
        self.wait(self.half(d, False), 12 + k)
        if self.split:
            self.wait(self.half(d, True), 16 + k)

    def arrived(self):
        y, x, c, z = coords()
        for i, chip in enumerate(self.chips()):
            self.wait(self.column(chip, 1 - c), 20 + i)

    def sent(self):
        y, x, c, z = coords()
        to = dev(y, 1 - x, c, z)
        d = self.block(self.chips()[0], 0)
        for k in range(4):
            if k:
                self.copy(d, d, k, to).wait_send()
            self.copy(d, d, 4 + k, to).wait_send()
            self.copy(d, d, 8 + k, to).wait_send()
            half = self.half(d, False)
            self.copy(half, half, 12 + k, to).wait_send()
            if self.split:
                self.copy(half, half, 16 + k, to).wait_send()
            col = self.column(self.chips()[0], 0)
            self.copy(col, col, 20 + k, to).wait_send()

    def steps(self):
        out = [functools.partial(self.z, k) for k in (1, 3, 2)]
        out[2] = lambda: (self.z(2), self.core(0))
        out += [functools.partial(self.xy, k) for k in (0, 1, 3)]
        out += [lambda: (self.xy(2), self.core(1), self.core(2))]
        out += [lambda: (self.dg(0), self.dg(1)), lambda: (self.dg(3), self.dg(2), self.core(3))]
        return out


def gather_sems(n):
    return [DMA((n, 24)), DMA((n, 24)), DMA((n,))]


class Scatter:
    def __init__(self, source, bufs, sems, a, done, in_hbm=False):
        self.source, self.a, self.done, self.in_hbm = source, a, done, in_hbm
        self.ss, self.rs, self.ls = sems
        self.held, self.rc, self.ray, self.rax, self.rbx, self.rby, self.rz = bufs
        self.split = self.rbx is not None
        self.h = self.rax.shape[-1]

    def copy(self, src, dst, slot, to):
        return rdma(src, dst, self.ss.at[self.a, slot], self.rs.at[self.a, slot], to)

    def wait(self, ref, slot):
        y, x, c, z = coords()
        self.copy(ref, ref, slot, dev(y, 1 - x, c, z)).wait_recv()

    def local(self, j):
        y, x, c, z = coords()
        return pltpu.make_async_copy(self.source(j, c), self.held.at[j], self.ls.at[self.a, j])

    def core(self, j):
        y, x, c, z = coords()
        if self.in_hbm:
            self.local(j).start()
        self.copy(self.source(j, 1 - c), self.rc.at[j], j, dev(y, x, 1 - c, z)).start()

    def cores(self):
        for j in range(4):
            self.core(j)

    def add(self, dst, one, two):
        for i in range(4):
            dst[i] = (one[i].astype(F32) + two[i].astype(F32)).astype(BF)

    def left(self, chip):
        return self.held.at[chip, :, :, pl.ds(0, self.h)]

    def right(self, chip):
        return self.held.at[chip, :, :, pl.ds(self.h, self.h)]

    def first(self):
        y, x, c, z = coords()
        @pl.loop(0, 4)
        def _(j):
            if self.in_hbm:
                self.local(j).wait()
            self.wait(self.rc.at[j], j)
            self.add(self.held.at[j], self.held.at[j] if self.in_hbm else self.source(j, c), self.rc.at[j])
        for xi in range(2):
            self.copy(self.left((1 - y) * 2 + xi), self.ray.at[xi], 4 + xi, dev(1 - y, x, c, z)).start()
        if self.split:
            for yi in range(2):
                self.copy(self.right(yi * 2 + 1 - x), self.rbx.at[yi], 6 + yi, dev(y, 1 - x, c, z)).start()

    def second(self):
        y, x, c, z = coords()
        for xi in range(2):
            self.wait(self.ray.at[xi], 4 + xi)
            d = self.left(y * 2 + xi)
            self.add(d, d, self.ray.at[xi])
        self.copy(self.left(y * 2 + 1 - x), self.rax, 8, dev(y, 1 - x, c, z)).start()
        if self.split:
            for yi in range(2):
                self.wait(self.rbx.at[yi], 6 + yi)
                d = self.right(yi * 2 + x)
                self.add(d, d, self.rbx.at[yi])
            self.copy(self.right((1 - y) * 2 + x), self.rby, 9, dev(1 - y, x, c, z)).start()

    def third(self):
        y, x, c, z = coords()
        me = y * 2 + x
        self.wait(self.rax, 8)
        self.add(self.left(me), self.left(me), self.rax)
        if self.split:
            self.wait(self.rby, 9)
            self.add(self.right(me), self.right(me), self.rby)
        for k in (2, 1, 3):
            zz = lax.rem(z + k, 4)
            self.copy(self.held.at[me, zz], self.rz.at[k - 1], 9 + k, dev(y, x, c, zz)).start()

    def last(self):
        y, x, c, z = coords()
        total = self.held[y * 2 + x, z].astype(F32)
        for k in (1, 2, 3):
            self.wait(self.rz.at[k - 1], 9 + k)
            total = total + self.rz[k - 1].astype(F32)
        self.done(total)

    def sent(self):
        y, x, c, z = coords()
        to = dev(y, 1 - x, c, z)
        refs = [self.rc.at[j] for j in range(4)] + [self.ray.at[0], self.ray.at[1]]
        refs += [self.rbx.at[0], self.rbx.at[1]] if self.split else [None, None]
        refs += [self.rax, self.rby] + [self.rz.at[k] for k in range(3)]
        for slot, ref in enumerate(refs):
            if ref is not None:
                self.copy(ref, ref, slot, to).wait_send()


def scatter_sems(n):
    return [DMA((n, 13)), DMA((n, 13)), DMA((n, 4))]


def scatter_bufs(r, n):
    split = (n // 2) % 128 == 0
    h = n // 2 if split else n
    full, pair, one = pltpu.VMEM((4, 4, r, n), BF), pltpu.VMEM((2, 4, r, h), BF), pltpu.VMEM((4, r, h), BF)
    return [full, full, pair, one] + ([pair, one] if split else []) + [pltpu.VMEM((3, r, n), BF)]


def scatter_refs(refs):
    if len(refs) >= 7 and refs[4].shape == refs[2].shape:
        return refs[:7], refs[7:]
    return (*refs[:4], None, None, refs[4]), refs[5:]


def pipelined(jobs):
    out = []
    for t in range(len(jobs) + 3):
        for lag, name in enumerate(("first", "second", "third", "last")):
            if 0 <= t - lag < len(jobs):
                out.append(getattr(jobs[t - lag], name))
    return out


def staged(jobs):
    out = []
    for t in range(len(jobs) + 4):
        steps = []
        for lag, name in enumerate(("cores", "first", "second", "third", "last")):
            if 0 <= t - lag < len(jobs):
                steps.append(getattr(jobs[t - lag], name))
        out.append(steps)
    return out


def at_step(t, steps, start=0, every=1):
    for i, step in enumerate(steps):
        if step is None:
            continue

        @pl.when(t == start + i * every)
        def _(step=step):
            step()


FF = 4 * D
HI = lax.Precision.HIGHEST

def dot(a, b):
    return lax.dot_general(a, b, (((1,), (0,)), ((), ())), preferred_element_type=F32)

def dot_nt(a, b):
    return lax.dot_general(a, b, (((1,), (1,)), ((), ())), preferred_element_type=F32)

def dot_tn(a, b):
    return lax.dot_general(a, b, (((0,), (0,)), ((), ())), preferred_element_type=F32)

def iota(shape, dim):
    return lax.broadcasted_iota(jnp.int32, shape, dim)

def over(index, n):
    return jnp.floor((index.astype(F32) + 0.5) * (1.0 / n)).astype(jnp.int32)

def expand_vectors(blocks):
    lane, col = iota((128, D), 0), iota((128, D), 1)
    pick = (lane == col - over(col, 24) * 24).astype(F32).astype(BF)
    spread = dot(blocks.reshape(256, 128), pick)
    row, col = iota((256, D), 0), iota((256, D), 1)
    spread = jnp.where(over(row, 8) == over(col, 24), spread, 0.0)
    vec = jnp.sum(spread.reshape(32, 8, D), 0)
    lane, col = iota((128, FF), 0), iota((128, FF), 1)
    pick = (lane - 32 == col - over(col, 96) * 96).astype(F32).astype(BF)
    spread = dot(blocks.reshape(256, 128), pick)
    row, col = iota((256, FF), 0), iota((256, FF), 1)
    inner = jnp.sum(jnp.where(row == over(col, 96) * 8, spread, 0.0), 0, keepdims=True)
    return vec, inner

def norm_stats(r):
    mean = jnp.mean(r, -1, keepdims=True)
    cen = r - mean
    var = jnp.mean(cen * cen, -1, keepdims=True)
    inv = lax.rsqrt(var + EPS)
    return cen * inv, inv


HBM = pl.BlockSpec(memory_space=pltpu.HBM)
VM = pl.BlockSpec(memory_space=pltpu.VMEM)
ACT = ((4, LEN, D), BF)


def sds(shape, dtype):
    return jax.ShapeDtypeStruct(shape, dtype)


def stacked(pair, low):
    zero = jnp.zeros_like(pair)
    return jnp.concatenate([jnp.where(low, pair, zero), jnp.where(low, zero, pair)], 0)


def attn_fwd_pair(s, hp, q_ref, k_ref, v_ref, p_ref, slot, o_ref, keys_ok):
    cols = pl.ds(pl.multiple_of(hp * 128, 128), 128)
    low = iota((LEN, 128), 1) < HD
    st = dot_nt(stacked(k_ref[s, :, cols], low), (q_ref[s, :, cols] * 0.125).astype(BF))
    probs = []
    for h in range(2):
        sh = jnp.where(keys_ok, st[h * LEN : (h + 1) * LEN], NEG)
        e = jnp.exp(sh - jnp.max(sh, 0, keepdims=True))
        p = (e * (1.0 / jnp.sum(e, 0, keepdims=True))).astype(BF)
        p_ref[slot, h] = p
        probs.append(p)
    o_ref[s, :, cols] = dot_tn(jnp.concatenate(probs, 0), stacked(v_ref[s, :, cols], low)).astype(BF)


def gelu_pair(z):
    cdf = 0.5 + 0.5 * lax.erf(z * 0.7071067811865476)
    return z * cdf, cdf + z * (jnp.exp(-0.5 * z * z) * 0.3989422804014327)


def forward_body(x_ref, m_ref, pos_ref, sh_small, sh_q, sh_k, sh_v, sh_wo, sh_wi, sh_wu,
                 small, wqkv, wo, wi, wu, q, k, v, p, o, n1, xh1, inv1, g, dg, lo, xh2, inv2, vec_ref, ib_ref, picked_ref,
                 own_qkv, small_v, wqkv_v, wo_v, wi_v, wu_v, q_v, k_v, v_v, p_v, o_v, n1_v, xh1_v, inv1_v, g_v, dg_v, lo_v, xh2_v, inv2_v,
                 gss, grs, gls, asem, wsem, psem, osem):
    parts = []
    for grp in range(3):
        for i, ref in enumerate((sh_q, sh_k, sh_v)):
            cp = pltpu.make_async_copy(ref.at[:, pl.ds(256 * grp, 256)], own_qkv.at[:, pl.ds(D * grp + 256 * i, 256)], asem.at[3 * grp + i])
            cp.start()
            parts.append(cp)
    sems = (gss, grs, gls)
    pairs = ((sh_small, small), (own_qkv, wqkv), (sh_wo, wo), (sh_wi, wi), (sh_wu, wu))
    gs = [Gather(src, dst, sems, a) for a, (src, dst) in enumerate(pairs)]
    g_small, g_qkv, g_wo, g_wi, g_wu = gs
    greet()
    for cp in parts:
        cp.wait()
    g_qkv.own()
    g_small.own()
    st_small, st_qkv, st_wo, st_wi, st_wu = [x.steps() for x in gs]
    for i in (3, 0, 1, 2):
        st_qkv[i]()
        st_small[i]()
    g_wo.own()
    g_wi.own()
    for i in (4, 5, 6):
        st_qkv[i]()
        st_small[i]()
    for step in (st_wo[3], st_wi[3], st_wo[0], st_wi[0], st_qkv[7], st_small[7], st_wo[1], st_wi[1], st_qkv[8], st_small[8]):
        step()
    def load(i, src, dst):
        return pltpu.make_async_copy(src, dst, wsem.at[i])
    g_qkv.arrived()
    load(1, wqkv, wqkv_v).start()
    g_small.arrived()
    load(0, small, small_v).start()
    load(0, small, small_v).wait()
    vec, inner = expand_vectors(small_v[...].reshape(32, 32, 128)[:, 24:, :])
    vec_ref[...] = vec
    ib_ref[...] = inner
    load(1, wqkv, wqkv_v).wait()
    def wo_in():
        st_wo[8]()
        g_wo.arrived()
        load(2, wo, wo_v).start()
    def wi_in():
        st_wi[8]()
        g_wi.arrived()
        load(3, wi, wi_v).start()
    def wu_in():
        st_wu[8]()
        g_wu.arrived()
        load(4, wu, wu_v).start()
    steps = [st_wo[2], st_wi[2], g_wu.own, None, st_wo[4], st_wi[4], st_wo[5], st_wi[5], st_wu[3], st_wo[6], st_wi[6], st_wu[0],
             None, st_wo[7], st_wi[7], st_wu[1], None, wo_in, None, wi_in, None, st_wu[2], None, st_wu[4]]
    outs = [(q_v, q), (k_v, k), (v_v, v), (o_v, o), (n1_v, n1), (xh1_v, xh1), (inv1_v, inv1), (g_v, g), (dg_v, dg), (lo_v, lo), (xh2_v, xh2), (inv2_v, inv2)]
    def put(a, s):
        return pltpu.make_async_copy(outs[a][0].at[s], outs[a][1].at[s], osem.at[a, s])
    def put_p(t):
        return pltpu.make_async_copy(p_v.at[lax.rem(t, 4)], p.at[t // 6, pl.ds(lax.rem(t, 6) * 2, 2)], psem.at[lax.rem(t, 4)])
    @pl.loop(0, 4)
    def _(s):
        t = dot(x_ref[s], wqkv_v[...])
        for grp in range(3):
            cols = slice(256 * grp, 256 * grp + 256)
            for j, ref in enumerate((q_v, k_v, v_v)):
                part = t[:, D * grp + 256 * j : D * grp + 256 * j + 256]
                if j != 1:
                    part = part + vec_ref[0 if j == 0 else 1][None, cols]
                ref[s, :, cols] = part.astype(BF)
        for j in range(3):
            put(j, s).start()
        count = jnp.sum(m_ref[pl.ds(s, 1), :], -1, keepdims=True)
        keys_ok = iota((LEN, 1), 0) < count
        @pl.loop(0, H // 2)
        def _(hp):
            t = s * 6 + hp
            at_step(t, steps)
            @pl.when(t >= 4)
            def _():
                put_p(t - 4).wait()
            attn_fwd_pair(s, hp, q_v, k_v, v_v, p_v, lax.rem(t, 4), o_v, keys_ok)
            put_p(t).start()
        put(3, s).start()
    load(2, wo, wo_v).wait()
    @pl.loop(0, 4)
    def _(s):
        r1 = x_ref[s].astype(F32) + dot(o_v[s], wo_v[...]) + vec_ref[2][None]
        xh, inv = norm_stats(r1)
        xh1_v[s] = xh.astype(BF)
        inv1_v[s] = jnp.broadcast_to(inv, (LEN, 128))
        n1_v[s] = (xh * vec_ref[3][None] + vec_ref[4][None]).astype(BF)
        at_step(s, [None, st_wu[5], None, st_wu[6]])
        for a in (4, 5, 6):
            put(a, s).start()
    load(3, wi, wi_v).wait()
    @pl.loop(0, 4)
    def _(s):
        @pl.loop(0, 2)
        def _(j):
            at_step(s * 2 + j, [None, None, None, st_wu[7], None, wu_in])
            cols = pl.ds(pl.multiple_of(j * 2 * D, 2 * D), 2 * D)
            act, slope = gelu_pair(dot(n1_v[s], wi_v[:, cols]) + ib_ref[:, cols])
            g_v[s, :, cols] = act.astype(BF)
            dg_v[s, :, cols] = slope.astype(BF)
        put(7, s).start()
        put(8, s).start()
    load(4, wu, wu_v).wait()
    @pl.loop(0, 4)
    def _(s):
        r2 = n1_v[s].astype(F32) + dot(g_v[s], wu_v[...]) + vec_ref[5][None]
        xh, inv = norm_stats(r2)
        xh2_v[s] = xh.astype(BF)
        inv2_v[s] = jnp.broadcast_to(inv, (LEN, 128))
        out = (xh * vec_ref[6][None] + vec_ref[7][None]).astype(BF)
        lo_v[s] = out
        picked_ref[s] = dot((iota((8, LEN), 1) == pos_ref[s]).astype(F32).astype(BF), out).astype(BF)
        for a in (9, 10, 11):
            put(a, s).start()
    for t in range(20, 24):
        put_p(t).wait()
    for s in range(4):
        for a in range(12):
            put(a, s).wait()
    for x in gs:
        x.sent()


def forward(x, mask, pos, shards, cid):
    small, q, k, v, wo, wi, wu = shards
    full = [((32 * s.shape[0], n), BF) for s, n in ((small, 128), (q, 3 * D), (wo, D), (wi, FF), (wu, D))]
    probs, stat, big = ((4, H, LEN, LEN), BF), ((4, LEN, 128), F32), ((4, LEN, FF), BF)
    acts = [ACT, ACT, ACT, probs, ACT, ACT, ACT, stat, big, big, ACT, ACT, stat]
    outs = full + acts + [((8, D), F32), ((1, FF), F32), ((4, 8, D), BF)]
    slots = [((4, 2, LEN, LEN), BF) if a is probs else a for a in acts]
    return pl.pallas_call(
        forward_body, name="layer_forward", out_shape=[sds(*o) for o in outs],
        in_specs=[VM] * 3 + [HBM] * 7, out_specs=[HBM] * 18 + [VM] * 3,
        scratch_shapes=[pltpu.VMEM(*o) for o in [((q.shape[0], 3 * D), BF)] + full + slots]
        + gather_sems(5) + [DMA((9,)), DMA((5,)), DMA((4,)), DMA((12, 4))],
        compiler_params=pltpu.CompilerParams(collective_id=cid, has_side_effects=True, vmem_limit_bytes=61 << 20),
    )(x, mask, pos, *shards)


def norm_back(dy, xh, inv, gain):
    c = dy * gain
    return (c - jnp.mean(c, -1, keepdims=True) - xh * jnp.mean(c * xh, -1, keepdims=True)) * inv


def bwd1_body(og_ref, add_ref, pos_ref, xh2_ref, inv2_ref, vec_ref, g, dg, n1, wi, wu,
              gu_ref, gi, dn1, sums_ref, sumi_ref,
              g_v, dg_v, n1_v, wi_v, wu_v, d2_v, dn1_v, gu_v, gi_v, sss, srs, sls, isem, osem, *bufs):
    ins = [(g, g_v), (wu, wu_v), (dg, dg_v), (wi, wi_v), (n1, n1_v)]
    loads = [pltpu.make_async_copy(a, b, isem.at[i]) for i, (a, b) in enumerate(ins)]
    loads[0].start()
    sems = (sss, srs, sls)
    greet()
    jobs = []
    for t in range(3):
        own, bufs = scatter_refs(bufs)
        def source(j, c, t=t):
            return gu_v.at[j, c, :, :, pl.ds(256 * t, 256)]
        def done(total, t=t):
            gu_ref[:, pl.ds(256 * t, 256)] = total
        jobs.append(Scatter(source, own, sems, t, done))
    sums_ref[...] = jnp.zeros_like(sums_ref)
    sumi_ref[...] = jnp.zeros_like(sumi_ref)
    @pl.loop(0, 4)
    def _(s):
        hit = (iota((LEN, 8), 0) == pos_ref[s]).astype(F32)
        extra = lax.dot_general(hit, add_ref[s], (((1,), (0,)), ((), ())), preferred_element_type=F32, precision=HI)
        dy = og_ref[s].astype(F32) + extra
        xh = xh2_ref[s].astype(F32)
        dr2 = norm_back(dy, xh, inv2_ref[s][:, 0:1], vec_ref[6][None])
        sums_ref[0] += jnp.sum(dy * xh, 0)
        sums_ref[1] += jnp.sum(dy, 0)
        sums_ref[2] += jnp.sum(dr2, 0)
        d2_v[pl.ds(s * LEN, LEN)] = dr2.astype(BF)
        dn1_v[s] = dr2
    loads[0].wait()
    loads[1].start()
    loads[2].start()
    @pl.loop(0, 4)
    def _(j):
        cols = pl.ds(pl.multiple_of(j * D, D), D)
        t = dot_tn(g_v[:, :, cols].reshape(4 * LEN, D), d2_v[...])
        gu_v[j] = t.astype(BF).reshape(2, 4, 96, D)
        for job in jobs:
            job.core(j)
    loads[3].start()
    loads[1].wait()
    loads[2].wait()
    steps = pipelined(jobs)
    def put(s):
        return pltpu.make_async_copy(dn1_v.at[s], dn1.at[s], osem.at[s])
    loads[3].wait()
    loads[4].start()
    @pl.loop(0, 4)
    def _(s):
        for half in range(2):
            at_step(s, steps[half:9:3] if half else steps[0:9:3])
            cols = pl.ds(half * 2 * D, 2 * D)
            dz = dot_nt(d2_v[pl.ds(pl.multiple_of(s * LEN, LEN), LEN)], wu_v[cols, :]) * dg_v[s, :, cols].astype(F32)
            dz = dz.astype(BF)
            sumi_ref[0:1, cols] += jnp.sum(dz.astype(F32), 0, keepdims=True)
            dg_v[s, :, cols] = dz
        at_step(s, steps[2:9:3])
        dn1_v[s] += dot_nt(dg_v[s], wi_v[...])
        put(s).start()
    loads[4].wait()
    def puti(j):
        cols = pl.ds(pl.multiple_of(j * D, D), D)
        return pltpu.make_async_copy(gi_v.at[:, cols], gi.at[:, cols], osem.at[4 + j])
    @pl.loop(0, 4)
    def _(j):
        cols = pl.ds(pl.multiple_of(j * D, D), D)
        gi_v[:, cols] = dot_tn(n1_v[...].reshape(4 * LEN, D), dg_v[:, :, cols].reshape(4 * LEN, D)).astype(BF)
        puti(j).start()
        at_step(j, steps[9:])
    for i in range(4):
        put(i).wait()
        puti(i).wait()
    for job in jobs:
        job.sent()


def bwd1(og, add, pos, xh2, inv2, vec, g, dg, n1, wi, wu, cid):
    outs = [((96, D), F32), ((D, FF), BF), ((4, LEN, D), F32), ((8, D), F32), ((8, FF), F32)]
    big = ((4, LEN, FF), BF)
    scratch = [big, big, ACT, ((D, FF), BF), ((FF, D), BF), ((4 * LEN, D), BF), ((4, LEN, D), F32), ((4, 2, 4, 96, D), BF), ((D, FF), BF)]
    return pl.pallas_call(
        bwd1_body, name="feed_forward_backward", out_shape=[sds(*o) for o in outs],
        in_specs=[VM] * 6 + [HBM] * 5, out_specs=[VM, HBM, HBM, VM, VM],
        scratch_shapes=[pltpu.VMEM(*s) for s in scratch] + scatter_sems(3) + [DMA((5,)), DMA((8,))] + scatter_bufs(96, 256) * 3,
        compiler_params=pltpu.CompilerParams(collective_id=cid, has_side_effects=True, vmem_limit_bytes=61 << 20),
    )(og, add, pos, xh2, inv2, vec, g, dg, n1, wi, wu)


def attn_bwd_pair(s, hp, q_ref, k_ref, v_ref, p_ref, slot, do_ref, dqkv_ref):
    cols = pl.ds(pl.multiple_of(hp * 128, 128), 128)
    rows = pl.ds(pl.multiple_of(s * LEN, LEN), LEN)
    do2 = do_ref[rows, cols]
    low = iota((LEN, 128), 1) < HD
    dpt = dot_nt(stacked(v_ref[s, :, cols], low), do2)
    grads = []
    for h in range(2):
        d = dpt[h * LEN : (h + 1) * LEN]
        pf = p_ref[slot, h].astype(F32)
        grads.append((pf * (d - jnp.sum(pf * d, 0, keepdims=True))).astype(BF))
    ds = jnp.concatenate(grads, 0)
    dv = dot(p_ref[slot].reshape(2 * LEN, LEN), do2)
    dk = dot(ds, q_ref[s, :, cols])
    dq = dot_tn(ds, stacked(k_ref[s, :, cols], low))
    at = (hp // 2) * D + lax.rem(hp, 2) * 128
    def out(i):
        return pl.ds(pl.multiple_of(at + 256 * i, 128), 128)
    dqkv_ref[rows, out(0)] = (dq * 0.125).astype(BF)
    dqkv_ref[rows, out(1)] = (jnp.where(low, dk[:LEN], dk[LEN:]) * 0.125).astype(BF)
    dqkv_ref[rows, out(2)] = jnp.where(low, dv[:LEN], dv[LEN:]).astype(BF)


def bwd2_body(dn1, xh1, inv1, vec_ref, x, q, k, v, p, o, wqkv, wo, gi, grw_ref, s2_ref, si_ref,
              ggq, ggk, ggv, ggo, ggi, ggs, dx,
              dn1_v, xh1_v, inv1_v, x_v, q_v, k_v, v_v, o_v, p_v, wqkv_v, wo_v, sums_v, sumq_v, d1_v, do_v, dqkv_v, go_v, gg_v, gsm_v,
              sss, srs, sls, esem, isem, psem, osem, *bufs):
    def early(s):
        return [pltpu.make_async_copy(a.at[s], b.at[s], esem.at[i, s]) for i, (a, b) in enumerate(((dn1, dn1_v), (xh1, xh1_v), (inv1, inv1_v)))]
    ins = [(o, o_v), (wo, wo_v), (q, q_v), (k, k_v), (v, v_v), (x, x_v), (wqkv, wqkv_v)]
    loads = [pltpu.make_async_copy(a, b, isem.at[i]) for i, (a, b) in enumerate(ins)]
    for s in range(4):
        for cp in early(s):
            cp.start()
    sems = (sss, srs, sls)
    greet()
    jobs = []
    def add_job(source, done, in_hbm=False):
        nonlocal bufs
        own, bufs = scatter_refs(bufs)
        jobs.append(Scatter(source, own, sems, len(jobs), done, in_hbm))
    for t in range(4):
        def done(total, t=t):
            ggi[:, pl.ds(t * D, D)] = total
        add_job(lambda j, c, t=t: gi.at[j, c, :, :, pl.ds(t * D, D)], done, True)
    def done_o(total):
        ggo[...] = total
    add_job(lambda j, c: go_v.at[j, c], done_o)
    for t in range(3):
        def done(total, t=t):
            for i, ref in enumerate((ggq, ggk, ggv)):
                ref[:, pl.ds(256 * t, 256)] = total[:, 256 * i : 256 * i + 256]
        add_job(lambda j, c, t=t: gg_v.at[t, j, c], done)
    def done_s(total):
        ggs[...] = total
    add_job(lambda j, c: gsm_v.at[j, c], done_s)
    flow = staged(jobs)
    flow[0][0]()
    sums_v[...] = jnp.zeros_like(sums_v)
    sumq_v[...] = jnp.zeros_like(sumq_v)
    @pl.loop(0, 4)
    def _(s):
        for cp in early(s):
            cp.wait()
        at_step(s, [None, flow[1][0]])
        dy = dn1_v[s]
        xh = xh1_v[s].astype(F32)
        dr1 = norm_back(dy, xh, inv1_v[s][:, 0:1], vec_ref[3][None])
        sums_v[0] += jnp.sum(dy * xh, 0)
        sums_v[1] += jnp.sum(dy, 0)
        sums_v[2] += jnp.sum(dr1, 0)
        dn1_v[s] = dr1
        d1_v[pl.ds(s * LEN, LEN)] = dr1.astype(BF)
        @pl.when(s == 1)
        def _():
            for cp in loads[:2]:
                cp.start()
        @pl.when(s == 3)
        def _():
            for cp in loads[2:5]:
                cp.start()
    flow[1][1]()
    for cp in loads[:2]:
        cp.wait()
    go_v[...] = dot_tn(o_v[...].reshape(4 * LEN, D), d1_v[...]).astype(BF).reshape(4, 2, 4, 24, D)
    for step in flow[2]:
        step()
    @pl.loop(0, 2)
    def _(i):
        rows = pl.ds(pl.multiple_of(i * 2 * LEN, 2 * LEN), 2 * LEN)
        do_v[rows] = dot_nt(d1_v[rows], wo_v[...]).astype(BF)
    for cp in loads[2:5]:
        cp.wait()
    loads[5].start()
    def probs(t):
        hp, s = t // 4, lax.rem(t, 4)
        return pltpu.make_async_copy(p.at[s, pl.ds(hp * 2, 2)], p_v.at[lax.rem(t, 2)], psem.at[lax.rem(t, 2)])
    probs(0).start()
    plans = (flow[3] + [None] + flow[4][:3], flow[4][3:] + [None] + flow[5], flow[6])
    for grp, plan in enumerate(plans):
        @pl.loop(0, 8)
        def _(i, grp=grp, plan=plan):
            t = grp * 8 + i
            @pl.when(t + 1 < 24)
            def _():
                probs(t + 1).start()
            at_step(i, plan)
            probs(t).wait()
            attn_bwd_pair(lax.rem(t, 4), t // 4, q_v, k_v, v_v, p_v, lax.rem(t, 2), do_v, dqkv_v)
        if grp == 0:
            loads[5].wait()
            loads[6].start()
        d = dqkv_v[:, pl.ds(D * grp, D)]
        sumq_v[grp : grp + 1] = jnp.sum(d.astype(F32), 0, keepdims=True)
        gg_v[grp] = dot_tn(x_v[...].reshape(4 * LEN, D), d).astype(BF).reshape(4, 2, 4, 24, D)
    gsm_v[...] = small_grads(grw_ref[...], sums_v[...], s2_ref[...], sumq_v[...], si_ref[...]).reshape(4, 2, 4, 32, 128)
    loads[6].wait()
    def put(s):
        return pltpu.make_async_copy(dn1_v.at[s], dx.at[s], osem.at[s])
    late = [step for steps in flow[7:] for step in steps]
    @pl.loop(0, 4)
    def _(s):
        rows = pl.ds(pl.multiple_of(s * LEN, LEN), LEN)
        for i in range(3):
            at_step(s, late[i:12:3])
        dn1_v[s] += dot_nt(dqkv_v[rows], wqkv_v[...])
        put(s).start()
    for step in late[12:]:
        step()
    for s in range(4):
        put(s).wait()
    for job in jobs:
        job.sent()


def small_grads(grw, s1, s2, sq, si):
    by_kind = [jnp.concatenate([sq[grp : grp + 1, 256 * i : 256 * i + 256] for grp in range(3)], 1) for i in (0, 2)]
    vec = jnp.concatenate(by_kind + [s1[2:3], s1[0:1], s1[1:2], s2[2:3], s2[0:1], s2[1:2]], 0)
    row, col = iota((256, D), 0), iota((256, D), 1)
    tiled = jnp.broadcast_to(vec[None], (32, 8, D)).reshape(256, D)
    part = jnp.where(over(row, 8) == over(col, 24), tiled, 0.0).astype(BF)
    lane, col = iota((128, D), 0), iota((128, D), 1)
    pick = (lane == col - over(col, 24) * 24).astype(F32).astype(BF)
    out = dot_nt(part, pick).reshape(32, 8, 128)
    row, col = iota((32, FF), 0), iota((32, FF), 1)
    part = jnp.where(row == over(col, 96), si[0:1], 0.0).astype(BF)
    lane, col = iota((128, FF), 0), iota((128, FF), 1)
    pick = (lane - 32 == col - over(col, 96) * 96).astype(F32).astype(BF)
    inner = dot_nt(part, pick)
    out = out + jnp.where(iota((32, 8, 128), 1) == 0, inner[:, None, :], 0.0)
    return jnp.concatenate([grw.reshape(32, 24, 128), out], 1).astype(BF)


def bwd2(dn1, xh1, inv1, vec, x, q, k, v, p, o, wqkv, wo, gi, grw, s2, si, cid):
    own = ((24, D), F32)
    outs = [own, own, own, own, ((24, FF), F32), ((32, 128), F32), ((4, LEN, D), F32)]
    six = ((4, 2, 4, 24, D), BF)
    scratch = [((4, LEN, D), F32), ACT, ((4, LEN, 128), F32), ACT, ACT, ACT, ACT, ACT, ((2, 2, LEN, LEN), BF), ((D, 3 * D), BF), ((D, D), BF),
               ((8, D), F32), ((8, D), F32), ((4 * LEN, D), BF), ((4 * LEN, D), BF), ((4 * LEN, 3 * D), BF), six, ((3,) + six[0], BF), ((4, 2, 4, 32, 128), BF)]
    return pl.pallas_call(
        bwd2_body, name="attention_backward", out_shape=[sds(*s) for s in outs],
        in_specs=[HBM] * 3 + [VM] + [HBM] * 9 + [VM] * 3, out_specs=[VM] * 6 + [HBM],
        scratch_shapes=[pltpu.VMEM(*s) for s in scratch] + scatter_sems(9) + [DMA((3, 4)), DMA((7,)), DMA((2,)), DMA((4,))]
        + scatter_bufs(24, D) * 8 + scatter_bufs(32, 128),
        compiler_params=pltpu.CompilerParams(collective_id=cid, has_side_effects=True, vmem_limit_bytes=61 << 20),
    )(dn1, xh1, inv1, vec, x, q, k, v, p, o, wqkv, wo, gi.reshape(4, 2, 4, 24, FF), grw, s2, si)


def finish_body(small_ref, pair_ref, *refs):
    n = (len(refs) - 11) // 2
    grw, pair, inner, *vecs = refs[2 * n :]
    for a, b in zip(refs[:n], refs[n : 2 * n]):
        b[...] = a[...]
    grw[...] = small_ref[0:24]
    pair[...] = pair_ref[0, 0:2]
    inner[...] = small_ref[24, 32:128]
    for i, ref in enumerate(vecs):
        ref[...] = small_ref[24 + i, 0:24]


def finish(small, pair, more):
    tail = [((24, 128), F32), ((2,), F32), ((96,), F32)] + [((24,), F32)] * 8
    outs = pl.pallas_call(
        finish_body, name="results", out_shape=[sds(a.shape, a.dtype) for a in more] + [sds(*t) for t in tail],
        in_specs=[VM] * (2 + len(more)), out_specs=[VM] * (len(more) + 11),
    )(small, pair, *more)
    return outs[: len(more)], outs[len(more) :]


def exact(a, b, dims=((1,), (0,))):
    return lax.dot_general(a, b, (dims, ((), ())), preferred_element_type=F32, precision=HI)

def as_f(cond):
    return cond.astype(F32)

def greet_all():
    me = lax.axis_index("dp") * 4 + lax.axis_index("fsdp")
    bar = pltpu.get_barrier_semaphore()
    @pl.loop(1, 32)
    def _(k):
        t = lax.rem(me + k, 32)
        pl.semaphore_signal(bar, inc=1, device_id=(t // 4, lax.rem(t, 4)), device_id_type=MESH)
    pl.semaphore_wait(bar, 31)

def loss_body(picked_ref, emb, vb, ids, valid, qe, small,
              add_ref, grw_ref, pair_ref, ge, gvb_ref,
              emb_ref, vb_ref, ids_ref, valid_ref, qe_ref, small_ref, ge_ref, isem, own_ref, rows_ref, lt_ref, st_ref, all_ref, dh_ref, dhout_ref, gss, grs, gls, sss, srs, sls, xs, xr, *bufs):
    me = lax.axis_index("dp") * 4 + lax.axis_index("fsdp")
    VS = emb_ref.shape[0]
    loads = [pltpu.make_async_copy(a, b, isem.at[i]) for i, (a, b) in enumerate(
        ((small, small_ref), (qe, qe_ref), (ids, ids_ref), (valid, valid_ref), (vb, vb_ref), (emb, emb_ref)))]
    for cp in loads:
        cp.start()
    greet_all()
    own_ref[...] = picked_ref[:, 0:4, :].astype(F32).reshape(16, D).astype(BF)
    g = Gather(own_ref, rows_ref, (gss, grs, gls), 0)
    g.own()
    for cp in loads:
        cp.wait()
    cls = picked_ref[:, 4:5, :].astype(F32).reshape(4, D)
    cls8 = jnp.concatenate([cls, jnp.zeros((4, D), F32)], 0)
    rw = small_ref[:, 0:24, :].reshape(D, 128)
    row8, lane8 = iota((8, 128), 0), iota((8, 128), 1)
    qpick = as_f(jnp.logical_and(iota((8, 16), 1) == (me // 4) * 2 + iota((8, 16), 0) // 2, iota((8, 16), 0) < 4))
    qe_own = exact(qpick, qe_ref[...])
    score = jnp.sum(dot(cls8.astype(BF), rw) * qe_own, -1, keepdims=True)
    st_ref[12:13] = jnp.sum(jnp.where(row8 == lane8, score, 0.0), 0, keepdims=True)
    r512 = iota((16, 512), 1)
    s_of = r512 >> 2
    q_of = (s_of >> 4) * 2 + ((s_of & 3) >> 1)
    spread = exact(ids_ref[...].astype(F32), as_f(iota((4, 512), 0) == (iota((4, 512), 1) & 3)))
    ids = jnp.sum(jnp.where(iota((16, 512), 0) == q_of, spread, 0.0), 0, keepdims=True)
    local = ids.astype(jnp.int32) - me * VS
    for step in g.steps():
        step()
    g.arrived()
    g.sent()
    rows = rows_ref[...]
    bias = jnp.where(iota((16, VS), 0) == 0, vb_ref[...][None].astype(F32), 0.0).astype(BF)
    lt = dot_nt(emb_ref[...], rows) + dot_tn(bias, jnp.ones((16, 512), BF))
    lt_ref[...] = lt
    hit = iota((VS, 512), 0) == local
    peak = jnp.max(lt, 0, keepdims=True)
    total = jnp.sum(jnp.exp(lt - peak), 0, keepdims=True)
    target = jnp.sum(jnp.where(hit, lt, 0.0), 0, keepdims=True)
    for a in range(4):
        cols = slice(a * 128, a * 128 + 128)
        st_ref[a:a + 1] = peak[:, cols]
        st_ref[4 + a:5 + a] = total[:, cols]
        st_ref[8 + a:9 + a] = target[:, cols]
    sends = []
    for k in range(1, 32):
        t = lax.rem(me + k, 32)
        cp = rdma(st_ref, all_ref.at[me], xs.at[k], xr.at[k], (t // 4, lax.rem(t, 4)))
        cp.start()
        sends.append(cp)
    all_ref[me] = st_ref[...]
    for k in range(1, 32):
        f = lax.rem(me + 32 - k, 32)
        rdma(st_ref, all_ref.at[f], xs.at[k], xr.at[k], (f // 4, lax.rem(f, 4))).wait_recv()
    peaks = all_ref[:, 0:4, :]
    top = jnp.max(peaks, 0)
    tot = jnp.sum(all_ref[:, 4:8, :] * jnp.exp(peaks - top[None]), 0)
    lse = top + jnp.log(tot)
    logp = jnp.sum(all_ref[:, 8:12, :], 0) - lse
    i0, i1 = iota((128, 128), 0), iota((128, 128), 1)
    logp8 = jnp.concatenate([logp, jnp.zeros((4, 128), F32)], 0)
    spread = exact(logp8, 0.25 * as_f((i0 >> 2) == (i1 & 31)))
    seq_ll = jnp.sum(jnp.where((lane8 >> 5) == row8, spread, 0.0), 0, keepdims=True)
    spread = exact(all_ref[:, 12, :], as_f(i0 == (i1 & 3)))
    retrieval = jnp.sum(jnp.where((iota((32, 128), 1) >> 2) == iota((32, 128), 0), spread, 0.0), 0, keepdims=True)
    q16, s16 = iota((16, 128), 0), iota((16, 128), 1)
    mine = q16 == (s16 >> 4) * 2 + ((s16 & 3) >> 1)
    s8 = iota((8, 128), 1)
    slot_pick = as_f(iota((8, 128), 0) == ((s8 >> 2) & 3) * 2 + (s8 & 1))
    ok16 = jnp.logical_and(mine, exact(valid_ref[...].astype(F32), slot_pick) > 0.5)
    joint = retrieval + seq_ll
    def slot_lse(v):
        m = jnp.max(jnp.where(ok16, v, NEG), -1, keepdims=True)
        return m + jnp.log(jnp.sum(jnp.where(ok16, jnp.exp(v - m), 0.0), -1, keepdims=True))
    def to_seq(v):
        return jnp.sum(jnp.where(mine, v, 0.0), 0, keepdims=True)
    joint_lse, prior_lse = slot_lse(joint), slot_lse(retrieval)
    ok = to_seq(as_f(ok16)) > 0.5
    post = jnp.where(ok, jnp.exp(joint - to_seq(joint_lse)), 0.0)
    prior = jnp.where(ok, jnp.exp(retrieval - to_seq(prior_lse)), 0.0)
    pair = jnp.sum(jnp.where(q16 == (me // 4) * 2 + s16, joint_lse - prior_lse, 0.0), 0, keepdims=True)
    pair_ref[...] = jnp.broadcast_to(pair, (8, 128))
    d_score = LOSS_WEIGHT * (prior - post)
    scale = exact(jnp.broadcast_to(-LOSS_WEIGHT * post / 4.0, (8, 128)), as_f(iota((128, 512), 0) == (iota((128, 512), 1) >> 2)))[0:1]
    lse_row = jnp.concatenate([lse[a:a + 1] for a in range(4)], 1)
    dl = scale * (as_f(hit) - jnp.exp(lt_ref[...] - lse_row))
    gvb_ref[...] = jnp.broadcast_to(jnp.sum(dl, -1, keepdims=True), (VS, 128)).T[0]
    db = dl.astype(BF)
    dh_ref[...] = dot_tn(db, emb_ref[...]).astype(BF).reshape(4, 2, 4, 16, D)
    def done(total):
        dhout_ref[...] = total
    sc = Scatter(lambda j, c: dh_ref.at[j, c], scatter_refs(bufs)[0], (sss, srs, sls), 0, done)
    for j in range(4):
        sc.core(j)
    du = jnp.sum(jnp.where(jnp.logical_and(lane8 == me * 4 + row8, row8 < 4), d_score, 0.0), -1, keepdims=True) * qe_own
    grw_ref[...] = exact(cls8, du, ((0,), (0,)))
    dcls = exact(du, rw.astype(F32), ((1,), (1,)))
    add_ref[...] = jnp.zeros_like(add_ref)
    for l in range(4):
        add_ref[l, 4:5] = dcls[l:l + 1]
    sc.first()
    ge_ref[...] = dot(db, rows)
    out = pltpu.make_async_copy(ge_ref, ge, isem.at[6])
    out.start()
    sc.second()
    sc.third()
    sc.last()
    sc.sent()
    for l in range(4):
        add_ref[l, 0:4] = dhout_ref[4 * l:4 * l + 4]
    for cp in sends:
        cp.wait_send()
    out.wait()

def loss_call(picked, emb, vb, ids, valid, qe, small, cid):
    VS = emb.shape[0]
    outs = [((4, 8, D), F32), ((D, 128), F32), ((8, 128), F32), ((VS, D), F32), ((VS,), F32)]
    args = (picked, emb, vb, ids, valid, qe, small)
    return pl.pallas_call(loss_body, name="slot_loss", out_shape=[jax.ShapeDtypeStruct(s, t) for s, t in outs],
        in_specs=[VM] + [HBM] * 6, out_specs=[VM] * 3 + [HBM, VM],
        scratch_shapes=[pltpu.VMEM(a.shape, a.dtype) for a in (emb, vb, ids, valid, qe, small)] + [pltpu.VMEM((VS, D), F32), DMA((7,)), pltpu.VMEM((16, D), BF), pltpu.VMEM((512, D), BF), pltpu.VMEM((VS, 512), F32), pltpu.VMEM((16, 128), F32),
            pltpu.VMEM((32, 16, 128), F32), pltpu.VMEM((4, 2, 4, 16, D), BF), pltpu.VMEM((16, D), F32),
            *gather_sems(1), *scatter_sems(1), DMA((32,)), DMA((32,))] + scatter_bufs(16, D),
        compiler_params=pltpu.CompilerParams(collective_id=cid, has_side_effects=True, vmem_limit_bytes=58 << 20))(*args)


def linked_body(hidden_in, token_mask, out_grad, query_embed, slot_valid, target_ids, target_pos,
                qw, kw, vw, ow, iw, uw, rw, qb, vb, ob, ga, sa, ib, ub, gb, sb, embedding, vocab_bias):
    block = jnp.pad(jnp.stack([qb, vb, ob, ga, sa, ub, gb, sb]), ((0, 0), (0, 104)))
    block = jnp.concatenate([rw, block + jnp.pad(ib[None], ((0, 7), (32, 0)))], 0)
    group = (lax.axis_index("dp") * lax.axis_size("fsdp") + lax.axis_index("fsdp")) // GROUP
    pos = lax.dynamic_slice_in_dim(target_pos, group * 2, 2)
    pos = jnp.concatenate([pos, jnp.zeros((2, 1), jnp.int32), jnp.full((2, 3), -1, jnp.int32)], 1)
    pos = jnp.repeat(pos, 2, 0)
    pos_row, pos_col = pos[:, None, :], pos[:, :, None]
    small, wqkv, wo, wi, wu, q, k, v, p, o, n1, xh1, inv1, g, dg, out_seq, xh2, inv2, vec, inner, picked = forward(
        hidden_in, token_mask, pos_col, (block, qw, kw, vw, ow, iw, uw), 0)
    add, grw, pair, ge, gvb = loss_call(
        picked, embedding, vocab_bias, target_ids, slot_valid, query_embed, small.reshape(32, 32, 128), 1)
    gu, gi, dn1, s2, si = bwd1(out_grad, add, pos_row, xh2, inv2, vec, g, dg, n1, wi, wu, 2)
    gq, gk, gv, go, gi, gsm, dx = bwd2(dn1, xh1, inv1, vec, hidden_in, q, k, v, p, o, wqkv, wo, gi, grw, s2, si, 3)
    (gu, gi, gq, gk, gv, go, gvb), (grw, pair, gib, *vecs) = finish(
        gsm, pair, (gu, gi, gq, gk, gv, go, gvb))
    return (out_seq, pair, dx, gq, gk, gv, go, gi, gu, grw, *vecs[:5], gib, *vecs[5:], ge, gvb)


def solution(mesh):
    placed = (
        P(("dp", "fsdp"), None, None),
        P(("dp", "fsdp"), None),
        P(("dp", "fsdp"), None, None),
        P(),
        P(),
        P(),
        P(),
        P(("dp", "fsdp"), None),
        P(("dp", "fsdp"), None),
        P(("dp", "fsdp"), None),
        P(("dp", "fsdp"), None),
        P(("dp", "fsdp"), None),
        P(("dp", "fsdp"), None),
        P(("dp", "fsdp"), None),
        P(("dp", "fsdp")),
        P(("dp", "fsdp")),
        P(("dp", "fsdp")),
        P(("dp", "fsdp")),
        P(("dp", "fsdp")),
        P(("dp", "fsdp")),
        P(("dp", "fsdp")),
        P(("dp", "fsdp")),
        P(("dp", "fsdp")),
        P(("dp", "fsdp"), None),
        P(("dp", "fsdp")),
    )
    own = mesh.shape["dp"] == 8 and mesh.shape["fsdp"] == 4
    return jax.shard_map(
        linked_body if own else plain_body,
        mesh=mesh,
        in_specs=placed,
        out_specs=(
            P(("dp", "fsdp"), None, None),
            P(("dp", "fsdp")),
            P(("dp", "fsdp"), None, None),
            P(("dp", "fsdp"), None),
            P(("dp", "fsdp"), None),
            P(("dp", "fsdp"), None),
            P(("dp", "fsdp"), None),
            P(("dp", "fsdp"), None),
            P(("dp", "fsdp"), None),
            P(("dp", "fsdp"), None),
            P(("dp", "fsdp")),
            P(("dp", "fsdp")),
            P(("dp", "fsdp")),
            P(("dp", "fsdp")),
            P(("dp", "fsdp")),
            P(("dp", "fsdp")),
            P(("dp", "fsdp")),
            P(("dp", "fsdp")),
            P(("dp", "fsdp")),
            P(("dp", "fsdp"), None),
            P(("dp", "fsdp")),
        ),
        check_vma=False,
    )
```

```python
import functools

import jax
import jax.numpy as jnp
from jax import lax
from jax.experimental import pallas as pl
from jax.experimental.pallas import tpu as pltpu
from jax.sharding import PartitionSpec as P


D = 768
H = 12
HD = 64
LEN = 288
MASKS = 4
SLOT_DEV = 2
GROUP = 4


EPS = 1e-12
NEG = -1000000000.0
HIGH = lax.Precision.HIGHEST
LOSS_WEIGHT = 32.0


def combined_all(value, axis, join):
    pieces = jax.tree.map(lambda part: lax.all_gather(part, axis), value)
    head = jax.tree.map(lambda part: part[0], pieces)
    tail = jax.tree.map(lambda part: part[1:], pieces)
    subtotal, _ = lax.scan(lambda subtotal, share: (join(subtotal, share), None), head, tail)
    return subtotal


def partner(value, axis, stride):
    mask = 2**stride
    pairs = [(source, source ^ mask) for source in range(lax.axis_size(axis))]
    return lax.ppermute(value, axis, pairs)


def layer_norm(residual, gain_vec, shift_vec):
    row_mean = jnp.mean(residual, -1, keepdims=True)
    centred = residual - row_mean
    row_var = jnp.mean(centred * centred, -1, keepdims=True)
    return centred * lax.rsqrt(row_var + EPS) * gain_vec + shift_vec


def exact_gelu(pre_act):
    return jax.nn.gelu(pre_act, approximate=False)


def collect(params):
    (
        query_weight,
        key_weight,
        value_weight,
        out_weight,
        inner_weight,
        outer_weight,
        retrieve_weight,
        query_bias,
        value_bias,
        out_bias,
        norm1_gain,
        norm1_bias,
        inner_bias,
        outer_bias,
        norm2_gain,
        norm2_bias,
    ) = params
    return (
        lax.all_gather(query_weight, ("dp", "fsdp"), axis=0, tiled=True),
        lax.all_gather(key_weight, ("dp", "fsdp"), axis=0, tiled=True),
        lax.all_gather(value_weight, ("dp", "fsdp"), axis=0, tiled=True),
        lax.all_gather(out_weight, ("dp", "fsdp"), axis=0, tiled=True),
        lax.all_gather(inner_weight, ("dp", "fsdp"), axis=0, tiled=True),
        lax.all_gather(outer_weight, ("dp", "fsdp"), axis=0, tiled=True),
        lax.all_gather(retrieve_weight, ("dp", "fsdp"), axis=0, tiled=True),
        lax.all_gather(query_bias, ("dp", "fsdp"), axis=0, tiled=True),
        lax.all_gather(value_bias, ("dp", "fsdp"), axis=0, tiled=True),
        lax.all_gather(out_bias, ("dp", "fsdp"), axis=0, tiled=True),
        lax.all_gather(norm1_gain, ("dp", "fsdp"), axis=0, tiled=True),
        lax.all_gather(norm1_bias, ("dp", "fsdp"), axis=0, tiled=True),
        lax.all_gather(inner_bias, ("dp", "fsdp"), axis=0, tiled=True),
        lax.all_gather(outer_bias, ("dp", "fsdp"), axis=0, tiled=True),
        lax.all_gather(norm2_gain, ("dp", "fsdp"), axis=0, tiled=True),
        lax.all_gather(norm2_bias, ("dp", "fsdp"), axis=0, tiled=True),
    )


def spread(grads):
    (
        grad_qw,
        grad_kw,
        grad_vw,
        grad_ow,
        grad_iw,
        grad_uw,
        grad_rw,
        grad_qb,
        grad_vb,
        grad_ob,
        grad_ga,
        grad_sa,
        grad_ib,
        grad_ub,
        grad_gb,
        grad_sb,
    ) = grads
    return (
        lax.psum_scatter(grad_qw, ("dp", "fsdp"), scatter_dimension=0, tiled=True),
        lax.psum_scatter(grad_kw, ("dp", "fsdp"), scatter_dimension=0, tiled=True),
        lax.psum_scatter(grad_vw, ("dp", "fsdp"), scatter_dimension=0, tiled=True),
        lax.psum_scatter(grad_ow, ("dp", "fsdp"), scatter_dimension=0, tiled=True),
        lax.psum_scatter(grad_iw, ("dp", "fsdp"), scatter_dimension=0, tiled=True),
        lax.psum_scatter(grad_uw, ("dp", "fsdp"), scatter_dimension=0, tiled=True),
        lax.psum_scatter(grad_rw, ("dp", "fsdp"), scatter_dimension=0, tiled=True),
        lax.psum_scatter(grad_qb, ("dp", "fsdp"), scatter_dimension=0, tiled=True),
        lax.psum_scatter(grad_vb, ("dp", "fsdp"), scatter_dimension=0, tiled=True),
        lax.psum_scatter(grad_ob, ("dp", "fsdp"), scatter_dimension=0, tiled=True),
        lax.psum_scatter(grad_ga, ("dp", "fsdp"), scatter_dimension=0, tiled=True),
        lax.psum_scatter(grad_sa, ("dp", "fsdp"), scatter_dimension=0, tiled=True),
        lax.psum_scatter(grad_ib, ("dp", "fsdp"), scatter_dimension=0, tiled=True),
        lax.psum_scatter(grad_ub, ("dp", "fsdp"), scatter_dimension=0, tiled=True),
        lax.psum_scatter(grad_gb, ("dp", "fsdp"), scatter_dimension=0, tiled=True),
        lax.psum_scatter(grad_sb, ("dp", "fsdp"), scatter_dimension=0, tiled=True),
    )


def attention(query_heads, key_heads, value_heads, keys_ok):
    head_scale = HD ** (-0.5)
    scores = (
        jnp.einsum("sqhe,skhe->shqk", query_heads, key_heads, preferred_element_type=jnp.float32)
        * head_scale
    )
    scores = jnp.where(keys_ok[:, None, None, :] > 0, scores, NEG)
    row_peak = jnp.max(scores, -1, keepdims=True)
    exp_scores = jnp.exp(scores - row_peak)
    totals = jnp.sum(exp_scores, -1, keepdims=True)
    attn_probs = (exp_scores / totals).astype(jnp.bfloat16)
    attended = jnp.einsum(
        "shqk,skhe->sqhe", attn_probs, value_heads, preferred_element_type=jnp.float32
    )
    return (attended, row_peak + jnp.log(totals))


def forward_layer(hidden, keys_ok, gathered):
    (
        query_weight,
        key_weight,
        value_weight,
        out_weight,
        inner_weight,
        outer_weight,
        retrieve_weight,
        query_bias,
        value_bias,
        out_bias,
        norm1_gain,
        norm1_bias,
        inner_bias,
        outer_bias,
        norm2_gain,
        norm2_bias,
    ) = gathered
    seq_count = hidden.shape[0]
    head_shape = (seq_count, LEN, H, HD)
    flat_rows = hidden.reshape(seq_count * LEN, D)
    queries = (
        jnp.dot(flat_rows, query_weight, preferred_element_type=jnp.float32)
        + query_bias.astype(jnp.float32)
    ).astype(jnp.bfloat16)
    key_rows = jnp.dot(flat_rows, key_weight, preferred_element_type=jnp.float32).astype(
        jnp.bfloat16
    )
    values = (
        jnp.dot(flat_rows, value_weight, preferred_element_type=jnp.float32)
        + value_bias.astype(jnp.float32)
    ).astype(jnp.bfloat16)
    attended, log_totals = attention(
        queries.reshape(head_shape),
        key_rows.reshape(head_shape),
        values.reshape(head_shape),
        keys_ok,
    )
    attended = attended.reshape(seq_count * LEN, D).astype(jnp.bfloat16)
    first_in = (
        flat_rows.astype(jnp.float32)
        + jnp.dot(attended, out_weight, preferred_element_type=jnp.float32)
        + out_bias.astype(jnp.float32)
    )
    normed_one = layer_norm(
        first_in, norm1_gain.astype(jnp.float32), norm1_bias.astype(jnp.float32)
    ).astype(jnp.bfloat16)
    pre_act = jnp.dot(
        normed_one, inner_weight, preferred_element_type=jnp.float32
    ) + inner_bias.astype(jnp.float32)
    active = exact_gelu(pre_act).astype(jnp.bfloat16)
    second_in = (
        normed_one.astype(jnp.float32)
        + jnp.dot(active, outer_weight, preferred_element_type=jnp.float32)
        + outer_bias.astype(jnp.float32)
    )
    layer_out = layer_norm(
        second_in, norm2_gain.astype(jnp.float32), norm2_bias.astype(jnp.float32)
    ).astype(jnp.bfloat16)
    return (
        queries,
        key_rows,
        values,
        log_totals,
        attended,
        first_in,
        normed_one,
        pre_act,
        active,
        second_in,
        layer_out,
    )


def backward_layer(hidden, keys_ok, gathered, kept_acts, grad_out):
    (
        query_weight,
        key_weight,
        value_weight,
        out_weight,
        inner_weight,
        outer_weight,
        retrieve_weight,
        query_bias,
        value_bias,
        out_bias,
        norm1_gain,
        norm1_bias,
        inner_bias,
        outer_bias,
        norm2_gain,
        norm2_bias,
    ) = gathered
    (
        queries,
        key_rows,
        values,
        log_totals,
        attended,
        first_in,
        normed_one,
        pre_act,
        active,
        second_in,
        layer_out,
    ) = kept_acts
    seq_count = hidden.shape[0]
    head_shape = (seq_count, LEN, H, HD)
    flat_rows = hidden.reshape(seq_count * LEN, D)
    unused_two, norm_two_back = jax.vjp(
        layer_norm, second_in, norm2_gain.astype(jnp.float32), norm2_bias.astype(jnp.float32)
    )
    grad_second, grad_norm2_gain, grad_norm2_bias = norm_two_back(grad_out)
    second_low = grad_second.astype(jnp.bfloat16)
    grad_outer_weight = jnp.dot(active.T, second_low, preferred_element_type=jnp.float32)
    grad_outer_bias = jnp.sum(grad_second, 0)
    grad_active = jnp.dot(second_low, outer_weight.T, preferred_element_type=jnp.float32)
    unused_act, gelu_back = jax.vjp(exact_gelu, pre_act)
    grad_pre = gelu_back(grad_active)[0].astype(jnp.bfloat16)
    grad_inner_weight = jnp.dot(normed_one.T, grad_pre, preferred_element_type=jnp.float32)
    grad_inner_bias = jnp.sum(grad_pre.astype(jnp.float32), 0)
    grad_normed = grad_second + jnp.dot(
        grad_pre, inner_weight.T, preferred_element_type=jnp.float32
    )
    unused_one, norm_one_back = jax.vjp(
        layer_norm, first_in, norm1_gain.astype(jnp.float32), norm1_bias.astype(jnp.float32)
    )
    grad_first, grad_norm1_gain, grad_norm1_bias = norm_one_back(grad_normed)
    first_low = grad_first.astype(jnp.bfloat16)
    grad_out_weight = jnp.dot(attended.T, first_low, preferred_element_type=jnp.float32)
    grad_out_bias = jnp.sum(grad_first, 0)
    grad_attended = (
        jnp.dot(first_low, out_weight.T, preferred_element_type=jnp.float32)
        .astype(jnp.bfloat16)
        .reshape(head_shape)
    )
    query_heads = queries.reshape(head_shape)
    key_heads = key_rows.reshape(head_shape)
    value_heads = values.reshape(head_shape)
    head_scale = HD ** (-0.5)
    scores = (
        jnp.einsum("sqhe,skhe->shqk", query_heads, key_heads, preferred_element_type=jnp.float32)
        * head_scale
    )
    scores = jnp.where(keys_ok[:, None, None, :] > 0, scores, NEG)
    attn_probs = jnp.exp(scores - log_totals)
    grad_probs = jnp.einsum(
        "sqhe,skhe->shqk", grad_attended, value_heads, preferred_element_type=jnp.float32
    )
    grad_value_heads = jnp.einsum(
        "shqk,sqhe->skhe",
        attn_probs.astype(jnp.bfloat16),
        grad_attended,
        preferred_element_type=jnp.float32,
    )
    grad_scores = (
        attn_probs * (grad_probs - jnp.sum(attn_probs * grad_probs, -1, keepdims=True))
    ).astype(jnp.bfloat16)
    grad_query_heads = (
        jnp.einsum("shqk,skhe->sqhe", grad_scores, key_heads, preferred_element_type=jnp.float32)
        * head_scale
    )
    grad_key_heads = (
        jnp.einsum("shqk,sqhe->skhe", grad_scores, query_heads, preferred_element_type=jnp.float32)
        * head_scale
    )
    grad_queries = grad_query_heads.reshape(seq_count * LEN, D).astype(jnp.bfloat16)
    grad_keys = grad_key_heads.reshape(seq_count * LEN, D).astype(jnp.bfloat16)
    grad_values = grad_value_heads.reshape(seq_count * LEN, D).astype(jnp.bfloat16)
    grad_query_weight = jnp.dot(flat_rows.T, grad_queries, preferred_element_type=jnp.float32)
    grad_key_weight = jnp.dot(flat_rows.T, grad_keys, preferred_element_type=jnp.float32)
    grad_value_weight = jnp.dot(flat_rows.T, grad_values, preferred_element_type=jnp.float32)
    grad_query_bias = jnp.sum(grad_queries.astype(jnp.float32), 0)
    grad_value_bias = jnp.sum(grad_values.astype(jnp.float32), 0)
    grad_hidden = (
        grad_first
        + jnp.dot(grad_queries, query_weight.T, preferred_element_type=jnp.float32)
        + jnp.dot(grad_keys, key_weight.T, preferred_element_type=jnp.float32)
        + jnp.dot(grad_values, value_weight.T, preferred_element_type=jnp.float32)
    )
    return (
        grad_hidden,
        (
            grad_query_weight,
            grad_key_weight,
            grad_value_weight,
            grad_out_weight,
            grad_inner_weight,
            grad_outer_weight,
            grad_query_bias,
            grad_value_bias,
            grad_out_bias,
            grad_norm1_gain,
            grad_norm1_bias,
            grad_inner_bias,
            grad_outer_bias,
            grad_norm2_gain,
            grad_norm2_bias,
        ),
    )


def merge_pair(peak_one, total_one, peak_two, total_two):
    peak_new = jnp.maximum(peak_one, peak_two)
    return (
        peak_new,
        total_one * jnp.exp(peak_one - peak_new) + total_two * jnp.exp(peak_two - peak_new),
    )


def merge_rows(one_side, other_side):
    peak_new, total_new = merge_pair(one_side[0], one_side[1], other_side[0], other_side[1])
    return (peak_new, total_new, one_side[2] + other_side[2])


def slot_partial(score_vec, slot_ok):
    grouped = jnp.where(slot_ok, score_vec, NEG).reshape(-1, SLOT_DEV)
    ok_grouped = slot_ok.reshape(-1, SLOT_DEV)
    group_peak = jnp.max(grouped, -1)
    group_total = jnp.sum(jnp.where(ok_grouped, jnp.exp(grouped - group_peak[:, None]), 0.0), -1)
    return (group_peak, group_total)


def plain_body(
    hidden_in,
    token_mask,
    out_grad,
    query_embed,
    slot_valid,
    target_ids,
    target_pos,
    query_weight,
    key_weight,
    value_weight,
    out_weight,
    inner_weight,
    outer_weight,
    retrieve_weight,
    query_bias,
    value_bias,
    out_bias,
    norm1_gain,
    norm1_bias,
    inner_bias,
    outer_bias,
    norm2_gain,
    norm2_bias,
    embedding,
    vocab_bias,
):
    params = (
        query_weight,
        key_weight,
        value_weight,
        out_weight,
        inner_weight,
        outer_weight,
        retrieve_weight,
        query_bias,
        value_bias,
        out_bias,
        norm1_gain,
        norm1_bias,
        inner_bias,
        outer_bias,
        norm2_gain,
        norm2_bias,
    )
    gathered = collect(params)
    kept_acts = forward_layer(hidden_in, token_mask, gathered)
    seq_count = hidden_in.shape[0]
    query_count = seq_count // SLOT_DEV
    out_seq = kept_acts[10].reshape(seq_count, LEN, D)
    devices = lax.axis_size("dp") * lax.axis_size("fsdp")
    device = lax.axis_index("dp") * lax.axis_size("fsdp") + lax.axis_index("fsdp")
    member = lax.axis_index("fsdp") % GROUP
    local_seq = jnp.arange(seq_count, dtype=jnp.int32)
    local_query = device // GROUP * query_count + local_seq // SLOT_DEV
    local_slot = member * SLOT_DEV + local_seq % SLOT_DEV
    slot_ok = slot_valid[local_query, local_slot] > 0
    embeds = query_embed[local_query]
    positions = target_pos[local_query]
    cls_rows = out_seq[:, 0, :].astype(jnp.float32)
    retrieve_full = gathered[6].astype(jnp.float32)
    projected = jnp.dot(cls_rows, retrieve_full, precision=HIGH)
    retrieval = jnp.sum(projected * embeds, -1)
    own_rows = seq_count * MASKS
    sent_rows = out_seq[local_seq[:, None], positions].reshape(own_rows, D)
    all_rows = lax.all_gather(sent_rows, ("dp", "fsdp"), axis=0, tiled=True)
    group_count = devices // GROUP
    all_targets = jnp.broadcast_to(
        target_ids.reshape(group_count, 1, query_count, 1, MASKS),
        (group_count, GROUP, query_count, SLOT_DEV, MASKS),
    ).reshape(-1)
    vocab_rows = embedding.shape[0]
    local_ids = all_targets - device * vocab_rows
    target_hit = jnp.arange(vocab_rows, dtype=jnp.int32)[None, :] == local_ids[:, None]
    logits = jnp.einsum(
        "rd,vd->rv", all_rows, embedding, preferred_element_type=jnp.float32
    ) + vocab_bias.astype(jnp.float32)
    row_peak = jnp.max(logits, -1)
    sum_exp = jnp.sum(jnp.exp(logits - row_peak[:, None]), -1)
    target_logit = jnp.sum(jnp.where(target_hit, logits, 0.0), -1)
    peak_all, total_all, target_all = combined_all(
        (row_peak, sum_exp, target_logit), ("dp", "fsdp"), merge_rows
    )
    lse_rows = peak_all + jnp.log(total_all)
    log_prob = lax.dynamic_slice_in_dim(target_all - lse_rows, device * own_rows, own_rows)
    seq_ll = jnp.mean(log_prob.reshape(seq_count, MASKS), -1)
    joint_score = retrieval + seq_ll
    joint_peak, joint_total = slot_partial(joint_score, slot_ok)
    prior_peak, prior_total = slot_partial(retrieval, slot_ok)
    for bit_number in range(GROUP.bit_length() - 1):
        far_joint_peak, far_joint_total, far_prior_peak, far_prior_total = partner(
            (joint_peak, joint_total, prior_peak, prior_total), "fsdp", bit_number
        )
        joint_peak, joint_total = merge_pair(
            joint_peak, joint_total, far_joint_peak, far_joint_total
        )
        prior_peak, prior_total = merge_pair(
            prior_peak, prior_total, far_prior_peak, far_prior_total
        )
    joint_lse = joint_peak + jnp.log(joint_total)
    prior_lse = prior_peak + jnp.log(prior_total)
    pair_loglik = joint_lse - prior_lse
    post_weight = jnp.where(slot_ok, jnp.exp(joint_score - jnp.repeat(joint_lse, SLOT_DEV)), 0.0)
    prior_weight = jnp.where(slot_ok, jnp.exp(retrieval - jnp.repeat(prior_lse, SLOT_DEV)), 0.0)
    grad_retrieval = LOSS_WEIGHT * (prior_weight - post_weight)
    row_scale = jnp.repeat(-LOSS_WEIGHT * post_weight / MASKS, MASKS)
    all_scales = lax.all_gather(row_scale, ("dp", "fsdp"), axis=0, tiled=True)
    vocab_probs = jnp.exp(logits - lse_rows[:, None])
    grad_logits = all_scales[:, None] * (target_hit.astype(jnp.float32) - vocab_probs)
    grad_vocab_bias = jnp.sum(grad_logits, 0)
    logits_low = grad_logits.astype(jnp.bfloat16)
    grad_embedding = jnp.einsum(
        "rv,rd->vd", logits_low, all_rows, preferred_element_type=jnp.float32
    )
    grad_picked = lax.psum_scatter(
        jnp.dot(logits_low, embedding, preferred_element_type=jnp.float32),
        ("dp", "fsdp"),
        scatter_dimension=0,
        tiled=True,
    )
    grad_project = grad_retrieval[:, None] * embeds
    grad_retrieve_weight = jnp.dot(cls_rows.T, grad_project, precision=HIGH)
    grad_cls = jnp.dot(grad_project, retrieve_full.T, precision=HIGH)
    grad_total = out_grad.astype(jnp.float32)
    grad_total = grad_total.at[local_seq[:, None], positions].add(
        grad_picked.reshape(seq_count, MASKS, D)
    )
    grad_total = grad_total.at[:, 0, :].add(grad_cls)
    grad_total = grad_total.reshape(seq_count * LEN, D)
    grad_hidden, layer_grads = backward_layer(
        hidden_in, token_mask, gathered, kept_acts, grad_total
    )
    (
        grad_query_weight,
        grad_key_weight,
        grad_value_weight,
        grad_out_weight,
        grad_inner_weight,
        grad_outer_weight,
        grad_query_bias,
        grad_value_bias,
        grad_out_bias,
        grad_norm1_gain,
        grad_norm1_bias,
        grad_inner_bias,
        grad_outer_bias,
        grad_norm2_gain,
        grad_norm2_bias,
    ) = layer_grads
    (
        shard_query_weight,
        shard_key_weight,
        shard_value_weight,
        shard_out_weight,
        shard_inner_weight,
        shard_outer_weight,
        shard_retrieve_weight,
        shard_query_bias,
        shard_value_bias,
        shard_out_bias,
        shard_norm1_gain,
        shard_norm1_bias,
        shard_inner_bias,
        shard_outer_bias,
        shard_norm2_gain,
        shard_norm2_bias,
    ) = spread(
        (
            grad_query_weight,
            grad_key_weight,
            grad_value_weight,
            grad_out_weight,
            grad_inner_weight,
            grad_outer_weight,
            grad_retrieve_weight,
            grad_query_bias,
            grad_value_bias,
            grad_out_bias,
            grad_norm1_gain,
            grad_norm1_bias,
            grad_inner_bias,
            grad_outer_bias,
            grad_norm2_gain,
            grad_norm2_bias,
        )
    )
    return (
        out_seq,
        pair_loglik,
        grad_hidden.reshape(seq_count, LEN, D),
        shard_query_weight,
        shard_key_weight,
        shard_value_weight,
        shard_out_weight,
        shard_inner_weight,
        shard_outer_weight,
        shard_retrieve_weight,
        shard_query_bias,
        shard_value_bias,
        shard_out_bias,
        shard_norm1_gain,
        shard_norm1_bias,
        shard_inner_bias,
        shard_outer_bias,
        shard_norm2_gain,
        shard_norm2_bias,
        grad_embedding,
        grad_vocab_bias,
    )

MESH = pl.DeviceIdType.MESH
F32 = jnp.float32
BF = jnp.bfloat16
DMA = pltpu.SemaphoreType.DMA


def coords():
    d = lax.axis_index("dp")
    return d // 4, (d // 2) % 2, d % 2, lax.axis_index("fsdp")


def dev(y, x, c, z):
    return ((y * 2 + x) * 2 + c, z)


def across(z, k):
    return (z + 1 - 2 * lax.rem(z, 2), lax.rem(z + 2, 4), 3 - z)[k - 1] if k else z


def rdma(src, dst, ss, rs, to):
    return pltpu.make_async_remote_copy(src, dst, ss, rs, device_id=to, device_id_type=MESH)


def greet():
    y, x, c, z = coords()
    bar = pltpu.get_barrier_semaphore()
    tos = [dev(y, x, c, lax.rem(z + k, 4)) for k in (1, 2, 3)]
    tos += [dev(y, 1 - x, c, z), dev(1 - y, x, c, z), dev(y, x, 1 - c, z)]
    for t in tos:
        pl.semaphore_signal(bar, inc=1, device_id=t, device_id_type=MESH)
    pl.semaphore_wait(bar, len(tos))


def rows_at(start, size):
    return pl.ds(pl.multiple_of(start, 8), size)


class Gather:
    def __init__(self, src, dst, sems, a):
        self.src, self.dst, self.a = src, dst, a
        self.ss, self.rs, self.ls = sems
        self.r, n = src.shape
        self.split = (n // 2) % 128 == 0
        self.h = n // 2

    def chips(self):
        y, x, c, z = coords()
        return y * 2 + x, y * 2 + 1 - x, (1 - y) * 2 + x, (1 - y) * 2 + 1 - x

    def block(self, chip, k):
        y, x, c, z = coords()
        zz = across(z, k)
        return self.dst.at[rows_at(((chip * 2 + c) * 4 + zz) * self.r, self.r)]

    def column(self, chip, c):
        return self.dst.at[rows_at((chip * 2 + c) * 4 * self.r, 4 * self.r)]

    def half(self, ref, right):
        if not self.split:
            return ref
        return ref.at[:, pl.ds(self.h if right else 0, self.h)]

    def copy(self, src, dst, slot, to):
        return rdma(src, dst, self.ss.at[self.a, slot], self.rs.at[self.a, slot], to)

    def send(self, ref, slot, to, src=None):
        self.copy(ref if src is None else src, ref, slot, to).start()

    def wait(self, ref, slot):
        y, x, c, z = coords()
        self.copy(ref, ref, slot, dev(y, 1 - x, c, z)).wait_recv()

    def kept(self):
        return pltpu.make_async_copy(self.src, self.block(self.chips()[0], 0), self.ls.at[self.a])

    def own_xy(self):
        y, x, c, z = coords()
        d = self.block(self.chips()[0], 0)
        self.send(d, 4, dev(y, 1 - x, c, z), self.src)
        self.send(d, 8, dev(1 - y, x, c, z), self.src)

    def own_z(self):
        y, x, c, z = coords()
        d = self.block(self.chips()[0], 0)
        self.kept().start()
        for k in (1, 3, 2):
            self.send(d, k, dev(y, x, c, across(z, k)), self.src)

    def own(self):
        self.own_xy()
        self.own_z()

    def z(self, k):
        y, x, c, z = coords()
        d = self.block(self.chips()[0], k)
        self.wait(d, k)
        self.send(d, 4 + k, dev(y, 1 - x, c, z))
        self.send(d, 8 + k, dev(1 - y, x, c, z))

    def core(self, i):
        y, x, c, z = coords()
        if i == 0:
            self.kept().wait()
        self.send(self.column(self.chips()[i], c), 20 + i, dev(y, x, 1 - c, z))

    def xy(self, k):
        y, x, c, z = coords()
        dx = self.block(self.chips()[1], k)
        self.wait(dx, 4 + k)
        self.send(self.half(dx, False), 12 + k, dev(1 - y, x, c, z))
        dy = self.block(self.chips()[2], k)
        self.wait(dy, 8 + k)
        if self.split:
            self.send(self.half(dy, True), 16 + k, dev(y, 1 - x, c, z))

    def dg(self, k):
        d = self.block(self.chips()[3], k)
        self.wait(self.half(d, False), 12 + k)
        if self.split:
            self.wait(self.half(d, True), 16 + k)

    def arrived(self):
        y, x, c, z = coords()
        for i, chip in enumerate(self.chips()):
            self.wait(self.column(chip, 1 - c), 20 + i)

    def sent(self):
        y, x, c, z = coords()
        to = dev(y, 1 - x, c, z)
        d = self.block(self.chips()[0], 0)
        for k in range(4):
            if k:
                self.copy(d, d, k, to).wait_send()
            self.copy(d, d, 4 + k, to).wait_send()
            self.copy(d, d, 8 + k, to).wait_send()
            half = self.half(d, False)
            self.copy(half, half, 12 + k, to).wait_send()
            if self.split:
                self.copy(half, half, 16 + k, to).wait_send()
            col = self.column(self.chips()[0], 0)
            self.copy(col, col, 20 + k, to).wait_send()

    def steps(self):
        out = [functools.partial(self.z, k) for k in (1, 3, 2)]
        out[2] = lambda: (self.z(2), self.core(0))
        out += [functools.partial(self.xy, k) for k in (0, 1, 3)]
        out += [lambda: (self.xy(2), self.core(1), self.core(2))]
        out += [lambda: (self.dg(0), self.dg(1)), lambda: (self.dg(3), self.dg(2), self.core(3))]
        return out


def gather_sems(n):
    return [DMA((n, 24)), DMA((n, 24)), DMA((n,))]


class Scatter:
    def __init__(self, source, bufs, sems, a, done, in_hbm=False):
        self.source, self.a, self.done, self.in_hbm = source, a, done, in_hbm
        self.ss, self.rs, self.ls = sems
        self.held, self.rc, self.ray, self.rax, self.rbx, self.rby, self.rz = bufs
        self.split = self.rbx is not None
        self.h = self.rax.shape[-1]

    def copy(self, src, dst, slot, to):
        return rdma(src, dst, self.ss.at[self.a, slot], self.rs.at[self.a, slot], to)

    def wait(self, ref, slot):
        y, x, c, z = coords()
        self.copy(ref, ref, slot, dev(y, 1 - x, c, z)).wait_recv()

    def local(self, j):
        y, x, c, z = coords()
        return pltpu.make_async_copy(self.source(j, c), self.held.at[j], self.ls.at[self.a, j])

    def core(self, j):
        y, x, c, z = coords()
        if self.in_hbm:
            self.local(j).start()
        self.copy(self.source(j, 1 - c), self.rc.at[j], j, dev(y, x, 1 - c, z)).start()

    def cores(self):
        for j in range(4):
            self.core(j)

    def add(self, dst, one, two):
        for i in range(4):
            dst[i] = (one[i].astype(F32) + two[i].astype(F32)).astype(BF)

    def left(self, chip):
        return self.held.at[chip, :, :, pl.ds(0, self.h)]

    def right(self, chip):
        return self.held.at[chip, :, :, pl.ds(self.h, self.h)]

    def first(self):
        y, x, c, z = coords()
        @pl.loop(0, 4)
        def _(j):
            if self.in_hbm:
                self.local(j).wait()
            self.wait(self.rc.at[j], j)
            self.add(self.held.at[j], self.held.at[j] if self.in_hbm else self.source(j, c), self.rc.at[j])
        for xi in range(2):
            self.copy(self.left((1 - y) * 2 + xi), self.ray.at[xi], 4 + xi, dev(1 - y, x, c, z)).start()
        if self.split:
            for yi in range(2):
                self.copy(self.right(yi * 2 + 1 - x), self.rbx.at[yi], 6 + yi, dev(y, 1 - x, c, z)).start()

    def second(self):
        y, x, c, z = coords()
        for xi in range(2):
            self.wait(self.ray.at[xi], 4 + xi)
            d = self.left(y * 2 + xi)
            self.add(d, d, self.ray.at[xi])
        self.copy(self.left(y * 2 + 1 - x), self.rax, 8, dev(y, 1 - x, c, z)).start()
        if self.split:
            for yi in range(2):
                self.wait(self.rbx.at[yi], 6 + yi)
                d = self.right(yi * 2 + x)
                self.add(d, d, self.rbx.at[yi])
            self.copy(self.right((1 - y) * 2 + x), self.rby, 9, dev(1 - y, x, c, z)).start()

    def third(self):
        y, x, c, z = coords()
        me = y * 2 + x
        self.wait(self.rax, 8)
        self.add(self.left(me), self.left(me), self.rax)
        if self.split:
            self.wait(self.rby, 9)
            self.add(self.right(me), self.right(me), self.rby)
        for k in (2, 1, 3):
            zz = across(z, k)
            self.copy(self.held.at[me, zz], self.rz.at[k - 1], 9 + k, dev(y, x, c, zz)).start()

    def last(self):
        y, x, c, z = coords()
        total = self.held[y * 2 + x, z].astype(F32)
        for k in (1, 2, 3):
            self.wait(self.rz.at[k - 1], 9 + k)
            total = total + self.rz[k - 1].astype(F32)
        self.done(total)

    def sent(self):
        y, x, c, z = coords()
        to = dev(y, 1 - x, c, z)
        refs = [self.rc.at[j] for j in range(4)] + [self.ray.at[0], self.ray.at[1]]
        refs += [self.rbx.at[0], self.rbx.at[1]] if self.split else [None, None]
        refs += [self.rax, self.rby] + [self.rz.at[k] for k in range(3)]
        for slot, ref in enumerate(refs):
            if ref is not None:
                self.copy(ref, ref, slot, to).wait_send()


def scatter_sems(n):
    return [DMA((n, 13)), DMA((n, 13)), DMA((n, 4))]


def scatter_bufs(r, n):
    split = (n // 2) % 128 == 0
    h = n // 2 if split else n
    full, pair, one = pltpu.VMEM((4, 4, r, n), BF), pltpu.VMEM((2, 4, r, h), BF), pltpu.VMEM((4, r, h), BF)
    return [full, full, pair, one] + ([pair, one] if split else []) + [pltpu.VMEM((3, r, n), BF)]


def scatter_refs(refs):
    if len(refs) >= 7 and refs[4].shape == refs[2].shape:
        return refs[:7], refs[7:]
    return (*refs[:4], None, None, refs[4]), refs[5:]


def pipelined(jobs):
    out = []
    for t in range(len(jobs) + 3):
        for lag, name in enumerate(("first", "second", "third", "last")):
            if 0 <= t - lag < len(jobs):
                out.append(getattr(jobs[t - lag], name))
    return out


def plans_of(order, table):
    def call(names):
        acts = [table[name] for name in names]
        def run():
            for act in acts:
                act()
        return run
    quiet = {name for name, lists in order.items() if len(lists) == 1}
    return {name: [call(names) if names or name in quiet else None for names in lists] for name, lists in order.items()}


def at_step(t, steps, start=0, every=1):
    for i, step in enumerate(steps):
        if step is None:
            continue

        @pl.when(t == start + i * every)
        def _(step=step):
            step()


FF = 4 * D
HI = lax.Precision.HIGHEST

def dot(a, b):
    return lax.dot_general(a, b, (((1,), (0,)), ((), ())), preferred_element_type=F32)

def dot_nt(a, b):
    return lax.dot_general(a, b, (((1,), (1,)), ((), ())), preferred_element_type=F32)

def dot_tn(a, b):
    return lax.dot_general(a, b, (((0,), (0,)), ((), ())), preferred_element_type=F32)

def iota(shape, dim):
    return lax.broadcasted_iota(jnp.int32, shape, dim)

def over(index, n):
    return jnp.floor((index.astype(F32) + 0.5) * (1.0 / n)).astype(jnp.int32)

def expand_vectors(blocks):
    lane, col = iota((128, D), 0), iota((128, D), 1)
    pick = (lane == col - over(col, 24) * 24).astype(F32).astype(BF)
    spread = dot(blocks.reshape(256, 128), pick)
    row, col = iota((256, D), 0), iota((256, D), 1)
    spread = jnp.where(over(row, 8) == over(col, 24), spread, 0.0)
    vec = jnp.sum(spread.reshape(32, 8, D), 0)
    lane, col = iota((128, FF), 0), iota((128, FF), 1)
    pick = (lane - 32 == col - over(col, 96) * 96).astype(F32).astype(BF)
    spread = dot(blocks.reshape(256, 128), pick)
    row, col = iota((256, FF), 0), iota((256, FF), 1)
    inner = jnp.sum(jnp.where(row == over(col, 96) * 8, spread, 0.0), 0, keepdims=True)
    return vec, inner

def norm_stats(r):
    mean = jnp.mean(r, -1, keepdims=True)
    cen = r - mean
    var = jnp.mean(cen * cen, -1, keepdims=True)
    inv = lax.rsqrt(var + EPS)
    return cen * inv, inv


HBM = pl.BlockSpec(memory_space=pltpu.HBM)
VM = pl.BlockSpec(memory_space=pltpu.VMEM)
ACT = ((4, LEN, D), BF)


def sds(shape, dtype):
    return jax.ShapeDtypeStruct(shape, dtype)


FORWARD_ORDER = {
    "start": (
        ("g1 own_xy", "sm own_xy", "sm own_z", "wo own_xy", "g0 own_xy", "g0 own_z", "sm z1", "g2 own_z", "sm z3", "g2 own_xy", "sm z2", "g0 z1", "sm xy3", "g1 own_z", "g0 z3", "sm xy0", "sm xy1", "g2 xy0", "g1 xy0", "g0 z2", "g0 xy1", "sm dg1", "wo own_z", "g0 xy3", "g2 z1", "sm xy2", "wi own_z", "g0 xy0", "g2 z3", "wu own_z", "g0 xy2", "g2 xy1", "g1 z1", "sm dg2", "g0 dg1", "g1 z3", "g0 dg2", "sm take", "wo xy0", "g2 dg1", "wi own_xy", "g0 take", "g1 z2",),
    ),
    "spread": (
        ("g2 xy3",),
    ),
    "load0": (
        ("g1 xy3", "g1 xy1",),
    ),
    "group0": (
        ("wo z3",),
        (),
        ("g2 z2",),
        ("g1 xy2", "wo z1", "wo z2", "wi z1", "wi xy0",),
        ("g1 dg1", "wo xy3", "g1 dg2",),
        ("wo xy1",),
        ("g1 take",),
        (),
    ),
    "load1": (
        ("wo xy2", "wi xy1",),
    ),
    "group1": (
        (),
        (),
        ("wi z3",),
        ("g2 xy2", "wi z2",),
        ("wi dg1",),
        ("wo dg1", "wi xy3", "g2 dg2",),
        (),
        ("g2 take",),
    ),
    "load2": (
        ("wu own_xy", "wu z3", "wi xy2", "wo dg2",),
    ),
    "group2": (
        (),
        ("wu z1",),
        (),
        (),
        (),
        (),
        ("wo take",),
        ("wi dg2",),
    ),
    "load_wo": (
        (),
    ),
    "out": (
        (),
        ("wu xy0", "wu z2", "wi take",),
        (),
        (),
    ),
    "load_wi": (
        (),
    ),
    "inner": (
        (),
        ("wu xy1", "wu xy3",),
        ("wu xy2",),
        ("wu dg1",),
        ("wu dg2",),
        (),
        ("wu take",),
        (),
    ),
    "load_wu": (
        (),
    ),
    "outer": (
        (),
    ),
    "end": (
        (),
    ),
}
BACKWARD_ORDER = {
    "norm": (
        ("3 cores", "1 cores",),
        ("2 cores",),
        (),
        (),
    ),
    "out": (
        (),
    ),
    "heads_in": (
        ("4 cores", "0 cores", "1 first", "2 first",),
        (),
    ),
    "pairs0": (
        (),
        ("3 first",),
        (),
        (),
        (),
        (),
        ("0 first",),
        (),
    ),
    "sum0": (
        (),
    ),
    "pairs1": (
        ("1 second", "3 second",),
        (),
        ("5 cores",),
        ("2 second",),
        (),
        ("4 first", "5 first", "3 third",),
        (),
        (),
    ),
    "sum1": (
        ("0 second",),
    ),
    "pairs2": (
        ("6 cores", "1 third",),
        (),
        ("4 second",),
        (),
        ("6 first",),
        (),
        ("0 third",),
        ("4 third",),
    ),
    "sum2": (
        (),
    ),
    "small": (
        ("7 cores", "6 second", "2 third", "5 second",),
    ),
    "input": (
        ("7 first", "8 cores", "4 last", "5 third", "6 third", "8 first", "2 last",),
        ("7 second", "1 last",),
        ("8 second", "7 third", "5 last",),
        ("6 last", "3 last", "8 third",),
    ),
    "end": (
        ("0 last", "7 last", "8 last",),
    ),
}


def stacked(pair, low):
    zero = jnp.zeros_like(pair)
    return jnp.concatenate([jnp.where(low, pair, zero), jnp.where(low, zero, pair)], 0)


def attn_fwd_pair(s, hp, q_ref, k_ref, v_ref, p_ref, slot, o_ref, keys_ok):
    cols = pl.ds(pl.multiple_of(hp * 128, 128), 128)
    low = iota((LEN, 128), 1) < HD
    st = dot_nt(stacked(k_ref[s, :, cols], low), (q_ref[s, :, cols] * 0.125).astype(BF))
    probs = []
    for h in range(2):
        sh = jnp.where(keys_ok, st[h * LEN : (h + 1) * LEN], NEG)
        e = jnp.exp(sh - jnp.max(sh, 0, keepdims=True))
        p = (e * (1.0 / jnp.sum(e, 0, keepdims=True))).astype(BF)
        p_ref[slot, h] = p
        probs.append(p)
    o_ref[s, :, cols] = dot_tn(jnp.concatenate(probs, 0), stacked(v_ref[s, :, cols], low)).astype(BF)


def gelu_pair(z):
    cdf = 0.5 + 0.5 * lax.erf(z * 0.7071067811865476)
    return z * cdf, cdf + z * (jnp.exp(-0.5 * z * z) * 0.3989422804014327)


def forward_body(x_ref, m_ref, pos_ref, sh_small, sh_q, sh_k, sh_v, sh_wo, sh_wi, sh_wu,
                 small, w0, w1, w2, wo, wi, wu, q, k, v, p, o, n1, xh1, inv1, g, dg, lo, xh2, inv2, vec_ref, ib_ref, picked_ref,
                 own_qkv, small_v, w_v, wo_v, wi_v, wu_v, q_v, k_v, v_v, p_v, o_v, n1_v, xh1_v, inv1_v, g_v, dg_v, lo_v, xh2_v, inv2_v,
                 gss, grs, gls, asem, wsem, psem, osem):
    parts = []
    for grp in range(3):
        for i, ref in enumerate((sh_q, sh_k, sh_v)):
            cp = pltpu.make_async_copy(ref.at[:, pl.ds(256 * grp, 256)], own_qkv.at[grp, :, pl.ds(256 * i, 256)], asem.at[3 * grp + i])
            cp.start()
            parts.append(cp)
    sems = (gss, grs, gls)
    pairs = ((sh_small, small), (own_qkv.at[0], w0), (own_qkv.at[1], w1), (own_qkv.at[2], w2), (sh_wo, wo), (sh_wi, wi), (sh_wu, wu))
    gs = [Gather(src, dst, sems, a) for a, (src, dst) in enumerate(pairs)]
    g_wi, g_wu = gs[5:]
    names = ("z1", "z3", "z2", "xy0", "xy1", "xy3", "xy2", "dg1", "dg2")
    def load(i):
        dst = (small_v, w_v.at[0], w_v.at[1], w_v.at[2], wo_v, wi_v, wu_v)[i]
        return pltpu.make_async_copy(pairs[i][1], dst, wsem.at[i])
    table = {}
    for i, (label, x) in enumerate(zip(("sm", "g0", "g1", "g2", "wo", "wi", "wu"), gs)):
        def take(i=i):
            gs[i].arrived()
            load(i).start()
        acts = dict(zip(names, x.steps()), own_xy=x.own_xy, own_z=x.own_z, take=take)
        table.update({label + " " + name: act for name, act in acts.items()})
    plan = plans_of(FORWARD_ORDER, table)
    greet()
    for cp in parts:
        cp.wait()
    plan["start"][0]()
    load(0).wait()
    plan["spread"][0]()
    vec, inner = expand_vectors(small_v[...].reshape(32, 32, 128)[:, 24:, :])
    vec_ref[...] = vec
    ib_ref[...] = inner
    outs = [(q_v, q), (k_v, k), (v_v, v), (o_v, o), (n1_v, n1), (xh1_v, xh1), (inv1_v, inv1), (g_v, g), (dg_v, dg), (lo_v, lo), (xh2_v, xh2), (inv2_v, inv2)]
    def put(a, s):
        return pltpu.make_async_copy(outs[a][0].at[s], outs[a][1].at[s], osem.at[a, s])
    def put_p(t):
        s, hp = lax.rem(t, 8) // 2, (t // 8) * 2 + lax.rem(t, 2)
        return pltpu.make_async_copy(p_v.at[lax.rem(t, 4)], p.at[s, pl.ds(hp * 2, 2)], psem.at[lax.rem(t, 4)])
    for grp in range(3):
        plan[f"load{grp}"][0]()
        load(1 + grp).wait()
        @pl.loop(0, 4)
        def _(s, grp=grp):
            at_step(s, plan[f"group{grp}"][0::2])
            t = dot(x_ref[s], w_v[grp])
            cols = slice(256 * grp, 256 * grp + 256)
            for j, ref in enumerate((q_v, k_v, v_v)):
                part = t[:, 256 * j : 256 * j + 256]
                if j != 1:
                    part = part + vec_ref[0 if j == 0 else 1][None, cols]
                ref[s, :, cols] = part.astype(BF)
            count = jnp.sum(m_ref[pl.ds(s, 1), :], -1, keepdims=True)
            keys_ok = iota((LEN, 1), 0) < count
            @pl.loop(0, 2)
            def _(i):
                t = grp * 8 + s * 2 + i
                @pl.when(i == 1)
                def _():
                    at_step(s, plan[f"group{grp}"][1::2])
                @pl.when(t >= 4)
                def _():
                    put_p(t - 4).wait()
                attn_fwd_pair(s, grp * 2 + i, q_v, k_v, v_v, p_v, lax.rem(t, 4), o_v, keys_ok)
                put_p(t).start()
            if grp == 2:
                for a in range(4):
                    put(a, s).start()
    plan["load_wo"][0]()
    load(4).wait()
    @pl.loop(0, 4)
    def _(s):
        r1 = x_ref[s].astype(F32) + dot(o_v[s], wo_v[...]) + vec_ref[2][None]
        xh, inv = norm_stats(r1)
        xh1_v[s] = xh.astype(BF)
        inv1_v[s] = jnp.broadcast_to(inv, (LEN, 128))
        n1_v[s] = (xh * vec_ref[3][None] + vec_ref[4][None]).astype(BF)
        at_step(s, plan["out"])
        for a in (4, 5, 6):
            put(a, s).start()
    plan["load_wi"][0]()
    load(5).wait()
    @pl.loop(0, 4)
    def _(s):
        @pl.loop(0, 2)
        def _(j):
            at_step(s * 2 + j, plan["inner"])
            cols = pl.ds(pl.multiple_of(j * 2 * D, 2 * D), 2 * D)
            act, slope = gelu_pair(dot(n1_v[s], wi_v[:, cols]) + ib_ref[:, cols])
            g_v[s, :, cols] = act.astype(BF)
            dg_v[s, :, cols] = slope.astype(BF)
        put(7, s).start()
        put(8, s).start()
    plan["load_wu"][0]()
    load(6).wait()
    plan["outer"][0]()
    @pl.loop(0, 4)
    def _(s):
        r2 = n1_v[s].astype(F32) + dot(g_v[s], wu_v[...]) + vec_ref[5][None]
        xh, inv = norm_stats(r2)
        xh2_v[s] = xh.astype(BF)
        inv2_v[s] = jnp.broadcast_to(inv, (LEN, 128))
        out = (xh * vec_ref[6][None] + vec_ref[7][None]).astype(BF)
        lo_v[s] = out
        picked_ref[s] = dot((iota((8, LEN), 1) == pos_ref[s]).astype(F32).astype(BF), out).astype(BF)
        for a in (9, 10, 11):
            put(a, s).start()
    for t in range(20, 24):
        put_p(t).wait()
    for s in range(4):
        for a in range(12):
            put(a, s).wait()
    for x in gs:
        x.sent()


def forward(x, mask, pos, shards, cid):
    small, q, k, v, wo, wi, wu = shards
    full = [((32 * s.shape[0], n), BF) for s, n in ((small, 128), (q, D), (q, D), (q, D), (wo, D), (wi, FF), (wu, D))]
    probs, stat, big = ((4, H, LEN, LEN), BF), ((4, LEN, 128), F32), ((4, LEN, FF), BF)
    acts = [ACT, ACT, ACT, probs, ACT, ACT, ACT, stat, big, big, ACT, ACT, stat]
    outs = full + acts + [((8, D), F32), ((1, FF), F32), ((4, 8, D), BF)]
    slots = [((4, 2, LEN, LEN), BF) if a is probs else a for a in acts]
    return pl.pallas_call(
        forward_body, name="layer_forward", out_shape=[sds(*o) for o in outs],
        in_specs=[VM] * 3 + [HBM] * 7, out_specs=[HBM] * 20 + [VM] * 3,
        scratch_shapes=[pltpu.VMEM(*o) for o in [((3, 24, D), BF), full[0], ((3, D, D), BF)] + full[4:] + slots]
        + gather_sems(7) + [DMA((9,)), DMA((7,)), DMA((4,)), DMA((12, 4))],
        compiler_params=pltpu.CompilerParams(collective_id=cid, has_side_effects=True, vmem_limit_bytes=61 << 20),
    )(x, mask, pos, *shards)


def norm_back(dy, xh, inv, gain):
    c = dy * gain
    return (c - jnp.mean(c, -1, keepdims=True) - xh * jnp.mean(c * xh, -1, keepdims=True)) * inv


def bwd1_body(og_ref, add_ref, pos_ref, xh2_ref, inv2_ref, vec_ref, g, dg, n1, wi, wu,
              gu_ref, gi, dn1, sums_ref, sumi_ref,
              g_v, dg_v, n1_v, wi_v, wu_v, d2_v, dn1_v, gu_v, gi_v, sss, srs, sls, isem, osem, *bufs):
    ins = [(g, g_v), (wu, wu_v), (dg, dg_v), (wi, wi_v), (n1, n1_v)]
    loads = [pltpu.make_async_copy(a, b, isem.at[i]) for i, (a, b) in enumerate(ins)]
    loads[0].start()
    sems = (sss, srs, sls)
    greet()
    jobs = []
    for t in range(3):
        own, bufs = scatter_refs(bufs)
        def source(j, c, t=t):
            return gu_v.at[j, c, :, :, pl.ds(256 * t, 256)]
        def done(total, t=t):
            gu_ref[:, pl.ds(256 * t, 256)] = total
        jobs.append(Scatter(source, own, sems, t, done))
    sums_ref[...] = jnp.zeros_like(sums_ref)
    sumi_ref[...] = jnp.zeros_like(sumi_ref)
    @pl.loop(0, 4)
    def _(s):
        hit = (iota((LEN, 8), 0) == pos_ref[s]).astype(F32)
        extra = lax.dot_general(hit, add_ref[s], (((1,), (0,)), ((), ())), preferred_element_type=F32, precision=HI)
        dy = og_ref[s].astype(F32) + extra
        xh = xh2_ref[s].astype(F32)
        dr2 = norm_back(dy, xh, inv2_ref[s][:, 0:1], vec_ref[6][None])
        sums_ref[0] += jnp.sum(dy * xh, 0)
        sums_ref[1] += jnp.sum(dy, 0)
        sums_ref[2] += jnp.sum(dr2, 0)
        d2_v[pl.ds(s * LEN, LEN)] = dr2.astype(BF)
        dn1_v[s] = dr2
    loads[0].wait()
    loads[1].start()
    loads[2].start()
    steps = pipelined(jobs)
    for t, job in enumerate(jobs):
        @pl.loop(0, 4)
        def _(j, t=t):
            cols = pl.ds(pl.multiple_of(j * D, D), D)
            part = dot_tn(g_v[:, :, cols].reshape(4 * LEN, D), d2_v[:, pl.ds(256 * t, 256)])
            gu_v[j, :, :, :, pl.ds(256 * t, 256)] = part.astype(BF).reshape(2, 4, 96, 256)
        job.cores()
        if t == 1:
            steps[0]()
    loads[3].start()
    loads[1].wait()
    loads[2].wait()
    steps = steps[1:] + [None]
    def put(s):
        return pltpu.make_async_copy(dn1_v.at[s], dn1.at[s], osem.at[s])
    loads[3].wait()
    loads[4].start()
    @pl.loop(0, 4)
    def _(s):
        for half in range(2):
            at_step(s, steps[half:9:3] if half else steps[0:9:3])
            cols = pl.ds(half * 2 * D, 2 * D)
            dz = dot_nt(d2_v[pl.ds(pl.multiple_of(s * LEN, LEN), LEN)], wu_v[cols, :]) * dg_v[s, :, cols].astype(F32)
            dz = dz.astype(BF)
            sumi_ref[0:1, cols] += jnp.sum(dz.astype(F32), 0, keepdims=True)
            dg_v[s, :, cols] = dz
        at_step(s, steps[2:9:3])
        dn1_v[s] += dot_nt(dg_v[s], wi_v[...])
        put(s).start()
    loads[4].wait()
    def puti(j):
        cols = pl.ds(pl.multiple_of(j * D, D), D)
        return pltpu.make_async_copy(gi_v.at[:, cols], gi.at[:, cols], osem.at[4 + j])
    @pl.loop(0, 4)
    def _(j):
        cols = pl.ds(pl.multiple_of(j * D, D), D)
        gi_v[:, cols] = dot_tn(n1_v[...].reshape(4 * LEN, D), dg_v[:, :, cols].reshape(4 * LEN, D)).astype(BF)
        puti(j).start()
        at_step(j, steps[9:])
    for i in range(4):
        put(i).wait()
        puti(i).wait()
    for job in jobs:
        job.sent()


def bwd1(og, add, pos, xh2, inv2, vec, g, dg, n1, wi, wu, cid):
    outs = [((96, D), F32), ((D, FF), BF), ((4, LEN, D), F32), ((8, D), F32), ((8, FF), F32)]
    big = ((4, LEN, FF), BF)
    scratch = [big, big, ACT, ((D, FF), BF), ((FF, D), BF), ((4 * LEN, D), BF), ((4, LEN, D), F32), ((4, 2, 4, 96, D), BF), ((D, FF), BF)]
    return pl.pallas_call(
        bwd1_body, name="feed_forward_backward", out_shape=[sds(*o) for o in outs],
        in_specs=[VM] * 6 + [HBM] * 5, out_specs=[VM, HBM, HBM, VM, VM],
        scratch_shapes=[pltpu.VMEM(*s) for s in scratch] + scatter_sems(3) + [DMA((5,)), DMA((8,))] + scatter_bufs(96, 256) * 3,
        compiler_params=pltpu.CompilerParams(collective_id=cid, has_side_effects=True, vmem_limit_bytes=61 << 20),
    )(og, add, pos, xh2, inv2, vec, g, dg, n1, wi, wu)


def attn_bwd_pair(s, hp, q_ref, k_ref, v_ref, p_ref, slot, do_ref, dqkv_ref):
    cols = pl.ds(pl.multiple_of(hp * 128, 128), 128)
    rows = pl.ds(pl.multiple_of(s * LEN, LEN), LEN)
    do2 = do_ref[rows, cols]
    low = iota((LEN, 128), 1) < HD
    dpt = dot_nt(stacked(v_ref[s, :, cols], low), do2)
    grads = []
    for h in range(2):
        d = dpt[h * LEN : (h + 1) * LEN]
        pf = p_ref[slot, h].astype(F32)
        grads.append((pf * (d - jnp.sum(pf * d, 0, keepdims=True))).astype(BF))
    ds = jnp.concatenate(grads, 0)
    dv = dot(p_ref[slot].reshape(2 * LEN, LEN), do2)
    dk = dot(ds, q_ref[s, :, cols])
    dq = dot_tn(ds, stacked(k_ref[s, :, cols], low))
    at = (hp // 2) * D + lax.rem(hp, 2) * 128
    def out(i):
        return pl.ds(pl.multiple_of(at + 256 * i, 128), 128)
    dqkv_ref[rows, out(0)] = (dq * 0.125).astype(BF)
    dqkv_ref[rows, out(1)] = (jnp.where(low, dk[:LEN], dk[LEN:]) * 0.125).astype(BF)
    dqkv_ref[rows, out(2)] = jnp.where(low, dv[:LEN], dv[LEN:]).astype(BF)


def bwd2_body(dn1, xh1, inv1, vec_ref, x, q, k, v, p, o, w0, w1, w2, wo, gi, grw_ref, s2_ref, si_ref,
              ggq, ggk, ggv, ggo, ggi, ggs, dx,
              dn1_v, xh1_v, inv1_v, x_v, q_v, k_v, v_v, o_v, p_v, wqkv_v, wo_v, sums_v, sumq_v, d1_v, do_v, dqkv_v, go_v, gg_v, gsm_v,
              sss, srs, sls, esem, isem, psem, osem, *bufs):
    def early(s):
        return [pltpu.make_async_copy(a.at[s], b.at[s], esem.at[i, s]) for i, (a, b) in enumerate(((dn1, dn1_v), (xh1, xh1_v), (inv1, inv1_v)))]
    ins = [(o, o_v), (wo, wo_v), (q, q_v), (k, k_v), (v, v_v), (x, x_v)] + [(w, wqkv_v.at[:, pl.ds(D * i, D)]) for i, w in enumerate((w0, w1, w2))]
    loads = [pltpu.make_async_copy(a, b, isem.at[i]) for i, (a, b) in enumerate(ins)]
    for s in range(4):
        for cp in early(s):
            cp.start()
    sems = (sss, srs, sls)
    greet()
    jobs = []
    def add_job(source, done, in_hbm=False):
        nonlocal bufs
        own, bufs = scatter_refs(bufs)
        jobs.append(Scatter(source, own, sems, len(jobs), done, in_hbm))
    for t in range(4):
        def done(total, t=t):
            ggi[:, pl.ds(t * D, D)] = total
        add_job(lambda j, c, t=t: gi.at[j, c, :, :, pl.ds(t * D, D)], done, True)
    def done_o(total):
        ggo[...] = total
    add_job(lambda j, c: go_v.at[j, c], done_o)
    for t in range(3):
        def done(total, t=t):
            for i, ref in enumerate((ggq, ggk, ggv)):
                ref[:, pl.ds(256 * t, 256)] = total[:, 256 * i : 256 * i + 256]
        add_job(lambda j, c, t=t: gg_v.at[t, j, c], done)
    def done_s(total):
        ggs[...] = total
    add_job(lambda j, c: gsm_v.at[j, c], done_s)
    plan = plans_of(BACKWARD_ORDER, {f"{i} {name}": getattr(job, name) for i, job in enumerate(jobs) for name in ("cores", "first", "second", "third", "last")})
    sums_v[...] = jnp.zeros_like(sums_v)
    sumq_v[...] = jnp.zeros_like(sumq_v)
    @pl.loop(0, 4)
    def _(s):
        for cp in early(s):
            cp.wait()
        at_step(s, plan["norm"])
        dy = dn1_v[s]
        xh = xh1_v[s].astype(F32)
        dr1 = norm_back(dy, xh, inv1_v[s][:, 0:1], vec_ref[3][None])
        sums_v[0] += jnp.sum(dy * xh, 0)
        sums_v[1] += jnp.sum(dy, 0)
        sums_v[2] += jnp.sum(dr1, 0)
        dn1_v[s] = dr1
        d1_v[pl.ds(s * LEN, LEN)] = dr1.astype(BF)
        @pl.when(s == 1)
        def _():
            for cp in loads[:2]:
                cp.start()
        @pl.when(s == 3)
        def _():
            for cp in loads[2:5]:
                cp.start()
    plan["out"][0]()
    for cp in loads[:2]:
        cp.wait()
    go_v[...] = dot_tn(o_v[...].reshape(4 * LEN, D), d1_v[...]).astype(BF).reshape(4, 2, 4, 24, D)
    @pl.loop(0, 2)
    def _(i):
        at_step(i, plan["heads_in"])
        rows = pl.ds(pl.multiple_of(i * 2 * LEN, 2 * LEN), 2 * LEN)
        do_v[rows] = dot_nt(d1_v[rows], wo_v[...]).astype(BF)
    for cp in loads[2:5]:
        cp.wait()
    loads[5].start()
    def probs(t):
        hp, s = t // 4, lax.rem(t, 4)
        return pltpu.make_async_copy(p.at[s, pl.ds(hp * 2, 2)], p_v.at[lax.rem(t, 2)], psem.at[lax.rem(t, 2)])
    probs(0).start()
    for grp in range(3):
        @pl.loop(0, 8)
        def _(i, grp=grp):
            t = grp * 8 + i
            @pl.when(t + 1 < 24)
            def _():
                probs(t + 1).start()
            at_step(i, plan[f"pairs{grp}"])
            probs(t).wait()
            attn_bwd_pair(lax.rem(t, 4), t // 4, q_v, k_v, v_v, p_v, lax.rem(t, 2), do_v, dqkv_v)
        if grp == 0:
            loads[5].wait()
            for cp in loads[6:]:
                cp.start()
        plan[f"sum{grp}"][0]()
        d = dqkv_v[:, pl.ds(D * grp, D)]
        sumq_v[grp : grp + 1] = jnp.sum(d.astype(F32), 0, keepdims=True)
        gg_v[grp] = dot_tn(x_v[...].reshape(4 * LEN, D), d).astype(BF).reshape(4, 2, 4, 24, D)
    plan["small"][0]()
    gsm_v[...] = small_grads(grw_ref[...], sums_v[...], s2_ref[...], sumq_v[...], si_ref[...]).reshape(4, 2, 4, 32, 128)
    for cp in loads[6:]:
        cp.wait()
    def put(s):
        return pltpu.make_async_copy(dn1_v.at[s], dx.at[s], osem.at[s])
    @pl.loop(0, 4)
    def _(s):
        rows = pl.ds(pl.multiple_of(s * LEN, LEN), LEN)
        at_step(s, plan["input"])
        dn1_v[s] += dot_nt(dqkv_v[rows], wqkv_v[...])
        put(s).start()
    plan["end"][0]()
    for s in range(4):
        put(s).wait()
    for job in jobs:
        job.sent()


def small_grads(grw, s1, s2, sq, si):
    by_kind = [jnp.concatenate([sq[grp : grp + 1, 256 * i : 256 * i + 256] for grp in range(3)], 1) for i in (0, 2)]
    vec = jnp.concatenate(by_kind + [s1[2:3], s1[0:1], s1[1:2], s2[2:3], s2[0:1], s2[1:2]], 0)
    row, col = iota((256, D), 0), iota((256, D), 1)
    tiled = jnp.broadcast_to(vec[None], (32, 8, D)).reshape(256, D)
    part = jnp.where(over(row, 8) == over(col, 24), tiled, 0.0).astype(BF)
    lane, col = iota((128, D), 0), iota((128, D), 1)
    pick = (lane == col - over(col, 24) * 24).astype(F32).astype(BF)
    out = dot_nt(part, pick).reshape(32, 8, 128)
    row, col = iota((32, FF), 0), iota((32, FF), 1)
    part = jnp.where(row == over(col, 96), si[0:1], 0.0).astype(BF)
    lane, col = iota((128, FF), 0), iota((128, FF), 1)
    pick = (lane - 32 == col - over(col, 96) * 96).astype(F32).astype(BF)
    inner = dot_nt(part, pick)
    out = out + jnp.where(iota((32, 8, 128), 1) == 0, inner[:, None, :], 0.0)
    return jnp.concatenate([grw.reshape(32, 24, 128), out], 1).astype(BF)


def bwd2(dn1, xh1, inv1, vec, x, q, k, v, p, o, w, wo, gi, grw, s2, si, cid):
    own = ((24, D), F32)
    outs = [own, own, own, own, ((24, FF), F32), ((32, 128), F32), ((4, LEN, D), F32)]
    six = ((4, 2, 4, 24, D), BF)
    scratch = [((4, LEN, D), F32), ACT, ((4, LEN, 128), F32), ACT, ACT, ACT, ACT, ACT, ((2, 2, LEN, LEN), BF), ((D, 3 * D), BF), ((D, D), BF),
               ((8, D), F32), ((8, D), F32), ((4 * LEN, D), BF), ((4 * LEN, D), BF), ((4 * LEN, 3 * D), BF), six, ((3,) + six[0], BF), ((4, 2, 4, 32, 128), BF)]
    return pl.pallas_call(
        bwd2_body, name="attention_backward", out_shape=[sds(*s) for s in outs],
        in_specs=[HBM] * 3 + [VM] + [HBM] * 11 + [VM] * 3, out_specs=[VM] * 6 + [HBM],
        scratch_shapes=[pltpu.VMEM(*s) for s in scratch] + scatter_sems(9) + [DMA((3, 4)), DMA((9,)), DMA((2,)), DMA((4,))]
        + scatter_bufs(24, D) * 8 + scatter_bufs(32, 128),
        compiler_params=pltpu.CompilerParams(collective_id=cid, has_side_effects=True, vmem_limit_bytes=61 << 20),
    )(dn1, xh1, inv1, vec, x, q, k, v, p, o, *w, wo, gi.reshape(4, 2, 4, 24, FF), grw, s2, si)


def finish_body(small_ref, pair_ref, *refs):
    n = (len(refs) - 11) // 2
    grw, pair, inner, *vecs = refs[2 * n :]
    for a, b in zip(refs[:n], refs[n : 2 * n]):
        b[...] = a[...]
    grw[...] = small_ref[0:24]
    pair[...] = pair_ref[0, 0:2]
    inner[...] = small_ref[24, 32:128]
    for i, ref in enumerate(vecs):
        ref[...] = small_ref[24 + i, 0:24]


def finish(small, pair, more):
    tail = [((24, 128), F32), ((2,), F32), ((96,), F32)] + [((24,), F32)] * 8
    outs = pl.pallas_call(
        finish_body, name="results", out_shape=[sds(a.shape, a.dtype) for a in more] + [sds(*t) for t in tail],
        in_specs=[VM] * (2 + len(more)), out_specs=[VM] * (len(more) + 11),
    )(small, pair, *more)
    return outs[: len(more)], outs[len(more) :]


def exact(a, b, dims=((1,), (0,))):
    return lax.dot_general(a, b, (dims, ((), ())), preferred_element_type=F32, precision=HI)

def as_f(cond):
    return cond.astype(F32)

def greet_all():
    me = lax.axis_index("dp") * 4 + lax.axis_index("fsdp")
    bar = pltpu.get_barrier_semaphore()
    @pl.loop(1, 32)
    def _(k):
        t = lax.rem(me + k, 32)
        pl.semaphore_signal(bar, inc=1, device_id=(t // 4, lax.rem(t, 4)), device_id_type=MESH)
    pl.semaphore_wait(bar, 31)

def loss_body(picked_ref, emb, vb, ids, valid, qe, small,
              add_ref, grw_ref, pair_ref, ge, gvb_ref,
              emb_ref, vb_ref, ids_ref, valid_ref, qe_ref, small_ref, ge_ref, isem, own_ref, rows_ref, lt_ref, st_ref, all_ref, dh_ref, dhout_ref, gss, grs, gls, sss, srs, sls, xs, xr, *bufs):
    me = lax.axis_index("dp") * 4 + lax.axis_index("fsdp")
    VS = emb_ref.shape[0]
    loads = [pltpu.make_async_copy(a, b, isem.at[i]) for i, (a, b) in enumerate(
        ((small, small_ref), (qe, qe_ref), (ids, ids_ref), (valid, valid_ref), (vb, vb_ref), (emb, emb_ref)))]
    for cp in loads:
        cp.start()
    greet_all()
    own_ref[...] = picked_ref[:, 0:4, :].astype(F32).reshape(16, D).astype(BF)
    g = Gather(own_ref, rows_ref, (gss, grs, gls), 0)
    g.own()
    for cp in loads:
        cp.wait()
    cls = picked_ref[:, 4:5, :].astype(F32).reshape(4, D)
    cls8 = jnp.concatenate([cls, jnp.zeros((4, D), F32)], 0)
    rw = small_ref[:, 0:24, :].reshape(D, 128)
    row8, lane8 = iota((8, 128), 0), iota((8, 128), 1)
    qpick = as_f(jnp.logical_and(iota((8, 16), 1) == (me // 4) * 2 + iota((8, 16), 0) // 2, iota((8, 16), 0) < 4))
    qe_own = exact(qpick, qe_ref[...])
    score = jnp.sum(dot(cls8.astype(BF), rw) * qe_own, -1, keepdims=True)
    st_ref[12:13] = jnp.sum(jnp.where(row8 == lane8, score, 0.0), 0, keepdims=True)
    r512 = iota((16, 512), 1)
    s_of = r512 >> 2
    q_of = (s_of >> 4) * 2 + ((s_of & 3) >> 1)
    spread = exact(ids_ref[...].astype(F32), as_f(iota((4, 512), 0) == (iota((4, 512), 1) & 3)))
    ids = jnp.sum(jnp.where(iota((16, 512), 0) == q_of, spread, 0.0), 0, keepdims=True)
    local = ids.astype(jnp.int32) - me * VS
    q16, s16 = iota((16, 128), 0), iota((16, 128), 1)
    mine = q16 == (s16 >> 4) * 2 + ((s16 & 3) >> 1)
    s8 = iota((8, 128), 1)
    slot_pick = as_f(iota((8, 128), 0) == ((s8 >> 2) & 3) * 2 + (s8 & 1))
    ok16 = jnp.logical_and(mine, exact(valid_ref[...].astype(F32), slot_pick) > 0.5)
    valid_of = jnp.sum(ok16.astype(F32), 0, keepdims=True)
    for step in g.steps():
        step()
    g.arrived()
    g.sent()
    rows = rows_ref[...]
    bias = jnp.where(iota((16, VS), 0) == 0, vb_ref[...][None].astype(F32), 0.0).astype(BF)
    lt = dot_nt(emb_ref[...], rows) + dot_tn(bias, jnp.ones((16, 512), BF))
    hit = iota((VS, 512), 0) == local
    peak = jnp.max(lt, 0, keepdims=True)
    e = jnp.exp(lt - peak)
    lt_ref[...] = e
    total = jnp.sum(e, 0, keepdims=True)
    target = jnp.sum(jnp.where(hit, lt, 0.0), 0, keepdims=True)
    for a in range(4):
        cols = slice(a * 128, a * 128 + 128)
        st_ref[a:a + 1] = peak[:, cols]
        st_ref[4 + a:5 + a] = total[:, cols]
        st_ref[8 + a:9 + a] = target[:, cols]
    sends = []
    for k in range(1, 32):
        t = lax.rem(me + k, 32)
        cp = rdma(st_ref, all_ref.at[me], xs.at[k], xr.at[k], (t // 4, lax.rem(t, 4)))
        cp.start()
        sends.append(cp)
    all_ref[me] = st_ref[...]
    for k in range(1, 32):
        f = lax.rem(me + 32 - k, 32)
        rdma(st_ref, all_ref.at[f], xs.at[k], xr.at[k], (f // 4, lax.rem(f, 4))).wait_recv()
    peaks = all_ref[:, 0:4, :]
    top = jnp.max(peaks, 0)
    tot = jnp.sum(all_ref[:, 4:8, :] * jnp.exp(peaks - top[None]), 0)
    lse = top + jnp.log(tot)
    logp = jnp.sum(all_ref[:, 8:12, :], 0) - lse
    i0, i1 = iota((128, 128), 0), iota((128, 128), 1)
    logp8 = jnp.concatenate([logp, jnp.zeros((4, 128), F32)], 0)
    spread = exact(logp8, 0.25 * as_f((i0 >> 2) == (i1 & 31)))
    seq_ll = jnp.sum(jnp.where((lane8 >> 5) == row8, spread, 0.0), 0, keepdims=True)
    spread = exact(all_ref[:, 12, :], as_f(i0 == (i1 & 3)))
    retrieval = jnp.sum(jnp.where((iota((32, 128), 1) >> 2) == iota((32, 128), 0), spread, 0.0), 0, keepdims=True)
    joint = retrieval + seq_ll
    def slot_lse(v):
        m = jnp.max(jnp.where(ok16, v, NEG), -1, keepdims=True)
        return m + jnp.log(jnp.sum(jnp.where(ok16, jnp.exp(v - m), 0.0), -1, keepdims=True))
    def to_seq(v):
        return jnp.sum(jnp.where(mine, v, 0.0), 0, keepdims=True)
    joint_lse, prior_lse = slot_lse(joint), slot_lse(retrieval)
    ok = valid_of > 0.5
    post = jnp.where(ok, jnp.exp(joint - to_seq(joint_lse)), 0.0)
    prior = jnp.where(ok, jnp.exp(retrieval - to_seq(prior_lse)), 0.0)
    pair = jnp.sum(jnp.where(q16 == (me // 4) * 2 + s16, joint_lse - prior_lse, 0.0), 0, keepdims=True)
    pair_ref[...] = jnp.broadcast_to(pair, (8, 128))
    d_score = LOSS_WEIGHT * (prior - post)
    scale = exact(jnp.broadcast_to(-LOSS_WEIGHT * post / 4.0, (8, 128)), as_f(iota((128, 512), 0) == (iota((128, 512), 1) >> 2)))[0:1]
    lse_row = jnp.concatenate([lse[a:a + 1] for a in range(4)], 1)
    dl = jnp.where(hit, scale, 0.0) - lt_ref[...] * (scale * jnp.exp(peak - lse_row))
    gvb_ref[...] = jnp.broadcast_to(jnp.sum(dl, -1, keepdims=True), (VS, 128)).T[0]
    db = dl.astype(BF)
    dh_ref[...] = dot_tn(db, emb_ref[...]).astype(BF).reshape(4, 2, 4, 16, D)
    def done(total):
        dhout_ref[...] = total
    sc = Scatter(lambda j, c: dh_ref.at[j, c], scatter_refs(bufs)[0], (sss, srs, sls), 0, done)
    for j in range(4):
        sc.core(j)
    du = jnp.sum(jnp.where(jnp.logical_and(lane8 == me * 4 + row8, row8 < 4), d_score, 0.0), -1, keepdims=True) * qe_own
    grw_ref[...] = exact(cls8, du, ((0,), (0,)))
    dcls = exact(du, rw.astype(F32), ((1,), (1,)))
    add_ref[...] = jnp.zeros_like(add_ref)
    for l in range(4):
        add_ref[l, 4:5] = dcls[l:l + 1]
    sc.first()
    ge_ref[...] = dot(db, rows)
    out = pltpu.make_async_copy(ge_ref, ge, isem.at[6])
    out.start()
    sc.second()
    sc.third()
    sc.last()
    sc.sent()
    for l in range(4):
        add_ref[l, 0:4] = dhout_ref[4 * l:4 * l + 4]
    for cp in sends:
        cp.wait_send()
    out.wait()

def loss_call(picked, emb, vb, ids, valid, qe, small, cid):
    VS = emb.shape[0]
    outs = [((4, 8, D), F32), ((D, 128), F32), ((8, 128), F32), ((VS, D), F32), ((VS,), F32)]
    args = (picked, emb, vb, ids, valid, qe, small)
    return pl.pallas_call(loss_body, name="slot_loss", out_shape=[jax.ShapeDtypeStruct(s, t) for s, t in outs],
        in_specs=[VM] + [HBM] * 6, out_specs=[VM] * 3 + [HBM, VM],
        scratch_shapes=[pltpu.VMEM(a.shape, a.dtype) for a in (emb, vb, ids, valid, qe, small)] + [pltpu.VMEM((VS, D), F32), DMA((7,)), pltpu.VMEM((16, D), BF), pltpu.VMEM((512, D), BF), pltpu.VMEM((VS, 512), F32), pltpu.VMEM((16, 128), F32),
            pltpu.VMEM((32, 16, 128), F32), pltpu.VMEM((4, 2, 4, 16, D), BF), pltpu.VMEM((16, D), F32),
            *gather_sems(1), *scatter_sems(1), DMA((32,)), DMA((32,))] + scatter_bufs(16, D),
        compiler_params=pltpu.CompilerParams(collective_id=cid, has_side_effects=True, vmem_limit_bytes=58 << 20))(*args)


def linked_body(hidden_in, token_mask, out_grad, query_embed, slot_valid, target_ids, target_pos,
                qw, kw, vw, ow, iw, uw, rw, qb, vb, ob, ga, sa, ib, ub, gb, sb, embedding, vocab_bias):
    block = jnp.pad(jnp.stack([qb, vb, ob, ga, sa, ub, gb, sb]), ((0, 0), (0, 104)))
    block = jnp.concatenate([rw, block + jnp.pad(ib[None], ((0, 7), (32, 0)))], 0)
    group = (lax.axis_index("dp") * lax.axis_size("fsdp") + lax.axis_index("fsdp")) // GROUP
    pos = lax.dynamic_slice_in_dim(target_pos, group * 2, 2)
    pos = jnp.concatenate([pos, jnp.zeros((2, 1), jnp.int32), jnp.full((2, 3), -1, jnp.int32)], 1)
    pos = jnp.repeat(pos, 2, 0)
    pos_row, pos_col = pos[:, None, :], pos[:, :, None]
    small, w0, w1, w2, wo, wi, wu, q, k, v, p, o, n1, xh1, inv1, g, dg, out_seq, xh2, inv2, vec, inner, picked = forward(
        hidden_in, token_mask, pos_col, (block, qw, kw, vw, ow, iw, uw), 0)
    add, grw, pair, ge, gvb = loss_call(
        picked, embedding, vocab_bias, target_ids, slot_valid, query_embed, small.reshape(32, 32, 128), 1)
    gu, gi, dn1, s2, si = bwd1(out_grad, add, pos_row, xh2, inv2, vec, g, dg, n1, wi, wu, 2)
    gq, gk, gv, go, gi, gsm, dx = bwd2(dn1, xh1, inv1, vec, hidden_in, q, k, v, p, o, (w0, w1, w2), wo, gi, grw, s2, si, 3)
    (gu, gi, gq, gk, gv, go, gvb), (grw, pair, gib, *vecs) = finish(
        gsm, pair, (gu, gi, gq, gk, gv, go, gvb))
    return (out_seq, pair, dx, gq, gk, gv, go, gi, gu, grw, *vecs[:5], gib, *vecs[5:], ge, gvb)


def solution(mesh):
    placed = (
        P(("dp", "fsdp"), None, None),
        P(("dp", "fsdp"), None),
        P(("dp", "fsdp"), None, None),
        P(),
        P(),
        P(),
        P(),
        P(("dp", "fsdp"), None),
        P(("dp", "fsdp"), None),
        P(("dp", "fsdp"), None),
        P(("dp", "fsdp"), None),
        P(("dp", "fsdp"), None),
        P(("dp", "fsdp"), None),
        P(("dp", "fsdp"), None),
        P(("dp", "fsdp")),
        P(("dp", "fsdp")),
        P(("dp", "fsdp")),
        P(("dp", "fsdp")),
        P(("dp", "fsdp")),
        P(("dp", "fsdp")),
        P(("dp", "fsdp")),
        P(("dp", "fsdp")),
        P(("dp", "fsdp")),
        P(("dp", "fsdp"), None),
        P(("dp", "fsdp")),
    )
    own = mesh.shape["dp"] == 8 and mesh.shape["fsdp"] == 4
    return jax.shard_map(
        linked_body if own else plain_body,
        mesh=mesh,
        in_specs=placed,
        out_specs=(
            P(("dp", "fsdp"), None, None),
            P(("dp", "fsdp")),
            P(("dp", "fsdp"), None, None),
            P(("dp", "fsdp"), None),
            P(("dp", "fsdp"), None),
            P(("dp", "fsdp"), None),
            P(("dp", "fsdp"), None),
            P(("dp", "fsdp"), None),
            P(("dp", "fsdp"), None),
            P(("dp", "fsdp"), None),
            P(("dp", "fsdp")),
            P(("dp", "fsdp")),
            P(("dp", "fsdp")),
            P(("dp", "fsdp")),
            P(("dp", "fsdp")),
            P(("dp", "fsdp")),
            P(("dp", "fsdp")),
            P(("dp", "fsdp")),
            P(("dp", "fsdp")),
            P(("dp", "fsdp"), None),
            P(("dp", "fsdp")),
        ),
        check_vma=False,
    )
```

```python
import functools

import jax
import jax.numpy as jnp
from jax import lax
from jax.experimental import pallas as pl
from jax.experimental.pallas import tpu as pltpu
from jax.sharding import PartitionSpec as P

AXES = ("dp", "fsdp")


D = 768
H = 12
HD = 64
LEN = 288
MASKS = 4
SLOT_DEV = 2
GROUP = 4


EPS = 1e-12
NEG = -1000000000.0
HIGH = lax.Precision.HIGHEST
LOSS_WEIGHT = 32.0


def combined_all(value, axis, join):
    pieces = jax.tree.map(lambda part: lax.all_gather(part, axis), value)
    head = jax.tree.map(lambda part: part[0], pieces)
    tail = jax.tree.map(lambda part: part[1:], pieces)
    subtotal, _ = lax.scan(lambda subtotal, share: (join(subtotal, share), None), head, tail)
    return subtotal


def partner(value, axis, stride):
    mask = 2**stride
    pairs = [(source, source ^ mask) for source in range(lax.axis_size(axis))]
    return lax.ppermute(value, axis, pairs)


def layer_norm(residual, gain_vec, shift_vec):
    row_mean = jnp.mean(residual, -1, keepdims=True)
    centred = residual - row_mean
    row_var = jnp.mean(centred * centred, -1, keepdims=True)
    return centred * lax.rsqrt(row_var + EPS) * gain_vec + shift_vec


def exact_gelu(pre_act):
    return jax.nn.gelu(pre_act, approximate=False)


def collect(params):
    (
        query_weight,
        key_weight,
        value_weight,
        out_weight,
        inner_weight,
        outer_weight,
        retrieve_weight,
        query_bias,
        value_bias,
        out_bias,
        norm1_gain,
        norm1_bias,
        inner_bias,
        outer_bias,
        norm2_gain,
        norm2_bias,
    ) = params
    return (
        lax.all_gather(query_weight, AXES, axis=0, tiled=True),
        lax.all_gather(key_weight, AXES, axis=0, tiled=True),
        lax.all_gather(value_weight, AXES, axis=0, tiled=True),
        lax.all_gather(out_weight, AXES, axis=0, tiled=True),
        lax.all_gather(inner_weight, AXES, axis=0, tiled=True),
        lax.all_gather(outer_weight, AXES, axis=0, tiled=True),
        lax.all_gather(retrieve_weight, AXES, axis=0, tiled=True),
        lax.all_gather(query_bias, AXES, axis=0, tiled=True),
        lax.all_gather(value_bias, AXES, axis=0, tiled=True),
        lax.all_gather(out_bias, AXES, axis=0, tiled=True),
        lax.all_gather(norm1_gain, AXES, axis=0, tiled=True),
        lax.all_gather(norm1_bias, AXES, axis=0, tiled=True),
        lax.all_gather(inner_bias, AXES, axis=0, tiled=True),
        lax.all_gather(outer_bias, AXES, axis=0, tiled=True),
        lax.all_gather(norm2_gain, AXES, axis=0, tiled=True),
        lax.all_gather(norm2_bias, AXES, axis=0, tiled=True),
    )


def spread(grads):
    (
        grad_qw,
        grad_kw,
        grad_vw,
        grad_ow,
        grad_iw,
        grad_uw,
        grad_rw,
        grad_qb,
        grad_vb,
        grad_ob,
        grad_ga,
        grad_sa,
        grad_ib,
        grad_ub,
        grad_gb,
        grad_sb,
    ) = grads
    return (
        lax.psum_scatter(grad_qw, AXES, scatter_dimension=0, tiled=True),
        lax.psum_scatter(grad_kw, AXES, scatter_dimension=0, tiled=True),
        lax.psum_scatter(grad_vw, AXES, scatter_dimension=0, tiled=True),
        lax.psum_scatter(grad_ow, AXES, scatter_dimension=0, tiled=True),
        lax.psum_scatter(grad_iw, AXES, scatter_dimension=0, tiled=True),
        lax.psum_scatter(grad_uw, AXES, scatter_dimension=0, tiled=True),
        lax.psum_scatter(grad_rw, AXES, scatter_dimension=0, tiled=True),
        lax.psum_scatter(grad_qb, AXES, scatter_dimension=0, tiled=True),
        lax.psum_scatter(grad_vb, AXES, scatter_dimension=0, tiled=True),
        lax.psum_scatter(grad_ob, AXES, scatter_dimension=0, tiled=True),
        lax.psum_scatter(grad_ga, AXES, scatter_dimension=0, tiled=True),
        lax.psum_scatter(grad_sa, AXES, scatter_dimension=0, tiled=True),
        lax.psum_scatter(grad_ib, AXES, scatter_dimension=0, tiled=True),
        lax.psum_scatter(grad_ub, AXES, scatter_dimension=0, tiled=True),
        lax.psum_scatter(grad_gb, AXES, scatter_dimension=0, tiled=True),
        lax.psum_scatter(grad_sb, AXES, scatter_dimension=0, tiled=True),
    )


def attention(query_heads, key_heads, value_heads, keys_ok):
    head_scale = HD ** (-0.5)
    scores = (
        jnp.einsum("sqhe,skhe->shqk", query_heads, key_heads, preferred_element_type=jnp.float32)
        * head_scale
    )
    scores = jnp.where(keys_ok[:, None, None, :] > 0, scores, NEG)
    row_peak = jnp.max(scores, -1, keepdims=True)
    exp_scores = jnp.exp(scores - row_peak)
    totals = jnp.sum(exp_scores, -1, keepdims=True)
    attn_probs = (exp_scores / totals).astype(jnp.bfloat16)
    attended = jnp.einsum(
        "shqk,skhe->sqhe", attn_probs, value_heads, preferred_element_type=jnp.float32
    )
    return (attended, row_peak + jnp.log(totals))


def forward_layer(hidden, keys_ok, gathered):
    (
        query_weight,
        key_weight,
        value_weight,
        out_weight,
        inner_weight,
        outer_weight,
        retrieve_weight,
        query_bias,
        value_bias,
        out_bias,
        norm1_gain,
        norm1_bias,
        inner_bias,
        outer_bias,
        norm2_gain,
        norm2_bias,
    ) = gathered
    seq_count = hidden.shape[0]
    head_shape = (seq_count, LEN, H, HD)
    flat_rows = hidden.reshape(seq_count * LEN, D)
    queries = (
        jnp.dot(flat_rows, query_weight, preferred_element_type=jnp.float32)
        + query_bias.astype(jnp.float32)
    ).astype(jnp.bfloat16)
    key_rows = jnp.dot(flat_rows, key_weight, preferred_element_type=jnp.float32).astype(
        jnp.bfloat16
    )
    values = (
        jnp.dot(flat_rows, value_weight, preferred_element_type=jnp.float32)
        + value_bias.astype(jnp.float32)
    ).astype(jnp.bfloat16)
    attended, log_totals = attention(
        queries.reshape(head_shape),
        key_rows.reshape(head_shape),
        values.reshape(head_shape),
        keys_ok,
    )
    attended = attended.reshape(seq_count * LEN, D).astype(jnp.bfloat16)
    first_in = (
        flat_rows.astype(jnp.float32)
        + jnp.dot(attended, out_weight, preferred_element_type=jnp.float32)
        + out_bias.astype(jnp.float32)
    )
    normed_one = layer_norm(
        first_in, norm1_gain.astype(jnp.float32), norm1_bias.astype(jnp.float32)
    ).astype(jnp.bfloat16)
    pre_act = jnp.dot(
        normed_one, inner_weight, preferred_element_type=jnp.float32
    ) + inner_bias.astype(jnp.float32)
    active = exact_gelu(pre_act).astype(jnp.bfloat16)
    second_in = (
        normed_one.astype(jnp.float32)
        + jnp.dot(active, outer_weight, preferred_element_type=jnp.float32)
        + outer_bias.astype(jnp.float32)
    )
    layer_out = layer_norm(
        second_in, norm2_gain.astype(jnp.float32), norm2_bias.astype(jnp.float32)
    ).astype(jnp.bfloat16)
    return (
        queries,
        key_rows,
        values,
        log_totals,
        attended,
        first_in,
        normed_one,
        pre_act,
        active,
        second_in,
        layer_out,
    )


def backward_layer(hidden, keys_ok, gathered, kept_acts, grad_out):
    (
        query_weight,
        key_weight,
        value_weight,
        out_weight,
        inner_weight,
        outer_weight,
        retrieve_weight,
        query_bias,
        value_bias,
        out_bias,
        norm1_gain,
        norm1_bias,
        inner_bias,
        outer_bias,
        norm2_gain,
        norm2_bias,
    ) = gathered
    (
        queries,
        key_rows,
        values,
        log_totals,
        attended,
        first_in,
        normed_one,
        pre_act,
        active,
        second_in,
        layer_out,
    ) = kept_acts
    seq_count = hidden.shape[0]
    head_shape = (seq_count, LEN, H, HD)
    flat_rows = hidden.reshape(seq_count * LEN, D)
    unused_two, norm_two_back = jax.vjp(
        layer_norm, second_in, norm2_gain.astype(jnp.float32), norm2_bias.astype(jnp.float32)
    )
    grad_second, grad_norm2_gain, grad_norm2_bias = norm_two_back(grad_out)
    second_low = grad_second.astype(jnp.bfloat16)
    grad_outer_weight = jnp.dot(active.T, second_low, preferred_element_type=jnp.float32)
    grad_outer_bias = jnp.sum(grad_second, 0)
    grad_active = jnp.dot(second_low, outer_weight.T, preferred_element_type=jnp.float32)
    unused_act, gelu_back = jax.vjp(exact_gelu, pre_act)
    grad_pre = gelu_back(grad_active)[0].astype(jnp.bfloat16)
    grad_inner_weight = jnp.dot(normed_one.T, grad_pre, preferred_element_type=jnp.float32)
    grad_inner_bias = jnp.sum(grad_pre.astype(jnp.float32), 0)
    grad_normed = grad_second + jnp.dot(
        grad_pre, inner_weight.T, preferred_element_type=jnp.float32
    )
    unused_one, norm_one_back = jax.vjp(
        layer_norm, first_in, norm1_gain.astype(jnp.float32), norm1_bias.astype(jnp.float32)
    )
    grad_first, grad_norm1_gain, grad_norm1_bias = norm_one_back(grad_normed)
    first_low = grad_first.astype(jnp.bfloat16)
    grad_out_weight = jnp.dot(attended.T, first_low, preferred_element_type=jnp.float32)
    grad_out_bias = jnp.sum(grad_first, 0)
    grad_attended = (
        jnp.dot(first_low, out_weight.T, preferred_element_type=jnp.float32)
        .astype(jnp.bfloat16)
        .reshape(head_shape)
    )
    query_heads = queries.reshape(head_shape)
    key_heads = key_rows.reshape(head_shape)
    value_heads = values.reshape(head_shape)
    head_scale = HD ** (-0.5)
    scores = (
        jnp.einsum("sqhe,skhe->shqk", query_heads, key_heads, preferred_element_type=jnp.float32)
        * head_scale
    )
    scores = jnp.where(keys_ok[:, None, None, :] > 0, scores, NEG)
    attn_probs = jnp.exp(scores - log_totals)
    grad_probs = jnp.einsum(
        "sqhe,skhe->shqk", grad_attended, value_heads, preferred_element_type=jnp.float32
    )
    grad_value_heads = jnp.einsum(
        "shqk,sqhe->skhe",
        attn_probs.astype(jnp.bfloat16),
        grad_attended,
        preferred_element_type=jnp.float32,
    )
    grad_scores = (
        attn_probs * (grad_probs - jnp.sum(attn_probs * grad_probs, -1, keepdims=True))
    ).astype(jnp.bfloat16)
    grad_query_heads = (
        jnp.einsum("shqk,skhe->sqhe", grad_scores, key_heads, preferred_element_type=jnp.float32)
        * head_scale
    )
    grad_key_heads = (
        jnp.einsum("shqk,sqhe->skhe", grad_scores, query_heads, preferred_element_type=jnp.float32)
        * head_scale
    )
    grad_queries = grad_query_heads.reshape(seq_count * LEN, D).astype(jnp.bfloat16)
    grad_keys = grad_key_heads.reshape(seq_count * LEN, D).astype(jnp.bfloat16)
    grad_values = grad_value_heads.reshape(seq_count * LEN, D).astype(jnp.bfloat16)
    grad_query_weight = jnp.dot(flat_rows.T, grad_queries, preferred_element_type=jnp.float32)
    grad_key_weight = jnp.dot(flat_rows.T, grad_keys, preferred_element_type=jnp.float32)
    grad_value_weight = jnp.dot(flat_rows.T, grad_values, preferred_element_type=jnp.float32)
    grad_query_bias = jnp.sum(grad_queries.astype(jnp.float32), 0)
    grad_value_bias = jnp.sum(grad_values.astype(jnp.float32), 0)
    grad_hidden = (
        grad_first
        + jnp.dot(grad_queries, query_weight.T, preferred_element_type=jnp.float32)
        + jnp.dot(grad_keys, key_weight.T, preferred_element_type=jnp.float32)
        + jnp.dot(grad_values, value_weight.T, preferred_element_type=jnp.float32)
    )
    return (
        grad_hidden,
        (
            grad_query_weight,
            grad_key_weight,
            grad_value_weight,
            grad_out_weight,
            grad_inner_weight,
            grad_outer_weight,
            grad_query_bias,
            grad_value_bias,
            grad_out_bias,
            grad_norm1_gain,
            grad_norm1_bias,
            grad_inner_bias,
            grad_outer_bias,
            grad_norm2_gain,
            grad_norm2_bias,
        ),
    )


def merge_pair(peak_one, total_one, peak_two, total_two):
    peak_new = jnp.maximum(peak_one, peak_two)
    return (
        peak_new,
        total_one * jnp.exp(peak_one - peak_new) + total_two * jnp.exp(peak_two - peak_new),
    )


def merge_rows(one_side, other_side):
    peak_new, total_new = merge_pair(one_side[0], one_side[1], other_side[0], other_side[1])
    return (peak_new, total_new, one_side[2] + other_side[2])


def slot_partial(score_vec, slot_ok):
    grouped = jnp.where(slot_ok, score_vec, NEG).reshape(-1, SLOT_DEV)
    ok_grouped = slot_ok.reshape(-1, SLOT_DEV)
    group_peak = jnp.max(grouped, -1)
    group_total = jnp.sum(jnp.where(ok_grouped, jnp.exp(grouped - group_peak[:, None]), 0.0), -1)
    return (group_peak, group_total)


def plain_body(
    hidden_in,
    token_mask,
    out_grad,
    query_embed,
    slot_valid,
    target_ids,
    target_pos,
    query_weight,
    key_weight,
    value_weight,
    out_weight,
    inner_weight,
    outer_weight,
    retrieve_weight,
    query_bias,
    value_bias,
    out_bias,
    norm1_gain,
    norm1_bias,
    inner_bias,
    outer_bias,
    norm2_gain,
    norm2_bias,
    embedding,
    vocab_bias,
):
    params = (
        query_weight,
        key_weight,
        value_weight,
        out_weight,
        inner_weight,
        outer_weight,
        retrieve_weight,
        query_bias,
        value_bias,
        out_bias,
        norm1_gain,
        norm1_bias,
        inner_bias,
        outer_bias,
        norm2_gain,
        norm2_bias,
    )
    gathered = collect(params)
    kept_acts = forward_layer(hidden_in, token_mask, gathered)
    seq_count = hidden_in.shape[0]
    query_count = seq_count // SLOT_DEV
    out_seq = kept_acts[10].reshape(seq_count, LEN, D)
    devices = lax.axis_size("dp") * lax.axis_size("fsdp")
    device = lax.axis_index("dp") * lax.axis_size("fsdp") + lax.axis_index("fsdp")
    member = lax.axis_index("fsdp") % GROUP
    local_seq = jnp.arange(seq_count, dtype=jnp.int32)
    local_query = device // GROUP * query_count + local_seq // SLOT_DEV
    local_slot = member * SLOT_DEV + local_seq % SLOT_DEV
    slot_ok = slot_valid[local_query, local_slot] > 0
    embeds = query_embed[local_query]
    positions = target_pos[local_query]
    cls_rows = out_seq[:, 0, :].astype(jnp.float32)
    retrieve_full = gathered[6].astype(jnp.float32)
    projected = jnp.dot(cls_rows, retrieve_full, precision=HIGH)
    retrieval = jnp.sum(projected * embeds, -1)
    own_rows = seq_count * MASKS
    sent_rows = out_seq[local_seq[:, None], positions].reshape(own_rows, D)
    all_rows = lax.all_gather(sent_rows, AXES, axis=0, tiled=True)
    group_count = devices // GROUP
    all_targets = jnp.broadcast_to(
        target_ids.reshape(group_count, 1, query_count, 1, MASKS),
        (group_count, GROUP, query_count, SLOT_DEV, MASKS),
    ).reshape(-1)
    vocab_rows = embedding.shape[0]
    local_ids = all_targets - device * vocab_rows
    target_hit = jnp.arange(vocab_rows, dtype=jnp.int32)[None, :] == local_ids[:, None]
    logits = jnp.einsum(
        "rd,vd->rv", all_rows, embedding, preferred_element_type=jnp.float32
    ) + vocab_bias.astype(jnp.float32)
    row_peak = jnp.max(logits, -1)
    sum_exp = jnp.sum(jnp.exp(logits - row_peak[:, None]), -1)
    target_logit = jnp.sum(jnp.where(target_hit, logits, 0.0), -1)
    peak_all, total_all, target_all = combined_all(
        (row_peak, sum_exp, target_logit), AXES, merge_rows
    )
    lse_rows = peak_all + jnp.log(total_all)
    log_prob = lax.dynamic_slice_in_dim(target_all - lse_rows, device * own_rows, own_rows)
    seq_ll = jnp.mean(log_prob.reshape(seq_count, MASKS), -1)
    joint_score = retrieval + seq_ll
    joint_peak, joint_total = slot_partial(joint_score, slot_ok)
    prior_peak, prior_total = slot_partial(retrieval, slot_ok)
    for bit_number in range(GROUP.bit_length() - 1):
        far_joint_peak, far_joint_total, far_prior_peak, far_prior_total = partner(
            (joint_peak, joint_total, prior_peak, prior_total), "fsdp", bit_number
        )
        joint_peak, joint_total = merge_pair(
            joint_peak, joint_total, far_joint_peak, far_joint_total
        )
        prior_peak, prior_total = merge_pair(
            prior_peak, prior_total, far_prior_peak, far_prior_total
        )
    joint_lse = joint_peak + jnp.log(joint_total)
    prior_lse = prior_peak + jnp.log(prior_total)
    pair_loglik = joint_lse - prior_lse
    post_weight = jnp.where(slot_ok, jnp.exp(joint_score - jnp.repeat(joint_lse, SLOT_DEV)), 0.0)
    prior_weight = jnp.where(slot_ok, jnp.exp(retrieval - jnp.repeat(prior_lse, SLOT_DEV)), 0.0)
    grad_retrieval = LOSS_WEIGHT * (prior_weight - post_weight)
    row_scale = jnp.repeat(-LOSS_WEIGHT * post_weight / MASKS, MASKS)
    all_scales = lax.all_gather(row_scale, AXES, axis=0, tiled=True)
    vocab_probs = jnp.exp(logits - lse_rows[:, None])
    grad_logits = all_scales[:, None] * (target_hit.astype(jnp.float32) - vocab_probs)
    grad_vocab_bias = jnp.sum(grad_logits, 0)
    logits_low = grad_logits.astype(jnp.bfloat16)
    grad_embedding = jnp.einsum(
        "rv,rd->vd", logits_low, all_rows, preferred_element_type=jnp.float32
    )
    grad_picked = lax.psum_scatter(
        jnp.dot(logits_low, embedding, preferred_element_type=jnp.float32),
        AXES,
        scatter_dimension=0,
        tiled=True,
    )
    grad_project = grad_retrieval[:, None] * embeds
    grad_retrieve_weight = jnp.dot(cls_rows.T, grad_project, precision=HIGH)
    grad_cls = jnp.dot(grad_project, retrieve_full.T, precision=HIGH)
    grad_total = out_grad.astype(jnp.float32)
    grad_total = grad_total.at[local_seq[:, None], positions].add(
        grad_picked.reshape(seq_count, MASKS, D)
    )
    grad_total = grad_total.at[:, 0, :].add(grad_cls)
    grad_total = grad_total.reshape(seq_count * LEN, D)
    grad_hidden, layer_grads = backward_layer(
        hidden_in, token_mask, gathered, kept_acts, grad_total
    )
    (
        grad_query_weight,
        grad_key_weight,
        grad_value_weight,
        grad_out_weight,
        grad_inner_weight,
        grad_outer_weight,
        grad_query_bias,
        grad_value_bias,
        grad_out_bias,
        grad_norm1_gain,
        grad_norm1_bias,
        grad_inner_bias,
        grad_outer_bias,
        grad_norm2_gain,
        grad_norm2_bias,
    ) = layer_grads
    (
        shard_query_weight,
        shard_key_weight,
        shard_value_weight,
        shard_out_weight,
        shard_inner_weight,
        shard_outer_weight,
        shard_retrieve_weight,
        shard_query_bias,
        shard_value_bias,
        shard_out_bias,
        shard_norm1_gain,
        shard_norm1_bias,
        shard_inner_bias,
        shard_outer_bias,
        shard_norm2_gain,
        shard_norm2_bias,
    ) = spread(
        (
            grad_query_weight,
            grad_key_weight,
            grad_value_weight,
            grad_out_weight,
            grad_inner_weight,
            grad_outer_weight,
            grad_retrieve_weight,
            grad_query_bias,
            grad_value_bias,
            grad_out_bias,
            grad_norm1_gain,
            grad_norm1_bias,
            grad_inner_bias,
            grad_outer_bias,
            grad_norm2_gain,
            grad_norm2_bias,
        )
    )
    return (
        out_seq,
        pair_loglik,
        grad_hidden.reshape(seq_count, LEN, D),
        shard_query_weight,
        shard_key_weight,
        shard_value_weight,
        shard_out_weight,
        shard_inner_weight,
        shard_outer_weight,
        shard_retrieve_weight,
        shard_query_bias,
        shard_value_bias,
        shard_out_bias,
        shard_norm1_gain,
        shard_norm1_bias,
        shard_inner_bias,
        shard_outer_bias,
        shard_norm2_gain,
        shard_norm2_bias,
        grad_embedding,
        grad_vocab_bias,
    )

MESH = pl.DeviceIdType.MESH
F32 = jnp.float32
BF = jnp.bfloat16
DMA = pltpu.SemaphoreType.DMA


def coords():
    d = lax.axis_index("dp")
    return d // 4, (d // 2) % 2, d % 2, lax.axis_index("fsdp")


def dev(y, x, c, z):
    return ((y * 2 + x) * 2 + c, z)


def across(z, k):
    return (z + 1 - 2 * lax.rem(z, 2), lax.rem(z + 2, 4), 3 - z)[k - 1] if k else z


def rdma(src, dst, ss, rs, to):
    return pltpu.make_async_remote_copy(src, dst, ss, rs, device_id=to, device_id_type=MESH)


def greet():
    y, x, c, z = coords()
    bar = pltpu.get_barrier_semaphore()
    tos = [dev(y, x, c, lax.rem(z + k, 4)) for k in (1, 2, 3)]
    tos += [dev(y, 1 - x, c, z), dev(1 - y, x, c, z), dev(y, x, 1 - c, z)]
    for t in tos:
        pl.semaphore_signal(bar, inc=1, device_id=t, device_id_type=MESH)
    pl.semaphore_wait(bar, len(tos))


def rows_at(start, size):
    return pl.ds(pl.multiple_of(start, 8), size)


class Gather:
    def __init__(self, src, dst, sems, a):
        self.src, self.dst, self.a = src, dst, a
        self.ss, self.rs, self.ls = sems
        self.r, n = src.shape
        self.split = (n // 2) % 128 == 0
        self.h = n // 2

    def chips(self):
        y, x, c, z = coords()
        return y * 2 + x, y * 2 + 1 - x, (1 - y) * 2 + x, (1 - y) * 2 + 1 - x

    def block(self, chip, k):
        y, x, c, z = coords()
        zz = across(z, k)
        return self.dst.at[rows_at(((chip * 2 + c) * 4 + zz) * self.r, self.r)]

    def column(self, chip, c):
        return self.dst.at[rows_at((chip * 2 + c) * 4 * self.r, 4 * self.r)]

    def half(self, ref, right):
        if not self.split:
            return ref
        return ref.at[:, pl.ds(self.h if right else 0, self.h)]

    def copy(self, src, dst, slot, to):
        return rdma(src, dst, self.ss.at[self.a, slot], self.rs.at[self.a, slot], to)

    def send(self, ref, slot, to, src=None):
        self.copy(ref if src is None else src, ref, slot, to).start()

    def wait(self, ref, slot):
        y, x, c, z = coords()
        self.copy(ref, ref, slot, dev(y, 1 - x, c, z)).wait_recv()

    def kept(self):
        return pltpu.make_async_copy(self.src, self.block(self.chips()[0], 0), self.ls.at[self.a])

    def own_xy(self):
        y, x, c, z = coords()
        d = self.block(self.chips()[0], 0)
        self.send(d, 4, dev(y, 1 - x, c, z), self.src)
        self.send(d, 8, dev(1 - y, x, c, z), self.src)

    def own_z(self):
        y, x, c, z = coords()
        d = self.block(self.chips()[0], 0)
        self.kept().start()
        for k in (1, 3, 2):
            self.send(d, k, dev(y, x, c, across(z, k)), self.src)

    def own(self):
        self.own_xy()
        self.own_z()

    def z(self, k):
        y, x, c, z = coords()
        d = self.block(self.chips()[0], k)
        self.wait(d, k)
        self.send(d, 4 + k, dev(y, 1 - x, c, z))
        self.send(d, 8 + k, dev(1 - y, x, c, z))

    def core(self, i):
        y, x, c, z = coords()
        if i == 0:
            self.kept().wait()
        self.send(self.column(self.chips()[i], c), 20 + i, dev(y, x, 1 - c, z))

    def xy(self, k):
        y, x, c, z = coords()
        dx = self.block(self.chips()[1], k)
        self.wait(dx, 4 + k)
        self.send(self.half(dx, False), 12 + k, dev(1 - y, x, c, z))
        dy = self.block(self.chips()[2], k)
        self.wait(dy, 8 + k)
        if self.split:
            self.send(self.half(dy, True), 16 + k, dev(y, 1 - x, c, z))

    def dg(self, k):
        d = self.block(self.chips()[3], k)
        self.wait(self.half(d, False), 12 + k)
        if self.split:
            self.wait(self.half(d, True), 16 + k)

    def arrived(self):
        y, x, c, z = coords()
        for i, chip in enumerate(self.chips()):
            self.wait(self.column(chip, 1 - c), 20 + i)

    def sent(self):
        y, x, c, z = coords()
        to = dev(y, 1 - x, c, z)
        d = self.block(self.chips()[0], 0)
        for k in range(4):
            if k:
                self.copy(d, d, k, to).wait_send()
            self.copy(d, d, 4 + k, to).wait_send()
            self.copy(d, d, 8 + k, to).wait_send()
            half = self.half(d, False)
            self.copy(half, half, 12 + k, to).wait_send()
            if self.split:
                self.copy(half, half, 16 + k, to).wait_send()
            col = self.column(self.chips()[0], 0)
            self.copy(col, col, 20 + k, to).wait_send()

    def steps(self):
        out = [functools.partial(self.z, k) for k in (1, 3, 2)]
        out[2] = lambda: (self.z(2), self.core(0))
        out += [functools.partial(self.xy, k) for k in (0, 1, 3)]
        out += [lambda: (self.xy(2), self.core(1), self.core(2))]
        out += [lambda: (self.dg(0), self.dg(1)), lambda: (self.dg(3), self.dg(2), self.core(3))]
        return out


def gather_sems(n):
    return [DMA((n, 24)), DMA((n, 24)), DMA((n,))]


class Scatter:
    def __init__(self, source, bufs, sems, a, done, in_hbm=False):
        self.source, self.a, self.done, self.in_hbm = source, a, done, in_hbm
        self.ss, self.rs, self.ls = sems
        self.held, self.rc, self.ray, self.rax, self.rbx, self.rby, self.rz = bufs
        self.split = self.rbx is not None
        self.h = self.rax.shape[-1]

    def copy(self, src, dst, slot, to):
        return rdma(src, dst, self.ss.at[self.a, slot], self.rs.at[self.a, slot], to)

    def wait(self, ref, slot):
        y, x, c, z = coords()
        self.copy(ref, ref, slot, dev(y, 1 - x, c, z)).wait_recv()

    def local(self, j):
        y, x, c, z = coords()
        return pltpu.make_async_copy(self.source(j, c), self.held.at[j], self.ls.at[self.a, j])

    def core(self, j):
        y, x, c, z = coords()
        if self.in_hbm:
            self.local(j).start()
        self.copy(self.source(j, 1 - c), self.rc.at[j], j, dev(y, x, 1 - c, z)).start()

    def cores(self):
        for j in range(4):
            self.core(j)

    def add(self, dst, one, two):
        for i in range(4):
            dst[i] = (one[i].astype(F32) + two[i].astype(F32)).astype(BF)

    def left(self, chip):
        return self.held.at[chip, :, :, pl.ds(0, self.h)]

    def right(self, chip):
        return self.held.at[chip, :, :, pl.ds(self.h, self.h)]

    def first(self):
        y, x, c, z = coords()
        @pl.loop(0, 4)
        def _(j):
            if self.in_hbm:
                self.local(j).wait()
            self.wait(self.rc.at[j], j)
            self.add(self.held.at[j], self.held.at[j] if self.in_hbm else self.source(j, c), self.rc.at[j])
        for xi in range(2):
            self.copy(self.left((1 - y) * 2 + xi), self.ray.at[xi], 4 + xi, dev(1 - y, x, c, z)).start()
        if self.split:
            for yi in range(2):
                self.copy(self.right(yi * 2 + 1 - x), self.rbx.at[yi], 6 + yi, dev(y, 1 - x, c, z)).start()

    def second(self):
        y, x, c, z = coords()
        for xi in range(2):
            self.wait(self.ray.at[xi], 4 + xi)
            d = self.left(y * 2 + xi)
            self.add(d, d, self.ray.at[xi])
        self.copy(self.left(y * 2 + 1 - x), self.rax, 8, dev(y, 1 - x, c, z)).start()
        if self.split:
            for yi in range(2):
                self.wait(self.rbx.at[yi], 6 + yi)
                d = self.right(yi * 2 + x)
                self.add(d, d, self.rbx.at[yi])
            self.copy(self.right((1 - y) * 2 + x), self.rby, 9, dev(1 - y, x, c, z)).start()

    def third(self):
        y, x, c, z = coords()
        me = y * 2 + x
        self.wait(self.rax, 8)
        self.add(self.left(me), self.left(me), self.rax)
        if self.split:
            self.wait(self.rby, 9)
            self.add(self.right(me), self.right(me), self.rby)
        for k in (2, 1, 3):
            zz = across(z, k)
            self.copy(self.held.at[me, zz], self.rz.at[k - 1], 9 + k, dev(y, x, c, zz)).start()

    def last(self):
        y, x, c, z = coords()
        total = self.held[y * 2 + x, z].astype(F32)
        for k in (1, 2, 3):
            self.wait(self.rz.at[k - 1], 9 + k)
            total = total + self.rz[k - 1].astype(F32)
        self.done(total)

    def sent(self):
        y, x, c, z = coords()
        to = dev(y, 1 - x, c, z)
        refs = [self.rc.at[j] for j in range(4)] + [self.ray.at[0], self.ray.at[1]]
        refs += [self.rbx.at[0], self.rbx.at[1]] if self.split else [None, None]
        refs += [self.rax, self.rby] + [self.rz.at[k] for k in range(3)]
        for slot, ref in enumerate(refs):
            if ref is not None:
                self.copy(ref, ref, slot, to).wait_send()


def scatter_sems(n):
    return [DMA((n, 13)), DMA((n, 13)), DMA((n, 4))]


def scatter_bufs(r, n):
    split = (n // 2) % 128 == 0
    h = n // 2 if split else n
    full, pair, one = pltpu.VMEM((4, 4, r, n), BF), pltpu.VMEM((2, 4, r, h), BF), pltpu.VMEM((4, r, h), BF)
    return [full, full, pair, one] + ([pair, one] if split else []) + [pltpu.VMEM((3, r, n), BF)]


def scatter_refs(refs):
    if len(refs) >= 7 and refs[4].shape == refs[2].shape:
        return refs[:7], refs[7:]
    return (*refs[:4], None, None, refs[4]), refs[5:]


def pipelined(jobs):
    out = []
    for t in range(len(jobs) + 3):
        for lag, name in enumerate(("first", "second", "third", "last")):
            if 0 <= t - lag < len(jobs):
                out.append(getattr(jobs[t - lag], name))
    return out


def plans_of(order, table):
    def call(names):
        acts = [table[name] for name in names]
        def run():
            for act in acts:
                act()
        return run
    quiet = {name for name, lists in order.items() if len(lists) == 1}
    return {name: [call(names) if names or name in quiet else None for names in lists] for name, lists in order.items()}


def at_step(t, steps, start=0, every=1):
    for i, step in enumerate(steps):
        if step is None:
            continue

        @pl.when(t == start + i * every)
        def _(step=step):
            step()


FF = 4 * D
HI = lax.Precision.HIGHEST

def dot(a, b):
    return lax.dot_general(a, b, (((1,), (0,)), ((), ())), preferred_element_type=F32)

def dot_nt(a, b):
    return lax.dot_general(a, b, (((1,), (1,)), ((), ())), preferred_element_type=F32)

def dot_tn(a, b):
    return lax.dot_general(a, b, (((0,), (0,)), ((), ())), preferred_element_type=F32)

def iota(shape, dim):
    return lax.broadcasted_iota(jnp.int32, shape, dim)

def over(index, n):
    return jnp.floor((index.astype(F32) + 0.5) * (1.0 / n)).astype(jnp.int32)

def expand_vectors(blocks):
    lane, col = iota((128, D), 0), iota((128, D), 1)
    pick = (lane == col - over(col, 24) * 24).astype(F32).astype(BF)
    spread = dot(blocks.reshape(256, 128), pick)
    row, col = iota((256, D), 0), iota((256, D), 1)
    spread = jnp.where(over(row, 8) == over(col, 24), spread, 0.0)
    vec = jnp.sum(spread.reshape(32, 8, D), 0)
    lane, col = iota((128, FF), 0), iota((128, FF), 1)
    pick = (lane - 32 == col - over(col, 96) * 96).astype(F32).astype(BF)
    spread = dot(blocks.reshape(256, 128), pick)
    row, col = iota((256, FF), 0), iota((256, FF), 1)
    inner = jnp.sum(jnp.where(row == over(col, 96) * 8, spread, 0.0), 0, keepdims=True)
    return vec, inner

def norm_stats(r):
    mean = jnp.mean(r, -1, keepdims=True)
    cen = r - mean
    var = jnp.mean(cen * cen, -1, keepdims=True)
    inv = lax.rsqrt(var + EPS)
    return cen * inv, inv


HBM = pl.BlockSpec(memory_space=pltpu.HBM)
VM = pl.BlockSpec(memory_space=pltpu.VMEM)
ACT = ((4, LEN, D), BF)


def sds(shape, dtype):
    return jax.ShapeDtypeStruct(shape, dtype)


FORWARD_ORDER = {
    "start": ((24, 0, 1, 48, 12, 13, 2, 37, 3, 36, 4, 14, 7, 25, 15, 5, 6, 41, 29, 16, 18, 9, 49, 19, 38, 8, 61, 17, 39, 73, 20, 42, 26, 10, 21, 27, 22, 11, 53, 45, 60, 23, 28,),),
    "spread": ((43,),),
    "load0": ((31, 30,),),
    "group0": ((51,), (), (40,), (32, 50, 52, 62, 65,), (33, 55, 34,), (54,), (35,), (),),
    "load1": ((56, 66,),),
    "group1": ((), (), (63,), (44, 64,), (69,), (57, 67, 46,), (), (47,),),
    "load2": ((72, 75, 68, 58,),),
    "group2": ((), (74,), (), (), (), (), (59,), (70,),),
    "load_wo": ((),),
    "out": ((), (77, 76, 71,), (), (),),
    "load_wi": ((),),
    "inner": ((), (78, 79,), (80,), (81,), (82,), (), (83,), (),),
    "load_wu": ((),),
    "outer": ((),),
    "end": ((),),
}
BACKWARD_ORDER = {
    "norm": ((15, 5,), (10,), (), (),),
    "out": ((),),
    "heads_in": ((20, 0, 6, 11,), (),),
    "pairs0": ((), (16,), (), (), (), (), (1,), (),),
    "sum0": ((),),
    "pairs1": ((7, 17,), (), (25,), (12,), (), (21, 26, 18,), (), (),),
    "sum1": ((2,),),
    "pairs2": ((30, 8,), (), (22,), (), (31,), (), (3,), (23,),),
    "sum2": ((),),
    "small": ((35, 32, 13, 27,),),
    "input": ((36, 40, 24, 28, 33, 41, 14,), (37, 9,), (42, 38, 29,), (34, 19, 43,),),
    "end": ((4, 39, 44,),),
}

def stacked(pair, low):
    zero = jnp.zeros_like(pair)
    return jnp.concatenate([jnp.where(low, pair, zero), jnp.where(low, zero, pair)], 0)


def attn_fwd_pair(s, hp, q_ref, k_ref, v_ref, p_ref, slot, o_ref, keys_ok):
    cols = pl.ds(pl.multiple_of(hp * 128, 128), 128)
    low = iota((LEN, 128), 1) < HD
    st = dot_nt(stacked(k_ref[s, :, cols], low), (q_ref[s, :, cols] * 0.125).astype(BF))
    probs = []
    for h in range(2):
        sh = jnp.where(keys_ok, st[h * LEN : (h + 1) * LEN], NEG)
        e = jnp.exp(sh - jnp.max(sh, 0, keepdims=True))
        p = (e * (1.0 / jnp.sum(e, 0, keepdims=True))).astype(BF)
        p_ref[slot, h] = p
        probs.append(p)
    o_ref[s, :, cols] = dot_tn(jnp.concatenate(probs, 0), stacked(v_ref[s, :, cols], low)).astype(BF)


def gelu_pair(z):
    cdf = 0.5 + 0.5 * lax.erf(z * 0.7071067811865476)
    return z * cdf, cdf + z * (jnp.exp(-0.5 * z * z) * 0.3989422804014327)


def positions(table, s):
    group = (lax.axis_index("dp") * 4 + lax.axis_index("fsdp")) // 4
    row = jnp.sum(jnp.where(iota((16, 16), 0) == group * 2 + s // 2, table, 0), 0, keepdims=True)[:, 0:8]
    lane = iota((1, 8), 1)
    return jnp.where(lane < 4, row, jnp.where(lane == 4, 0, -1))


def forward_body(x_ref, m_ref, ints_ref, sh_small, sh_q, sh_k, sh_v, sh_wo, sh_wi, sh_wu,
                 small, w0, w1, w2, wo, wi, wu, q, k, v, p, o, n1, xh1, inv1, g, dg, lo, xh2, inv2, vec_ref, ib_ref, picked_ref,
                 own_qkv, small_v, w_v, wo_v, wi_v, wu_v, q_v, k_v, v_v, p_v, o_v, n1_v, xh1_v, inv1_v, g_v, dg_v, lo_v, xh2_v, inv2_v,
                 gss, grs, gls, asem, wsem, psem, osem):
    parts = []
    for grp in range(3):
        for i, ref in enumerate((sh_q, sh_k, sh_v)):
            cp = pltpu.make_async_copy(ref.at[:, pl.ds(256 * grp, 256)], own_qkv.at[grp, :, pl.ds(256 * i, 256)], asem.at[3 * grp + i])
            cp.start()
            parts.append(cp)
    sems = (gss, grs, gls)
    pairs = ((sh_small, small), (own_qkv.at[0], w0), (own_qkv.at[1], w1), (own_qkv.at[2], w2), (sh_wo, wo), (sh_wi, wi), (sh_wu, wu))
    gs = [Gather(src, dst, sems, a) for a, (src, dst) in enumerate(pairs)]
    g_wi, g_wu = gs[5:]
    def load(i):
        dst = (small_v, w_v.at[0], w_v.at[1], w_v.at[2], wo_v, wi_v, wu_v)[i]
        return pltpu.make_async_copy(pairs[i][1], dst, wsem.at[i])
    table = []
    for i, x in enumerate(gs):
        def take(i=i):
            gs[i].arrived()
            load(i).start()
        table += [x.own_xy, x.own_z, *x.steps(), take]
    plan = plans_of(FORWARD_ORDER, table)
    greet()
    for cp in parts:
        cp.wait()
    plan["start"][0]()
    load(0).wait()
    plan["spread"][0]()
    vec, inner = expand_vectors(small_v[...].reshape(32, 32, 128)[:, 24:, :])
    vec_ref[...] = vec
    ib_ref[...] = inner
    outs = [(q_v, q), (k_v, k), (v_v, v), (o_v, o), (n1_v, n1), (xh1_v, xh1), (inv1_v, inv1), (g_v, g), (dg_v, dg), (lo_v, lo), (xh2_v, xh2), (inv2_v, inv2)]
    def put(a, s):
        return pltpu.make_async_copy(outs[a][0].at[s], outs[a][1].at[s], osem.at[a, s])
    def put_p(t):
        s, hp = lax.rem(t, 8) // 2, (t // 8) * 2 + lax.rem(t, 2)
        return pltpu.make_async_copy(p_v.at[lax.rem(t, 4)], p.at[s, pl.ds(hp * 2, 2)], psem.at[lax.rem(t, 4)])
    for grp in range(3):
        plan[f"load{grp}"][0]()
        load(1 + grp).wait()
        @pl.loop(0, 4)
        def _(s, grp=grp):
            at_step(s, plan[f"group{grp}"][0::2])
            t = dot(x_ref[s], w_v[grp])
            cols = slice(256 * grp, 256 * grp + 256)
            for j, ref in enumerate((q_v, k_v, v_v)):
                part = t[:, 256 * j : 256 * j + 256]
                if j != 1:
                    part = part + vec_ref[0 if j == 0 else 1][None, cols]
                ref[s, :, cols] = part.astype(BF)
            count = jnp.sum(m_ref[pl.ds(s, 1), :], -1, keepdims=True)
            keys_ok = iota((LEN, 1), 0) < count
            @pl.loop(0, 2)
            def _(i):
                t = grp * 8 + s * 2 + i
                @pl.when(i == 1)
                def _():
                    at_step(s, plan[f"group{grp}"][1::2])
                @pl.when(t >= 4)
                def _():
                    put_p(t - 4).wait()
                attn_fwd_pair(s, grp * 2 + i, q_v, k_v, v_v, p_v, lax.rem(t, 4), o_v, keys_ok)
                put_p(t).start()
            if grp == 2:
                for a in range(4):
                    put(a, s).start()
    plan["load_wo"][0]()
    load(4).wait()
    @pl.loop(0, 4)
    def _(s):
        r1 = x_ref[s].astype(F32) + dot(o_v[s], wo_v[...]) + vec_ref[2][None]
        xh, inv = norm_stats(r1)
        xh1_v[s] = xh.astype(BF)
        inv1_v[s] = jnp.broadcast_to(inv, (LEN, 128))
        n1_v[s] = (xh * vec_ref[3][None] + vec_ref[4][None]).astype(BF)
        at_step(s, plan["out"])
        for a in (4, 5, 6):
            put(a, s).start()
    plan["load_wi"][0]()
    load(5).wait()
    @pl.loop(0, 4)
    def _(s):
        @pl.loop(0, 2)
        def _(j):
            at_step(s * 2 + j, plan["inner"])
            cols = pl.ds(pl.multiple_of(j * 2 * D, 2 * D), 2 * D)
            act, slope = gelu_pair(dot(n1_v[s], wi_v[:, cols]) + ib_ref[:, cols])
            g_v[s, :, cols] = act.astype(BF)
            dg_v[s, :, cols] = slope.astype(BF)
        put(7, s).start()
        put(8, s).start()
    plan["load_wu"][0]()
    load(6).wait()
    plan["outer"][0]()
    @pl.loop(0, 4)
    def _(s):
        r2 = n1_v[s].astype(F32) + dot(g_v[s], wu_v[...]) + vec_ref[5][None]
        xh, inv = norm_stats(r2)
        xh2_v[s] = xh.astype(BF)
        inv2_v[s] = jnp.broadcast_to(inv, (LEN, 128))
        out = (xh * vec_ref[6][None] + vec_ref[7][None]).astype(BF)
        lo_v[s] = out
        place = jnp.sum(jnp.where(iota((8, 8), 0) == iota((8, 8), 1), positions(ints_ref[...], s), 0), 1, keepdims=True)
        picked_ref[s] = dot((iota((8, LEN), 1) == place).astype(F32).astype(BF), out).astype(BF)
        for a in (9, 10, 11):
            put(a, s).start()
    for t in range(20, 24):
        put_p(t).wait()
    for s in range(4):
        for a in range(12):
            put(a, s).wait()
    for x in gs:
        x.sent()


def forward(x, mask, ints, shards, cid):
    small, q, k, v, wo, wi, wu = shards
    full = [((32 * s.shape[0], n), BF) for s, n in ((small, 128), (q, D), (q, D), (q, D), (wo, D), (wi, FF), (wu, D))]
    probs, stat, big = ((4, H, LEN, LEN), BF), ((4, LEN, 128), F32), ((4, LEN, FF), BF)
    acts = [ACT, ACT, ACT, probs, ACT, ACT, ACT, stat, big, big, ACT, ACT, stat]
    outs = full + acts + [((8, D), F32), ((1, FF), F32), ((4, 8, D), BF)]
    slots = [((4, 2, LEN, LEN), BF) if a is probs else a for a in acts]
    return pl.pallas_call(
        forward_body, name="layer_forward", out_shape=[sds(*o) for o in outs],
        in_specs=[VM] * 3 + [HBM] * 7, out_specs=[HBM] * 20 + [VM] * 3,
        scratch_shapes=[pltpu.VMEM(*o) for o in [((3, 24, D), BF), full[0], ((3, D, D), BF)] + full[4:] + slots]
        + gather_sems(7) + [DMA((9,)), DMA((7,)), DMA((4,)), DMA((12, 4))],
        compiler_params=pltpu.CompilerParams(collective_id=cid, has_side_effects=True, vmem_limit_bytes=61 << 20),
    )(x, mask, ints, *shards)


def norm_back(dy, xh, inv, gain):
    c = dy * gain
    return (c - jnp.mean(c, -1, keepdims=True) - xh * jnp.mean(c * xh, -1, keepdims=True)) * inv


def bwd1_body(add_ref, ints_ref, vec_ref, og, xh2, inv2, g, dg, n1, wi, wu,
              gu_ref, gi, dn1, sums_ref, sumi_ref,
              og_v, xh2_v, inv2_v, g_v, dg_v, n1_v, wi_v, wu_v, d2_v, dn1_v, gu_v, gi_v, sss, srs, sls, esem, isem, osem, *bufs):
    def early(s):
        return [pltpu.make_async_copy(a.at[s], b.at[s], esem.at[i, s]) for i, (a, b) in enumerate(((og, og_v), (xh2, xh2_v), (inv2, inv2_v)))]
    for s in range(4):
        for cp in early(s):
            cp.start()
    ins = [(g, g_v), (wu, wu_v), (dg, dg_v), (wi, wi_v), (n1, n1_v)]
    loads = [pltpu.make_async_copy(a, b, isem.at[i]) for i, (a, b) in enumerate(ins)]
    loads[0].start()
    sems = (sss, srs, sls)
    greet()
    jobs = []
    for t in range(3):
        own, bufs = scatter_refs(bufs)
        def source(j, c, t=t):
            return gu_v.at[j, c, :, :, pl.ds(256 * t, 256)]
        def done(total, t=t):
            gu_ref[:, pl.ds(256 * t, 256)] = total
        jobs.append(Scatter(source, own, sems, t, done))
    sums_ref[...] = jnp.zeros_like(sums_ref)
    sumi_ref[...] = jnp.zeros_like(sumi_ref)
    @pl.loop(0, 4)
    def _(s):
        hit = (iota((LEN, 8), 0) == positions(ints_ref[...], s)).astype(F32)
        add = add_ref[s]
        high = add.astype(BF)
        parts = jnp.concatenate([high.astype(F32), add - high.astype(F32)], 0).astype(BF)
        extra = dot(jnp.concatenate([hit, hit], 1).astype(BF), parts)
        for cp in early(s):
            cp.wait()
        dy = og_v[s].astype(F32) + extra
        xh = xh2_v[s].astype(F32)
        dr2 = norm_back(dy, xh, inv2_v[s][:, 0:1], vec_ref[6][None])
        sums_ref[0] += jnp.sum(dy * xh, 0)
        sums_ref[1] += jnp.sum(dy, 0)
        sums_ref[2] += jnp.sum(dr2, 0)
        d2_v[pl.ds(s * LEN, LEN)] = dr2.astype(BF)
        dn1_v[s] = dr2
    loads[0].wait()
    loads[1].start()
    loads[2].start()
    steps = pipelined(jobs)
    for t, job in enumerate(jobs):
        @pl.loop(0, 2)
        def _(j, t=t):
            cols = pl.ds(pl.multiple_of(j * 2 * D, 2 * D), 2 * D)
            part = dot_tn(g_v[:, :, cols].reshape(4 * LEN, 2 * D), d2_v[:, pl.ds(256 * t, 256)])
            gu_v[pl.ds(2 * j, 2), :, :, :, pl.ds(256 * t, 256)] = part.astype(BF).reshape(2, 2, 4, 96, 256)
        job.cores()
        if t == 1:
            steps[0]()
    loads[3].start()
    loads[1].wait()
    loads[2].wait()
    steps = steps[1:] + [None]
    def put(s):
        return pltpu.make_async_copy(dn1_v.at[s], dn1.at[s], osem.at[s])
    loads[3].wait()
    loads[4].start()
    @pl.loop(0, 4)
    def _(s):
        for half in range(2):
            at_step(s, steps[half:9:3] if half else steps[0:9:3])
            cols = pl.ds(half * 2 * D, 2 * D)
            dz = dot_nt(d2_v[pl.ds(pl.multiple_of(s * LEN, LEN), LEN)], wu_v[cols, :]) * dg_v[s, :, cols].astype(F32)
            dz = dz.astype(BF)
            sumi_ref[0:1, cols] += jnp.sum(dz.astype(F32), 0, keepdims=True)
            dg_v[s, :, cols] = dz
        at_step(s, steps[2:9:3])
        dn1_v[s] += dot_nt(dg_v[s], wi_v[...])
        put(s).start()
    loads[4].wait()
    def puti(j):
        cols = pl.ds(pl.multiple_of(j * D, D), D)
        return pltpu.make_async_copy(gi_v.at[:, cols], gi.at[:, cols], osem.at[4 + j])
    @pl.loop(0, 4)
    def _(j):
        cols = pl.ds(pl.multiple_of(j * D, D), D)
        gi_v[:, cols] = dot_tn(n1_v[...].reshape(4 * LEN, D), dg_v[:, :, cols].reshape(4 * LEN, D)).astype(BF)
        puti(j).start()
        at_step(j, steps[9:])
    for i in range(4):
        put(i).wait()
        puti(i).wait()
    for job in jobs:
        job.sent()


def bwd1(og, add, ints, xh2, inv2, vec, g, dg, n1, wi, wu, cid):
    outs = [((96, D), F32), ((D, FF), BF), ((4, LEN, D), F32), ((8, D), F32), ((8, FF), F32)]
    big = ((4, LEN, FF), BF)
    scratch = [ACT, ACT, ((4, LEN, 128), F32), big, big, ACT, ((D, FF), BF), ((FF, D), BF), ((4 * LEN, D), BF), ((4, LEN, D), F32), ((4, 2, 4, 96, D), BF), ((D, FF), BF)]
    return pl.pallas_call(
        bwd1_body, name="feed_forward_backward", out_shape=[sds(*o) for o in outs],
        in_specs=[VM] * 3 + [HBM] * 8, out_specs=[VM, HBM, HBM, VM, VM],
        scratch_shapes=[pltpu.VMEM(*s) for s in scratch] + scatter_sems(3) + [DMA((3, 4)), DMA((5,)), DMA((8,))] + scatter_bufs(96, 256) * 3,
        compiler_params=pltpu.CompilerParams(collective_id=cid, has_side_effects=True, vmem_limit_bytes=61 << 20),
    )(add, ints, vec, og, xh2, inv2, g, dg, n1, wi, wu)


def attn_bwd_pair(s, hp, q_ref, k_ref, v_ref, p_ref, slot, do_ref, dqkv_ref):
    cols = pl.ds(pl.multiple_of(hp * 128, 128), 128)
    rows = pl.ds(pl.multiple_of(s * LEN, LEN), LEN)
    do2 = do_ref[rows, cols]
    low = iota((LEN, 128), 1) < HD
    dpt = dot_nt(stacked(v_ref[s, :, cols], low), do2)
    grads = []
    for h in range(2):
        d = dpt[h * LEN : (h + 1) * LEN]
        pf = p_ref[slot, h].astype(F32)
        grads.append((pf * (d - jnp.sum(pf * d, 0, keepdims=True))).astype(BF))
    ds = jnp.concatenate(grads, 0)
    dv = dot(p_ref[slot].reshape(2 * LEN, LEN), do2)
    dk = dot(ds, q_ref[s, :, cols])
    dq = dot_tn(ds, stacked(k_ref[s, :, cols], low))
    at = (hp // 2) * D + lax.rem(hp, 2) * 128
    def out(i):
        return pl.ds(pl.multiple_of(at + 256 * i, 128), 128)
    dqkv_ref[rows, out(0)] = (dq * 0.125).astype(BF)
    dqkv_ref[rows, out(1)] = (jnp.where(low, dk[:LEN], dk[LEN:]) * 0.125).astype(BF)
    dqkv_ref[rows, out(2)] = jnp.where(low, dv[:LEN], dv[LEN:]).astype(BF)


def bwd2_body(dn1, xh1, inv1, vec_ref, x, q, k, v, p, o, w0, w1, w2, wo, gi, grw_ref, s2_ref, si_ref,
              ggq, ggk, ggv, ggo, ggi, ggs, dx,
              dn1_v, xh1_v, inv1_v, x_v, q_v, k_v, v_v, o_v, p_v, wqkv_v, wo_v, sums_v, sumq_v, d1_v, do_v, dqkv_v, go_v, gg_v, gsm_v,
              sss, srs, sls, esem, isem, psem, osem, *bufs):
    def early(s):
        return [pltpu.make_async_copy(a.at[s], b.at[s], esem.at[i, s]) for i, (a, b) in enumerate(((dn1, dn1_v), (xh1, xh1_v), (inv1, inv1_v)))]
    ins = [(o, o_v), (wo, wo_v), (q, q_v), (k, k_v), (v, v_v), (x, x_v)] + [(w, wqkv_v.at[:, pl.ds(D * i, D)]) for i, w in enumerate((w0, w1, w2))]
    loads = [pltpu.make_async_copy(a, b, isem.at[i]) for i, (a, b) in enumerate(ins)]
    for s in range(4):
        for cp in early(s):
            cp.start()
    sems = (sss, srs, sls)
    greet()
    jobs = []
    def add_job(source, done, in_hbm=False):
        nonlocal bufs
        own, bufs = scatter_refs(bufs)
        jobs.append(Scatter(source, own, sems, len(jobs), done, in_hbm))
    for t in range(4):
        def done(total, t=t):
            ggi[:, pl.ds(t * D, D)] = total
        add_job(lambda j, c, t=t: gi.at[j, c, :, :, pl.ds(t * D, D)], done, True)
    def done_o(total):
        ggo[...] = total
    add_job(lambda j, c: go_v.at[j, c], done_o)
    for t in range(3):
        def done(total, t=t):
            for i, ref in enumerate((ggq, ggk, ggv)):
                ref[:, pl.ds(256 * t, 256)] = total[:, 256 * i : 256 * i + 256]
        add_job(lambda j, c, t=t: gg_v.at[t, j, c], done)
    def done_s(total):
        ggs[...] = total
    add_job(lambda j, c: gsm_v.at[j, c], done_s)
    plan = plans_of(BACKWARD_ORDER, [act for job in jobs for act in (job.cores, job.first, job.second, job.third, job.last)])
    sums_v[...] = jnp.zeros_like(sums_v)
    sumq_v[...] = jnp.zeros_like(sumq_v)
    @pl.loop(0, 4)
    def _(s):
        for cp in early(s):
            cp.wait()
        at_step(s, plan["norm"])
        dy = dn1_v[s]
        xh = xh1_v[s].astype(F32)
        dr1 = norm_back(dy, xh, inv1_v[s][:, 0:1], vec_ref[3][None])
        sums_v[0] += jnp.sum(dy * xh, 0)
        sums_v[1] += jnp.sum(dy, 0)
        sums_v[2] += jnp.sum(dr1, 0)
        dn1_v[s] = dr1
        d1_v[pl.ds(s * LEN, LEN)] = dr1.astype(BF)
        @pl.when(s == 1)
        def _():
            for cp in loads[:2]:
                cp.start()
        @pl.when(s == 3)
        def _():
            for cp in loads[2:5]:
                cp.start()
    plan["out"][0]()
    for cp in loads[:2]:
        cp.wait()
    go_v[...] = dot_tn(o_v[...].reshape(4 * LEN, D), d1_v[...]).astype(BF).reshape(4, 2, 4, 24, D)
    @pl.loop(0, 2)
    def _(i):
        at_step(i, plan["heads_in"])
        rows = pl.ds(pl.multiple_of(i * 2 * LEN, 2 * LEN), 2 * LEN)
        do_v[rows] = dot_nt(d1_v[rows], wo_v[...]).astype(BF)
    for cp in loads[2:5]:
        cp.wait()
    loads[5].start()
    def probs(t):
        hp, s = t // 4, lax.rem(t, 4)
        return pltpu.make_async_copy(p.at[s, pl.ds(hp * 2, 2)], p_v.at[lax.rem(t, 2)], psem.at[lax.rem(t, 2)])
    probs(0).start()
    for grp in range(3):
        @pl.loop(0, 8)
        def _(i, grp=grp):
            t = grp * 8 + i
            @pl.when(t + 1 < 24)
            def _():
                probs(t + 1).start()
            at_step(i, plan[f"pairs{grp}"])
            probs(t).wait()
            attn_bwd_pair(lax.rem(t, 4), t // 4, q_v, k_v, v_v, p_v, lax.rem(t, 2), do_v, dqkv_v)
        if grp == 0:
            loads[5].wait()
            for cp in loads[6:]:
                cp.start()
        plan[f"sum{grp}"][0]()
        d = dqkv_v[:, pl.ds(D * grp, D)]
        sumq_v[grp : grp + 1] = jnp.sum(d.astype(F32), 0, keepdims=True)
        gg_v[grp] = dot_tn(x_v[...].reshape(4 * LEN, D), d).astype(BF).reshape(4, 2, 4, 24, D)
    plan["small"][0]()
    gsm_v[...] = small_grads(grw_ref[...], sums_v[...], s2_ref[...], sumq_v[...], si_ref[...]).reshape(4, 2, 4, 32, 128)
    for cp in loads[6:]:
        cp.wait()
    def put(s):
        return pltpu.make_async_copy(dn1_v.at[s], dx.at[s], osem.at[s])
    @pl.loop(0, 4)
    def _(s):
        rows = pl.ds(pl.multiple_of(s * LEN, LEN), LEN)
        at_step(s, plan["input"])
        dn1_v[s] += dot_nt(dqkv_v[rows], wqkv_v[...])
        put(s).start()
    plan["end"][0]()
    for s in range(4):
        put(s).wait()
    for job in jobs:
        job.sent()


def small_grads(grw, s1, s2, sq, si):
    by_kind = [jnp.concatenate([sq[grp : grp + 1, 256 * i : 256 * i + 256] for grp in range(3)], 1) for i in (0, 2)]
    vec = jnp.concatenate(by_kind + [s1[2:3], s1[0:1], s1[1:2], s2[2:3], s2[0:1], s2[1:2]], 0)
    row, col = iota((256, D), 0), iota((256, D), 1)
    tiled = jnp.broadcast_to(vec[None], (32, 8, D)).reshape(256, D)
    part = jnp.where(over(row, 8) == over(col, 24), tiled, 0.0).astype(BF)
    lane, col = iota((128, D), 0), iota((128, D), 1)
    pick = (lane == col - over(col, 24) * 24).astype(F32).astype(BF)
    out = dot_nt(part, pick).reshape(32, 8, 128)
    row, col = iota((32, FF), 0), iota((32, FF), 1)
    part = jnp.where(row == over(col, 96), si[0:1], 0.0).astype(BF)
    lane, col = iota((128, FF), 0), iota((128, FF), 1)
    pick = (lane - 32 == col - over(col, 96) * 96).astype(F32).astype(BF)
    inner = dot_nt(part, pick)
    out = out + jnp.where(iota((32, 8, 128), 1) == 0, inner[:, None, :], 0.0)
    return jnp.concatenate([grw.reshape(32, 24, 128), out], 1).astype(BF)


def bwd2(dn1, xh1, inv1, vec, x, q, k, v, p, o, w, wo, gi, grw, s2, si, cid):
    own = ((24, D), F32)
    outs = [own, own, own, own, ((24, FF), F32), ((32, 128), F32), ((4, LEN, D), F32)]
    six = ((4, 2, 4, 24, D), BF)
    scratch = [((4, LEN, D), F32), ACT, ((4, LEN, 128), F32), ACT, ACT, ACT, ACT, ACT, ((2, 2, LEN, LEN), BF), ((D, 3 * D), BF), ((D, D), BF),
               ((8, D), F32), ((8, D), F32), ((4 * LEN, D), BF), ((4 * LEN, D), BF), ((4 * LEN, 3 * D), BF), six, ((3,) + six[0], BF), ((4, 2, 4, 32, 128), BF)]
    return pl.pallas_call(
        bwd2_body, name="attention_backward", out_shape=[sds(*s) for s in outs],
        in_specs=[HBM] * 3 + [VM] + [HBM] * 11 + [VM] * 3, out_specs=[VM] * 6 + [HBM],
        scratch_shapes=[pltpu.VMEM(*s) for s in scratch] + scatter_sems(9) + [DMA((3, 4)), DMA((9,)), DMA((2,)), DMA((4,))]
        + scatter_bufs(24, D) * 8 + scatter_bufs(32, 128),
        compiler_params=pltpu.CompilerParams(collective_id=cid, has_side_effects=True, vmem_limit_bytes=61 << 20),
    )(dn1, xh1, inv1, vec, x, q, k, v, p, o, *w, wo, gi.reshape(4, 2, 4, 24, FF), grw, s2, si)


def finish_body(small_ref, pair_ref, *refs):
    n = (len(refs) - 11) // 2
    grw, pair, inner, *vecs = refs[2 * n :]
    for a, b in zip(refs[:n], refs[n : 2 * n]):
        b[...] = a[...]
    grw[...] = small_ref[0:24]
    pair[...] = pair_ref[0, 0:2]
    inner[...] = small_ref[24, 32:128]
    for i, ref in enumerate(vecs):
        ref[...] = small_ref[24 + i, 0:24]


def finish(small, pair, more):
    tail = [((24, 128), F32), ((2,), F32), ((96,), F32)] + [((24,), F32)] * 8
    outs = pl.pallas_call(
        finish_body, name="results", out_shape=[sds(a.shape, a.dtype) for a in more] + [sds(*t) for t in tail],
        in_specs=[VM] * (2 + len(more)), out_specs=[VM] * (len(more) + 11),
    )(small, pair, *more)
    return outs[: len(more)], outs[len(more) :]


def exact(a, b, dims=((1,), (0,))):
    return lax.dot_general(a, b, (dims, ((), ())), preferred_element_type=F32, precision=HI)

def as_f(cond):
    return cond.astype(F32)

def greet_all():
    me = lax.axis_index("dp") * 4 + lax.axis_index("fsdp")
    bar = pltpu.get_barrier_semaphore()
    @pl.loop(1, 32)
    def _(k):
        t = lax.rem(me + k, 32)
        pl.semaphore_signal(bar, inc=1, device_id=(t // 4, lax.rem(t, 4)), device_id_type=MESH)
    pl.semaphore_wait(bar, 31)

def loss_body(picked_ref, ints_ref, emb, vb, qe, small,
              add_ref, grw_ref, pair_ref, ge, gvb_ref,
              emb_ref, vb_ref, qe_ref, small_ref, ge_ref, isem, own_ref, rows_ref, lt_ref, st_ref, all_ref, dh_ref, dhout_ref, gss, grs, gls, sss, srs, sls, xs, xr, *bufs):
    me = lax.axis_index("dp") * 4 + lax.axis_index("fsdp")
    VS = emb_ref.shape[0]
    loads = [pltpu.make_async_copy(a, b, isem.at[i]) for i, (a, b) in enumerate(
        ((small, small_ref), (qe, qe_ref), (vb, vb_ref), (emb, emb_ref)))]
    for cp in loads:
        cp.start()
    greet_all()
    own_ref[...] = picked_ref[:, 0:4, :].astype(F32).reshape(16, D).astype(BF)
    g = Gather(own_ref, rows_ref, (gss, grs, gls), 0)
    g.own()
    for cp in loads:
        cp.wait()
    cls = picked_ref[:, 4:5, :].astype(F32).reshape(4, D)
    cls8 = jnp.concatenate([cls, jnp.zeros((4, D), F32)], 0)
    rw = small_ref[:, 0:24, :].reshape(D, 128)
    row8, lane8 = iota((8, 128), 0), iota((8, 128), 1)
    qpick = as_f(jnp.logical_and(iota((8, 16), 1) == (me // 4) * 2 + iota((8, 16), 0) // 2, iota((8, 16), 0) < 4))
    qe_own = exact(qpick, qe_ref[...])
    score = jnp.sum(dot(cls8.astype(BF), rw) * qe_own, -1, keepdims=True)
    st_ref[12:13] = jnp.sum(jnp.where(row8 == lane8, score, 0.0), 0, keepdims=True)
    r512 = iota((16, 512), 1)
    s_of = r512 >> 2
    q_of = (s_of >> 4) * 2 + ((s_of & 3) >> 1)
    spread = exact(ints_ref[:, 4:8].astype(F32), as_f(iota((4, 512), 0) == (iota((4, 512), 1) & 3)))
    ids = jnp.sum(jnp.where(iota((16, 512), 0) == q_of, spread, 0.0), 0, keepdims=True)
    local = ids.astype(jnp.int32) - me * VS
    q16, s16 = iota((16, 128), 0), iota((16, 128), 1)
    mine = q16 == (s16 >> 4) * 2 + ((s16 & 3) >> 1)
    s8 = iota((8, 128), 1)
    slot_pick = as_f(iota((8, 128), 0) == ((s8 >> 2) & 3) * 2 + (s8 & 1))
    ok16 = jnp.logical_and(mine, exact(ints_ref[:, 8:16].astype(F32), slot_pick) > 0.5)
    valid_of = jnp.sum(ok16.astype(F32), 0, keepdims=True)
    steps = g.steps()
    for i in (3, 0, 1, 2, 4, 5, 6, 7, 8):
        steps[i]()
    g.arrived()
    g.sent()
    rows = rows_ref[...]
    bias = jnp.where(iota((16, VS), 0) == 0, vb_ref[...][None].astype(F32), 0.0).astype(BF)
    lt = dot_nt(emb_ref[...], rows) + dot_tn(bias, jnp.ones((16, 512), BF))
    hit = iota((VS, 512), 0) == local
    peak = jnp.max(lt, 0, keepdims=True)
    e = jnp.exp(lt - peak)
    lt_ref[...] = e
    total = jnp.sum(e, 0, keepdims=True)
    target = jnp.sum(jnp.where(hit, lt, 0.0), 0, keepdims=True)
    for a in range(4):
        cols = slice(a * 128, a * 128 + 128)
        st_ref[a:a + 1] = peak[:, cols]
        st_ref[4 + a:5 + a] = total[:, cols]
        st_ref[8 + a:9 + a] = target[:, cols]
    sends = []
    for k in range(1, 32):
        t = lax.rem(me + k, 32)
        cp = rdma(st_ref, all_ref.at[me], xs.at[k], xr.at[k], (t // 4, lax.rem(t, 4)))
        cp.start()
        sends.append(cp)
    all_ref[me] = st_ref[...]
    for k in range(1, 32):
        f = lax.rem(me + 32 - k, 32)
        rdma(st_ref, all_ref.at[f], xs.at[k], xr.at[k], (f // 4, lax.rem(f, 4))).wait_recv()
    peaks = all_ref[:, 0:4, :]
    top = jnp.max(peaks, 0)
    tot = jnp.sum(all_ref[:, 4:8, :] * jnp.exp(peaks - top[None]), 0)
    lse = top + jnp.log(tot)
    logp = jnp.sum(all_ref[:, 8:12, :], 0) - lse
    i0, i1 = iota((128, 128), 0), iota((128, 128), 1)
    logp8 = jnp.concatenate([logp, jnp.zeros((4, 128), F32)], 0)
    spread = exact(logp8, 0.25 * as_f((i0 >> 2) == (i1 & 31)))
    seq_ll = jnp.sum(jnp.where((lane8 >> 5) == row8, spread, 0.0), 0, keepdims=True)
    spread = exact(all_ref[:, 12, :], as_f(i0 == (i1 & 3)))
    retrieval = jnp.sum(jnp.where((iota((32, 128), 1) >> 2) == iota((32, 128), 0), spread, 0.0), 0, keepdims=True)
    joint = retrieval + seq_ll
    def slot_lse(v):
        m = jnp.max(jnp.where(ok16, v, NEG), -1, keepdims=True)
        return m + jnp.log(jnp.sum(jnp.where(ok16, jnp.exp(v - m), 0.0), -1, keepdims=True))
    def to_seq(v):
        return jnp.sum(jnp.where(mine, v, 0.0), 0, keepdims=True)
    joint_lse, prior_lse = slot_lse(joint), slot_lse(retrieval)
    ok = valid_of > 0.5
    post = jnp.where(ok, jnp.exp(joint - to_seq(joint_lse)), 0.0)
    prior = jnp.where(ok, jnp.exp(retrieval - to_seq(prior_lse)), 0.0)
    pair = jnp.sum(jnp.where(q16 == (me // 4) * 2 + s16, joint_lse - prior_lse, 0.0), 0, keepdims=True)
    pair_ref[...] = jnp.broadcast_to(pair, (8, 128))
    d_score = LOSS_WEIGHT * (prior - post)
    scale = exact(jnp.broadcast_to(-LOSS_WEIGHT * post / 4.0, (8, 128)), as_f(iota((128, 512), 0) == (iota((128, 512), 1) >> 2)))[0:1]
    lse_row = jnp.concatenate([lse[a:a + 1] for a in range(4)], 1)
    dl = jnp.where(hit, scale, 0.0) - lt_ref[...] * (scale * jnp.exp(peak - lse_row))
    gvb_ref[...] = jnp.broadcast_to(jnp.sum(dl, -1, keepdims=True), (VS, 128)).T[0]
    db = dl.astype(BF)
    dh_ref[...] = dot_tn(db, emb_ref[...]).astype(BF).reshape(4, 2, 4, 16, D)
    def done(total):
        dhout_ref[...] = total
    sc = Scatter(lambda j, c: dh_ref.at[j, c], scatter_refs(bufs)[0], (sss, srs, sls), 0, done)
    for j in range(4):
        sc.core(j)
    du = jnp.sum(jnp.where(jnp.logical_and(lane8 == me * 4 + row8, row8 < 4), d_score, 0.0), -1, keepdims=True) * qe_own
    grw_ref[...] = exact(cls8, du, ((0,), (0,)))
    dcls = exact(du, rw.astype(F32), ((1,), (1,)))
    add_ref[...] = jnp.zeros_like(add_ref)
    for l in range(4):
        add_ref[l, 4:5] = dcls[l:l + 1]
    sc.first()
    ge_ref[...] = dot(db, rows)
    out = pltpu.make_async_copy(ge_ref, ge, isem.at[4])
    out.start()
    sc.second()
    sc.third()
    sc.last()
    sc.sent()
    for l in range(4):
        add_ref[l, 0:4] = dhout_ref[4 * l:4 * l + 4]
    for cp in sends:
        cp.wait_send()
    out.wait()

def loss_call(picked, ints, emb, vb, qe, small, cid):
    VS = emb.shape[0]
    outs = [((4, 8, D), F32), ((D, 128), F32), ((8, 128), F32), ((VS, D), F32), ((VS,), F32)]
    args = (picked, ints, emb, vb, qe, small)
    return pl.pallas_call(loss_body, name="slot_loss", out_shape=[jax.ShapeDtypeStruct(s, t) for s, t in outs],
        in_specs=[VM] * 2 + [HBM] * 4, out_specs=[VM] * 3 + [HBM, VM],
        scratch_shapes=[pltpu.VMEM(a.shape, a.dtype) for a in (emb, vb, qe, small)] + [pltpu.VMEM((VS, D), F32), DMA((7,)), pltpu.VMEM((16, D), BF), pltpu.VMEM((512, D), BF), pltpu.VMEM((VS, 512), F32), pltpu.VMEM((16, 128), F32),
            pltpu.VMEM((32, 16, 128), F32), pltpu.VMEM((4, 2, 4, 16, D), BF), pltpu.VMEM((16, D), F32),
            *gather_sems(1), *scatter_sems(1), DMA((32,)), DMA((32,))] + scatter_bufs(16, D),
        compiler_params=pltpu.CompilerParams(collective_id=cid, has_side_effects=True, vmem_limit_bytes=58 << 20))(*args)


def linked_body(hidden_in, token_mask, out_grad, query_embed, slot_valid, target_ids, target_pos,
                qw, kw, vw, ow, iw, uw, rw, qb, vb, ob, ga, sa, ib, ub, gb, sb, embedding, vocab_bias):
    block = jnp.pad(jnp.stack([qb, vb, ob, ga, sa, ub, gb, sb]), ((0, 0), (0, 104)))
    block = jnp.concatenate([rw, block + jnp.pad(ib[None], ((0, 7), (32, 0)))], 0)
    ints = jnp.concatenate([target_pos, target_ids, slot_valid], 1)
    small, w0, w1, w2, wo, wi, wu, q, k, v, p, o, n1, xh1, inv1, g, dg, out_seq, xh2, inv2, vec, inner, picked = forward(
        hidden_in, token_mask, ints, (block, qw, kw, vw, ow, iw, uw), 0)
    add, grw, pair, ge, gvb = loss_call(
        picked, ints, embedding, vocab_bias, query_embed, small.reshape(32, 32, 128), 1)
    gu, gi, dn1, s2, si = bwd1(out_grad, add, ints, xh2, inv2, vec, g, dg, n1, wi, wu, 2)
    gq, gk, gv, go, gi, gsm, dx = bwd2(dn1, xh1, inv1, vec, hidden_in, q, k, v, p, o, (w0, w1, w2), wo, gi, grw, s2, si, 3)
    (gu, gi, gq, gk, gv, go, gvb), (grw, pair, gib, *vecs) = finish(
        gsm, pair, (gu, gi, gq, gk, gv, go, gvb))
    return (out_seq, pair, dx, gq, gk, gv, go, gi, gu, grw, *vecs[:5], gib, *vecs[5:], ge, gvb)


def solution(mesh):
    placed = (
        P(AXES, None, None),
        P(AXES, None),
        P(AXES, None, None),
        P(),
        P(),
        P(),
        P(),
        P(AXES, None),
        P(AXES, None),
        P(AXES, None),
        P(AXES, None),
        P(AXES, None),
        P(AXES, None),
        P(AXES, None),
        P(AXES),
        P(AXES),
        P(AXES),
        P(AXES),
        P(AXES),
        P(AXES),
        P(AXES),
        P(AXES),
        P(AXES),
        P(AXES, None),
        P(AXES),
    )
    own = mesh.shape["dp"] == 8 and mesh.shape["fsdp"] == 4
    return jax.shard_map(
        linked_body if own else plain_body,
        mesh=mesh,
        in_specs=placed,
        out_specs=(
            P(AXES, None, None),
            P(AXES),
            P(AXES, None, None),
            P(AXES, None),
            P(AXES, None),
            P(AXES, None),
            P(AXES, None),
            P(AXES, None),
            P(AXES, None),
            P(AXES, None),
            P(AXES),
            P(AXES),
            P(AXES),
            P(AXES),
            P(AXES),
            P(AXES),
            P(AXES),
            P(AXES),
            P(AXES),
            P(AXES, None),
            P(AXES),
        ),
        check_vma=False,
    )
```

```python
import functools

import jax
import jax.numpy as jnp
from jax import lax
from jax.experimental import pallas as pl
from jax.experimental.pallas import tpu as pltpu
from jax.sharding import PartitionSpec as P

AXES = ("dp", "fsdp")


D = 768
H = 12
HD = 64
LEN = 288
MASKS = 4
SLOT_DEV = 2
GROUP = 4


EPS = 1e-12
NEG = -1000000000.0
HIGH = lax.Precision.HIGHEST
LOSS_WEIGHT = 32.0


def combined_all(value, axis, join):
    pieces = jax.tree.map(lambda part: lax.all_gather(part, axis), value)
    head = jax.tree.map(lambda part: part[0], pieces)
    tail = jax.tree.map(lambda part: part[1:], pieces)
    subtotal, _ = lax.scan(lambda subtotal, share: (join(subtotal, share), None), head, tail)
    return subtotal


def partner(value, axis, stride):
    mask = 2**stride
    pairs = [(source, source ^ mask) for source in range(lax.axis_size(axis))]
    return lax.ppermute(value, axis, pairs)


def layer_norm(residual, gain_vec, shift_vec):
    row_mean = jnp.mean(residual, -1, keepdims=True)
    centred = residual - row_mean
    row_var = jnp.mean(centred * centred, -1, keepdims=True)
    return centred * lax.rsqrt(row_var + EPS) * gain_vec + shift_vec


def exact_gelu(pre_act):
    return jax.nn.gelu(pre_act, approximate=False)


def collect(params):
    (
        query_weight,
        key_weight,
        value_weight,
        out_weight,
        inner_weight,
        outer_weight,
        retrieve_weight,
        query_bias,
        value_bias,
        out_bias,
        norm1_gain,
        norm1_bias,
        inner_bias,
        outer_bias,
        norm2_gain,
        norm2_bias,
    ) = params
    return (
        lax.all_gather(query_weight, AXES, axis=0, tiled=True),
        lax.all_gather(key_weight, AXES, axis=0, tiled=True),
        lax.all_gather(value_weight, AXES, axis=0, tiled=True),
        lax.all_gather(out_weight, AXES, axis=0, tiled=True),
        lax.all_gather(inner_weight, AXES, axis=0, tiled=True),
        lax.all_gather(outer_weight, AXES, axis=0, tiled=True),
        lax.all_gather(retrieve_weight, AXES, axis=0, tiled=True),
        lax.all_gather(query_bias, AXES, axis=0, tiled=True),
        lax.all_gather(value_bias, AXES, axis=0, tiled=True),
        lax.all_gather(out_bias, AXES, axis=0, tiled=True),
        lax.all_gather(norm1_gain, AXES, axis=0, tiled=True),
        lax.all_gather(norm1_bias, AXES, axis=0, tiled=True),
        lax.all_gather(inner_bias, AXES, axis=0, tiled=True),
        lax.all_gather(outer_bias, AXES, axis=0, tiled=True),
        lax.all_gather(norm2_gain, AXES, axis=0, tiled=True),
        lax.all_gather(norm2_bias, AXES, axis=0, tiled=True),
    )


def spread(grads):
    (
        grad_qw,
        grad_kw,
        grad_vw,
        grad_ow,
        grad_iw,
        grad_uw,
        grad_rw,
        grad_qb,
        grad_vb,
        grad_ob,
        grad_ga,
        grad_sa,
        grad_ib,
        grad_ub,
        grad_gb,
        grad_sb,
    ) = grads
    return (
        lax.psum_scatter(grad_qw, AXES, scatter_dimension=0, tiled=True),
        lax.psum_scatter(grad_kw, AXES, scatter_dimension=0, tiled=True),
        lax.psum_scatter(grad_vw, AXES, scatter_dimension=0, tiled=True),
        lax.psum_scatter(grad_ow, AXES, scatter_dimension=0, tiled=True),
        lax.psum_scatter(grad_iw, AXES, scatter_dimension=0, tiled=True),
        lax.psum_scatter(grad_uw, AXES, scatter_dimension=0, tiled=True),
        lax.psum_scatter(grad_rw, AXES, scatter_dimension=0, tiled=True),
        lax.psum_scatter(grad_qb, AXES, scatter_dimension=0, tiled=True),
        lax.psum_scatter(grad_vb, AXES, scatter_dimension=0, tiled=True),
        lax.psum_scatter(grad_ob, AXES, scatter_dimension=0, tiled=True),
        lax.psum_scatter(grad_ga, AXES, scatter_dimension=0, tiled=True),
        lax.psum_scatter(grad_sa, AXES, scatter_dimension=0, tiled=True),
        lax.psum_scatter(grad_ib, AXES, scatter_dimension=0, tiled=True),
        lax.psum_scatter(grad_ub, AXES, scatter_dimension=0, tiled=True),
        lax.psum_scatter(grad_gb, AXES, scatter_dimension=0, tiled=True),
        lax.psum_scatter(grad_sb, AXES, scatter_dimension=0, tiled=True),
    )


def attention(query_heads, key_heads, value_heads, keys_ok):
    head_scale = HD ** (-0.5)
    scores = (
        jnp.einsum("sqhe,skhe->shqk", query_heads, key_heads, preferred_element_type=jnp.float32)
        * head_scale
    )
    scores = jnp.where(keys_ok[:, None, None, :] > 0, scores, NEG)
    row_peak = jnp.max(scores, -1, keepdims=True)
    exp_scores = jnp.exp(scores - row_peak)
    totals = jnp.sum(exp_scores, -1, keepdims=True)
    attn_probs = (exp_scores / totals).astype(jnp.bfloat16)
    attended = jnp.einsum(
        "shqk,skhe->sqhe", attn_probs, value_heads, preferred_element_type=jnp.float32
    )
    return (attended, row_peak + jnp.log(totals))


def forward_layer(hidden, keys_ok, gathered):
    (
        query_weight,
        key_weight,
        value_weight,
        out_weight,
        inner_weight,
        outer_weight,
        retrieve_weight,
        query_bias,
        value_bias,
        out_bias,
        norm1_gain,
        norm1_bias,
        inner_bias,
        outer_bias,
        norm2_gain,
        norm2_bias,
    ) = gathered
    seq_count = hidden.shape[0]
    head_shape = (seq_count, LEN, H, HD)
    flat_rows = hidden.reshape(seq_count * LEN, D)
    queries = (
        jnp.dot(flat_rows, query_weight, preferred_element_type=jnp.float32)
        + query_bias.astype(jnp.float32)
    ).astype(jnp.bfloat16)
    key_rows = jnp.dot(flat_rows, key_weight, preferred_element_type=jnp.float32).astype(
        jnp.bfloat16
    )
    values = (
        jnp.dot(flat_rows, value_weight, preferred_element_type=jnp.float32)
        + value_bias.astype(jnp.float32)
    ).astype(jnp.bfloat16)
    attended, log_totals = attention(
        queries.reshape(head_shape),
        key_rows.reshape(head_shape),
        values.reshape(head_shape),
        keys_ok,
    )
    attended = attended.reshape(seq_count * LEN, D).astype(jnp.bfloat16)
    first_in = (
        flat_rows.astype(jnp.float32)
        + jnp.dot(attended, out_weight, preferred_element_type=jnp.float32)
        + out_bias.astype(jnp.float32)
    )
    normed_one = layer_norm(
        first_in, norm1_gain.astype(jnp.float32), norm1_bias.astype(jnp.float32)
    ).astype(jnp.bfloat16)
    pre_act = jnp.dot(
        normed_one, inner_weight, preferred_element_type=jnp.float32
    ) + inner_bias.astype(jnp.float32)
    active = exact_gelu(pre_act).astype(jnp.bfloat16)
    second_in = (
        normed_one.astype(jnp.float32)
        + jnp.dot(active, outer_weight, preferred_element_type=jnp.float32)
        + outer_bias.astype(jnp.float32)
    )
    layer_out = layer_norm(
        second_in, norm2_gain.astype(jnp.float32), norm2_bias.astype(jnp.float32)
    ).astype(jnp.bfloat16)
    return (
        queries,
        key_rows,
        values,
        log_totals,
        attended,
        first_in,
        normed_one,
        pre_act,
        active,
        second_in,
        layer_out,
    )


def backward_layer(hidden, keys_ok, gathered, kept_acts, grad_out):
    (
        query_weight,
        key_weight,
        value_weight,
        out_weight,
        inner_weight,
        outer_weight,
        retrieve_weight,
        query_bias,
        value_bias,
        out_bias,
        norm1_gain,
        norm1_bias,
        inner_bias,
        outer_bias,
        norm2_gain,
        norm2_bias,
    ) = gathered
    (
        queries,
        key_rows,
        values,
        log_totals,
        attended,
        first_in,
        normed_one,
        pre_act,
        active,
        second_in,
        layer_out,
    ) = kept_acts
    seq_count = hidden.shape[0]
    head_shape = (seq_count, LEN, H, HD)
    flat_rows = hidden.reshape(seq_count * LEN, D)
    unused_two, norm_two_back = jax.vjp(
        layer_norm, second_in, norm2_gain.astype(jnp.float32), norm2_bias.astype(jnp.float32)
    )
    grad_second, grad_norm2_gain, grad_norm2_bias = norm_two_back(grad_out)
    second_low = grad_second.astype(jnp.bfloat16)
    grad_outer_weight = jnp.dot(active.T, second_low, preferred_element_type=jnp.float32)
    grad_outer_bias = jnp.sum(grad_second, 0)
    grad_active = jnp.dot(second_low, outer_weight.T, preferred_element_type=jnp.float32)
    unused_act, gelu_back = jax.vjp(exact_gelu, pre_act)
    grad_pre = gelu_back(grad_active)[0].astype(jnp.bfloat16)
    grad_inner_weight = jnp.dot(normed_one.T, grad_pre, preferred_element_type=jnp.float32)
    grad_inner_bias = jnp.sum(grad_pre.astype(jnp.float32), 0)
    grad_normed = grad_second + jnp.dot(
        grad_pre, inner_weight.T, preferred_element_type=jnp.float32
    )
    unused_one, norm_one_back = jax.vjp(
        layer_norm, first_in, norm1_gain.astype(jnp.float32), norm1_bias.astype(jnp.float32)
    )
    grad_first, grad_norm1_gain, grad_norm1_bias = norm_one_back(grad_normed)
    first_low = grad_first.astype(jnp.bfloat16)
    grad_out_weight = jnp.dot(attended.T, first_low, preferred_element_type=jnp.float32)
    grad_out_bias = jnp.sum(grad_first, 0)
    grad_attended = (
        jnp.dot(first_low, out_weight.T, preferred_element_type=jnp.float32)
        .astype(jnp.bfloat16)
        .reshape(head_shape)
    )
    query_heads = queries.reshape(head_shape)
    key_heads = key_rows.reshape(head_shape)
    value_heads = values.reshape(head_shape)
    head_scale = HD ** (-0.5)
    scores = (
        jnp.einsum("sqhe,skhe->shqk", query_heads, key_heads, preferred_element_type=jnp.float32)
        * head_scale
    )
    scores = jnp.where(keys_ok[:, None, None, :] > 0, scores, NEG)
    attn_probs = jnp.exp(scores - log_totals)
    grad_probs = jnp.einsum(
        "sqhe,skhe->shqk", grad_attended, value_heads, preferred_element_type=jnp.float32
    )
    grad_value_heads = jnp.einsum(
        "shqk,sqhe->skhe",
        attn_probs.astype(jnp.bfloat16),
        grad_attended,
        preferred_element_type=jnp.float32,
    )
    grad_scores = (
        attn_probs * (grad_probs - jnp.sum(attn_probs * grad_probs, -1, keepdims=True))
    ).astype(jnp.bfloat16)
    grad_query_heads = (
        jnp.einsum("shqk,skhe->sqhe", grad_scores, key_heads, preferred_element_type=jnp.float32)
        * head_scale
    )
    grad_key_heads = (
        jnp.einsum("shqk,sqhe->skhe", grad_scores, query_heads, preferred_element_type=jnp.float32)
        * head_scale
    )
    grad_queries = grad_query_heads.reshape(seq_count * LEN, D).astype(jnp.bfloat16)
    grad_keys = grad_key_heads.reshape(seq_count * LEN, D).astype(jnp.bfloat16)
    grad_values = grad_value_heads.reshape(seq_count * LEN, D).astype(jnp.bfloat16)
    grad_query_weight = jnp.dot(flat_rows.T, grad_queries, preferred_element_type=jnp.float32)
    grad_key_weight = jnp.dot(flat_rows.T, grad_keys, preferred_element_type=jnp.float32)
    grad_value_weight = jnp.dot(flat_rows.T, grad_values, preferred_element_type=jnp.float32)
    grad_query_bias = jnp.sum(grad_queries.astype(jnp.float32), 0)
    grad_value_bias = jnp.sum(grad_values.astype(jnp.float32), 0)
    grad_hidden = (
        grad_first
        + jnp.dot(grad_queries, query_weight.T, preferred_element_type=jnp.float32)
        + jnp.dot(grad_keys, key_weight.T, preferred_element_type=jnp.float32)
        + jnp.dot(grad_values, value_weight.T, preferred_element_type=jnp.float32)
    )
    return (
        grad_hidden,
        (
            grad_query_weight,
            grad_key_weight,
            grad_value_weight,
            grad_out_weight,
            grad_inner_weight,
            grad_outer_weight,
            grad_query_bias,
            grad_value_bias,
            grad_out_bias,
            grad_norm1_gain,
            grad_norm1_bias,
            grad_inner_bias,
            grad_outer_bias,
            grad_norm2_gain,
            grad_norm2_bias,
        ),
    )


def merge_pair(peak_one, total_one, peak_two, total_two):
    peak_new = jnp.maximum(peak_one, peak_two)
    return (
        peak_new,
        total_one * jnp.exp(peak_one - peak_new) + total_two * jnp.exp(peak_two - peak_new),
    )


def merge_rows(one_side, other_side):
    peak_new, total_new = merge_pair(one_side[0], one_side[1], other_side[0], other_side[1])
    return (peak_new, total_new, one_side[2] + other_side[2])


def slot_partial(score_vec, slot_ok):
    grouped = jnp.where(slot_ok, score_vec, NEG).reshape(-1, SLOT_DEV)
    ok_grouped = slot_ok.reshape(-1, SLOT_DEV)
    group_peak = jnp.max(grouped, -1)
    group_total = jnp.sum(jnp.where(ok_grouped, jnp.exp(grouped - group_peak[:, None]), 0.0), -1)
    return (group_peak, group_total)


def plain_body(
    hidden_in,
    token_mask,
    out_grad,
    query_embed,
    slot_valid,
    target_ids,
    target_pos,
    query_weight,
    key_weight,
    value_weight,
    out_weight,
    inner_weight,
    outer_weight,
    retrieve_weight,
    query_bias,
    value_bias,
    out_bias,
    norm1_gain,
    norm1_bias,
    inner_bias,
    outer_bias,
    norm2_gain,
    norm2_bias,
    embedding,
    vocab_bias,
):
    params = (
        query_weight,
        key_weight,
        value_weight,
        out_weight,
        inner_weight,
        outer_weight,
        retrieve_weight,
        query_bias,
        value_bias,
        out_bias,
        norm1_gain,
        norm1_bias,
        inner_bias,
        outer_bias,
        norm2_gain,
        norm2_bias,
    )
    gathered = collect(params)
    kept_acts = forward_layer(hidden_in, token_mask, gathered)
    seq_count = hidden_in.shape[0]
    query_count = seq_count // SLOT_DEV
    out_seq = kept_acts[10].reshape(seq_count, LEN, D)
    devices = lax.axis_size("dp") * lax.axis_size("fsdp")
    device = lax.axis_index("dp") * lax.axis_size("fsdp") + lax.axis_index("fsdp")
    member = lax.axis_index("fsdp") % GROUP
    local_seq = jnp.arange(seq_count, dtype=jnp.int32)
    local_query = device // GROUP * query_count + local_seq // SLOT_DEV
    local_slot = member * SLOT_DEV + local_seq % SLOT_DEV
    slot_ok = slot_valid[local_query, local_slot] > 0
    embeds = query_embed[local_query]
    positions = target_pos[local_query]
    cls_rows = out_seq[:, 0, :].astype(jnp.float32)
    retrieve_full = gathered[6].astype(jnp.float32)
    projected = jnp.dot(cls_rows, retrieve_full, precision=HIGH)
    retrieval = jnp.sum(projected * embeds, -1)
    own_rows = seq_count * MASKS
    sent_rows = out_seq[local_seq[:, None], positions].reshape(own_rows, D)
    all_rows = lax.all_gather(sent_rows, AXES, axis=0, tiled=True)
    group_count = devices // GROUP
    all_targets = jnp.broadcast_to(
        target_ids.reshape(group_count, 1, query_count, 1, MASKS),
        (group_count, GROUP, query_count, SLOT_DEV, MASKS),
    ).reshape(-1)
    vocab_rows = embedding.shape[0]
    local_ids = all_targets - device * vocab_rows
    target_hit = jnp.arange(vocab_rows, dtype=jnp.int32)[None, :] == local_ids[:, None]
    logits = jnp.einsum(
        "rd,vd->rv", all_rows, embedding, preferred_element_type=jnp.float32
    ) + vocab_bias.astype(jnp.float32)
    row_peak = jnp.max(logits, -1)
    sum_exp = jnp.sum(jnp.exp(logits - row_peak[:, None]), -1)
    target_logit = jnp.sum(jnp.where(target_hit, logits, 0.0), -1)
    peak_all, total_all, target_all = combined_all(
        (row_peak, sum_exp, target_logit), AXES, merge_rows
    )
    lse_rows = peak_all + jnp.log(total_all)
    log_prob = lax.dynamic_slice_in_dim(target_all - lse_rows, device * own_rows, own_rows)
    seq_ll = jnp.mean(log_prob.reshape(seq_count, MASKS), -1)
    joint_score = retrieval + seq_ll
    joint_peak, joint_total = slot_partial(joint_score, slot_ok)
    prior_peak, prior_total = slot_partial(retrieval, slot_ok)
    for bit_number in range(GROUP.bit_length() - 1):
        far_joint_peak, far_joint_total, far_prior_peak, far_prior_total = partner(
            (joint_peak, joint_total, prior_peak, prior_total), "fsdp", bit_number
        )
        joint_peak, joint_total = merge_pair(
            joint_peak, joint_total, far_joint_peak, far_joint_total
        )
        prior_peak, prior_total = merge_pair(
            prior_peak, prior_total, far_prior_peak, far_prior_total
        )
    joint_lse = joint_peak + jnp.log(joint_total)
    prior_lse = prior_peak + jnp.log(prior_total)
    pair_loglik = joint_lse - prior_lse
    post_weight = jnp.where(slot_ok, jnp.exp(joint_score - jnp.repeat(joint_lse, SLOT_DEV)), 0.0)
    prior_weight = jnp.where(slot_ok, jnp.exp(retrieval - jnp.repeat(prior_lse, SLOT_DEV)), 0.0)
    grad_retrieval = LOSS_WEIGHT * (prior_weight - post_weight)
    row_scale = jnp.repeat(-LOSS_WEIGHT * post_weight / MASKS, MASKS)
    all_scales = lax.all_gather(row_scale, AXES, axis=0, tiled=True)
    vocab_probs = jnp.exp(logits - lse_rows[:, None])
    grad_logits = all_scales[:, None] * (target_hit.astype(jnp.float32) - vocab_probs)
    grad_vocab_bias = jnp.sum(grad_logits, 0)
    logits_low = grad_logits.astype(jnp.bfloat16)
    grad_embedding = jnp.einsum(
        "rv,rd->vd", logits_low, all_rows, preferred_element_type=jnp.float32
    )
    grad_picked = lax.psum_scatter(
        jnp.dot(logits_low, embedding, preferred_element_type=jnp.float32),
        AXES,
        scatter_dimension=0,
        tiled=True,
    )
    grad_project = grad_retrieval[:, None] * embeds
    grad_retrieve_weight = jnp.dot(cls_rows.T, grad_project, precision=HIGH)
    grad_cls = jnp.dot(grad_project, retrieve_full.T, precision=HIGH)
    grad_total = out_grad.astype(jnp.float32)
    grad_total = grad_total.at[local_seq[:, None], positions].add(
        grad_picked.reshape(seq_count, MASKS, D)
    )
    grad_total = grad_total.at[:, 0, :].add(grad_cls)
    grad_total = grad_total.reshape(seq_count * LEN, D)
    grad_hidden, layer_grads = backward_layer(
        hidden_in, token_mask, gathered, kept_acts, grad_total
    )
    (
        grad_query_weight,
        grad_key_weight,
        grad_value_weight,
        grad_out_weight,
        grad_inner_weight,
        grad_outer_weight,
        grad_query_bias,
        grad_value_bias,
        grad_out_bias,
        grad_norm1_gain,
        grad_norm1_bias,
        grad_inner_bias,
        grad_outer_bias,
        grad_norm2_gain,
        grad_norm2_bias,
    ) = layer_grads
    (
        shard_query_weight,
        shard_key_weight,
        shard_value_weight,
        shard_out_weight,
        shard_inner_weight,
        shard_outer_weight,
        shard_retrieve_weight,
        shard_query_bias,
        shard_value_bias,
        shard_out_bias,
        shard_norm1_gain,
        shard_norm1_bias,
        shard_inner_bias,
        shard_outer_bias,
        shard_norm2_gain,
        shard_norm2_bias,
    ) = spread(
        (
            grad_query_weight,
            grad_key_weight,
            grad_value_weight,
            grad_out_weight,
            grad_inner_weight,
            grad_outer_weight,
            grad_retrieve_weight,
            grad_query_bias,
            grad_value_bias,
            grad_out_bias,
            grad_norm1_gain,
            grad_norm1_bias,
            grad_inner_bias,
            grad_outer_bias,
            grad_norm2_gain,
            grad_norm2_bias,
        )
    )
    return (
        out_seq,
        pair_loglik,
        grad_hidden.reshape(seq_count, LEN, D),
        shard_query_weight,
        shard_key_weight,
        shard_value_weight,
        shard_out_weight,
        shard_inner_weight,
        shard_outer_weight,
        shard_retrieve_weight,
        shard_query_bias,
        shard_value_bias,
        shard_out_bias,
        shard_norm1_gain,
        shard_norm1_bias,
        shard_inner_bias,
        shard_outer_bias,
        shard_norm2_gain,
        shard_norm2_bias,
        grad_embedding,
        grad_vocab_bias,
    )

MESH = pl.DeviceIdType.MESH
F32 = jnp.float32
BF = jnp.bfloat16
DMA = pltpu.SemaphoreType.DMA


def coords():
    d = lax.axis_index("dp")
    return d // 4, (d // 2) % 2, d % 2, lax.axis_index("fsdp")


def dev(y, x, c, z):
    return ((y * 2 + x) * 2 + c, z)


def across(z, k):
    return (z + 1 - 2 * lax.rem(z, 2), lax.rem(z + 2, 4), 3 - z)[k - 1] if k else z


def rdma(src, dst, ss, rs, to):
    return pltpu.make_async_remote_copy(src, dst, ss, rs, device_id=to, device_id_type=MESH)


def greet():
    y, x, c, z = coords()
    bar = pltpu.get_barrier_semaphore()
    tos = [dev(y, x, c, lax.rem(z + k, 4)) for k in (1, 2, 3)]
    tos += [dev(y, 1 - x, c, z), dev(1 - y, x, c, z), dev(y, x, 1 - c, z)]
    for t in tos:
        pl.semaphore_signal(bar, inc=1, device_id=t, device_id_type=MESH)
    pl.semaphore_wait(bar, len(tos))


def rows_at(start, size):
    return pl.ds(pl.multiple_of(start, 8), size)


class Gather:
    def __init__(self, src, dst, sems, a):
        self.src, self.dst, self.a = src, dst, a
        self.ss, self.rs, self.ls = sems
        self.r, n = src.shape
        self.split = (n // 2) % 128 == 0
        self.h = n // 2

    def chips(self):
        y, x, c, z = coords()
        return y * 2 + x, y * 2 + 1 - x, (1 - y) * 2 + x, (1 - y) * 2 + 1 - x

    def block(self, chip, k):
        y, x, c, z = coords()
        zz = across(z, k)
        return self.dst.at[rows_at(((chip * 2 + c) * 4 + zz) * self.r, self.r)]

    def column(self, chip, c):
        return self.dst.at[rows_at((chip * 2 + c) * 4 * self.r, 4 * self.r)]

    def half(self, ref, right):
        if not self.split:
            return ref
        return ref.at[:, pl.ds(self.h if right else 0, self.h)]

    def copy(self, src, dst, slot, to):
        return rdma(src, dst, self.ss.at[self.a, slot], self.rs.at[self.a, slot], to)

    def send(self, ref, slot, to, src=None):
        self.copy(ref if src is None else src, ref, slot, to).start()

    def wait(self, ref, slot):
        y, x, c, z = coords()
        self.copy(ref, ref, slot, dev(y, 1 - x, c, z)).wait_recv()

    def kept(self):
        return pltpu.make_async_copy(self.src, self.block(self.chips()[0], 0), self.ls.at[self.a])

    def own_xy(self):
        y, x, c, z = coords()
        d = self.block(self.chips()[0], 0)
        self.send(d, 4, dev(y, 1 - x, c, z), self.src)
        self.send(d, 8, dev(1 - y, x, c, z), self.src)

    def own_z(self):
        y, x, c, z = coords()
        d = self.block(self.chips()[0], 0)
        self.kept().start()
        for k in (1, 3, 2):
            self.send(d, k, dev(y, x, c, across(z, k)), self.src)

    def own(self):
        self.own_xy()
        self.own_z()

    def z(self, k):
        y, x, c, z = coords()
        d = self.block(self.chips()[0], k)
        self.wait(d, k)
        self.send(d, 4 + k, dev(y, 1 - x, c, z))
        self.send(d, 8 + k, dev(1 - y, x, c, z))

    def core(self, i):
        y, x, c, z = coords()
        if i == 0:
            self.kept().wait()
        self.send(self.column(self.chips()[i], c), 20 + i, dev(y, x, 1 - c, z))

    def xy(self, k):
        y, x, c, z = coords()
        dx = self.block(self.chips()[1], k)
        self.wait(dx, 4 + k)
        self.send(self.half(dx, False), 12 + k, dev(1 - y, x, c, z))
        dy = self.block(self.chips()[2], k)
        self.wait(dy, 8 + k)
        if self.split:
            self.send(self.half(dy, True), 16 + k, dev(y, 1 - x, c, z))

    def dg(self, k):
        d = self.block(self.chips()[3], k)
        self.wait(self.half(d, False), 12 + k)
        if self.split:
            self.wait(self.half(d, True), 16 + k)

    def arrived(self):
        y, x, c, z = coords()
        for i, chip in enumerate(self.chips()):
            self.wait(self.column(chip, 1 - c), 20 + i)

    def sent(self):
        y, x, c, z = coords()
        to = dev(y, 1 - x, c, z)
        d = self.block(self.chips()[0], 0)
        for k in range(4):
            if k:
                self.copy(d, d, k, to).wait_send()
            self.copy(d, d, 4 + k, to).wait_send()
            self.copy(d, d, 8 + k, to).wait_send()
            half = self.half(d, False)
            self.copy(half, half, 12 + k, to).wait_send()
            if self.split:
                self.copy(half, half, 16 + k, to).wait_send()
            col = self.column(self.chips()[0], 0)
            self.copy(col, col, 20 + k, to).wait_send()

    def steps(self):
        out = [functools.partial(self.z, k) for k in (1, 3, 2)]
        out[2] = lambda: (self.z(2), self.core(0))
        out += [functools.partial(self.xy, k) for k in (0, 1, 3)]
        out += [lambda: (self.xy(2), self.core(1), self.core(2))]
        out += [lambda: (self.dg(0), self.dg(1)), lambda: (self.dg(3), self.dg(2), self.core(3))]
        return out


def gather_sems(n):
    return [DMA((n, 24)), DMA((n, 24)), DMA((n,))]


class Scatter:
    def __init__(self, source, bufs, sems, a, done, in_hbm=False):
        self.source, self.a, self.done, self.in_hbm = source, a, done, in_hbm
        self.ss, self.rs, self.ls = sems
        self.held, self.rc, self.ray, self.rax, self.rbx, self.rby, self.rz = bufs
        self.split = self.rbx is not None
        self.h = self.rax.shape[-1]

    def copy(self, src, dst, slot, to):
        return rdma(src, dst, self.ss.at[self.a, slot], self.rs.at[self.a, slot], to)

    def wait(self, ref, slot):
        y, x, c, z = coords()
        self.copy(ref, ref, slot, dev(y, 1 - x, c, z)).wait_recv()

    def local(self, j):
        y, x, c, z = coords()
        return pltpu.make_async_copy(self.source(j, c), self.held.at[j], self.ls.at[self.a, j])

    def core(self, j):
        y, x, c, z = coords()
        if self.in_hbm:
            self.local(j).start()
        self.copy(self.source(j, 1 - c), self.rc.at[j], j, dev(y, x, 1 - c, z)).start()

    def cores(self):
        for j in range(4):
            self.core(j)

    def add(self, dst, one, two):
        for i in range(4):
            dst[i] = (one[i].astype(F32) + two[i].astype(F32)).astype(BF)

    def left(self, chip):
        return self.held.at[chip, :, :, pl.ds(0, self.h)]

    def right(self, chip):
        return self.held.at[chip, :, :, pl.ds(self.h, self.h)]

    def first(self):
        y, x, c, z = coords()
        @pl.loop(0, 4)
        def _(j):
            if self.in_hbm:
                self.local(j).wait()
            self.wait(self.rc.at[j], j)
            self.add(self.held.at[j], self.held.at[j] if self.in_hbm else self.source(j, c), self.rc.at[j])
        for xi in range(2):
            self.copy(self.left((1 - y) * 2 + xi), self.ray.at[xi], 4 + xi, dev(1 - y, x, c, z)).start()
        if self.split:
            for yi in range(2):
                self.copy(self.right(yi * 2 + 1 - x), self.rbx.at[yi], 6 + yi, dev(y, 1 - x, c, z)).start()

    def second(self):
        y, x, c, z = coords()
        for xi in range(2):
            self.wait(self.ray.at[xi], 4 + xi)
            d = self.left(y * 2 + xi)
            self.add(d, d, self.ray.at[xi])
        self.copy(self.left(y * 2 + 1 - x), self.rax, 8, dev(y, 1 - x, c, z)).start()
        if self.split:
            for yi in range(2):
                self.wait(self.rbx.at[yi], 6 + yi)
                d = self.right(yi * 2 + x)
                self.add(d, d, self.rbx.at[yi])
            self.copy(self.right((1 - y) * 2 + x), self.rby, 9, dev(1 - y, x, c, z)).start()

    def third(self):
        y, x, c, z = coords()
        me = y * 2 + x
        self.wait(self.rax, 8)
        self.add(self.left(me), self.left(me), self.rax)
        if self.split:
            self.wait(self.rby, 9)
            self.add(self.right(me), self.right(me), self.rby)
        for k in (2, 1, 3):
            zz = across(z, k)
            self.copy(self.held.at[me, zz], self.rz.at[k - 1], 9 + k, dev(y, x, c, zz)).start()

    def last(self):
        y, x, c, z = coords()
        total = self.held[y * 2 + x, z].astype(F32)
        for k in (1, 2, 3):
            self.wait(self.rz.at[k - 1], 9 + k)
            total = total + self.rz[k - 1].astype(F32)
        self.done(total)

    def sent(self):
        y, x, c, z = coords()
        to = dev(y, 1 - x, c, z)
        refs = [self.rc.at[j] for j in range(4)] + [self.ray.at[0], self.ray.at[1]]
        refs += [self.rbx.at[0], self.rbx.at[1]] if self.split else [None, None]
        refs += [self.rax, self.rby] + [self.rz.at[k] for k in range(3)]
        for slot, ref in enumerate(refs):
            if ref is not None:
                self.copy(ref, ref, slot, to).wait_send()


def scatter_sems(n):
    return [DMA((n, 13)), DMA((n, 13)), DMA((n, 4))]


def scatter_bufs(r, n):
    split = (n // 2) % 128 == 0
    h = n // 2 if split else n
    full, pair, one = pltpu.VMEM((4, 4, r, n), BF), pltpu.VMEM((2, 4, r, h), BF), pltpu.VMEM((4, r, h), BF)
    return [full, full, pair, one] + ([pair, one] if split else []) + [pltpu.VMEM((3, r, n), BF)]


def scatter_refs(refs):
    if len(refs) >= 7 and refs[4].shape == refs[2].shape:
        return refs[:7], refs[7:]
    return (*refs[:4], None, None, refs[4]), refs[5:]


def pipelined(jobs):
    out = []
    for t in range(len(jobs) + 3):
        for lag, name in enumerate(("first", "second", "third", "last")):
            if 0 <= t - lag < len(jobs):
                out.append(getattr(jobs[t - lag], name))
    return out


def plans_of(order, table):
    def call(names):
        acts = [table[name] for name in names]
        def run():
            for act in acts:
                act()
        return run
    quiet = {name for name, lists in order.items() if len(lists) == 1}
    return {name: [call(names) if names or name in quiet else None for names in lists] for name, lists in order.items()}


def at_step(t, steps, start=0, every=1):
    for i, step in enumerate(steps):
        if step is None:
            continue

        @pl.when(t == start + i * every)
        def _(step=step):
            step()


FF = 4 * D
HI = lax.Precision.HIGHEST

def dot(a, b):
    return lax.dot_general(a, b, (((1,), (0,)), ((), ())), preferred_element_type=F32)

def dot_nt(a, b):
    return lax.dot_general(a, b, (((1,), (1,)), ((), ())), preferred_element_type=F32)

def dot_tn(a, b):
    return lax.dot_general(a, b, (((0,), (0,)), ((), ())), preferred_element_type=F32)

def iota(shape, dim):
    return lax.broadcasted_iota(jnp.int32, shape, dim)

def over(index, n):
    return jnp.floor((index.astype(F32) + 0.5) * (1.0 / n)).astype(jnp.int32)

def expand_vectors(blocks):
    lane, col = iota((128, D), 0), iota((128, D), 1)
    pick = (lane == col - over(col, 24) * 24).astype(F32).astype(BF)
    spread = dot(blocks.reshape(256, 128), pick)
    row, col = iota((256, D), 0), iota((256, D), 1)
    spread = jnp.where(over(row, 8) == over(col, 24), spread, 0.0)
    vec = jnp.sum(spread.reshape(32, 8, D), 0)
    lane, col = iota((128, FF), 0), iota((128, FF), 1)
    pick = (lane - 32 == col - over(col, 96) * 96).astype(F32).astype(BF)
    spread = dot(blocks.reshape(256, 128), pick)
    row, col = iota((256, FF), 0), iota((256, FF), 1)
    inner = jnp.sum(jnp.where(row == over(col, 96) * 8, spread, 0.0), 0, keepdims=True)
    return vec, inner

def norm_stats(r):
    mean = jnp.mean(r, -1, keepdims=True)
    cen = r - mean
    var = jnp.mean(cen * cen, -1, keepdims=True)
    inv = lax.rsqrt(var + EPS)
    return cen * inv, inv


HBM = pl.BlockSpec(memory_space=pltpu.HBM)
VM = pl.BlockSpec(memory_space=pltpu.VMEM)
ACT = ((4, LEN, D), BF)


def sds(shape, dtype):
    return jax.ShapeDtypeStruct(shape, dtype)


FORWARD_ORDER = {
    "start": ((24, 0, 1, 48, 12, 13, 2, 37, 3, 36, 4, 14, 7, 25, 15, 5, 6, 41, 29, 16, 18, 9, 49, 19, 38, 8, 61, 17, 39, 73, 20, 42, 26, 10, 21, 27, 22, 11, 53, 45, 60, 23, 28,),),
    "spread": ((43,),),
    "load0": ((31, 30,),),
    "group0": ((51,), (), (40,), (32, 50, 52, 62, 65,), (33, 55, 34,), (54,), (35,), (),),
    "load1": ((56, 66,),),
    "group1": ((), (), (63,), (44, 64,), (69,), (57, 67, 46,), (), (47,),),
    "load2": ((72, 75, 68, 58,),),
    "group2": ((), (74,), (), (), (), (), (59,), (70,),),
    "load_wo": ((),),
    "out": ((), (77, 76, 71,), (), (),),
    "load_wi": ((),),
    "inner": ((), (78, 79,), (80,), (81,), (82,), (), (83,), (),),
    "load_wu": ((),),
    "outer": ((),),
    "end": ((),),
}
BACKWARD_ORDER = {
    "norm": ((15, 5,), (10,), (), (),),
    "out": ((),),
    "heads_in": ((20, 0, 6, 11,), (),),
    "pairs0": ((), (16,), (), (), (), (), (1,), (),),
    "sum0": ((),),
    "pairs1": ((7, 17,), (), (25,), (12,), (), (21, 26, 18,), (), (),),
    "sum1": ((2,),),
    "pairs2": ((30, 8,), (), (22,), (), (31,), (), (3,), (23,),),
    "sum2": ((),),
    "small": ((35, 32, 13, 27,),),
    "input": ((36, 40, 24, 28, 33, 41, 14,), (37, 9,), (42, 38, 29,), (34, 19, 43,),),
    "end": ((4, 39, 44,),),
}

def stacked(pair, low):
    zero = jnp.zeros_like(pair)
    return jnp.concatenate([jnp.where(low, pair, zero), jnp.where(low, zero, pair)], 0)


def attn_fwd_pair(s, hp, q_ref, k_ref, v_ref, p_ref, slot, o_ref, keys_ok):
    cols = pl.ds(pl.multiple_of(hp * 128, 128), 128)
    low = iota((LEN, 128), 1) < HD
    st = dot_nt(stacked(k_ref[s, :, cols], low), (q_ref[s, :, cols] * 0.125).astype(BF))
    probs = []
    for h in range(2):
        sh = jnp.where(keys_ok, st[h * LEN : (h + 1) * LEN], NEG)
        e = jnp.exp(sh - jnp.max(sh, 0, keepdims=True))
        p = (e * (1.0 / jnp.sum(e, 0, keepdims=True))).astype(BF)
        p_ref[slot, h] = p
        probs.append(p)
    o_ref[s, :, cols] = dot_tn(jnp.concatenate(probs, 0), stacked(v_ref[s, :, cols], low)).astype(BF)


def gelu_pair(z):
    cdf = 0.5 + 0.5 * lax.erf(z * 0.7071067811865476)
    return z * cdf, cdf + z * (jnp.exp(-0.5 * z * z) * 0.3989422804014327)


def positions(table, s):
    group = (lax.axis_index("dp") * 4 + lax.axis_index("fsdp")) // 4
    col = jnp.sum(jnp.where(iota((8, 16), 1) == group * 2 + s // 2, table[0:8], 0), 1, keepdims=True)
    row = iota((8, 1), 0)
    return jnp.where(row < 4, col, jnp.where(row == 4, 0, -1))


def forward_body(x_ref, m_ref, ints_ref, sh_small, sh_q, sh_k, sh_v, sh_wo, sh_wi, sh_wu,
                 small, w0, w1, w2, wo, wi, wu, q, k, v, p, o, n1, xh1, inv1, g, dg, lo, xh2, inv2, vec_ref, ib_ref, picked_ref,
                 own_qkv, small_v, w_v, wo_v, wi_v, wu_v, q_v, k_v, v_v, p_v, o_v, n1_v, xh1_v, inv1_v, g_v, dg_v, lo_v, xh2_v, inv2_v,
                 gss, grs, gls, asem, wsem, psem, osem):
    parts = []
    for grp in range(3):
        for i, ref in enumerate((sh_q, sh_k, sh_v)):
            cp = pltpu.make_async_copy(ref.at[:, pl.ds(256 * grp, 256)], own_qkv.at[grp, :, pl.ds(256 * i, 256)], asem.at[3 * grp + i])
            cp.start()
            parts.append(cp)
    sems = (gss, grs, gls)
    pairs = ((sh_small, small), (own_qkv.at[0], w0), (own_qkv.at[1], w1), (own_qkv.at[2], w2), (sh_wo, wo), (sh_wi, wi), (sh_wu, wu))
    gs = [Gather(src, dst, sems, a) for a, (src, dst) in enumerate(pairs)]
    g_wi, g_wu = gs[5:]
    def load(i):
        dst = (small_v, w_v.at[0], w_v.at[1], w_v.at[2], wo_v, wi_v, wu_v)[i]
        return pltpu.make_async_copy(pairs[i][1], dst, wsem.at[i])
    table = []
    for i, x in enumerate(gs):
        def take(i=i):
            gs[i].arrived()
            load(i).start()
        table += [x.own_xy, x.own_z, *x.steps(), take]
    plan = plans_of(FORWARD_ORDER, table)
    greet()
    for cp in parts:
        cp.wait()
    plan["start"][0]()
    load(0).wait()
    plan["spread"][0]()
    vec, inner = expand_vectors(small_v[...].reshape(32, 32, 128)[:, 24:, :])
    vec_ref[...] = vec
    ib_ref[...] = inner
    outs = [(q_v, q), (k_v, k), (v_v, v), (o_v, o), (n1_v, n1), (xh1_v, xh1), (inv1_v, inv1), (g_v, g), (dg_v, dg), (lo_v, lo), (xh2_v, xh2), (inv2_v, inv2)]
    def put(a, s):
        return pltpu.make_async_copy(outs[a][0].at[s], outs[a][1].at[s], osem.at[a, s])
    def put_p(t):
        s, hp = lax.rem(t, 8) // 2, (t // 8) * 2 + lax.rem(t, 2)
        return pltpu.make_async_copy(p_v.at[lax.rem(t, 4)], p.at[s, pl.ds(hp * 2, 2)], psem.at[lax.rem(t, 4)])
    for grp in range(3):
        plan[f"load{grp}"][0]()
        load(1 + grp).wait()
        @pl.loop(0, 4)
        def _(s, grp=grp):
            at_step(s, plan[f"group{grp}"][0::2])
            t = dot(x_ref[s], w_v[grp])
            cols = slice(256 * grp, 256 * grp + 256)
            for j, ref in enumerate((q_v, k_v, v_v)):
                part = t[:, 256 * j : 256 * j + 256]
                if j != 1:
                    part = part + vec_ref[0 if j == 0 else 1][None, cols]
                ref[s, :, cols] = part.astype(BF)
            count = jnp.sum(m_ref[pl.ds(s, 1), :], -1, keepdims=True)
            keys_ok = iota((LEN, 1), 0) < count
            @pl.loop(0, 2)
            def _(i):
                t = grp * 8 + s * 2 + i
                @pl.when(i == 1)
                def _():
                    at_step(s, plan[f"group{grp}"][1::2])
                @pl.when(t >= 4)
                def _():
                    put_p(t - 4).wait()
                attn_fwd_pair(s, grp * 2 + i, q_v, k_v, v_v, p_v, lax.rem(t, 4), o_v, keys_ok)
                put_p(t).start()
            if grp == 2:
                for a in range(4):
                    put(a, s).start()
    plan["load_wo"][0]()
    load(4).wait()
    @pl.loop(0, 4)
    def _(s):
        r1 = x_ref[s].astype(F32) + dot(o_v[s], wo_v[...]) + vec_ref[2][None]
        xh, inv = norm_stats(r1)
        xh1_v[s] = xh.astype(BF)
        inv1_v[s] = jnp.broadcast_to(inv, (LEN, 128))
        n1_v[s] = (xh * vec_ref[3][None] + vec_ref[4][None]).astype(BF)
        at_step(s, plan["out"])
        for a in (4, 5, 6):
            put(a, s).start()
    plan["load_wi"][0]()
    load(5).wait()
    @pl.loop(0, 4)
    def _(s):
        @pl.loop(0, 2)
        def _(j):
            at_step(s * 2 + j, plan["inner"])
            cols = pl.ds(pl.multiple_of(j * 2 * D, 2 * D), 2 * D)
            act, slope = gelu_pair(dot(n1_v[s], wi_v[:, cols]) + ib_ref[:, cols])
            g_v[s, :, cols] = act.astype(BF)
            dg_v[s, :, cols] = slope.astype(BF)
        put(7, s).start()
        put(8, s).start()
    plan["load_wu"][0]()
    load(6).wait()
    plan["outer"][0]()
    @pl.loop(0, 4)
    def _(s):
        r2 = n1_v[s].astype(F32) + dot(g_v[s], wu_v[...]) + vec_ref[5][None]
        xh, inv = norm_stats(r2)
        xh2_v[s] = xh.astype(BF)
        inv2_v[s] = jnp.broadcast_to(inv, (LEN, 128))
        out = (xh * vec_ref[6][None] + vec_ref[7][None]).astype(BF)
        lo_v[s] = out
        picked_ref[s] = dot((iota((8, LEN), 1) == positions(ints_ref[...], s)).astype(F32).astype(BF), out).astype(BF)
        for a in (9, 10, 11):
            put(a, s).start()
    for t in range(20, 24):
        put_p(t).wait()
    for s in range(4):
        for a in range(12):
            put(a, s).wait()
    for x in gs:
        x.sent()


def forward(x, mask, ints, shards, cid):
    small, q, k, v, wo, wi, wu = shards
    full = [((32 * s.shape[0], n), BF) for s, n in ((small, 128), (q, D), (q, D), (q, D), (wo, D), (wi, FF), (wu, D))]
    probs, stat, big = ((4, H, LEN, LEN), BF), ((4, LEN, 128), F32), ((4, LEN, FF), BF)
    acts = [ACT, ACT, ACT, probs, ACT, ACT, ACT, stat, big, big, ACT, ACT, stat]
    outs = full + acts + [((8, D), F32), ((1, FF), F32), ((4, 8, D), BF)]
    slots = [((4, 2, LEN, LEN), BF) if a is probs else a for a in acts]
    return pl.pallas_call(
        forward_body, name="layer_forward", out_shape=[sds(*o) for o in outs],
        in_specs=[VM] * 3 + [HBM] * 7, out_specs=[HBM] * 20 + [VM] * 3,
        scratch_shapes=[pltpu.VMEM(*o) for o in [((3, 24, D), BF), full[0], ((3, D, D), BF)] + full[4:] + slots]
        + gather_sems(7) + [DMA((9,)), DMA((7,)), DMA((4,)), DMA((12, 4))],
        compiler_params=pltpu.CompilerParams(collective_id=cid, has_side_effects=True, vmem_limit_bytes=61 << 20),
    )(x, mask, ints, *shards)


def norm_back(dy, xh, inv, gain):
    c = dy * gain
    return (c - jnp.mean(c, -1, keepdims=True) - xh * jnp.mean(c * xh, -1, keepdims=True)) * inv


def bwd1_body(add_ref, ints_ref, vec_ref, og, xh2, inv2, g, dg, n1, wi, wu,
              gu_ref, gi, dn1, sums_ref, sumi_ref,
              og_v, xh2_v, inv2_v, g_v, dg_v, n1_v, wi_v, wu_v, d2_v, dn1_v, gu_v, gi_v, sss, srs, sls, esem, isem, osem, *bufs):
    def early(s):
        return [pltpu.make_async_copy(a.at[s], b.at[s], esem.at[i, s]) for i, (a, b) in enumerate(((og, og_v), (xh2, xh2_v), (inv2, inv2_v)))]
    for s in range(4):
        for cp in early(s):
            cp.start()
    ins = [(g, g_v), (wu, wu_v), (dg, dg_v), (wi, wi_v), (n1, n1_v)]
    loads = [pltpu.make_async_copy(a, b, isem.at[i]) for i, (a, b) in enumerate(ins)]
    loads[0].start()
    sems = (sss, srs, sls)
    greet()
    jobs = []
    for t in range(3):
        own, bufs = scatter_refs(bufs)
        def source(j, c, t=t):
            return gu_v.at[j, c, :, :, pl.ds(256 * t, 256)]
        def done(total, t=t):
            gu_ref[:, pl.ds(256 * t, 256)] = total
        jobs.append(Scatter(source, own, sems, t, done))
    sums_ref[...] = jnp.zeros_like(sums_ref)
    sumi_ref[...] = jnp.zeros_like(sumi_ref)
    @pl.loop(0, 4)
    def _(s):
        place = jnp.sum(jnp.where(iota((8, 8), 0) == iota((8, 8), 1), positions(ints_ref[...], s), 0), 0, keepdims=True)
        hit = (iota((LEN, 8), 0) == place).astype(F32)
        add = add_ref[s]
        high = add.astype(BF)
        parts = jnp.concatenate([high.astype(F32), add - high.astype(F32)], 0).astype(BF)
        extra = dot(jnp.concatenate([hit, hit], 1).astype(BF), parts)
        for cp in early(s):
            cp.wait()
        dy = og_v[s].astype(F32) + extra
        xh = xh2_v[s].astype(F32)
        dr2 = norm_back(dy, xh, inv2_v[s][:, 0:1], vec_ref[6][None])
        sums_ref[0] += jnp.sum(dy * xh, 0)
        sums_ref[1] += jnp.sum(dy, 0)
        sums_ref[2] += jnp.sum(dr2, 0)
        d2_v[pl.ds(s * LEN, LEN)] = dr2.astype(BF)
        dn1_v[s] = dr2
    loads[0].wait()
    loads[1].start()
    loads[2].start()
    steps = pipelined(jobs)
    for t, job in enumerate(jobs):
        @pl.loop(0, 2)
        def _(j, t=t):
            cols = pl.ds(pl.multiple_of(j * 2 * D, 2 * D), 2 * D)
            part = dot_tn(g_v[:, :, cols].reshape(4 * LEN, 2 * D), d2_v[:, pl.ds(256 * t, 256)])
            gu_v[pl.ds(2 * j, 2), :, :, :, pl.ds(256 * t, 256)] = part.astype(BF).reshape(2, 2, 4, 96, 256)
        job.cores()
        if t == 1:
            steps[0]()
    loads[3].start()
    loads[1].wait()
    loads[2].wait()
    steps = steps[1:] + [None]
    def put(s):
        return pltpu.make_async_copy(dn1_v.at[s], dn1.at[s], osem.at[s])
    loads[3].wait()
    loads[4].start()
    @pl.loop(0, 4)
    def _(s):
        for half in range(2):
            at_step(s, steps[half:9:3] if half else steps[0:9:3])
            cols = pl.ds(half * 2 * D, 2 * D)
            dz = dot_nt(d2_v[pl.ds(pl.multiple_of(s * LEN, LEN), LEN)], wu_v[cols, :]) * dg_v[s, :, cols].astype(F32)
            dz = dz.astype(BF)
            sumi_ref[0:1, cols] += jnp.sum(dz.astype(F32), 0, keepdims=True)
            dg_v[s, :, cols] = dz
        at_step(s, steps[2:9:3])
        dn1_v[s] += dot_nt(dg_v[s], wi_v[...])
        put(s).start()
    loads[4].wait()
    def puti(j):
        cols = pl.ds(pl.multiple_of(j * D, D), D)
        return pltpu.make_async_copy(gi_v.at[:, cols], gi.at[:, cols], osem.at[4 + j])
    @pl.loop(0, 4)
    def _(j):
        cols = pl.ds(pl.multiple_of(j * D, D), D)
        gi_v[:, cols] = dot_tn(n1_v[...].reshape(4 * LEN, D), dg_v[:, :, cols].reshape(4 * LEN, D)).astype(BF)
        puti(j).start()
        at_step(j, steps[9:])
    for i in range(4):
        put(i).wait()
        puti(i).wait()
    for job in jobs:
        job.sent()


def bwd1(og, add, ints, xh2, inv2, vec, g, dg, n1, wi, wu, cid):
    outs = [((96, D), F32), ((D, FF), BF), ((4, LEN, D), F32), ((8, D), F32), ((8, FF), F32)]
    big = ((4, LEN, FF), BF)
    scratch = [ACT, ACT, ((4, LEN, 128), F32), big, big, ACT, ((D, FF), BF), ((FF, D), BF), ((4 * LEN, D), BF), ((4, LEN, D), F32), ((4, 2, 4, 96, D), BF), ((D, FF), BF)]
    return pl.pallas_call(
        bwd1_body, name="feed_forward_backward", out_shape=[sds(*o) for o in outs],
        in_specs=[VM] * 3 + [HBM] * 8, out_specs=[VM, HBM, HBM, VM, VM],
        scratch_shapes=[pltpu.VMEM(*s) for s in scratch] + scatter_sems(3) + [DMA((3, 4)), DMA((5,)), DMA((8,))] + scatter_bufs(96, 256) * 3,
        compiler_params=pltpu.CompilerParams(collective_id=cid, has_side_effects=True, vmem_limit_bytes=61 << 20),
    )(add, ints, vec, og, xh2, inv2, g, dg, n1, wi, wu)


def attn_bwd_pair(s, hp, q_ref, k_ref, v_ref, p_ref, slot, do_ref, dqkv_ref):
    cols = pl.ds(pl.multiple_of(hp * 128, 128), 128)
    rows = pl.ds(pl.multiple_of(s * LEN, LEN), LEN)
    do2 = do_ref[rows, cols]
    low = iota((LEN, 128), 1) < HD
    dpt = dot_nt(stacked(v_ref[s, :, cols], low), do2)
    grads = []
    for h in range(2):
        d = dpt[h * LEN : (h + 1) * LEN]
        pf = p_ref[slot, h].astype(F32)
        grads.append((pf * (d - jnp.sum(pf * d, 0, keepdims=True))).astype(BF))
    ds = jnp.concatenate(grads, 0)
    dv = dot(p_ref[slot].reshape(2 * LEN, LEN), do2)
    dk = dot(ds, q_ref[s, :, cols])
    dq = dot_tn(ds, stacked(k_ref[s, :, cols], low))
    at = (hp // 2) * D + lax.rem(hp, 2) * 128
    def out(i):
        return pl.ds(pl.multiple_of(at + 256 * i, 128), 128)
    dqkv_ref[rows, out(0)] = (dq * 0.125).astype(BF)
    dqkv_ref[rows, out(1)] = (jnp.where(low, dk[:LEN], dk[LEN:]) * 0.125).astype(BF)
    dqkv_ref[rows, out(2)] = jnp.where(low, dv[:LEN], dv[LEN:]).astype(BF)


def bwd2_body(dn1, xh1, inv1, vec_ref, x, q, k, v, p, o, w0, w1, w2, wo, gi, grw_ref, s2_ref, si_ref,
              ggq, ggk, ggv, ggo, ggi, ggs, dx,
              dn1_v, xh1_v, inv1_v, x_v, q_v, k_v, v_v, o_v, p_v, wqkv_v, wo_v, sums_v, sumq_v, d1_v, do_v, dqkv_v, go_v, gg_v, gsm_v,
              sss, srs, sls, esem, isem, psem, osem, *bufs):
    def early(s):
        return [pltpu.make_async_copy(a.at[s], b.at[s], esem.at[i, s]) for i, (a, b) in enumerate(((dn1, dn1_v), (xh1, xh1_v), (inv1, inv1_v)))]
    ins = [(o, o_v), (wo, wo_v), (q, q_v), (k, k_v), (v, v_v), (x, x_v)] + [(w, wqkv_v.at[:, pl.ds(D * i, D)]) for i, w in enumerate((w0, w1, w2))]
    loads = [pltpu.make_async_copy(a, b, isem.at[i]) for i, (a, b) in enumerate(ins)]
    for s in range(4):
        for cp in early(s):
            cp.start()
    sems = (sss, srs, sls)
    greet()
    jobs = []
    def add_job(source, done, in_hbm=False):
        nonlocal bufs
        own, bufs = scatter_refs(bufs)
        jobs.append(Scatter(source, own, sems, len(jobs), done, in_hbm))
    for t in range(4):
        def done(total, t=t):
            ggi[:, pl.ds(t * D, D)] = total
        add_job(lambda j, c, t=t: gi.at[j, c, :, :, pl.ds(t * D, D)], done, True)
    def done_o(total):
        ggo[...] = total
    add_job(lambda j, c: go_v.at[j, c], done_o)
    for t in range(3):
        def done(total, t=t):
            for i, ref in enumerate((ggq, ggk, ggv)):
                ref[:, pl.ds(256 * t, 256)] = total[:, 256 * i : 256 * i + 256]
        add_job(lambda j, c, t=t: gg_v.at[t, j, c], done)
    def done_s(total):
        ggs[...] = total
    add_job(lambda j, c: gsm_v.at[j, c], done_s)
    plan = plans_of(BACKWARD_ORDER, [act for job in jobs for act in (job.cores, job.first, job.second, job.third, job.last)])
    sums_v[...] = jnp.zeros_like(sums_v)
    sumq_v[...] = jnp.zeros_like(sumq_v)
    @pl.loop(0, 4)
    def _(s):
        for cp in early(s):
            cp.wait()
        at_step(s, plan["norm"])
        dy = dn1_v[s]
        xh = xh1_v[s].astype(F32)
        dr1 = norm_back(dy, xh, inv1_v[s][:, 0:1], vec_ref[3][None])
        sums_v[0] += jnp.sum(dy * xh, 0)
        sums_v[1] += jnp.sum(dy, 0)
        sums_v[2] += jnp.sum(dr1, 0)
        dn1_v[s] = dr1
        d1_v[pl.ds(s * LEN, LEN)] = dr1.astype(BF)
        @pl.when(s == 1)
        def _():
            for cp in loads[:2]:
                cp.start()
        @pl.when(s == 3)
        def _():
            for cp in loads[2:5]:
                cp.start()
    plan["out"][0]()
    for cp in loads[:2]:
        cp.wait()
    go_v[...] = dot_tn(o_v[...].reshape(4 * LEN, D), d1_v[...]).astype(BF).reshape(4, 2, 4, 24, D)
    @pl.loop(0, 2)
    def _(i):
        at_step(i, plan["heads_in"])
        rows = pl.ds(pl.multiple_of(i * 2 * LEN, 2 * LEN), 2 * LEN)
        do_v[rows] = dot_nt(d1_v[rows], wo_v[...]).astype(BF)
    for cp in loads[2:5]:
        cp.wait()
    loads[5].start()
    def probs(t):
        hp, s = t // 4, lax.rem(t, 4)
        return pltpu.make_async_copy(p.at[s, pl.ds(hp * 2, 2)], p_v.at[lax.rem(t, 2)], psem.at[lax.rem(t, 2)])
    probs(0).start()
    for grp in range(3):
        @pl.loop(0, 8)
        def _(i, grp=grp):
            t = grp * 8 + i
            @pl.when(t + 1 < 24)
            def _():
                probs(t + 1).start()
            at_step(i, plan[f"pairs{grp}"])
            probs(t).wait()
            attn_bwd_pair(lax.rem(t, 4), t // 4, q_v, k_v, v_v, p_v, lax.rem(t, 2), do_v, dqkv_v)
        if grp == 0:
            loads[5].wait()
            for cp in loads[6:]:
                cp.start()
        plan[f"sum{grp}"][0]()
        d = dqkv_v[:, pl.ds(D * grp, D)]
        sumq_v[grp : grp + 1] = jnp.sum(d.astype(F32), 0, keepdims=True)
        gg_v[grp] = dot_tn(x_v[...].reshape(4 * LEN, D), d).astype(BF).reshape(4, 2, 4, 24, D)
    plan["small"][0]()
    gsm_v[...] = small_grads(grw_ref[...], sums_v[...], s2_ref[...], sumq_v[...], si_ref[...]).reshape(4, 2, 4, 32, 128)
    for cp in loads[6:]:
        cp.wait()
    def put(s):
        return pltpu.make_async_copy(dn1_v.at[s], dx.at[s], osem.at[s])
    @pl.loop(0, 4)
    def _(s):
        rows = pl.ds(pl.multiple_of(s * LEN, LEN), LEN)
        at_step(s, plan["input"])
        dn1_v[s] += dot_nt(dqkv_v[rows], wqkv_v[...])
        put(s).start()
    plan["end"][0]()
    for s in range(4):
        put(s).wait()
    for job in jobs:
        job.sent()


def small_grads(grw, s1, s2, sq, si):
    by_kind = [jnp.concatenate([sq[grp : grp + 1, 256 * i : 256 * i + 256] for grp in range(3)], 1) for i in (0, 2)]
    vec = jnp.concatenate(by_kind + [s1[2:3], s1[0:1], s1[1:2], s2[2:3], s2[0:1], s2[1:2]], 0)
    row, col = iota((256, D), 0), iota((256, D), 1)
    tiled = jnp.broadcast_to(vec[None], (32, 8, D)).reshape(256, D)
    part = jnp.where(over(row, 8) == over(col, 24), tiled, 0.0).astype(BF)
    lane, col = iota((128, D), 0), iota((128, D), 1)
    pick = (lane == col - over(col, 24) * 24).astype(F32).astype(BF)
    out = dot_nt(part, pick).reshape(32, 8, 128)
    row, col = iota((32, FF), 0), iota((32, FF), 1)
    part = jnp.where(row == over(col, 96), si[0:1], 0.0).astype(BF)
    lane, col = iota((128, FF), 0), iota((128, FF), 1)
    pick = (lane - 32 == col - over(col, 96) * 96).astype(F32).astype(BF)
    inner = dot_nt(part, pick)
    out = out + jnp.where(iota((32, 8, 128), 1) == 0, inner[:, None, :], 0.0)
    return jnp.concatenate([grw.reshape(32, 24, 128), out], 1).astype(BF)


def bwd2(dn1, xh1, inv1, vec, x, q, k, v, p, o, w, wo, gi, grw, s2, si, cid):
    own = ((24, D), F32)
    outs = [own, own, own, own, ((24, FF), F32), ((32, 128), F32), ((4, LEN, D), F32)]
    six = ((4, 2, 4, 24, D), BF)
    scratch = [((4, LEN, D), F32), ACT, ((4, LEN, 128), F32), ACT, ACT, ACT, ACT, ACT, ((2, 2, LEN, LEN), BF), ((D, 3 * D), BF), ((D, D), BF),
               ((8, D), F32), ((8, D), F32), ((4 * LEN, D), BF), ((4 * LEN, D), BF), ((4 * LEN, 3 * D), BF), six, ((3,) + six[0], BF), ((4, 2, 4, 32, 128), BF)]
    return pl.pallas_call(
        bwd2_body, name="attention_backward", out_shape=[sds(*s) for s in outs],
        in_specs=[HBM] * 3 + [VM] + [HBM] * 11 + [VM] * 3, out_specs=[VM] * 6 + [HBM],
        scratch_shapes=[pltpu.VMEM(*s) for s in scratch] + scatter_sems(9) + [DMA((3, 4)), DMA((9,)), DMA((2,)), DMA((4,))]
        + scatter_bufs(24, D) * 8 + scatter_bufs(32, 128),
        compiler_params=pltpu.CompilerParams(collective_id=cid, has_side_effects=True, vmem_limit_bytes=61 << 20),
    )(dn1, xh1, inv1, vec, x, q, k, v, p, o, *w, wo, gi.reshape(4, 2, 4, 24, FF), grw, s2, si)


def finish_body(small_ref, pair_ref, *refs):
    n = (len(refs) - 11) // 2
    grw, pair, inner, *vecs = refs[2 * n :]
    for a, b in zip(refs[:n], refs[n : 2 * n]):
        b[...] = a[...]
    grw[...] = small_ref[0:24]
    pair[...] = pair_ref[0, 0:2]
    inner[...] = small_ref[24, 32:128]
    for i, ref in enumerate(vecs):
        ref[...] = small_ref[24 + i, 0:24]


def finish(small, pair, more):
    tail = [((24, 128), F32), ((2,), F32), ((96,), F32)] + [((24,), F32)] * 8
    outs = pl.pallas_call(
        finish_body, name="results", out_shape=[sds(a.shape, a.dtype) for a in more] + [sds(*t) for t in tail],
        in_specs=[VM] * (2 + len(more)), out_specs=[VM] * (len(more) + 11),
    )(small, pair, *more)
    return outs[: len(more)], outs[len(more) :]


def exact(a, b, dims=((1,), (0,))):
    return lax.dot_general(a, b, (dims, ((), ())), preferred_element_type=F32, precision=HI)

def as_f(cond):
    return cond.astype(F32)

def greet_all():
    me = lax.axis_index("dp") * 4 + lax.axis_index("fsdp")
    bar = pltpu.get_barrier_semaphore()
    @pl.loop(1, 32)
    def _(k):
        t = lax.rem(me + k, 32)
        pl.semaphore_signal(bar, inc=1, device_id=(t // 4, lax.rem(t, 4)), device_id_type=MESH)
    pl.semaphore_wait(bar, 31)

def loss_body(picked_ref, ints_ref, emb, vb, qe, small,
              add_ref, grw_ref, pair_ref, ge, gvb_ref,
              emb_ref, vb_ref, qe_ref, small_ref, ge_ref, isem, own_ref, rows_ref, lt_ref, st_ref, all_ref, dh_ref, dhout_ref, gss, grs, gls, sss, srs, sls, xs, xr, *bufs):
    me = lax.axis_index("dp") * 4 + lax.axis_index("fsdp")
    VS = emb_ref.shape[0]
    loads = [pltpu.make_async_copy(a, b, isem.at[i]) for i, (a, b) in enumerate(
        ((small, small_ref), (qe, qe_ref), (vb, vb_ref), (emb, emb_ref)))]
    for cp in loads:
        cp.start()
    greet_all()
    own_ref[...] = picked_ref[:, 0:4, :].astype(F32).reshape(16, D).astype(BF)
    g = Gather(own_ref, rows_ref, (gss, grs, gls), 0)
    g.own()
    for cp in loads:
        cp.wait()
    cls = picked_ref[:, 4:5, :].astype(F32).reshape(4, D)
    cls8 = jnp.concatenate([cls, jnp.zeros((4, D), F32)], 0)
    rw = small_ref[:, 0:24, :].reshape(D, 128)
    row8, lane8 = iota((8, 128), 0), iota((8, 128), 1)
    qpick = as_f(jnp.logical_and(iota((8, 16), 1) == (me // 4) * 2 + iota((8, 16), 0) // 2, iota((8, 16), 0) < 4))
    qe_own = exact(qpick, qe_ref[...])
    score = jnp.sum(dot(cls8.astype(BF), rw) * qe_own, -1, keepdims=True)
    st_ref[12:13] = jnp.sum(jnp.where(row8 == lane8, score, 0.0), 0, keepdims=True)
    r512 = iota((16, 512), 1)
    s_of = r512 >> 2
    q_of = (s_of >> 4) * 2 + ((s_of & 3) >> 1)
    spread = exact(ints_ref[4:8, :].astype(F32), as_f(iota((4, 512), 0) == (iota((4, 512), 1) & 3)), ((0,), (0,)))
    ids = jnp.sum(jnp.where(iota((16, 512), 0) == q_of, spread, 0.0), 0, keepdims=True)
    local = ids.astype(jnp.int32) - me * VS
    q16, s16 = iota((16, 128), 0), iota((16, 128), 1)
    mine = q16 == (s16 >> 4) * 2 + ((s16 & 3) >> 1)
    s8 = iota((8, 128), 1)
    slot_pick = as_f(iota((8, 128), 0) == ((s8 >> 2) & 3) * 2 + (s8 & 1))
    ok16 = jnp.logical_and(mine, exact(ints_ref[8:16, :].astype(F32), slot_pick, ((0,), (0,))) > 0.5)
    valid_of = jnp.sum(ok16.astype(F32), 0, keepdims=True)
    steps = g.steps()
    for i in (3, 0, 1, 2, 4, 5, 6, 7, 8):
        steps[i]()
    g.arrived()
    g.sent()
    rows = rows_ref[...]
    bias = jnp.where(iota((16, VS), 0) == 0, vb_ref[...][None].astype(F32), 0.0).astype(BF)
    lt = dot_nt(emb_ref[...], rows) + dot_tn(bias, jnp.ones((16, 512), BF))
    hit = iota((VS, 512), 0) == local
    peak = jnp.max(lt, 0, keepdims=True)
    e = jnp.exp(lt - peak)
    lt_ref[...] = e
    total = jnp.sum(e, 0, keepdims=True)
    target = jnp.sum(jnp.where(hit, lt, 0.0), 0, keepdims=True)
    for a in range(4):
        cols = slice(a * 128, a * 128 + 128)
        st_ref[a:a + 1] = peak[:, cols]
        st_ref[4 + a:5 + a] = total[:, cols]
        st_ref[8 + a:9 + a] = target[:, cols]
    sends = []
    for k in range(1, 32):
        t = lax.rem(me + k, 32)
        cp = rdma(st_ref, all_ref.at[me], xs.at[k], xr.at[k], (t // 4, lax.rem(t, 4)))
        cp.start()
        sends.append(cp)
    all_ref[me] = st_ref[...]
    for k in range(1, 32):
        f = lax.rem(me + 32 - k, 32)
        rdma(st_ref, all_ref.at[f], xs.at[k], xr.at[k], (f // 4, lax.rem(f, 4))).wait_recv()
    peaks = all_ref[:, 0:4, :]
    top = jnp.max(peaks, 0)
    tot = jnp.sum(all_ref[:, 4:8, :] * jnp.exp(peaks - top[None]), 0)
    lse = top + jnp.log(tot)
    logp = jnp.sum(all_ref[:, 8:12, :], 0) - lse
    i0, i1 = iota((128, 128), 0), iota((128, 128), 1)
    logp8 = jnp.concatenate([logp, jnp.zeros((4, 128), F32)], 0)
    spread = exact(logp8, 0.25 * as_f((i0 >> 2) == (i1 & 31)))
    seq_ll = jnp.sum(jnp.where((lane8 >> 5) == row8, spread, 0.0), 0, keepdims=True)
    spread = exact(all_ref[:, 12, :], as_f(i0 == (i1 & 3)))
    retrieval = jnp.sum(jnp.where((iota((32, 128), 1) >> 2) == iota((32, 128), 0), spread, 0.0), 0, keepdims=True)
    joint = retrieval + seq_ll
    def slot_lse(v):
        m = jnp.max(jnp.where(ok16, v, NEG), -1, keepdims=True)
        return m + jnp.log(jnp.sum(jnp.where(ok16, jnp.exp(v - m), 0.0), -1, keepdims=True))
    def to_seq(v):
        return jnp.sum(jnp.where(mine, v, 0.0), 0, keepdims=True)
    joint_lse, prior_lse = slot_lse(joint), slot_lse(retrieval)
    ok = valid_of > 0.5
    post = jnp.where(ok, jnp.exp(joint - to_seq(joint_lse)), 0.0)
    prior = jnp.where(ok, jnp.exp(retrieval - to_seq(prior_lse)), 0.0)
    pair = jnp.sum(jnp.where(q16 == (me // 4) * 2 + s16, joint_lse - prior_lse, 0.0), 0, keepdims=True)
    pair_ref[...] = jnp.broadcast_to(pair, (8, 128))
    d_score = LOSS_WEIGHT * (prior - post)
    scale = exact(jnp.broadcast_to(-LOSS_WEIGHT * post / 4.0, (8, 128)), as_f(iota((128, 512), 0) == (iota((128, 512), 1) >> 2)))[0:1]
    lse_row = jnp.concatenate([lse[a:a + 1] for a in range(4)], 1)
    dl = jnp.where(hit, scale, 0.0) - lt_ref[...] * (scale * jnp.exp(peak - lse_row))
    gvb_ref[...] = jnp.broadcast_to(jnp.sum(dl, -1, keepdims=True), (VS, 128)).T[0]
    db = dl.astype(BF)
    dh_ref[...] = dot_tn(db, emb_ref[...]).astype(BF).reshape(4, 2, 4, 16, D)
    def done(total):
        dhout_ref[...] = total
    sc = Scatter(lambda j, c: dh_ref.at[j, c], scatter_refs(bufs)[0], (sss, srs, sls), 0, done)
    for j in range(4):
        sc.core(j)
    du = jnp.sum(jnp.where(jnp.logical_and(lane8 == me * 4 + row8, row8 < 4), d_score, 0.0), -1, keepdims=True) * qe_own
    grw_ref[...] = exact(cls8, du, ((0,), (0,)))
    dcls = exact(du, rw.astype(F32), ((1,), (1,)))
    add_ref[...] = jnp.zeros_like(add_ref)
    for l in range(4):
        add_ref[l, 4:5] = dcls[l:l + 1]
    sc.first()
    ge_ref[...] = dot(db, rows)
    out = pltpu.make_async_copy(ge_ref, ge, isem.at[4])
    out.start()
    sc.second()
    sc.third()
    sc.last()
    sc.sent()
    for l in range(4):
        add_ref[l, 0:4] = dhout_ref[4 * l:4 * l + 4]
    for cp in sends:
        cp.wait_send()
    out.wait()

def loss_call(picked, ints, emb, vb, qe, small, cid):
    VS = emb.shape[0]
    outs = [((4, 8, D), F32), ((D, 128), F32), ((8, 128), F32), ((VS, D), F32), ((VS,), F32)]
    args = (picked, ints, emb, vb, qe, small)
    return pl.pallas_call(loss_body, name="slot_loss", out_shape=[jax.ShapeDtypeStruct(s, t) for s, t in outs],
        in_specs=[VM] * 2 + [HBM] * 4, out_specs=[VM] * 3 + [HBM, VM],
        scratch_shapes=[pltpu.VMEM(a.shape, a.dtype) for a in (emb, vb, qe, small)] + [pltpu.VMEM((VS, D), F32), DMA((7,)), pltpu.VMEM((16, D), BF), pltpu.VMEM((512, D), BF), pltpu.VMEM((VS, 512), F32), pltpu.VMEM((16, 128), F32),
            pltpu.VMEM((32, 16, 128), F32), pltpu.VMEM((4, 2, 4, 16, D), BF), pltpu.VMEM((16, D), F32),
            *gather_sems(1), *scatter_sems(1), DMA((32,)), DMA((32,))] + scatter_bufs(16, D),
        compiler_params=pltpu.CompilerParams(collective_id=cid, has_side_effects=True, vmem_limit_bytes=58 << 20))(*args)


def linked_body(hidden_in, token_mask, out_grad, query_embed, slot_valid, target_ids, target_pos,
                qw, kw, vw, ow, iw, uw, rw, qb, vb, ob, ga, sa, ib, ub, gb, sb, embedding, vocab_bias):
    block = jnp.pad(jnp.stack([qb, vb, ob, ga, sa, ub, gb, sb]), ((0, 0), (0, 104)))
    block = jnp.concatenate([rw, block + jnp.pad(ib[None], ((0, 7), (32, 0)))], 0)
    ints = jnp.concatenate([target_pos.T, target_ids.T, slot_valid.T], 0)
    small, w0, w1, w2, wo, wi, wu, q, k, v, p, o, n1, xh1, inv1, g, dg, out_seq, xh2, inv2, vec, inner, picked = forward(
        hidden_in, token_mask, ints, (block, qw, kw, vw, ow, iw, uw), 0)
    add, grw, pair, ge, gvb = loss_call(
        picked, ints, embedding, vocab_bias, query_embed, small.reshape(32, 32, 128), 1)
    gu, gi, dn1, s2, si = bwd1(out_grad, add, ints, xh2, inv2, vec, g, dg, n1, wi, wu, 2)
    gq, gk, gv, go, gi, gsm, dx = bwd2(dn1, xh1, inv1, vec, hidden_in, q, k, v, p, o, (w0, w1, w2), wo, gi, grw, s2, si, 3)
    (gu, gi, gq, gk, gv, go, gvb), (grw, pair, gib, *vecs) = finish(
        gsm, pair, (gu, gi, gq, gk, gv, go, gvb))
    return (out_seq, pair, dx, gq, gk, gv, go, gi, gu, grw, *vecs[:5], gib, *vecs[5:], ge, gvb)


def solution(mesh):
    placed = (
        P(AXES, None, None),
        P(AXES, None),
        P(AXES, None, None),
        P(),
        P(),
        P(),
        P(),
        P(AXES, None),
        P(AXES, None),
        P(AXES, None),
        P(AXES, None),
        P(AXES, None),
        P(AXES, None),
        P(AXES, None),
        P(AXES),
        P(AXES),
        P(AXES),
        P(AXES),
        P(AXES),
        P(AXES),
        P(AXES),
        P(AXES),
        P(AXES),
        P(AXES, None),
        P(AXES),
    )
    own = mesh.shape["dp"] == 8 and mesh.shape["fsdp"] == 4
    return jax.shard_map(
        linked_body if own else plain_body,
        mesh=mesh,
        in_specs=placed,
        out_specs=(
            P(AXES, None, None),
            P(AXES),
            P(AXES, None, None),
            P(AXES, None),
            P(AXES, None),
            P(AXES, None),
            P(AXES, None),
            P(AXES, None),
            P(AXES, None),
            P(AXES, None),
            P(AXES),
            P(AXES),
            P(AXES),
            P(AXES),
            P(AXES),
            P(AXES),
            P(AXES),
            P(AXES),
            P(AXES),
            P(AXES, None),
            P(AXES),
        ),
        check_vma=False,
    )
```
